32 devices in a mesh: seq: 8 (over y, x, core), ft: 4 (over z).
Axes of the slice: x: 2, y: 2, z: 4, core: 2. Of those that a mesh axis runs over, the one named last changes fastest.
Arguments:
- video: bfloat16 [8, 8, 196, 768], P('seq', None, 'ft'), may hold values from -6 to 6
- class_token: bfloat16 [8, 768], P('seq'), may hold values from -6 to 6
- frame_clip: int32 [8, 8], P('seq'), may hold values from 0 to 2, never falling along the last dimension, each value on 1 to 4 neighbouring positions
- patch_clip: int32 [8, 196], P('seq'), may hold values from 0 to 3, never falling along the last dimension, each value on 1 to 98 neighbouring positions
- padding: int32 [8, 196], P('seq'), may hold values 0 or 1
- time_gain: bfloat16 [768], P('ft'), may hold values from 0.099609375 to 1.8984375
- time_shift: bfloat16 [768], P('ft'), may hold values from -1 to 1
- time_project: bfloat16 [768, 2304], P('ft'), may hold values from -0.21875 to 0.21875
- time_output: bfloat16 [768, 768], P('ft'), may hold values from -0.3125 to 0.3125
- time_output_bias: bfloat16 [768], P('ft'), may hold values from -1 to 1
- time_mixer: bfloat16 [768, 768], P('ft'), may hold values from -0.21875 to 0.21875
- time_mixer_bias: bfloat16 [768], P('ft'), may hold values from -1 to 1
- space_gain: bfloat16 [768], P('ft'), may hold values from 0.099609375 to 1.8984375
- space_shift: bfloat16 [768], P('ft'), may hold values from -1 to 1
- space_project: bfloat16 [768, 2304], P('ft'), may hold values from -0.21875 to 0.21875
- space_output: bfloat16 [768, 768], P('ft'), may hold values from -1.25 to 1.25
- space_output_bias: bfloat16 [768], P('ft'), may hold values from -1 to 1
- feed_gain: bfloat16 [768], P('ft'), may hold values from 0.099609375 to 1.8984375
- feed_shift: bfloat16 [768], P('ft'), may hold values from -1 to 1
- feed_expand: bfloat16 [768, 3072], P('ft'), may hold values from -0.21875 to 0.21875
- feed_expand_bias: bfloat16 [3072], P('ft'), may hold values from -1 to 1
- feed_reduce: bfloat16 [3072, 768], P('ft'), may hold values from -0.109375 to 0.109375
- feed_reduce_bias: bfloat16 [768], P('ft'), may hold values from -1 to 1
- grad_output: bfloat16 [8, 8, 196, 768], P('seq', 'ft'), may hold values from -6 to 6
- grad_class_out: bfloat16 [8, 768], P('seq'), may hold values from -6 to 6
Outputs:
- output: bfloat16 [8, 8, 196, 768], P('seq', 'ft')
- class_output: bfloat16 [8, 768], P('seq')
- grad_video: float32 [8, 8, 196, 768], P('seq', None, 'ft')
- grad_class: float32 [8, 768], P('seq')
- grad_time_gain: float32 [768], P(('seq', 'ft'))
- grad_time_shift: float32 [768], P(('seq', 'ft'))
- grad_time_project: float32 [768, 2304], P(('seq', 'ft'))
- grad_time_output: float32 [768, 768], P(('seq', 'ft'))
- grad_time_output_bias: float32 [768], P(('seq', 'ft'))
- grad_time_mixer: float32 [768, 768], P(('seq', 'ft'))
- grad_time_mixer_bias: float32 [768], P(('seq', 'ft'))
- grad_space_gain: float32 [768], P(('seq', 'ft'))
- grad_space_shift: float32 [768], P(('seq', 'ft'))
- grad_space_project: float32 [768, 2304], P(('seq', 'ft'))
- grad_space_output: float32 [768, 768], P(('seq', 'ft'))
- grad_space_output_bias: float32 [768], P(('seq', 'ft'))
- grad_feed_gain: float32 [768], P(('seq', 'ft'))
- grad_feed_shift: float32 [768], P(('seq', 'ft'))
- grad_feed_expand: float32 [768, 3072], P(('seq', 'ft'))
- grad_feed_expand_bias: float32 [3072], P(('seq', 'ft'))
- grad_feed_reduce: float32 [3072, 768], P(('seq', 'ft'))
- grad_feed_reduce_bias: float32 [768], P(('seq', 'ft'))
The draws below stay inside these ranges and needn't reach their ends.
Inputs may be any that keep to these rules, and one draw needn't show every extreme that they name: Along the 8 frames of a sequence frame_clip never falls; frames with equal values form one clip. Along the 196 patch positions patch_clip never falls. 1 marks a padding patch position.
All inputs are finite; a program needn't handle non-finite values. No bound on the sum of `padding` on one device may be relied on, other than what follows from the above.
Results may differ from the reference program's by a relative error of at most 0.025.
Values may be sent and summed in bfloat16 or wider, within the bound.
A program may use at most 256 MiB of HBM per device.

```python
import math
import jax
import jax.numpy as jnp
import numpy as np
from jax import lax

D = 768
HEADS = 12
HD = 64
FF = 3072
F = 8
P_SIZE = 196
SEQS = 8


def place_ends(drawn, own_key, low, top_value):
    longest = drawn.shape.index(max(drawn.shape))
    spots = []
    for shift in (0, 1):
        where = [jax.random.randint(jax.random.fold_in(own_key, axis), (), 0, length) for axis, length in enumerate(drawn.shape)]
        where[longest] = (where[longest] + shift) % drawn.shape[longest]
        spots.append(tuple(where))
    return drawn.at[spots[0]].set(low).at[spots[1]].set(top_value)


def with_spikes(values, rng, source, target, shards_of, factor):
    def block_of(axis_at):
        return (jnp.arange(values.shape[axis_at]) // (values.shape[axis_at] // shards_of)).reshape((-1,) + (1,) * (values.ndim - 1 - axis_at))

    one_side = jax.random.permutation(rng, shards_of)[block_of(target)]
    other_side = (block_of(target) + shards_of // 2) % shards_of
    return jnp.where((block_of(source) == one_side) | (block_of(source) == other_side), factor * values, values)


def shard_levels(rng, extent, shards, least, largest):
    level, own = 1.0, jax.random.fold_in(rng, 6)
    for dim, parts in shards:
        heights = jnp.exp(jax.random.uniform(jax.random.fold_in(own, dim), (parts,), jnp.float32, least / len(shards), largest / len(shards)))
        level = level * jnp.repeat(heights, extent[dim] // parts).reshape([-1 if axis == dim else 1 for axis in range(len(extent))])
    return level


def length_profile(number_of, total, most, slope):
    loads = [(1 << 20) // math.isqrt(grade ** slope) + 1 for grade in range(2, number_of + 1)]
    surplus, holding = total - most - (number_of - 1), [1] * (number_of - 1)
    while surplus > 0:
        movable = [i for i in range(number_of - 1) if holding[i] < most]
        whole, left = sum([loads[i] for i in movable]), surplus
        for i in movable:
            addition = min(most - holding[i], max(1, left * loads[i] // whole), surplus)
            holding[i] = holding[i] + addition
            surplus = surplus - addition
    return np.array([most] + holding)


def ragged(stream_key, count, total, limit, slope):
    if count == 2:
        one = jax.random.randint(stream_key, (), max(1, total - limit), min(limit, total - 1) + 1)
        return jnp.stack([one, total - one])
    sizes = jnp.asarray(length_profile(count, total, limit, slope), jnp.int32)
    twos = (count - 1) // 2
    donor, taker = sizes[1:1 + 2 * twos:2], sizes[2:2 + 2 * twos:2]
    slack = jnp.minimum(donor - 1, limit - taker)
    passed = jax.random.randint(jax.random.fold_in(stream_key, 1), (twos,), 0, 1 << 20) % (slack + 1)
    sizes = sizes.at[1:1 + 2 * twos:2].set(donor - passed).at[2:2 + 2 * twos:2].set(taker + passed)
    return sizes[jax.random.permutation(jax.random.fold_in(stream_key, 2), count)]


def scatter_about(own_key, shape, scale, most, cuts=(), held_as=jnp.bfloat16):
    level = shard_levels(own_key, shape, cuts, -0.22, 0.18) if cuts else 1.0
    values = jax.random.normal(own_key, shape, jnp.float32) * scale * level
    return jnp.minimum(jnp.maximum(values, -most), most).astype(held_as)


def gaussian_with(own_key, dims, scale, bound, cuts, heavy, kind=jnp.bfloat16):
    drawn = scale * jax.random.normal(own_key, dims, jnp.float32)
    if cuts:
        drawn = drawn * shard_levels(own_key, dims, cuts, -0.22, 0.18)
    return jnp.clip(with_spikes(drawn, jax.random.fold_in(own_key, 3), *heavy), -bound, bound).astype(kind)


def setup_inputs(seed: int = 0) -> dict:
    splits = jax.random.split(jax.random.key(seed), 26)
    video = scatter_about(splits[0], (SEQS, F, P_SIZE, D), 1.0, 6.0, ((0, 8), (2, 4)))
    class_token = scatter_about(splits[1], (SEQS, D), 1.0, 6.0, ((0, 8),))
    frame_clip = jax.vmap(lambda own: jnp.searchsorted(jnp.cumsum(ragged(own, 3, F, 4, 0)), jnp.arange(F), side="right"))(jax.random.split(splits[2], SEQS)).reshape((SEQS, F)).astype(jnp.int32)
    patch_clip = jax.vmap(lambda own: jnp.searchsorted(jnp.cumsum(ragged(own, max(3, P_SIZE // 49), P_SIZE, P_SIZE // 2, 0)), jnp.arange(P_SIZE), side="right"))(jax.random.split(splits[3], SEQS)).reshape((SEQS, P_SIZE)).astype(jnp.int32)
    padding = place_ends((jax.random.randint(splits[4], (SEQS, P_SIZE), 0, 8) < 1).astype(jnp.int32), jax.random.fold_in(splits[4], 1), 0, 1)
    time_gain = jnp.clip(1.0 + 0.18 * jax.random.normal(splits[5], (D,), jnp.float32), 0.099609375, 1.8984375).astype(jnp.bfloat16)
    time_shift = scatter_about(splits[6], (D,), 0.2, 1.0, ((0, 4),))
    time_project = scatter_about(splits[7], (D, 3 * D), D ** -0.5, 0.21875, ((0, 4),))
    time_output = scatter_about(splits[8], (D, D), (D // 2) ** -0.5, 0.3125, ((0, 4),))
    time_output_bias = scatter_about(splits[9], (D,), 0.2, 1.0, ((0, 4),))
    time_mixer = scatter_about(splits[10], (D, D), D ** -0.5, 0.21875, ((0, 4),))
    time_mixer_bias = scatter_about(splits[11], (D,), 0.2, 1.0, ((0, 4),))
    space_gain = jnp.clip(1.0 + 0.18 * jax.random.normal(splits[12], (D,), jnp.float32), 0.099609375, 1.8984375).astype(jnp.bfloat16)
    space_shift = scatter_about(splits[13], (D,), 0.2, 1.0, ((0, 4),))
    space_project = scatter_about(splits[14], (D, 3 * D), D ** -0.5, 0.21875, ((0, 4),))
    space_output = scatter_about(splits[15], (D, D), (D // 32) ** -0.5, 1.25, ((0, 4),))
    space_output_bias = scatter_about(splits[16], (D,), 0.2, 1.0, ((0, 4),))
    feed_gain = jnp.clip(1.0 + 0.18 * jax.random.normal(splits[17], (D,), jnp.float32), 0.099609375, 1.8984375).astype(jnp.bfloat16)
    feed_shift = scatter_about(splits[18], (D,), 0.2, 1.0, ((0, 4),))
    feed_expand = scatter_about(splits[19], (D, FF), D ** -0.5, 0.21875, ((0, 4),))
    feed_expand_bias = scatter_about(splits[20], (FF,), 0.2, 1.0, ((0, 4),))
    feed_reduce = scatter_about(splits[21], (FF, D), FF ** -0.5, 0.109375, ((0, 4),))
    feed_reduce_bias = scatter_about(splits[22], (D,), 0.2, 1.0, ((0, 4),))
    grad_output = gaussian_with(splits[23], (SEQS, F, P_SIZE, D), 1.0, 6.0, ((0, 8), (1, 4)), (0, 3, 8, 2.0))
    grad_class_out = scatter_about(splits[24], (SEQS, D), 1.0, 6.0, ((0, 8),))
    return {"video": video, "class_token": class_token, "frame_clip": frame_clip, "patch_clip": patch_clip, "padding": padding, "time_gain": time_gain, "time_shift": time_shift, "time_project": time_project, "time_output": time_output, "time_output_bias": time_output_bias, "time_mixer": time_mixer, "time_mixer_bias": time_mixer_bias, "space_gain": space_gain, "space_shift": space_shift, "space_project": space_project, "space_output": space_output, "space_output_bias": space_output_bias, "feed_gain": feed_gain, "feed_shift": feed_shift, "feed_expand": feed_expand, "feed_expand_bias": feed_expand_bias, "feed_reduce": feed_reduce, "feed_reduce_bias": feed_reduce_bias, "grad_output": grad_output, "grad_class_out": grad_class_out}


epsilon = 1e-06

@jax.custom_vjp
def low(v):
    return lax.optimization_barrier(v.astype(jnp.bfloat16)).astype(jnp.float32)

@jax.custom_vjp
def low_back(v):
    return v

def low_keep(v):
    return (low(v), None)

def low_pass(kept, grad):
    return (grad,)

def back_keep(v):
    return (v, None)

def back_low(kept, grad):
    return (low(grad),)
low.defvjp(low_keep, low_pass)
low_back.defvjp(back_keep, back_low)

def layer_norm(values, gain, shift):
    centre = lax.optimization_barrier(jnp.mean(values, axis=-1, keepdims=True))
    centred = values - centre
    spread = lax.optimization_barrier(jnp.mean(centred * centred, axis=-1, keepdims=True))
    return centred * lax.rsqrt(spread + epsilon) * gain + shift

def matmul(left, right):
    return jnp.dot(left, right, precision=lax.Precision.HIGHEST)

def attend(joined, allowed):
    group = joined.shape[0]
    length = joined.shape[1]
    split = joined.reshape(group, length, 3, HEADS, HD)
    scores = jnp.einsum('glhe,gmhe->ghlm', split[:, :, 0], split[:, :, 1], precision=lax.Precision.HIGHEST) * HD ** (-0.5)
    scores = low_back(scores)
    scores = jnp.where(allowed, scores, -1e+30)
    row_top = lax.optimization_barrier(jnp.max(scores, axis=-1, keepdims=True))
    exponent = jnp.exp(scores - row_top)
    probability = low(exponent / lax.optimization_barrier(jnp.sum(exponent, axis=-1, keepdims=True)))
    mixed = jnp.einsum('ghlm,gmhe->glhe', probability, split[:, :, 2], precision=lax.Precision.HIGHEST)
    return mixed.reshape(group, length, HEADS * HD)

def forward(video, class_token, params, frame_clip, patch_clip, padding):
    time_gain, time_shift, time_project, time_output, time_output_bias, time_mixer, time_mixer_bias, space_gain, space_shift, space_project, space_output, space_output_bias, feed_gain, feed_shift, feed_expand, feed_expand_bias, feed_reduce, feed_reduce_bias = params
    frames = video.shape[0]
    patches = video.shape[1]
    width = video.shape[2]
    time_rows = jnp.transpose(video, (1, 0, 2))
    normed = low(layer_norm(time_rows, time_gain, time_shift))
    joined = low(low_back(matmul(normed, time_project)))
    same_clip = frame_clip[:, None] == frame_clip[None, :]
    mixed = low(low_back(attend(joined, same_clip[None, None])))
    outer = low(low_back(matmul(mixed, time_output) + time_output_bias))
    after_time = low(low_back(time_rows + matmul(outer, time_mixer) + time_mixer_bias))
    after_time = jnp.transpose(after_time, (1, 0, 2))
    length = patches + 1
    tokens = jnp.concatenate([jnp.broadcast_to(class_token, (frames, 1, width)), after_time], axis=1)
    normed = low(layer_norm(tokens, space_gain, space_shift))
    joined = low(low_back(matmul(normed, space_project)))
    key_open = jnp.concatenate([jnp.ones((1,), jnp.bool_), padding == 0])
    group_ids = jnp.concatenate([jnp.full((1,), -1, jnp.int32), patch_clip.astype(jnp.int32)])
    position = jnp.arange(length)
    from_class = position == 0
    allowed = key_open[None, :] & ((group_ids[:, None] == group_ids[None, :]) | from_class[:, None] | from_class[None, :])
    mixed = low(low_back(attend(joined, allowed[None, None])))
    branch = low_back(matmul(mixed, space_output) + space_output_bias)
    class_mid = class_token + lax.optimization_barrier(jnp.mean(branch[:, 0], axis=0))
    patch_mid = after_time + branch[:, 1:]
    feed_rows = jnp.concatenate([class_mid[None], patch_mid.reshape(frames * patches, width)], axis=0)
    normed = low(layer_norm(feed_rows, feed_gain, feed_shift))
    hidden = low_back(matmul(normed, feed_expand) + feed_expand_bias)
    active = low(jax.nn.gelu(hidden, approximate=False))
    result = feed_rows + matmul(active, feed_reduce) + feed_reduce_bias
    return (result[1:].reshape(frames, patches, width), result[0])

def reference(video, class_token, frame_clip, patch_clip, padding, time_gain, time_shift, time_project, time_output, time_output_bias, time_mixer, time_mixer_bias, space_gain, space_shift, space_project, space_output, space_output_bias, feed_gain, feed_shift, feed_expand, feed_expand_bias, feed_reduce, feed_reduce_bias, grad_output, grad_class_out):
    params = tuple((item.astype(jnp.float32) for item in (time_gain, time_shift, time_project, time_output, time_output_bias, time_mixer, time_mixer_bias, space_gain, space_shift, space_project, space_output, space_output_bias, feed_gain, feed_shift, feed_expand, feed_expand_bias, feed_reduce, feed_reduce_bias)))

    def one_sequence(totals, item):
        clip_video, clip_class, clip_frames, clip_patches, clip_padding, clip_grad, clip_grad_class = item

        def run(inputs, token, weights):
            return forward(inputs, token, weights, clip_frames, clip_patches, clip_padding)
        outputs, pull = jax.vjp(run, clip_video.astype(jnp.float32), clip_class.astype(jnp.float32), params)
        grad_in, grad_token, grad_weights = pull((clip_grad.astype(jnp.float32), clip_grad_class.astype(jnp.float32)))
        totals = tuple((total + extra for total, extra in zip(totals, grad_weights)))
        return (totals, (outputs[0].astype(jnp.bfloat16), outputs[1].astype(jnp.bfloat16), grad_in, grad_token))
    zeros = tuple((jnp.zeros(item.shape, jnp.float32) for item in params))
    totals, stacked = lax.scan(one_sequence, zeros, (video, class_token, frame_clip, patch_clip, padding, grad_output, grad_class_out))
    return (stacked[0], stacked[1], stacked[2], stacked[3], totals[0], totals[1], totals[2], totals[3], totals[4], totals[5], totals[6], totals[7], totals[8], totals[9], totals[10], totals[11], totals[12], totals[13], totals[14], totals[15], totals[16], totals[17])
```

```python
import functools
from functools import partial

import jax
import jax.numpy as jnp
from jax import lax
from jax.experimental import pallas as pl
from jax.experimental.pallas import tpu as pltpu
from jax.sharding import PartitionSpec as P

HEADS = 12
HD = 64


epsilon = 1e-06


MESH = pl.DeviceIdType.MESH


def place():
    s = lax.axis_index("seq")
    f = lax.axis_index("ft")
    core = lax.rem(s, 2)
    col = lax.rem(s // 2, 2)
    row = lax.rem(s // 4, 2)
    return s, f, core, col, row


def peers(s, core, col, row):
    return (s + 1 - 2 * core, s + 2 - 4 * col, s + 4 - 8 * row)


def greet(f, targets):
    bar = pltpu.get_barrier_semaphore()
    for t in targets:
        pl.semaphore_signal(bar, inc=1, device_id=t, device_id_type=MESH)
    pl.semaphore_wait(bar, len(targets))


def remote(src, dst, send, recv, target):
    return pltpu.make_async_remote_copy(
        src_ref=src, dst_ref=dst, send_sem=send, recv_sem=recv, device_id=target, device_id_type=MESH
    )


def gather_kernel(count, *refs):
    shards = refs[:count]
    fulls = refs[count : 2 * count]
    own, sz, rz, sx, rx, sy, ry, sc, rc, sd, rd = refs[2 * count :]
    s, f, core, col, row = place()
    sib, across, down = peers(s, core, col, row)
    half = lax.rem(col + row, 2)
    mine = 2 * half + core
    other = 2 * (1 - half) + core
    upper = f // 2
    near = f + upper * (3 - 2 * f)
    order = [upper * 3 + (1 - 2 * upper) * v for v in (1 - near, 2, 3)]

    bar = pltpu.get_barrier_semaphore()
    for t in (sib, across, down):
        pl.semaphore_signal(bar, inc=1, device_id=(t, f), device_id_type=MESH)

    @pl.when(f < 3)
    def _():
        pl.semaphore_signal(bar, inc=1, device_id=(s, f + 1), device_id_type=MESH)

    @pl.when(f > 0)
    def _():
        pl.semaphore_signal(bar, inc=1, device_id=(s, f - 1), device_id_type=MESH)

    @pl.when((f == 0) | (f == 3))
    def _():
        pl.semaphore_wait(bar, 4)

    @pl.when((f > 0) & (f < 3))
    def _():
        pl.semaphore_wait(bar, 5)

    def block(w, z, quarter):
        rows = shards[w].shape[0]
        part = rows // 4
        return fulls[w].at[pl.ds(pl.multiple_of(z * rows + quarter * part, 16), part), :]

    def side(w, z, quarter, which):
        rows, wide = shards[w].shape
        part = rows // 4
        return fulls[w].at[
            pl.ds(pl.multiple_of(z * rows + quarter * part, 16), part),
            pl.ds(which * (wide // 2), wide // 2),
        ]

    def up(w, z, src):
        return remote(src, block(w, z, mine), sz.at[w, 0, z], rz.at[w, z], (s, f + 1))

    def low(w, z, src):
        return remote(src, block(w, z, mine), sz.at[w, 1, z], rz.at[w, z], (s, f - 1))

    def start_own(w):
        rows = shards[w].shape[0]
        part = rows // 4
        src = shards[w].at[pl.ds(pl.multiple_of(mine * part, 16), part), :]

        @pl.when(f < 3)
        def _():
            up(w, f, src).start()

        @pl.when(f > 0)
        def _():
            low(w, f, src).start()

        keep = pltpu.make_async_copy(
            shards[w], fulls[w].at[pl.ds(pl.multiple_of(f * rows, 16), rows), :], own.at[w]
        )
        keep.start()

    def to_across(w, z):
        return remote(side(w, z, mine, 0), side(w, z, mine, 0), sx.at[w, z], rx.at[w, z], (across, f))

    def to_down(w, z):
        return remote(side(w, z, mine, 1), side(w, z, mine, 1), sy.at[w, z], ry.at[w, z], (down, f))

    def to_sib(w, z):
        return remote(block(w, z, mine), block(w, z, mine), sc.at[w, z], rc.at[w, z], (sib, f))

    def to_sib_late(w, z):
        return remote(block(w, z, other), block(w, z, other), sd.at[w, z], rd.at[w, z], (sib, f))

    def relay(w):
        for z in order:
            low(w, z, block(w, z, mine)).wait_recv()

            @pl.when((z < f) & (f < 3))
            def _():
                up(w, z, block(w, z, mine)).start()

            @pl.when((z > f) & (f > 0))
            def _():
                low(w, z, block(w, z, mine)).start()

            to_across(w, z).start()
            to_down(w, z).start()
            to_sib(w, z).start()

    def late(w):
        for z in order:
            src = side(w, z, other, 0)
            remote(src, src, sx.at[w, z], rx.at[w, z], (across, f)).wait_recv()
            src = side(w, z, other, 1)
            remote(src, src, sy.at[w, z], ry.at[w, z], (down, f)).wait_recv()
            to_sib_late(w, z).start()

    def finish(w):
        for z in order:
            to_sib(w, z).wait_recv()
            to_sib_late(w, z).wait_recv()
        rows = shards[w].shape[0]
        pltpu.make_async_copy(
            shards[w], fulls[w].at[pl.ds(pl.multiple_of(f * rows, 16), rows), :], own.at[w]
        ).wait()

    def drain(w):
        for z in order:
            to_across(w, z).wait_send()
            to_down(w, z).wait_send()
            to_sib(w, z).wait_send()
            to_sib_late(w, z).wait_send()

            @pl.when((z < f) & (f < 3))
            def _():
                up(w, z, block(w, z, mine)).wait_send()

            @pl.when((z > f) & (f > 0))
            def _():
                low(w, z, block(w, z, mine)).wait_send()

        rows = shards[w].shape[0]
        part = rows // 4
        src = shards[w].at[pl.ds(pl.multiple_of(mine * part, 16), part), :]

        @pl.when(f < 3)
        def _():
            up(w, f, src).wait_send()

        @pl.when(f > 0)
        def _():
            low(w, f, src).wait_send()

    start_own(0)
    start_own(1)
    for w in range(count):
        relay(w)
        if w + 2 < count:
            start_own(w + 2)
        if w > 0:
            late(w - 1)
            finish(w - 1)
    late(count - 1)
    finish(count - 1)
    for w in range(count):
        drain(w)


def gather(shards):
    count = len(shards)
    sem = pltpu.SemaphoreType.DMA
    return pl.pallas_call(
        functools.partial(gather_kernel, count),
        out_shape=[jax.ShapeDtypeStruct((4 * a.shape[0], a.shape[1]), a.dtype) for a in shards],
        in_specs=[pl.BlockSpec(memory_space=pl.ANY)] * count,
        out_specs=[pl.BlockSpec(memory_space=pl.ANY)] * count,
        scratch_shapes=[sem((count,)), sem((count, 2, 4))] + [sem((count, 4))] * 9,
        compiler_params=pltpu.CompilerParams(collective_id=1, has_side_effects=True),
        name="gather_weights",
    )(*shards)


def layer_norm(values, gain, shift):
    centre = jnp.mean(values, axis=-1, keepdims=True)
    centred = values - centre
    spread = jnp.mean(centred * centred, axis=-1, keepdims=True)
    return centred * lax.rsqrt(spread + epsilon) * gain + shift


def norm_pull(values, gain, shift, cotangent):
    unused, pull = jax.vjp(layer_norm, values, gain, shift)
    return pull(cotangent)


def matmul(left, right):
    return jnp.dot(left, right, preferred_element_type=jnp.float32)


def times_transposed(left, right):
    return lax.dot_general(
        left, right, (((1,), (1,)), ((), ())), preferred_element_type=jnp.float32
    )


def transposed_times(left, right):
    return lax.dot_general(
        left, right, (((0,), (0,)), ((), ())), preferred_element_type=jnp.float32
    )


def column_sum(values):
    return jnp.sum(values, axis=0, dtype=jnp.float32)


def reorder_rows(values, outer_count, inner_count):
    rest = values.shape[1:]
    blocks = values.reshape((outer_count, inner_count, -1) + rest)
    blocks = jnp.swapaxes(blocks, 0, 1)
    return blocks.reshape(values.shape)


def row_blocks(values, count):
    return values.reshape((count, values.shape[0] // count) + values.shape[1:])


def split_heads(joined):
    shape = joined.shape[:-1]
    split = joined.reshape(shape + (3, HEADS, HD))
    return (split[..., 0, :, :], split[..., 1, :, :], split[..., 2, :, :])


def score_blocks(query, keys, allowed, form, other):
    scores = jnp.einsum(
        form + "he," + other + "he->abhlm", query, keys, preferred_element_type=jnp.float32
    ) * HD ** (-0.5)
    return jnp.where(allowed, scores, -1e30)


def attend_forward(joined, allowed, form):
    other = form.replace("l", "m")
    query, keys, values = split_heads(joined)
    scores = score_blocks(query, keys, allowed, form, other)
    row_top = jnp.max(scores, axis=-1, keepdims=True)
    exponent = jnp.exp(scores - row_top)
    row_total = jnp.sum(exponent, axis=-1, keepdims=True)
    probability = (exponent / row_total).astype(jnp.bfloat16)
    mixed = jnp.einsum(
        "abhlm," + other + "he->" + form + "he",
        probability,
        values,
        preferred_element_type=jnp.float32,
    )
    return (
        mixed.reshape(joined.shape[:-1] + (HEADS * HD,)).astype(jnp.bfloat16),
        row_top + jnp.log(row_total),
    )


def attend_backward(joined, allowed, log_total, grad_mixed, form):
    other = form.replace("l", "m")
    query, keys, values = split_heads(joined)
    scores = score_blocks(query, keys, allowed, form, other)
    probability = jnp.exp(scores - log_total)
    grad_heads = grad_mixed.reshape(query.shape)
    grad_prob = jnp.einsum(
        form + "he," + other + "he->abhlm", grad_heads, values, preferred_element_type=jnp.float32
    )
    grad_values = jnp.einsum(
        "abhlm," + form + "he->" + other + "he",
        probability.astype(jnp.bfloat16),
        grad_heads,
        preferred_element_type=jnp.float32,
    )
    inner = jnp.sum(probability * grad_prob, axis=-1, keepdims=True)
    grad_scores = (probability * (grad_prob - inner)).astype(jnp.bfloat16)
    grad_query = jnp.einsum(
        "abhlm," + other + "he->" + form + "he",
        grad_scores,
        keys,
        preferred_element_type=jnp.float32,
    ) * HD ** (-0.5)
    grad_keys = jnp.einsum(
        "abhlm," + form + "he->" + other + "he",
        grad_scores,
        query,
        preferred_element_type=jnp.float32,
    ) * HD ** (-0.5)
    stacked = jnp.stack([grad_query, grad_keys, grad_values], axis=-3)
    return stacked.reshape(joined.shape).astype(jnp.bfloat16)


def shards(
    video,
    class_token,
    frame_clip,
    patch_clip,
    padding,
    time_gain,
    time_shift,
    time_project,
    time_output,
    time_output_bias,
    time_mixer,
    time_mixer_bias,
    space_gain,
    space_shift,
    space_project,
    space_output,
    space_output_bias,
    feed_gain,
    feed_shift,
    feed_expand,
    feed_expand_bias,
    feed_reduce,
    feed_reduce_bias,
    grad_output,
    grad_class_out,
):
    vectors = jnp.stack(
        [
            time_gain,
            time_shift,
            time_output_bias,
            time_mixer_bias,
            space_gain,
            space_shift,
            space_output_bias,
            feed_gain,
            feed_shift,
            feed_reduce_bias,
        ]
        + [feed_expand_bias[192 * i : 192 * (i + 1)] for i in range(4)]
        + [jnp.zeros_like(time_gain)] * 50
    )
    vectors = jnp.pad(vectors, ((0, 0), (0, 64)))
    (
        time_project,
        time_output,
        time_mixer,
        space_project,
        space_output,
        feed_expand,
        feed_reduce,
        vectors,
    ) = gather(
        (
            time_project,
            time_output,
            time_mixer,
            space_project,
            space_output,
            feed_expand,
            feed_reduce,
            vectors,
        )
    )
    vectors = vectors.reshape(4, 64, 256)[:, :14, :192]
    wide = jnp.swapaxes(vectors, 0, 1)[:10].reshape(10, 768)
    (
        time_gain,
        time_shift,
        time_output_bias,
        time_mixer_bias,
        space_gain,
        space_shift,
        space_output_bias,
        feed_gain,
        feed_shift,
        feed_reduce_bias,
    ) = [wide[i] for i in range(10)]
    feed_expand_bias = vectors[:, 10:14].reshape(3072)
    time_gain = time_gain.astype(jnp.float32)
    time_shift = time_shift.astype(jnp.float32)
    space_gain = space_gain.astype(jnp.float32)
    space_shift = space_shift.astype(jnp.float32)
    feed_gain = feed_gain.astype(jnp.float32)
    feed_shift = feed_shift.astype(jnp.float32)
    time_output_bias = time_output_bias.astype(jnp.float32)
    time_mixer_bias = time_mixer_bias.astype(jnp.float32)
    space_output_bias = space_output_bias.astype(jnp.float32)
    feed_expand_bias = feed_expand_bias.astype(jnp.float32)
    feed_reduce_bias = feed_reduce_bias.astype(jnp.float32)
    seqs_here, frames, patch_here, width = video.shape
    frames_here = frames // lax.axis_size("ft")
    patches = patch_clip.shape[1]
    length = patches + 1
    total_rows = seqs_here * frames * patch_here
    patch_count = seqs_here * frames_here * patches
    time_rows = video.astype(jnp.float32).reshape(total_rows, width)
    time_normed = layer_norm(time_rows, time_gain, time_shift).astype(jnp.bfloat16)
    time_joined = (
        matmul(time_normed, time_project)
        .astype(jnp.bfloat16)
        .reshape(seqs_here, frames, patch_here, 3 * width)
    )
    same_clip = frame_clip[:, :, None] == frame_clip[:, None, :]
    time_allowed = same_clip[:, None, None, :, :]
    time_mixed, time_total = attend_forward(time_joined, time_allowed, "alb")
    time_outer = (
        matmul(time_mixed.reshape(total_rows, width), time_output) + time_output_bias
    ).astype(jnp.bfloat16)
    time_branch = matmul(time_outer, time_mixer) + time_mixer_bias
    after_time = (
        (time_rows + time_branch).astype(jnp.bfloat16).reshape(seqs_here, frames, patch_here, width)
    )
    after_space = lax.all_to_all(after_time, "ft", split_axis=1, concat_axis=2, tiled=True)
    class_rows = class_token.astype(jnp.float32)
    space_rows = jnp.concatenate(
        [
            jnp.broadcast_to(class_rows[:, None, None, :], (seqs_here, frames_here, 1, width)),
            after_space.astype(jnp.float32),
        ],
        axis=2,
    )
    space_normed = layer_norm(space_rows, space_gain, space_shift).astype(jnp.bfloat16)
    space_joined = (
        matmul(space_normed.reshape(-1, width), space_project)
        .astype(jnp.bfloat16)
        .reshape(seqs_here, frames_here, length, 3 * width)
    )
    key_open = jnp.concatenate([jnp.ones((seqs_here, 1), jnp.bool_), padding == 0], axis=1)
    group_ids = jnp.concatenate([jnp.full((seqs_here, 1), -1, jnp.int32), patch_clip], axis=1)
    position = jnp.arange(length)
    from_class = position == 0
    space_allowed = key_open[:, None, :] & (
        (group_ids[:, :, None] == group_ids[:, None, :])
        | from_class[None, :, None]
        | from_class[None, None, :]
    )
    space_allowed = space_allowed[:, None, None, :, :]
    space_mixed, space_total = attend_forward(space_joined, space_allowed, "abl")
    space_branch = (
        matmul(space_mixed.reshape(-1, width), space_output) + space_output_bias
    ).reshape(seqs_here, frames_here, length, width)
    class_sum = lax.psum(jnp.sum(space_branch[:, :, 0], axis=1), "ft")
    class_mid = class_rows + class_sum / frames
    patch_mid = after_space.astype(jnp.float32) + space_branch[:, :, 1:]
    feed_rows = jnp.concatenate([patch_mid.reshape(patch_count, width), class_mid], axis=0)
    feed_normed = layer_norm(feed_rows, feed_gain, feed_shift).astype(jnp.bfloat16)
    hidden = matmul(feed_normed, feed_expand) + feed_expand_bias
    active = jax.nn.gelu(hidden, approximate=False).astype(jnp.bfloat16)
    result = feed_rows + matmul(active, feed_reduce) + feed_reduce_bias
    output = (
        result[:patch_count].reshape(seqs_here, frames_here, patches, width).astype(jnp.bfloat16)
    )
    class_output = result[patch_count:].astype(jnp.bfloat16)
    first = (lax.axis_index("ft") == 0).astype(jnp.bfloat16)
    first_wide = first.astype(jnp.float32)
    grad_patch_rows = grad_output.reshape(patch_count, width)
    grad_result = jnp.concatenate([grad_patch_rows, grad_class_out], axis=0)
    grad_counted = jnp.concatenate([grad_patch_rows, grad_class_out * first], axis=0)
    grad_feed_reduce = transposed_times(active, grad_counted)
    grad_feed_reduce_bias = column_sum(grad_counted)
    grad_active = times_transposed(grad_result, feed_reduce)
    unused, gelu_pull = jax.vjp(partial(jax.nn.gelu, approximate=False), hidden)
    grad_hidden = gelu_pull(grad_active)[0].astype(jnp.bfloat16)
    hidden_counted = jnp.concatenate(
        [grad_hidden[:patch_count], grad_hidden[patch_count:] * first], axis=0
    )
    grad_feed_expand = transposed_times(feed_normed, hidden_counted)
    grad_feed_expand_bias = column_sum(hidden_counted)
    grad_feed_normed = times_transposed(grad_hidden, feed_expand)
    patch_grad, gain_patch, shift_patch = norm_pull(
        feed_rows[:patch_count], feed_gain, feed_shift, grad_feed_normed[:patch_count]
    )
    class_grad, gain_class, shift_class = norm_pull(
        feed_rows[patch_count:], feed_gain, feed_shift, grad_feed_normed[patch_count:]
    )
    grad_feed_gain = gain_patch + first_wide * gain_class
    grad_feed_shift = shift_patch + first_wide * shift_class
    grad_patch_mid = grad_patch_rows.astype(jnp.float32) + patch_grad
    grad_class_mid = grad_class_out.astype(jnp.float32) + class_grad
    grad_branch = jnp.concatenate(
        [
            jnp.broadcast_to(
                (grad_class_mid / frames)[:, None, None, :], (seqs_here, frames_here, 1, width)
            ),
            grad_patch_mid.reshape(seqs_here, frames_here, patches, width),
        ],
        axis=2,
    ).astype(jnp.bfloat16)
    grad_branch_rows = grad_branch.reshape(-1, width)
    grad_space_output = transposed_times(space_mixed.reshape(-1, width), grad_branch_rows)
    grad_space_output_bias = column_sum(grad_branch_rows)
    grad_space_mixed = times_transposed(grad_branch_rows, space_output).astype(jnp.bfloat16)
    grad_space_joined = attend_backward(
        space_joined, space_allowed, space_total, grad_space_mixed, "abl"
    ).reshape(-1, 3 * width)
    grad_space_project = transposed_times(space_normed.reshape(-1, width), grad_space_joined)
    grad_space_normed = times_transposed(grad_space_joined, space_project).reshape(
        seqs_here, frames_here, length, width
    )
    grad_space_rows, grad_space_gain, grad_space_shift = norm_pull(
        space_rows, space_gain, space_shift, grad_space_normed
    )
    class_frames = lax.psum(jnp.sum(grad_space_rows[:, :, 0], axis=1), "ft")
    grad_class = grad_class_mid + class_frames
    grad_after_space = (
        grad_patch_mid.reshape(seqs_here, frames_here, patches, width) + grad_space_rows[:, :, 1:]
    ).astype(jnp.bfloat16)
    grad_after_time = lax.all_to_all(
        grad_after_space, "ft", split_axis=2, concat_axis=1, tiled=True
    )
    grad_time_branch = grad_after_time.reshape(total_rows, width)
    grad_time_mixer = transposed_times(time_outer, grad_time_branch)
    grad_time_mixer_bias = column_sum(grad_time_branch)
    grad_time_outer = times_transposed(grad_time_branch, time_mixer).astype(jnp.bfloat16)
    grad_time_output = transposed_times(time_mixed.reshape(total_rows, width), grad_time_outer)
    grad_time_output_bias = column_sum(grad_time_outer)
    grad_time_mixed = times_transposed(grad_time_outer, time_output).astype(jnp.bfloat16)
    grad_time_joined = attend_backward(
        time_joined, time_allowed, time_total, grad_time_mixed, "alb"
    ).reshape(total_rows, 3 * width)
    grad_time_project = transposed_times(time_normed, grad_time_joined)
    grad_time_normed = times_transposed(grad_time_joined, time_project)
    grad_time_rows, grad_time_gain, grad_time_shift = norm_pull(
        time_rows, time_gain, time_shift, grad_time_normed
    )
    grad_video = (grad_time_branch.astype(jnp.float32) + grad_time_rows).reshape(
        seqs_here, frames, patch_here, width
    )
    local = (
        grad_time_gain,
        grad_time_shift,
        grad_time_project,
        grad_time_output,
        grad_time_output_bias,
        grad_time_mixer,
        grad_time_mixer_bias,
        grad_space_gain,
        grad_space_shift,
        grad_space_project,
        grad_space_output,
        grad_space_output_bias,
        grad_feed_gain,
        grad_feed_shift,
        grad_feed_expand,
        grad_feed_expand_bias,
        grad_feed_reduce,
        grad_feed_reduce_bias,
    )
    seq_count = lax.axis_size("seq")
    ft_count = lax.axis_size("ft")
    blocks = tuple(
        (row_blocks(reorder_rows(item, seq_count, ft_count), ft_count) for item in local)
    )
    moved = (
        lax.all_to_all(
            blocks[0].astype(jnp.bfloat16), "ft", split_axis=0, concat_axis=0, tiled=True
        ).astype(jnp.float32),
        lax.all_to_all(
            blocks[1].astype(jnp.bfloat16), "ft", split_axis=0, concat_axis=0, tiled=True
        ).astype(jnp.float32),
        lax.all_to_all(
            blocks[2].astype(jnp.bfloat16), "ft", split_axis=0, concat_axis=0, tiled=True
        ).astype(jnp.float32),
        lax.all_to_all(
            blocks[3].astype(jnp.bfloat16), "ft", split_axis=0, concat_axis=0, tiled=True
        ).astype(jnp.float32),
        lax.all_to_all(
            blocks[4].astype(jnp.bfloat16), "ft", split_axis=0, concat_axis=0, tiled=True
        ).astype(jnp.float32),
        lax.all_to_all(
            blocks[5].astype(jnp.bfloat16), "ft", split_axis=0, concat_axis=0, tiled=True
        ).astype(jnp.float32),
        lax.all_to_all(
            blocks[6].astype(jnp.bfloat16), "ft", split_axis=0, concat_axis=0, tiled=True
        ).astype(jnp.float32),
        lax.all_to_all(
            blocks[7].astype(jnp.bfloat16), "ft", split_axis=0, concat_axis=0, tiled=True
        ).astype(jnp.float32),
        lax.all_to_all(
            blocks[8].astype(jnp.bfloat16), "ft", split_axis=0, concat_axis=0, tiled=True
        ).astype(jnp.float32),
        lax.all_to_all(
            blocks[9].astype(jnp.bfloat16), "ft", split_axis=0, concat_axis=0, tiled=True
        ).astype(jnp.float32),
        lax.all_to_all(
            blocks[10].astype(jnp.bfloat16), "ft", split_axis=0, concat_axis=0, tiled=True
        ).astype(jnp.float32),
        lax.all_to_all(
            blocks[11].astype(jnp.bfloat16), "ft", split_axis=0, concat_axis=0, tiled=True
        ).astype(jnp.float32),
        lax.all_to_all(
            blocks[12].astype(jnp.bfloat16), "ft", split_axis=0, concat_axis=0, tiled=True
        ).astype(jnp.float32),
        lax.all_to_all(
            blocks[13].astype(jnp.bfloat16), "ft", split_axis=0, concat_axis=0, tiled=True
        ).astype(jnp.float32),
        lax.all_to_all(
            blocks[14].astype(jnp.bfloat16), "ft", split_axis=0, concat_axis=0, tiled=True
        ).astype(jnp.float32),
        lax.all_to_all(
            blocks[15].astype(jnp.bfloat16), "ft", split_axis=0, concat_axis=0, tiled=True
        ).astype(jnp.float32),
        lax.all_to_all(
            blocks[16].astype(jnp.bfloat16), "ft", split_axis=0, concat_axis=0, tiled=True
        ).astype(jnp.float32),
        lax.all_to_all(
            blocks[17].astype(jnp.bfloat16), "ft", split_axis=0, concat_axis=0, tiled=True
        ).astype(jnp.float32),
    )
    summed = tuple((jnp.sum(item, axis=0) for item in moved))
    shares = (
        lax.psum_scatter(summed[0], "seq", scatter_dimension=0, tiled=True),
        lax.psum_scatter(summed[1], "seq", scatter_dimension=0, tiled=True),
        lax.psum_scatter(summed[2], "seq", scatter_dimension=0, tiled=True),
        lax.psum_scatter(summed[3], "seq", scatter_dimension=0, tiled=True),
        lax.psum_scatter(summed[4], "seq", scatter_dimension=0, tiled=True),
        lax.psum_scatter(summed[5], "seq", scatter_dimension=0, tiled=True),
        lax.psum_scatter(summed[6], "seq", scatter_dimension=0, tiled=True),
        lax.psum_scatter(summed[7], "seq", scatter_dimension=0, tiled=True),
        lax.psum_scatter(summed[8], "seq", scatter_dimension=0, tiled=True),
        lax.psum_scatter(summed[9], "seq", scatter_dimension=0, tiled=True),
        lax.psum_scatter(summed[10], "seq", scatter_dimension=0, tiled=True),
        lax.psum_scatter(summed[11], "seq", scatter_dimension=0, tiled=True),
        lax.psum_scatter(summed[12], "seq", scatter_dimension=0, tiled=True),
        lax.psum_scatter(summed[13], "seq", scatter_dimension=0, tiled=True),
        lax.psum_scatter(summed[14], "seq", scatter_dimension=0, tiled=True),
        lax.psum_scatter(summed[15], "seq", scatter_dimension=0, tiled=True),
        lax.psum_scatter(summed[16], "seq", scatter_dimension=0, tiled=True),
        lax.psum_scatter(summed[17], "seq", scatter_dimension=0, tiled=True),
    )
    return (output, class_output, grad_video, grad_class) + tuple(shares)


def solution(mesh):
    in_specs = (
        P("seq", None, "ft", None),
        P("seq", None),
        P("seq", None),
        P("seq", None),
        P("seq", None),
        P("ft"),
        P("ft"),
        P("ft", None),
        P("ft", None),
        P("ft"),
        P("ft", None),
        P("ft"),
        P("ft"),
        P("ft"),
        P("ft", None),
        P("ft", None),
        P("ft"),
        P("ft"),
        P("ft"),
        P("ft", None),
        P("ft"),
        P("ft", None),
        P("ft"),
        P("seq", "ft", None, None),
        P("seq", None),
    )
    out_specs = (
        P("seq", "ft", None, None),
        P("seq", None),
        P("seq", None, "ft", None),
        P("seq", None),
        P(("seq", "ft")),
        P(("seq", "ft")),
        P(("seq", "ft"), None),
        P(("seq", "ft"), None),
        P(("seq", "ft")),
        P(("seq", "ft"), None),
        P(("seq", "ft")),
        P(("seq", "ft")),
        P(("seq", "ft")),
        P(("seq", "ft"), None),
        P(("seq", "ft"), None),
        P(("seq", "ft")),
        P(("seq", "ft")),
        P(("seq", "ft")),
        P(("seq", "ft"), None),
        P(("seq", "ft")),
        P(("seq", "ft"), None),
        P(("seq", "ft")),
    )
    return jax.shard_map(shards, mesh=mesh, in_specs=in_specs, out_specs=out_specs, check_vma=False)
```

```python
import functools
from functools import partial

import jax
import jax.numpy as jnp
from jax import lax
from jax.experimental import pallas as pl
from jax.experimental.pallas import tpu as pltpu
from jax.sharding import PartitionSpec as P

HEADS = 12
HD = 64


epsilon = 1e-06


MESH = pl.DeviceIdType.MESH


def place():
    s = lax.axis_index("seq")
    f = lax.axis_index("ft")
    core = lax.rem(s, 2)
    col = lax.rem(s // 2, 2)
    row = lax.rem(s // 4, 2)
    return s, f, core, col, row


def peers(s, core, col, row):
    return (s + 1 - 2 * core, s + 2 - 4 * col, s + 4 - 8 * row)


def greet(f, targets):
    bar = pltpu.get_barrier_semaphore()
    for t in targets:
        pl.semaphore_signal(bar, inc=1, device_id=t, device_id_type=MESH)
    pl.semaphore_wait(bar, len(targets))


def remote(src, dst, send, recv, target):
    return pltpu.make_async_remote_copy(
        src_ref=src, dst_ref=dst, send_sem=send, recv_sem=recv, device_id=target, device_id_type=MESH
    )


def gather_kernel(count, *refs):
    shards = refs[:count]
    fulls = refs[count : 2 * count]
    own, sz, rz, sx, rx, sy, ry, sc, rc, sd, rd = refs[2 * count :]
    s, f, core, col, row = place()
    sib, across, down = peers(s, core, col, row)
    half = lax.rem(col + row, 2)
    mine = 2 * half + core
    other = 2 * (1 - half) + core
    upper = f // 2
    near = f + upper * (3 - 2 * f)
    order = [upper * 3 + (1 - 2 * upper) * v for v in (1 - near, 2, 3)]

    bar = pltpu.get_barrier_semaphore()
    for t in (sib, across, down):
        pl.semaphore_signal(bar, inc=1, device_id=(t, f), device_id_type=MESH)

    @pl.when(f < 3)
    def _():
        pl.semaphore_signal(bar, inc=1, device_id=(s, f + 1), device_id_type=MESH)

    @pl.when(f > 0)
    def _():
        pl.semaphore_signal(bar, inc=1, device_id=(s, f - 1), device_id_type=MESH)

    @pl.when((f == 0) | (f == 3))
    def _():
        pl.semaphore_wait(bar, 4)

    @pl.when((f > 0) & (f < 3))
    def _():
        pl.semaphore_wait(bar, 5)

    def block(w, z, quarter):
        rows = shards[w].shape[0]
        part = rows // 4
        return fulls[w].at[pl.ds(pl.multiple_of(z * rows + quarter * part, 16), part), :]

    def side(w, z, quarter, which):
        rows, wide = shards[w].shape
        part = rows // 4
        return fulls[w].at[
            pl.ds(pl.multiple_of(z * rows + quarter * part, 16), part),
            pl.ds(which * (wide // 2), wide // 2),
        ]

    def up(w, z, src):
        return remote(src, block(w, z, mine), sz.at[w, 0, z], rz.at[w, z], (s, f + 1))

    def low(w, z, src):
        return remote(src, block(w, z, mine), sz.at[w, 1, z], rz.at[w, z], (s, f - 1))

    def start_own(w):
        rows = shards[w].shape[0]
        part = rows // 4
        src = shards[w].at[pl.ds(pl.multiple_of(mine * part, 16), part), :]

        @pl.when(f < 3)
        def _():
            up(w, f, src).start()

        @pl.when(f > 0)
        def _():
            low(w, f, src).start()

        keep = pltpu.make_async_copy(
            shards[w], fulls[w].at[pl.ds(pl.multiple_of(f * rows, 16), rows), :], own.at[w]
        )
        keep.start()

    def to_across(w, z):
        return remote(side(w, z, mine, 0), side(w, z, mine, 0), sx.at[w, z], rx.at[w, z], (across, f))

    def to_down(w, z):
        return remote(side(w, z, mine, 1), side(w, z, mine, 1), sy.at[w, z], ry.at[w, z], (down, f))

    def to_sib(w, z):
        return remote(block(w, z, mine), block(w, z, mine), sc.at[w, z], rc.at[w, z], (sib, f))

    def to_sib_late(w, z):
        return remote(block(w, z, other), block(w, z, other), sd.at[w, z], rd.at[w, z], (sib, f))

    def relay(w):
        for z in order:
            low(w, z, block(w, z, mine)).wait_recv()

            @pl.when((z < f) & (f < 3))
            def _():
                up(w, z, block(w, z, mine)).start()

            @pl.when((z > f) & (f > 0))
            def _():
                low(w, z, block(w, z, mine)).start()

            to_across(w, z).start()
            to_down(w, z).start()
            to_sib(w, z).start()

    def late(w):
        for z in order:
            src = side(w, z, other, 0)
            remote(src, src, sx.at[w, z], rx.at[w, z], (across, f)).wait_recv()
            src = side(w, z, other, 1)
            remote(src, src, sy.at[w, z], ry.at[w, z], (down, f)).wait_recv()
            to_sib_late(w, z).start()

    def finish(w):
        for z in order:
            to_sib(w, z).wait_recv()
            to_sib_late(w, z).wait_recv()
        rows = shards[w].shape[0]
        pltpu.make_async_copy(
            shards[w], fulls[w].at[pl.ds(pl.multiple_of(f * rows, 16), rows), :], own.at[w]
        ).wait()

    def drain(w):
        for z in order:
            to_across(w, z).wait_send()
            to_down(w, z).wait_send()
            to_sib(w, z).wait_send()
            to_sib_late(w, z).wait_send()

            @pl.when((z < f) & (f < 3))
            def _():
                up(w, z, block(w, z, mine)).wait_send()

            @pl.when((z > f) & (f > 0))
            def _():
                low(w, z, block(w, z, mine)).wait_send()

        rows = shards[w].shape[0]
        part = rows // 4
        src = shards[w].at[pl.ds(pl.multiple_of(mine * part, 16), part), :]

        @pl.when(f < 3)
        def _():
            up(w, f, src).wait_send()

        @pl.when(f > 0)
        def _():
            low(w, f, src).wait_send()

    start_own(0)
    start_own(1)
    for w in range(count):
        relay(w)
        if w + 2 < count:
            start_own(w + 2)
        if w > 0:
            late(w - 1)
            finish(w - 1)
    late(count - 1)
    finish(count - 1)
    for w in range(count):
        drain(w)


def gather(shards):
    count = len(shards)
    sem = pltpu.SemaphoreType.DMA
    return pl.pallas_call(
        functools.partial(gather_kernel, count),
        out_shape=[jax.ShapeDtypeStruct((4 * a.shape[0], a.shape[1]), a.dtype) for a in shards],
        in_specs=[pl.BlockSpec(memory_space=pl.ANY)] * count,
        out_specs=[pl.BlockSpec(memory_space=pl.ANY)] * count,
        scratch_shapes=[sem((count,)), sem((count, 2, 4))] + [sem((count, 4))] * 9,
        compiler_params=pltpu.CompilerParams(collective_id=1, has_side_effects=True),
        name="gather_weights",
    )(*shards)


class Reduce:
    def __init__(self, parts, outs, scratch):
        self.parts, self.outs = parts, outs
        (self.ra, self.rb, self.ra2, self.rb2, self.sz, self.rz, self.total, self.rc) = scratch[:8]
        self.sems = scratch[8]
        self.s, self.f, self.core, self.col, self.row = place()
        self.sib, self.across, self.down = peers(self.s, self.core, self.col, self.row)

    def greet(self):
        bar = pltpu.get_barrier_semaphore()
        f = self.f
        targets = [(t, f) for t in (self.sib, self.across, self.down)]
        targets += [(self.s, lax.rem(f + j, 4)) for j in (1, 2, 3)]
        for t in targets:
            pl.semaphore_signal(bar, inc=1, device_id=t, device_id_type=MESH)
        pl.semaphore_wait(bar, len(targets))

    def sem(self, w, i):
        return self.sems.at[w, i]

    def copies1(self, w):
        g = self.parts[w]
        rows = self.ra[w].shape[1]
        return (
            remote(g.at[:, 1 - self.col, 0], self.ra[w], self.sem(w, 0), self.sem(w, 1), (self.across, self.f)),
            remote(g.at[1 - self.row, :, 1], self.rb[w], self.sem(w, 2), self.sem(w, 3), (self.down, self.f)),
        )

    def copies2(self, w):
        return (
            remote(self.ra[w].at[1 - self.row], self.ra2[w], self.sem(w, 4), self.sem(w, 5), (self.down, self.f)),
            remote(self.rb[w].at[1 - self.col], self.rb2[w], self.sem(w, 6), self.sem(w, 7), (self.across, self.f)),
        )

    def copies3(self, w):
        out = []
        for j in (1, 2, 3):
            z = lax.rem(self.f + j, 4)
            out.append(
                remote(self.sz[w].at[z], self.rz[w].at[3 - j], self.sem(w, 7 + j), self.sem(w, 14 - j), (self.s, z))
            )
        return out

    def copies4(self, w):
        return remote(self.total[w].at[1 - self.core], self.rc[w], self.sem(w, 14), self.sem(w, 15), (self.sib, self.f))

    def step1(self, w):
        for c in self.copies1(w):
            c.start()

    def step2(self, w):
        a, b = self.copies1(w)
        g, ra, rb = self.parts[w], self.ra[w], self.rb[w]
        row, col = self.row, self.col
        a2, b2 = self.copies2(w)
        a.wait_recv()
        ra[1 - row] = (ra[1 - row].astype(jnp.float32) + g[1 - row, col, 0].astype(jnp.float32)).astype(jnp.bfloat16)
        a2.start()
        b.wait_recv()
        rb[1 - col] = (rb[1 - col].astype(jnp.float32) + g[row, 1 - col, 1].astype(jnp.float32)).astype(jnp.bfloat16)
        b2.start()

    def step3(self, w):
        a2, b2 = self.copies2(w)
        g, ra, rb = self.parts[w], self.ra[w], self.rb[w]
        row, col = self.row, self.col
        part = self.sz[w].shape[2]
        b2.wait_recv()
        a2.wait_recv()
        for z in range(4):
            rows = pl.ds(z * part, part)
            for k, near, far in ((0, ra.at[row], self.ra2[w]), (1, rb.at[col], self.rb2[w])):
                own = g.at[row, col, k]
                self.sz[w][z, k] = (
                    own[rows].astype(jnp.float32) + near[rows].astype(jnp.float32) + far[rows].astype(jnp.float32)
                ).astype(jnp.bfloat16)
        for c in self.copies3(w):
            c.start()

    def step4(self, w):
        for c in self.copies3(w):
            c.wait_recv()
        rz = self.rz[w]
        self.total[w][...] = (
            (self.sz[w][self.f].astype(jnp.float32) + rz[0].astype(jnp.float32))
            + (rz[1].astype(jnp.float32) + rz[2].astype(jnp.float32))
        )
        self.copies4(w).start()
        half = self.rc[w].shape[1]
        self.outs[w][:, pl.ds(pl.multiple_of(self.core * half, 128), half)] = self.total[w][self.core]

    def step5(self, w):
        self.copies4(w).wait_recv()
        half = self.rc[w].shape[1]
        self.outs[w][:, pl.ds(pl.multiple_of((1 - self.core) * half, 128), half)] = self.rc[w][...]

    def drain(self, w):
        for c in self.copies1(w) + self.copies2(w) + tuple(self.copies3(w)) + (self.copies4(w),):
            c.wait_send()


def scratch_of(shapes):
    bf, f32 = jnp.bfloat16, jnp.float32
    v = pltpu.VMEM
    return [
        [v((2, k // 8, h), bf) for k, h in shapes],
        [v((2, k // 8, h), bf) for k, h in shapes],
        [v((k // 8, h), bf) for k, h in shapes],
        [v((k // 8, h), bf) for k, h in shapes],
        [v((4, 2, k // 32, h), bf) for k, h in shapes],
        [v((3, 2, k // 32, h), bf) for k, h in shapes],
        [v((2, k // 32, h), f32) for k, h in shapes],
        [v((k // 32, h), f32) for k, h in shapes],
        pltpu.SemaphoreType.DMA((len(shapes), 16)),
    ]


def reduce_kernel(count, *refs):
    red = Reduce(refs[:count], refs[count : 2 * count], refs[2 * count :])
    red.greet()
    steps = (red.step1, red.step2, red.step3, red.step4, red.step5)
    for t in range(count + len(steps) - 1):
        for k, step in enumerate(steps):
            if 0 <= t - k < count:
                step(t - k)
    for w in range(count):
        red.drain(w)


def reduce_scatter(parts):
    count = len(parts)
    shapes = [(p.shape[0] * p.shape[1] * p.shape[2] * p.shape[3], p.shape[4]) for p in parts]
    vm = pl.BlockSpec(memory_space=pltpu.VMEM)
    return pl.pallas_call(
        functools.partial(reduce_kernel, count),
        out_shape=[jax.ShapeDtypeStruct((k // 32, 2 * h), jnp.float32) for k, h in shapes],
        in_specs=[vm] * count,
        out_specs=[vm] * count,
        scratch_shapes=scratch_of(shapes),
        compiler_params=pltpu.CompilerParams(collective_id=2, has_side_effects=True, vmem_limit_bytes=60 << 20),
        name="reduce_gradients",
    )(*parts)


def swap(values):
    count = lax.axis_size("seq")
    return lax.ppermute(values, "seq", [(i, i ^ 1) for i in range(count)])


def half_gradient(left, right):
    core = lax.rem(lax.axis_index("seq"), 2)
    half = right.shape[1] // 2
    mine = lax.dynamic_slice_in_dim(right, core * half, half, 1)
    theirs = lax.dynamic_slice_in_dim(right, (1 - core) * half, half, 1)
    both_left = jnp.concatenate([left, swap(left)], axis=0)
    both_right = jnp.concatenate([mine, swap(theirs)], axis=0)
    return (
        transposed_times(both_left, both_right)
        .astype(jnp.bfloat16)
        .reshape(2, 2, 2, left.shape[1] // 8, half)
    )


def settle(share):
    count = lax.axis_size("seq")
    if count == 8:
        return share
    more = count // 8
    groups = [[low + 8 * high for high in range(more)] for low in range(8)]
    share = lax.psum_scatter(share, "seq", scatter_dimension=0, tiled=True, axis_index_groups=groups)
    moves = [
        ((high * 8 + low) * 4 + f, (low * 4 + f) * more + high)
        for high in range(more)
        for low in range(8)
        for f in range(4)
    ]
    return lax.ppermute(share, ("seq", "ft"), moves)


def layer_norm(values, gain, shift):
    centre = jnp.mean(values, axis=-1, keepdims=True)
    centred = values - centre
    spread = jnp.mean(centred * centred, axis=-1, keepdims=True)
    return centred * lax.rsqrt(spread + epsilon) * gain + shift


def norm_pull(values, gain, shift, cotangent):
    unused, pull = jax.vjp(layer_norm, values, gain, shift)
    return pull(cotangent)


def matmul(left, right):
    return jnp.dot(left, right, preferred_element_type=jnp.float32)


def times_transposed(left, right):
    return lax.dot_general(
        left, right, (((1,), (1,)), ((), ())), preferred_element_type=jnp.float32
    )


def transposed_times(left, right):
    return lax.dot_general(
        left, right, (((0,), (0,)), ((), ())), preferred_element_type=jnp.float32
    )


def column_sum(values):
    return jnp.sum(values, axis=0, dtype=jnp.float32)


def reorder_rows(values, outer_count, inner_count):
    rest = values.shape[1:]
    blocks = values.reshape((outer_count, inner_count, -1) + rest)
    blocks = jnp.swapaxes(blocks, 0, 1)
    return blocks.reshape(values.shape)


def row_blocks(values, count):
    return values.reshape((count, values.shape[0] // count) + values.shape[1:])


def split_heads(joined):
    shape = joined.shape[:-1]
    split = joined.reshape(shape + (3, HEADS, HD))
    return (split[..., 0, :, :], split[..., 1, :, :], split[..., 2, :, :])


def score_blocks(query, keys, allowed, form, other):
    scores = jnp.einsum(
        form + "he," + other + "he->abhlm", query, keys, preferred_element_type=jnp.float32
    ) * HD ** (-0.5)
    return jnp.where(allowed, scores, -1e30)


def attend_forward(joined, allowed, form):
    other = form.replace("l", "m")
    query, keys, values = split_heads(joined)
    scores = score_blocks(query, keys, allowed, form, other)
    row_top = jnp.max(scores, axis=-1, keepdims=True)
    exponent = jnp.exp(scores - row_top)
    row_total = jnp.sum(exponent, axis=-1, keepdims=True)
    probability = (exponent / row_total).astype(jnp.bfloat16)
    mixed = jnp.einsum(
        "abhlm," + other + "he->" + form + "he",
        probability,
        values,
        preferred_element_type=jnp.float32,
    )
    return (
        mixed.reshape(joined.shape[:-1] + (HEADS * HD,)).astype(jnp.bfloat16),
        row_top + jnp.log(row_total),
    )


def attend_backward(joined, allowed, log_total, grad_mixed, form):
    other = form.replace("l", "m")
    query, keys, values = split_heads(joined)
    scores = score_blocks(query, keys, allowed, form, other)
    probability = jnp.exp(scores - log_total)
    grad_heads = grad_mixed.reshape(query.shape)
    grad_prob = jnp.einsum(
        form + "he," + other + "he->abhlm", grad_heads, values, preferred_element_type=jnp.float32
    )
    grad_values = jnp.einsum(
        "abhlm," + form + "he->" + other + "he",
        probability.astype(jnp.bfloat16),
        grad_heads,
        preferred_element_type=jnp.float32,
    )
    inner = jnp.sum(probability * grad_prob, axis=-1, keepdims=True)
    grad_scores = (probability * (grad_prob - inner)).astype(jnp.bfloat16)
    grad_query = jnp.einsum(
        "abhlm," + other + "he->" + form + "he",
        grad_scores,
        keys,
        preferred_element_type=jnp.float32,
    ) * HD ** (-0.5)
    grad_keys = jnp.einsum(
        "abhlm," + form + "he->" + other + "he",
        grad_scores,
        query,
        preferred_element_type=jnp.float32,
    ) * HD ** (-0.5)
    stacked = jnp.stack([grad_query, grad_keys, grad_values], axis=-3)
    return stacked.reshape(joined.shape).astype(jnp.bfloat16)


def shards(
    video,
    class_token,
    frame_clip,
    patch_clip,
    padding,
    time_gain,
    time_shift,
    time_project,
    time_output,
    time_output_bias,
    time_mixer,
    time_mixer_bias,
    space_gain,
    space_shift,
    space_project,
    space_output,
    space_output_bias,
    feed_gain,
    feed_shift,
    feed_expand,
    feed_expand_bias,
    feed_reduce,
    feed_reduce_bias,
    grad_output,
    grad_class_out,
):
    vectors = jnp.stack(
        [
            time_gain,
            time_shift,
            time_output_bias,
            time_mixer_bias,
            space_gain,
            space_shift,
            space_output_bias,
            feed_gain,
            feed_shift,
            feed_reduce_bias,
        ]
        + [feed_expand_bias[192 * i : 192 * (i + 1)] for i in range(4)]
        + [jnp.zeros_like(time_gain)] * 50
    )
    vectors = jnp.pad(vectors, ((0, 0), (0, 64)))
    (
        time_project,
        time_output,
        time_mixer,
        space_project,
        space_output,
        feed_expand,
        feed_reduce,
        vectors,
    ) = gather(
        (
            time_project,
            time_output,
            time_mixer,
            space_project,
            space_output,
            feed_expand,
            feed_reduce,
            vectors,
        )
    )
    vectors = vectors.reshape(4, 64, 256)[:, :14, :192]
    wide = jnp.swapaxes(vectors, 0, 1)[:10].reshape(10, 768)
    (
        time_gain,
        time_shift,
        time_output_bias,
        time_mixer_bias,
        space_gain,
        space_shift,
        space_output_bias,
        feed_gain,
        feed_shift,
        feed_reduce_bias,
    ) = [wide[i] for i in range(10)]
    feed_expand_bias = vectors[:, 10:14].reshape(3072)
    time_gain = time_gain.astype(jnp.float32)
    time_shift = time_shift.astype(jnp.float32)
    space_gain = space_gain.astype(jnp.float32)
    space_shift = space_shift.astype(jnp.float32)
    feed_gain = feed_gain.astype(jnp.float32)
    feed_shift = feed_shift.astype(jnp.float32)
    time_output_bias = time_output_bias.astype(jnp.float32)
    time_mixer_bias = time_mixer_bias.astype(jnp.float32)
    space_output_bias = space_output_bias.astype(jnp.float32)
    feed_expand_bias = feed_expand_bias.astype(jnp.float32)
    feed_reduce_bias = feed_reduce_bias.astype(jnp.float32)
    seqs_here, frames, patch_here, width = video.shape
    frames_here = frames // lax.axis_size("ft")
    patches = patch_clip.shape[1]
    length = patches + 1
    total_rows = seqs_here * frames * patch_here
    patch_count = seqs_here * frames_here * patches
    time_rows = video.astype(jnp.float32).reshape(total_rows, width)
    time_normed = layer_norm(time_rows, time_gain, time_shift).astype(jnp.bfloat16)
    time_joined = (
        matmul(time_normed, time_project)
        .astype(jnp.bfloat16)
        .reshape(seqs_here, frames, patch_here, 3 * width)
    )
    same_clip = frame_clip[:, :, None] == frame_clip[:, None, :]
    time_allowed = same_clip[:, None, None, :, :]
    time_mixed, time_total = attend_forward(time_joined, time_allowed, "alb")
    time_outer = (
        matmul(time_mixed.reshape(total_rows, width), time_output) + time_output_bias
    ).astype(jnp.bfloat16)
    time_branch = matmul(time_outer, time_mixer) + time_mixer_bias
    after_time = (
        (time_rows + time_branch).astype(jnp.bfloat16).reshape(seqs_here, frames, patch_here, width)
    )
    after_space = lax.all_to_all(after_time, "ft", split_axis=1, concat_axis=2, tiled=True)
    class_rows = class_token.astype(jnp.float32)
    space_rows = jnp.concatenate(
        [
            jnp.broadcast_to(class_rows[:, None, None, :], (seqs_here, frames_here, 1, width)),
            after_space.astype(jnp.float32),
        ],
        axis=2,
    )
    space_normed = layer_norm(space_rows, space_gain, space_shift).astype(jnp.bfloat16)
    space_joined = (
        matmul(space_normed.reshape(-1, width), space_project)
        .astype(jnp.bfloat16)
        .reshape(seqs_here, frames_here, length, 3 * width)
    )
    key_open = jnp.concatenate([jnp.ones((seqs_here, 1), jnp.bool_), padding == 0], axis=1)
    group_ids = jnp.concatenate([jnp.full((seqs_here, 1), -1, jnp.int32), patch_clip], axis=1)
    position = jnp.arange(length)
    from_class = position == 0
    space_allowed = key_open[:, None, :] & (
        (group_ids[:, :, None] == group_ids[:, None, :])
        | from_class[None, :, None]
        | from_class[None, None, :]
    )
    space_allowed = space_allowed[:, None, None, :, :]
    space_mixed, space_total = attend_forward(space_joined, space_allowed, "abl")
    space_branch = (
        matmul(space_mixed.reshape(-1, width), space_output) + space_output_bias
    ).reshape(seqs_here, frames_here, length, width)
    class_sum = lax.psum(jnp.sum(space_branch[:, :, 0], axis=1), "ft")
    class_mid = class_rows + class_sum / frames
    patch_mid = after_space.astype(jnp.float32) + space_branch[:, :, 1:]
    feed_rows = jnp.concatenate([patch_mid.reshape(patch_count, width), class_mid], axis=0)
    feed_normed = layer_norm(feed_rows, feed_gain, feed_shift).astype(jnp.bfloat16)
    hidden = matmul(feed_normed, feed_expand) + feed_expand_bias
    active = jax.nn.gelu(hidden, approximate=False).astype(jnp.bfloat16)
    result = feed_rows + matmul(active, feed_reduce) + feed_reduce_bias
    output = (
        result[:patch_count].reshape(seqs_here, frames_here, patches, width).astype(jnp.bfloat16)
    )
    class_output = result[patch_count:].astype(jnp.bfloat16)
    first = (lax.axis_index("ft") == 0).astype(jnp.bfloat16)
    first_wide = first.astype(jnp.float32)
    grad_patch_rows = grad_output.reshape(patch_count, width)
    grad_result = jnp.concatenate([grad_patch_rows, grad_class_out], axis=0)
    grad_counted = jnp.concatenate([grad_patch_rows, grad_class_out * first], axis=0)
    grad_feed_reduce = half_gradient(active, grad_counted)
    grad_feed_reduce_bias = column_sum(grad_counted)
    grad_active = times_transposed(grad_result, feed_reduce)
    unused, gelu_pull = jax.vjp(partial(jax.nn.gelu, approximate=False), hidden)
    grad_hidden = gelu_pull(grad_active)[0].astype(jnp.bfloat16)
    hidden_counted = jnp.concatenate(
        [grad_hidden[:patch_count], grad_hidden[patch_count:] * first], axis=0
    )
    grad_feed_expand = half_gradient(feed_normed, hidden_counted)
    grad_feed_expand_bias = column_sum(hidden_counted)
    grad_feed_normed = times_transposed(grad_hidden, feed_expand)
    patch_grad, gain_patch, shift_patch = norm_pull(
        feed_rows[:patch_count], feed_gain, feed_shift, grad_feed_normed[:patch_count]
    )
    class_grad, gain_class, shift_class = norm_pull(
        feed_rows[patch_count:], feed_gain, feed_shift, grad_feed_normed[patch_count:]
    )
    grad_feed_gain = gain_patch + first_wide * gain_class
    grad_feed_shift = shift_patch + first_wide * shift_class
    grad_patch_mid = grad_patch_rows.astype(jnp.float32) + patch_grad
    grad_class_mid = grad_class_out.astype(jnp.float32) + class_grad
    grad_branch = jnp.concatenate(
        [
            jnp.broadcast_to(
                (grad_class_mid / frames)[:, None, None, :], (seqs_here, frames_here, 1, width)
            ),
            grad_patch_mid.reshape(seqs_here, frames_here, patches, width),
        ],
        axis=2,
    ).astype(jnp.bfloat16)
    grad_branch_rows = grad_branch.reshape(-1, width)
    grad_space_output = half_gradient(space_mixed.reshape(-1, width), grad_branch_rows)
    grad_space_output_bias = column_sum(grad_branch_rows)
    grad_space_mixed = times_transposed(grad_branch_rows, space_output).astype(jnp.bfloat16)
    grad_space_joined = attend_backward(
        space_joined, space_allowed, space_total, grad_space_mixed, "abl"
    ).reshape(-1, 3 * width)
    grad_space_project = half_gradient(space_normed.reshape(-1, width), grad_space_joined)
    grad_space_normed = times_transposed(grad_space_joined, space_project).reshape(
        seqs_here, frames_here, length, width
    )
    grad_space_rows, grad_space_gain, grad_space_shift = norm_pull(
        space_rows, space_gain, space_shift, grad_space_normed
    )
    class_frames = lax.psum(jnp.sum(grad_space_rows[:, :, 0], axis=1), "ft")
    grad_class = grad_class_mid + class_frames
    grad_after_space = (
        grad_patch_mid.reshape(seqs_here, frames_here, patches, width) + grad_space_rows[:, :, 1:]
    ).astype(jnp.bfloat16)
    grad_after_time = lax.all_to_all(
        grad_after_space, "ft", split_axis=2, concat_axis=1, tiled=True
    )
    grad_time_branch = grad_after_time.reshape(total_rows, width)
    grad_time_mixer = half_gradient(time_outer, grad_time_branch)
    grad_time_mixer_bias = column_sum(grad_time_branch)
    grad_time_outer = times_transposed(grad_time_branch, time_mixer).astype(jnp.bfloat16)
    grad_time_output = half_gradient(time_mixed.reshape(total_rows, width), grad_time_outer)
    grad_time_output_bias = column_sum(grad_time_outer)
    grad_time_mixed = times_transposed(grad_time_outer, time_output).astype(jnp.bfloat16)
    grad_time_joined = attend_backward(
        time_joined, time_allowed, time_total, grad_time_mixed, "alb"
    ).reshape(total_rows, 3 * width)
    grad_time_project = half_gradient(time_normed, grad_time_joined)
    grad_time_normed = times_transposed(grad_time_joined, time_project)
    grad_time_rows, grad_time_gain, grad_time_shift = norm_pull(
        time_rows, time_gain, time_shift, grad_time_normed
    )
    grad_video = (grad_time_branch.astype(jnp.float32) + grad_time_rows).reshape(
        seqs_here, frames, patch_here, width
    )
    narrow = jnp.stack(
        [
            grad_time_gain,
            grad_time_shift,
            grad_time_output_bias,
            grad_time_mixer_bias,
            grad_space_gain,
            grad_space_shift,
            grad_space_output_bias,
            grad_feed_gain,
            grad_feed_shift,
            grad_feed_reduce_bias,
        ],
        axis=1,
    )
    narrow = jnp.concatenate([narrow, grad_feed_expand_bias.reshape(768, 4)], axis=1)
    narrow = jnp.pad(narrow + swap(narrow), ((0, 0), (0, 242)))
    core = lax.rem(lax.axis_index("seq"), 2)
    narrow = lax.dynamic_slice_in_dim(narrow, core * 128, 128, 1).astype(jnp.bfloat16)
    (
        grad_feed_reduce,
        grad_feed_expand,
        grad_space_output,
        grad_space_project,
        grad_time_mixer,
        grad_time_output,
        grad_time_project,
        narrow,
    ) = [
        settle(item)
        for item in reduce_scatter(
            (
                grad_feed_reduce,
                grad_feed_expand,
                grad_space_output,
                grad_space_project,
                grad_time_mixer,
                grad_time_output,
                grad_time_project,
                narrow.reshape(2, 2, 2, 96, 128),
            )
        )
    ]
    shares = (
        narrow[:, 0],
        narrow[:, 1],
        grad_time_project,
        grad_time_output,
        narrow[:, 2],
        grad_time_mixer,
        narrow[:, 3],
        narrow[:, 4],
        narrow[:, 5],
        grad_space_project,
        grad_space_output,
        narrow[:, 6],
        narrow[:, 7],
        narrow[:, 8],
        grad_feed_expand,
        narrow[:, 10:14].reshape(-1),
        grad_feed_reduce,
        narrow[:, 9],
    )
    return (output, class_output, grad_video, grad_class) + tuple(shares)


def solution(mesh):
    in_specs = (
        P("seq", None, "ft", None),
        P("seq", None),
        P("seq", None),
        P("seq", None),
        P("seq", None),
        P("ft"),
        P("ft"),
        P("ft", None),
        P("ft", None),
        P("ft"),
        P("ft", None),
        P("ft"),
        P("ft"),
        P("ft"),
        P("ft", None),
        P("ft", None),
        P("ft"),
        P("ft"),
        P("ft"),
        P("ft", None),
        P("ft"),
        P("ft", None),
        P("ft"),
        P("seq", "ft", None, None),
        P("seq", None),
    )
    out_specs = (
        P("seq", "ft", None, None),
        P("seq", None),
        P("seq", None, "ft", None),
        P("seq", None),
        P(("seq", "ft")),
        P(("seq", "ft")),
        P(("seq", "ft"), None),
        P(("seq", "ft"), None),
        P(("seq", "ft")),
        P(("seq", "ft"), None),
        P(("seq", "ft")),
        P(("seq", "ft")),
        P(("seq", "ft")),
        P(("seq", "ft"), None),
        P(("seq", "ft"), None),
        P(("seq", "ft")),
        P(("seq", "ft")),
        P(("seq", "ft")),
        P(("seq", "ft"), None),
        P(("seq", "ft")),
        P(("seq", "ft"), None),
        P(("seq", "ft")),
    )
    return jax.shard_map(shards, mesh=mesh, in_specs=in_specs, out_specs=out_specs, check_vma=False)
```

```python
import jax
import jax.numpy as jnp
from jax import lax
from jax.experimental import pallas as pl
from jax.experimental.pallas import tpu as pltpu
from jax.sharding import PartitionSpec as P

MESH = pl.DeviceIdType.MESH
bf16 = jnp.bfloat16
f32 = jnp.float32
D = 768
FRAMES = 8
HERE = 49
OWN = 2
PATCHES = 196
TIME_ROWS = 400
TIME_BLOCK = 80
FRAME = 208
CLASS = 196
SPACE_ROWS = OWN * FRAME
SLOT = 64
EPSILON = 1e-06
UNITS = 7


def iota(shape, axis):
    return lax.broadcasted_iota(jnp.int32, shape, axis)


def dot(left, right):
    return jnp.dot(left, right, preferred_element_type=f32)


def dot_nt(left, right):
    return lax.dot_general(left, right, (((1,), (1,)), ((), ())), preferred_element_type=f32)


def dot_tn(left, right):
    return lax.dot_general(left, right, (((0,), (0,)), ((), ())), preferred_element_type=f32)


def picks(condition):
    return jnp.where(condition, 1.0, 0.0).astype(bf16)


def to_patches():
    r, c = iota((TIME_ROWS, FRAMES * SLOT), 0), iota((TIME_ROWS, FRAMES * SLOT), 1)
    return picks((c == (r & 7) * SLOT + (r >> 3)) & (r < FRAMES * HERE))


def to_frames():
    c, r = iota((FRAMES * SLOT, TIME_ROWS), 0), iota((FRAMES * SLOT, TIME_ROWS), 1)
    return picks((c == (r & 7) * SLOT + (r >> 3)) & (r < FRAMES * HERE))


def source_of(token, frame):
    late = (token >= HERE).astype(jnp.int32) + (token >= 2 * HERE) + (token >= 3 * HERE)
    return token + late * (OWN * SLOT - HERE) + frame * SLOT


def to_tokens():
    r, c = iota((SPACE_ROWS, FRAMES * SLOT), 0), iota((SPACE_ROWS, FRAMES * SLOT), 1)
    frame = (r >= FRAME).astype(jnp.int32)
    token = r - frame * FRAME
    return picks((c == source_of(token, frame)) & (token < PATCHES))


def from_tokens():
    c, r = iota((FRAMES * SLOT, SPACE_ROWS), 0), iota((FRAMES * SLOT, SPACE_ROWS), 1)
    frame = (r >= FRAME).astype(jnp.int32)
    token = r - frame * FRAME
    return picks((c == source_of(token, frame)) & (token < PATCHES))


def normed(rows):
    centred = rows - jnp.mean(rows, axis=-1, keepdims=True)
    scale = lax.rsqrt(jnp.mean(centred * centred, axis=-1, keepdims=True) + EPSILON)
    return centred * scale, scale


def over_blocks(count, size, step):
    def body(i, carry):
        step(pl.ds(pl.multiple_of(i * size, 16), size))
        return carry

    lax.fori_loop(0, count, body, 0)


def halves(scale):
    lane = iota((1, 128), 1)
    first = jnp.where(lane < 64, scale, 0.0).astype(bf16)
    second = jnp.where(lane < 64, 0.0, scale).astype(bf16)
    return first, second


def softmax(scores):
    top = jnp.max(scores, axis=-1, keepdims=True)
    power = jnp.exp(scores - top)
    return power * (1.0 / jnp.sum(power, axis=-1, keepdims=True))


def pair(i, j, size):
    rows = pl.ds(pl.multiple_of(i * size, 16), size)
    return rows, [pl.ds(pl.multiple_of(k * D + j * 128, 128), 128) for k in range(3)]


def attend(joined, bias, mixed, blocks, size):
    first8, second8 = halves(0.125)

    def body(n, carry):
        rows, (ql, kl, vl) = pair(n // 6, lax.rem(n, 6), size)
        query, keys, values = joined[rows, ql], joined[rows, kl], joined[rows, vl]
        shut = bias[...]
        one = softmax(dot_nt(query * first8, keys) + shut).astype(bf16)
        two = softmax(dot_nt(query * second8, keys) + shut).astype(bf16)
        out = jnp.where(iota((size, 128), 1) < 64, dot(one, values), dot(two, values))
        mixed[rows, ql] = out.astype(bf16)
        return carry

    lax.fori_loop(0, blocks * 6, body, 0)


def attend_back(joined, bias, grad_mixed, grad_joined, blocks, size):
    first8, second8 = halves(0.125)
    first, second = halves(1.0)

    def body(n, carry):
        rows, (ql, kl, vl) = pair(n // 6, lax.rem(n, 6), size)
        query, keys, values = joined[rows, ql], joined[rows, kl], joined[rows, vl]
        grad = grad_mixed[rows, ql]
        shut = bias[...]
        parts = []
        for q8, one in ((query * first8, grad * first), (query * second8, grad * second)):
            chance = softmax(dot_nt(q8, keys) + shut)
            pull = dot_nt(one, values)
            inner = jnp.sum(chance * pull, axis=-1, keepdims=True)
            scores = (chance * (pull - inner)).astype(bf16)
            parts.append((dot(scores, keys), dot_tn(scores, q8), dot_tn(chance.astype(bf16), one)))
        (dq1, dk1, dv1), (dq2, dk2, dv2) = parts
        left = iota((size, 128), 1) < 64
        grad_joined[rows, ql] = (jnp.where(left, dq1, dq2) * 0.125).astype(bf16)
        grad_joined[rows, kl] = (dk1 + dk2).astype(bf16)
        grad_joined[rows, vl] = (dv1 + dv2).astype(bf16)
        return carry

    lax.fori_loop(0, blocks * 6, body, 0)


def time_bias(frame_clip, bias):
    shape = (TIME_BLOCK, TIME_BLOCK)
    r, c = iota(shape, 0), iota(shape, 1)
    clip_r, clip_c = jnp.zeros(shape, jnp.int32), jnp.zeros(shape, jnp.int32)
    for f in range(FRAMES):
        clip_r = jnp.where((r & 7) == f, frame_clip[0, f], clip_r)
        clip_c = jnp.where((c & 7) == f, frame_clip[0, f], clip_c)
    bias[...] = jnp.where(((r >> 3) == (c >> 3)) & (clip_r == clip_c), 0.0, -1e30)


def space_bias(patch_clip, padding, spare, bias):
    shape = (FRAME, FRAME)
    r, c = iota(shape, 0), iota(shape, 1)
    spare[...] = jnp.full(spare.shape, -1, jnp.int32)
    spare[0:1, 0:PATCHES] = patch_clip[...]
    spare[8:9, 0:PATCHES] = padding[...]
    clip = jnp.broadcast_to(spare[0:1, 0:FRAME], shape).astype(f32)
    shut = jnp.broadcast_to(spare[8:9, 0:FRAME], shape)
    own = jnp.sum(jnp.where(r == c, clip, 0.0), axis=1, keepdims=True)
    opened = (c == CLASS) | ((shut == 0) & ((clip == own) | (r == CLASS)))
    bias[...] = jnp.where(opened, 0.0, -1e30)


def place():
    s = lax.axis_index("seq")
    f = lax.axis_index("ft")
    core = lax.rem(s, 2)
    col = lax.rem(s // 2, 2)
    row = lax.rem(s // 4, 2)
    return s, f, core, col, row


def remote(src, dst, send, recv, target):
    return pltpu.make_async_remote_copy(
        src_ref=src, dst_ref=dst, send_sem=send, recv_sem=recv, device_id=target, device_id_type=MESH
    )


class Spread:
    def __init__(self, shards, fulls, own, send, recv):
        self.shards, self.fulls, self.own, self.send, self.recv = shards, fulls, own, send, recv
        self.s, self.f, self.core, self.col, self.row = place()
        s = self.s
        self.sib = s + 1 - 2 * self.core
        dx, dy = 2 - 4 * self.col, 4 - 8 * self.row
        self.plane = ((s + dx, 1, 0), (s + dy, 0, 1), (s + dx + dy, 1, 1))
        upper = self.f // 2
        near = self.f + upper * (3 - 2 * self.f)
        self.order = [upper * 3 + (1 - 2 * upper) * v for v in (1 - near, 2, 3)]

    def greet(self):
        bar = pltpu.get_barrier_semaphore()
        targets = [(t, self.f) for t in (self.sib,) + tuple(p[0] for p in self.plane)]
        targets += [(self.s, lax.rem(self.f + j, 4)) for j in (1, 2, 3)]
        for t in targets:
            pl.semaphore_signal(bar, inc=1, device_id=t, device_id_type=MESH)
        pl.semaphore_wait(bar, len(targets))

    def cut(self, w, base, row, col):
        rows, wide = self.shards[w].shape
        start = base + self.core * (rows // 2) + row * (rows // 4)
        return (
            pl.ds(pl.multiple_of(start, 16), rows // 4),
            pl.ds(pl.multiple_of(col * (wide // 2), 128), wide // 2),
        )

    def keep(self, w):
        rows = self.shards[w].shape[0]
        dst = self.fulls[w].at[pl.ds(pl.multiple_of(self.f * rows, 16), rows), :]
        return pltpu.make_async_copy(self.shards[w], dst, self.own.at[w])

    def along(self, w, k):
        z = lax.rem(self.f + k, 4)
        rows = self.shards[w].shape[0]
        src = self.shards[w].at[self.cut(w, 0, self.row, self.col)]
        dst = self.fulls[w].at[self.cut(w, self.f * rows, self.row, self.col)]
        return remote(src, dst, self.send.at[w, k - 1], self.recv.at[w, 0, self.f], (self.s, z))

    def start(self, w):
        for k in (1, 3, 2):
            self.along(w, k).start()
        self.keep(w).start()

    def over(self, w, z, i, mine=True):
        target, dx, dy = self.plane[i]
        rows = self.shards[w].shape[0]
        row, col = (self.row, self.col) if mine else (self.row + dy - 2 * dy * self.row, self.col + dx - 2 * dx * self.col)
        ref = self.fulls[w].at[self.cut(w, z * rows, row, col)]
        return remote(ref, ref, self.send.at[w, 3 + 4 * i + z], self.recv.at[w, 1 + i, z], (target, self.f))

    def across(self, w, z, mine=True):
        rows = self.shards[w].shape[0]
        core = self.core if mine else 1 - self.core
        ref = self.fulls[w].at[pl.ds(pl.multiple_of(z * rows + core * (rows // 2), 16), rows // 2), :]
        return remote(ref, ref, self.send.at[w, 15 + z], self.recv.at[w, 4, z], (self.sib, self.f))

    def fan(self, w):
        rows = self.shards[w].shape[0]
        for z in self.order:
            ref = self.fulls[w].at[self.cut(w, z * rows, self.row, self.col)]
            remote(ref, ref, self.send.at[w, 0], self.recv.at[w, 0, z], (self.s, z)).wait_recv()
            for i in (2, 0, 1):
                self.over(w, z, i).start()

    def lend(self, w):
        for z in self.order:
            for i in range(3):
                self.over(w, z, i, False).wait_recv()
            self.across(w, z).start()

    def finish(self, w):
        for z in self.order:
            self.across(w, z, False).wait_recv()
        self.keep(w).wait()

    def drain(self, w):
        for k in (1, 2, 3):
            self.along(w, k).wait_send()
        for z in self.order:
            for i in range(3):
                self.over(w, z, i).wait_send()
            self.across(w, z).wait_send()


class Loads:
    def __init__(self, slots, sems, sources):
        self.slots, self.sems, self.sources = slots, sems, sources

    def copies(self, i):
        n = i % self.slots.shape[0]
        out = []
        for k, (src, rows, cols) in enumerate(self.sources[i]):
            out.append(pltpu.make_async_copy(src, self.slots.at[n, rows, cols], self.sems.at[n, k]))
        return out

    def start(self, i):
        for c in self.copies(i):
            c.start()

    def get(self, i):
        for c in self.copies(i):
            c.wait()
        return self.slots[i % self.slots.shape[0]]


ALL = slice(None)


def squares(ref, count):
    return [[(ref.at[:, i * D : (i + 1) * D], ALL, ALL)] for i in range(count)]


def feed_pieces(expand, reduce, core, high):
    wide, tall = [], []
    for x in range(2):
        start = pl.multiple_of(((high * 2 + x) * 2 + core) * 384, 128)
        at = slice(x * 384, (x + 1) * 384)
        wide.append((expand.at[:, pl.ds(start, 384)], ALL, at))
        tall.append((reduce.at[pl.ds(start, 384), :], at, ALL))
    return wide, tall


def forward_kernel(*refs):
    (video, class_token, frame_clip, patch_clip, padding, vectors, grad_output, grad_class_out) = refs[:8]
    shards = refs[8:15]
    outs = refs[15:43]
    (output, class_output) = outs[:2]
    fulls = outs[2:9]
    (x_t, n_t, j_t, m_t, o_t, x_s, n_s, j_s, m_s, n_f, cot, act, gh, act_sib, gh_sib, gmid, gb, sums, small_out) = outs[9:28]
    (own, send, recv, vec, vec32, vsend, vrecv, slots, slot_sems, xf, a2s, a2r, asend, arecv, tbias, sbias, spare,
     rows_f, acc, acc2, hid, gact, cls, csend, crecv, psend, precv, act_go, gh_go) = refs[43:]

    net = Spread(shards, fulls, own, send, recv)
    s, f, core = net.s, net.f, net.core
    net.greet()

    def vec_copy(k):
        return remote(vectors, vec.at[f], vsend.at[k - 1], vrecv.at[f], (s, lax.rem(f + k, 4)))

    for k in (1, 3, 2):
        vec_copy(k).start()
    net.start(0)
    net.start(1)
    net.start(2)
    vec[f] = vectors[...]

    for i in range(FRAMES):
        xf[i, 48:SLOT] = jnp.zeros((SLOT - 48, D), bf16)
        xf[i, 0:HERE] = video[i]
    x_t[...] = dot(to_patches(), xf[...].reshape(FRAMES * SLOT, D)).astype(bf16)
    time_bias(frame_clip, tbias)
    space_bias(patch_clip, padding, spare, sbias)

    cot[...] = jnp.zeros_like(cot)
    cot[0:PATCHES] = grad_output[0]
    cot[FRAME : FRAME + PATCHES] = grad_output[1]
    at_class = iota((16, D), 0) == CLASS - 192
    tail = jnp.where(at_class, grad_class_out[...].astype(f32), cot[192:FRAME].astype(f32))
    cot[192:FRAME] = tail.astype(bf16)

    for k in (1, 3, 2):
        z = lax.rem(f + k, 4)
        remote(vectors, vec.at[z], vsend.at[0], vrecv.at[z], (s, z)).wait_recv()
    small = jnp.zeros((16, D), f32)
    for z in range(4):
        r, c = iota((384, D), 0), iota((384, D), 1)
        small += dot(vec[z], picks((c == r + z * 192) & (r < 192)))
    vec32[0] = small
    small_out[...] = small
    for z in range(4):
        vec32[1 + z] = jnp.concatenate([vec[z].astype(f32), jnp.zeros((16, 384), f32)], axis=1)

    def vector(i):
        return vec32[0, i : i + 1, :]

    gain, shift = vector(0), vector(1)

    def norm_time(rows):
        scaled, unused = normed(x_t[rows].astype(f32))
        n_t[rows] = (scaled * gain + shift).astype(bf16)

    over_blocks(5, 80, norm_time)

    sources = (
        squares(fulls[0], 3) + squares(fulls[1], 1) + squares(fulls[2], 1) + squares(fulls[3], 3) + squares(fulls[4], 1)
    )
    for c, high in ((1 - core, 0), (1 - core, 1), (core, 0), (core, 1)):
        wide, tall = feed_pieces(fulls[5], fulls[6], c, high)
        sources += [wide, tall]
    loads = Loads(slots, slot_sems, sources)

    net.fan(0)
    net.start(3)
    net.lend(0)
    net.fan(1)
    net.fan(2)
    net.start(4)
    net.finish(0)
    for i in range(3):
        loads.start(i)
    net.lend(1)
    net.lend(2)
    for i in range(3):
        j_t[:, i * D : (i + 1) * D] = dot(n_t[...], loads.get(i)).astype(bf16)
    net.fan(3)
    net.start(5)
    net.finish(1)
    loads.start(3)
    net.finish(2)
    loads.start(4)
    attend(j_t, tbias, m_t, 5, TIME_BLOCK)
    net.lend(3)
    net.fan(4)
    net.start(6)
    o_t[...] = (dot(m_t[...], loads.get(3)) + vector(2)).astype(bf16)
    after = (x_t[...].astype(f32) + (dot(o_t[...], loads.get(4)) + vector(3))).astype(bf16)
    a2s[...] = dot(to_frames(), after).astype(bf16).reshape(4, OWN, SLOT, D)

    def a_copy(k):
        z = lax.rem(f + k, 4)
        return remote(a2s.at[z], a2r.at[f], asend.at[k - 1], arecv.at[f], (s, z))

    for k in (1, 3, 2):
        a_copy(k).start()
    a2r[f] = a2s[f]
    net.finish(3)
    for i in range(5, 8):
        loads.start(i)
    net.lend(4)
    net.fan(5)
    for k in (1, 3, 2):
        z = lax.rem(f + k, 4)
        remote(a2s.at[z], a2r.at[z], asend.at[0], arecv.at[z], (s, z)).wait_recv()

    spread_rows = dot(to_tokens(), a2r[...].reshape(FRAMES * SLOT, D))
    r = iota((SPACE_ROWS, D), 0)
    is_class = (r == CLASS) | (r == FRAME + CLASS)
    x_s[...] = jnp.where(is_class, class_token[...].astype(f32), spread_rows).astype(bf16)
    gain, shift = vector(4), vector(5)

    def norm_space(rows):
        scaled, unused = normed(x_s[rows].astype(f32))
        n_s[rows] = (scaled * gain + shift).astype(bf16)

    over_blocks(13, 32, norm_space)
    for i in range(3):
        j_s[:, i * D : (i + 1) * D] = dot(n_s[...], loads.get(5 + i)).astype(bf16)
    net.finish(4)
    loads.start(8)
    net.lend(5)
    net.fan(6)
    attend(j_s, sbias, m_s, OWN, FRAME)
    net.lend(6)
    rows_f[...] = dot(m_s[...], loads.get(8)) + vector(6)
    token = class_token[...].astype(f32)
    cls[f] = jnp.broadcast_to(
        rows_f[CLASS : CLASS + 1] + rows_f[FRAME + CLASS : FRAME + CLASS + 1], (8, D)
    )

    def c_copy(k):
        return remote(cls.at[f], cls.at[f], csend.at[k - 1], crecv.at[f], (s, lax.rem(f + k, 4)))

    for k in (1, 3, 2):
        c_copy(k).start()
    net.finish(5)
    net.finish(6)
    for i in range(9, 12):
        loads.start(i)
    for k in (1, 3, 2):
        z = lax.rem(f + k, 4)
        remote(cls.at[f], cls.at[z], csend.at[0], crecv.at[z], (s, z)).wait_recv()
    mid = token + ((cls[0] + cls[1]) + (cls[2] + cls[3]))[0:1] * (1.0 / FRAMES)
    gain, shift = vector(7), vector(8)
    first = jnp.where(f == 0, 1.0, 0.0)

    def norm_feed(rows):
        r = iota((32, D), 0) + rows.start
        at_class = r == CLASS
        other = r == FRAME + CLASS
        values = x_s[rows].astype(f32) + rows_f[rows]
        values = jnp.where(at_class, mid, jnp.where(other, 0.0, values))
        rows_f[rows] = values
        scaled, unused = normed(values)
        n_f[rows] = (scaled * gain + shift).astype(bf16)
        acc[rows] = values + vector(9)
        acc2[rows] = jnp.zeros((32, D), f32)

    over_blocks(13, 32, norm_feed)

    def sib_copy(k, half, src, dst):
        return remote(src.at[half], dst.at[half], psend.at[k, half], precv.at[k, half], (net.sib, f))

    for j in range(4):
        c = 1 - core if j < 2 else core
        high = j & 1
        bias = jnp.concatenate(
            [vec32[1 + 2 * high + x, pl.ds(10 + c, 1), 0:384] for x in range(2)], axis=1
        )
        w1 = loads.get(9 + 2 * j)
        hid[...] = dot(n_f[...], w1) + bias
        w2 = loads.get(10 + 2 * j)
        gact[...] = dot_nt(cot[...], w2)
        act_to, gh_to = (act_go, gh_go) if j < 2 else (act, gh)

        def feed(rows):
            hidden = hid[rows]
            tail = 0.5 + 0.5 * lax.erf(hidden * 0.7071067811865476)
            slope = tail + hidden * (jnp.exp(hidden * hidden * -0.5) * 0.3989422804014327)
            act_to[high, rows] = (hidden * tail).astype(bf16)
            gh_to[high, rows] = (gact[rows] * slope).astype(bf16)

        over_blocks(13, 32, feed)
        acc[...] += dot(act_to[high], w2)
        acc2[...] += dot_nt(gh_to[high], w1)
        if j < 3:
            for i in (12 + 2 * j, 13 + 2 * j):
                if i < 17:
                    loads.start(i)

        at_class = iota((16, D), 0) == CLASS - 192
        for ref in (act_to, gh_to):
            piece = ref[high, 192:FRAME].astype(f32)
            ref[high, 192:FRAME] = jnp.where(at_class, piece * first, piece).astype(bf16)
        if j < 2:
            sib_copy(0, high, act_go, act_sib).start()
            sib_copy(1, high, gh_go, gh_sib).start()

    output[0] = acc[0:PATCHES].astype(bf16)
    output[1] = acc[FRAME : FRAME + PATCHES].astype(bf16)
    class_output[...] = acc[CLASS : CLASS + 1].astype(bf16)
    gain = vector(7)
    sums[...] = jnp.zeros_like(sums)

    def feed_back(rows):
        r = iota((32, D), 0) + rows.start
        scaled, scale = normed(rows_f[rows])
        pulled = acc2[rows]
        counted = jnp.where(r == CLASS, pulled * first, pulled)
        sums[0:8] += jnp.sum((counted * scaled).reshape(4, 8, D), axis=0)
        sums[8:16] += jnp.sum(counted.reshape(4, 8, D), axis=0)
        up = pulled * gain
        back = scale * (
            up - jnp.mean(up, axis=-1, keepdims=True) - scaled * jnp.mean(up * scaled, axis=-1, keepdims=True)
        )
        grad = cot[rows].astype(f32) + back
        gmid[rows] = grad
        gb[rows] = grad.astype(bf16)

    over_blocks(13, 32, feed_back)
    row = (gmid[CLASS : CLASS + 1] * (1.0 / FRAMES)).astype(bf16).astype(f32)
    for start in (192, FRAME + 192):
        piece = gb[start : start + 16].astype(f32)
        gb[start : start + 16] = jnp.where(at_class, row, piece).astype(bf16)

    for half in range(2):
        for k, src, dst in ((0, act_go, act_sib), (1, gh_go, gh_sib)):
            sib_copy(k, half, src, dst).wait()
    for k in (1, 2, 3):
        vec_copy(k).wait_send()
        a_copy(k).wait_send()
        c_copy(k).wait_send()
    for w in range(UNITS):
        net.drain(w)


def forward(video, class_token, frame_clip, patch_clip, padding, vectors, grad_output, grad_class_out, shards):
    vm = pl.BlockSpec(memory_space=pltpu.VMEM)
    sm = pl.BlockSpec(memory_space=pltpu.SMEM)
    hbm = pl.BlockSpec(memory_space=pl.ANY)
    sds = jax.ShapeDtypeStruct
    sem = pltpu.SemaphoreType.DMA
    v = pltpu.VMEM
    t, p = TIME_ROWS, SPACE_ROWS
    outs = [sds((OWN, PATCHES, D), bf16), sds((1, D), bf16)]
    outs += [sds((4 * a.shape[0], a.shape[1]), bf16) for a in shards]
    outs += [sds((t, D), bf16), sds((t, D), bf16), sds((t, 3 * D), bf16), sds((t, D), bf16), sds((t, D), bf16)]
    outs += [sds((p, D), bf16), sds((p, D), bf16), sds((p, 3 * D), bf16), sds((p, D), bf16), sds((p, D), bf16)]
    outs += [sds((p, D), bf16)] + [sds((2, p, D), bf16)] * 4 + [sds((p, D), f32), sds((p, D), bf16), sds((16, D), f32), sds((16, D), f32)]
    return pl.pallas_call(
        forward_kernel,
        out_shape=outs,
        in_specs=[vm, vm, sm, vm, vm, vm, vm, vm] + [hbm] * 7,
        out_specs=[vm, vm] + [hbm] * 7 + [vm] * 19,
        scratch_shapes=[
            sem((UNITS,)),
            sem((UNITS, 19)),
            sem((UNITS, 5, 4)),
            v((4, 16, 384), bf16),
            v((5, 16, D), f32),
            sem((3,)),
            sem((4,)),
            v((4, D, D), bf16),
            sem((4, 2)),
            v((FRAMES, SLOT, D), bf16),
            v((4, OWN, SLOT, D), bf16),
            v((4, OWN, SLOT, D), bf16),
            sem((3,)),
            sem((4,)),
            v((TIME_BLOCK, TIME_BLOCK), f32),
            v((FRAME, FRAME), f32),
            v((16, 256), jnp.int32),
            v((p, D), f32),
            v((p, D), f32),
            v((p, D), f32),
            v((p, D), f32),
            v((p, D), f32),
            v((4, 8, D), f32),
            sem((3,)),
            sem((4,)),
            sem((2, 2)),
            sem((2, 2)),
            v((2, p, D), bf16),
            v((2, p, D), bf16),
        ],
        compiler_params=pltpu.CompilerParams(
            collective_id=1, has_side_effects=True, vmem_limit_bytes=63 << 20
        ),
        name="forward",
    )(video, class_token, frame_clip, patch_clip, padding, vectors, grad_output, grad_class_out, *shards)


class Reduce:
    def __init__(self, parts, ra, rb, ra2, rb2, rz, total, rc, sems):
        self.parts, self.ra, self.rb, self.ra2, self.rb2 = parts, ra, rb, ra2, rb2
        self.rz, self.total, self.rc, self.sems = rz, total, rc, sems
        self.s, self.f, self.core, self.col, self.row = place()
        s = self.s
        self.sib = s + 1 - 2 * self.core
        self.across, self.down = s + 2 - 4 * self.col, s + 4 - 8 * self.row

    def greet(self):
        bar = pltpu.get_barrier_semaphore()
        targets = [(t, self.f) for t in (self.sib, self.across, self.down)]
        targets += [(self.s, lax.rem(self.f + j, 4)) for j in (1, 2, 3)]
        for t in targets:
            pl.semaphore_signal(bar, inc=1, device_id=t, device_id_type=MESH)
        pl.semaphore_wait(bar, len(targets))

    def sem(self, w, i):
        return self.sems.at[w, i]

    def copies1(self, w):
        g = self.parts[w]
        return (
            remote(g.at[:, 1 - self.col, 0], self.ra[w], self.sem(w, 0), self.sem(w, 1), (self.across, self.f)),
            remote(g.at[1 - self.row, :, 1], self.rb[w], self.sem(w, 2), self.sem(w, 3), (self.down, self.f)),
        )

    def copies2(self, w):
        return (
            remote(self.ra[w].at[1 - self.row], self.ra2[w], self.sem(w, 4), self.sem(w, 5), (self.down, self.f)),
            remote(self.rb[w].at[1 - self.col], self.rb2[w], self.sem(w, 6), self.sem(w, 7), (self.across, self.f)),
        )

    def block(self, w, z):
        g = self.parts[w]
        rows = g.shape[3] // 2
        return g.at[z // 2, 1 - self.col, 0, pl.ds(pl.multiple_of(lax.rem(z, 2) * rows, 16), rows), :]

    def copies3(self, w):
        out = []
        for j in (1, 3, 2):
            z = lax.rem(self.f + j, 4)
            out.append(
                remote(self.block(w, z), self.rz[w].at[3 - j], self.sem(w, 7 + j), self.sem(w, 14 - j), (self.s, z))
            )
        return out

    def copy4(self, w):
        return remote(
            self.total[w].at[1 - self.core], self.rc[w], self.sem(w, 14), self.sem(w, 15), (self.sib, self.f)
        )

    def step1(self, w):
        for c in self.copies1(w):
            c.start()

    def step2(self, w):
        a, b = self.copies1(w)
        g, ra, rb = self.parts[w], self.ra[w], self.rb[w]
        row, col = self.row, self.col
        a2, b2 = self.copies2(w)
        a.wait_recv()
        ra[1 - row] = (ra[1 - row].astype(f32) + g[1 - row, col, 0].astype(f32)).astype(bf16)
        a2.start()
        b.wait_recv()
        rb[1 - col] = (rb[1 - col].astype(f32) + g[row, 1 - col, 1].astype(f32)).astype(bf16)
        b2.start()

    def step3(self, w):
        a, b = self.copies1(w)
        a2, b2 = self.copies2(w)
        g = self.parts[w]
        row, col = self.row, self.col
        part = g.shape[3] // 4
        a.wait_send()
        b2.wait_recv()
        a2.wait_recv()
        for z in range(4):
            rows = pl.ds(z * part, part)
            sums = []
            for k, near, far in ((0, self.ra[w].at[row], self.ra2[w]), (1, self.rb[w].at[col], self.rb2[w])):
                own = g.at[row, col, k]
                if part % 16:
                    tops = z * part // 16 * 16
                    high = -(-(z + 1) * part // 16) * 16
                    wide = [ref[tops:high].astype(f32) for ref in (own, near, far)]
                    low = z * part - tops
                    sums.append((wide[0] + wide[1] + wide[2])[low : low + part])
                else:
                    sums.append(own[rows].astype(f32) + near[rows].astype(f32) + far[rows].astype(f32))
            at = self.block(w, z)
            at[...] = jnp.concatenate(sums, axis=0).astype(bf16)
        for c in self.copies3(w):
            c.start()

    def step4(self, w, swap=True):
        for c in self.copies3(w):
            c.wait_recv()
        rz, part = self.rz[w], self.parts[w].shape[3] // 4
        whole = (self.block(w, self.f)[...].astype(f32) + rz[0].astype(f32)) + (
            rz[1].astype(f32) + rz[2].astype(f32)
        )
        self.total[w][0] = whole[:part]
        self.total[w][1] = whole[part:]
        if swap:
            self.copy4(w).start()

    def step5(self, w):
        self.copy4(w).wait_recv()

    def drain(self, w, swap=True):
        a, b = self.copies1(w)
        b.wait_send()
        for c in list(self.copies2(w)) + self.copies3(w) + ([self.copy4(w)] if swap else []):
            c.wait_send()


REDUCE, EXPAND, SPACE_OUT, SPACE_JOIN, MIX, TIME_OUT, TIME_JOIN, NARROW = range(8)
PARTS = ((384, 384), (96, 1536), (96, 384), (96, 1152), (96, 384), (96, 384), (96, 1152), (96, 128))


def backward_kernel(*refs):
    (frame_clip, patch_clip, padding, vec, sums, x_t, n_t, j_t, m_t, o_t, x_s, n_s, j_s, m_s, n_f, cot, gmid, gb) = refs[:18]
    act, gh, act_sib, gh_sib, w_tp, w_to, w_tm, w_sp, w_so = refs[18:27]
    (d_video, d_class, d_reduce, d_expand, d_so, d_sp, d_tm, d_to, d_tp, d_narrow) = refs[27:37]
    (parts, ra, rb, ra2, rb2, rz, total, rc, rsems, slots, slot_sems, act_v, gh_v, feed_sems, tbias, sbias, spare,
     gsm, wide, gat, gto, gtm, a2s, a2r, asend, arecv, cls, csend, crecv, bias_col, vt,
     n_f2, cot2, m_s2, gb2, n_s2, gjs2, o_t2, gat2, m_t2, gto2, n_t2, gjt2, xsend, xrecv) = refs[37:]
    red = Reduce(parts, ra, rb, ra2, rb2, rz, total, rc, rsems)
    s, f, core, sib = red.s, red.f, red.core, red.sib
    red.greet()

    def half_of(ref, wide_half, which):
        return ref.at[:, pl.ds(pl.multiple_of(which * wide_half, 128), wide_half)]

    exchange = [
        (cot, cot2), (n_f, n_f2), (m_s, m_s2), (half_of(gb, 384, 1 - core), gb2), (n_s, n_s2), (o_t, o_t2),
        (m_t, m_t2), (n_t, n_t2),
    ]
    gjs = act_v.at[:, 0 : 3 * D]
    gjt = gh_v.at[0:TIME_ROWS, 0 : 3 * D]
    exchange += [
        (half_of(gjs, 1152, 1 - core), gjs2), (half_of(gat, 384, 1 - core), gat2),
        (half_of(gto, 384, 1 - core), gto2), (half_of(gjt, 1152, 1 - core), gjt2),
    ]
    GJS, GAT, GTO, GJT = 8, 9, 10, 11

    def trade(k):
        src, dst = exchange[k]
        return remote(src, dst, xsend.at[k], xrecv.at[k], (sib, f))

    loads_feed = []
    for k, (src, dst, at) in enumerate(
        ((act, act_v, 0), (act_sib, act_v, 2), (gh, gh_v, 0), (gh_sib, gh_v, 2))
    ):
        for half in range(2):
            lanes = slice((at + half) * D, (at + half + 1) * D)
            loads_feed.append(pltpu.make_async_copy(src.at[half], dst.at[:, lanes], feed_sems.at[2 * k + half]))
    for c in loads_feed:
        c.start()
    for k in range(8):
        trade(k).start()
    loads = Loads(slots, slot_sems, squares(w_so, 1) + squares(w_sp, 3) + squares(w_tm, 1) + squares(w_to, 1) + squares(w_tp, 3))
    for i in range(3):
        loads.start(i)
    time_bias(frame_clip, tbias)
    space_bias(patch_clip, padding, spare, sbias)

    first = jnp.where(f == 0, 1.0, 0.0)
    vt[...] = jnp.zeros_like(vt)
    counts = jnp.where(iota((16, SPACE_ROWS), 1) == CLASS, first, 1.0).astype(bf16)
    ones_s = jnp.ones((16, SPACE_ROWS), bf16)
    ones_t = jnp.ones((16, TIME_ROWS), bf16)
    vt[7:8] = jnp.sum(sums[0:8], axis=0, keepdims=True)
    vt[8:9] = jnp.sum(sums[8:16], axis=0, keepdims=True)
    vt[9:10] = dot(counts, cot[...])[0:1]
    vt[6:7] = dot(ones_s, gb[...])[0:1]

    for c in loads_feed[:4]:
        c.wait()
    trade(0).wait_recv()
    for y in range(2):
        grad = dot_tn(act_v[:, y * D : (y + 1) * D], cot[...]) + dot_tn(act_v[:, (2 + y) * D : (3 + y) * D], cot2[...])
        for x in range(2):
            for k in range(2):
                parts[REDUCE][y, x, k] = grad[x * 384 : (x + 1) * 384, k * 384 : (k + 1) * 384].astype(bf16)
    red.step1(REDUCE)
    for c in loads_feed[4:]:
        c.wait()
    trade(1).wait_recv()

    def put(w, lanes, grad):
        for y in range(2):
            for x in range(2):
                for k in range(2):
                    start = ((y * 2 + x) * 2 + k) * 96
                    parts[w][y, x, k, :, lanes] = grad[start : start + 96].astype(bf16)

    for y in range(2):
        own, other = gh_v[:, y * D : (y + 1) * D], gh_v[:, (2 + y) * D : (3 + y) * D]
        grad = dot_tn(n_f[...], own) + dot_tn(n_f2[...], other)
        put(EXPAND, slice(y * D, (y + 1) * D), grad)
        ones = jnp.ones((SPACE_ROWS, 128), bf16)
        bias_col[y] = dot_tn(own, ones) + dot_tn(other, ones)
    red.step1(EXPAND)

    trade(2).wait_recv()
    trade(3).wait_recv()
    mine = half_of(gb, 384, core)
    put(SPACE_OUT, ALL, dot_tn(m_s[...], mine[...]) + dot_tn(m_s2[...], gb2[...]))
    red.step1(SPACE_OUT)
    gsm[...] = dot_nt(gb[...], loads.get(0)).astype(bf16)
    loads.start(3)
    attend_back(j_s, sbias, gsm, gjs, OWN, FRAME)
    trade(GJS).start()
    red.step2(REDUCE)
    wide[...] = dot_nt(gjs[:, 0:D], loads.get(1))
    loads.start(4)
    wide[...] += dot_nt(gjs[:, D : 2 * D], loads.get(2))
    loads.start(5)
    wide[...] += dot_nt(gjs[:, 2 * D : 3 * D], loads.get(3))
    loads.start(6)
    gain = vec[4:5]

    def norm_back(source, gain, at, size, rows):
        scaled, scale = normed(source[rows].astype(f32))
        pulled = wide[rows]
        vt[at : at + 8] += jnp.sum((pulled * scaled).reshape(size // 8, 8, D), axis=0)
        vt[at + 8 : at + 16] += jnp.sum(pulled.reshape(size // 8, 8, D), axis=0)
        up = pulled * gain
        return scale * (
            up - jnp.mean(up, axis=-1, keepdims=True) - scaled * jnp.mean(up * scaled, axis=-1, keepdims=True)
        )

    def space_back(rows):
        back = norm_back(x_s, gain, 16, 32, rows)
        wide[rows] = back
        gsm[rows] = (gmid[rows] + back).astype(bf16)

    over_blocks(13, 32, space_back)
    a2s[...] = dot(from_tokens(), gsm[...]).astype(bf16).reshape(4, OWN, SLOT, D)

    def a_copy(k):
        z = lax.rem(f + k, 4)
        return remote(a2s.at[z], a2r.at[f], asend.at[k - 1], arecv.at[f], (s, z))

    for k in (1, 3, 2):
        a_copy(k).start()
    a2r[f] = a2s[f]
    cls[f] = jnp.broadcast_to(wide[CLASS : CLASS + 1] + wide[FRAME + CLASS : FRAME + CLASS + 1], (8, D))

    def c_copy(k):
        return remote(cls.at[f], cls.at[f], csend.at[k - 1], crecv.at[f], (s, lax.rem(f + k, 4)))

    for k in (1, 3, 2):
        c_copy(k).start()
    red.step2(EXPAND)
    red.step3(REDUCE)
    trade(4).wait_recv()
    trade(GJS).wait_recv()
    mine = half_of(gjs, 1152, core)
    put(SPACE_JOIN, ALL, dot_tn(n_s[...], mine[...]) + dot_tn(n_s2[...], gjs2[...]))
    red.step1(SPACE_JOIN)
    for k in (1, 3, 2):
        z = lax.rem(f + k, 4)
        remote(a2s.at[z], a2r.at[z], asend.at[0], arecv.at[z], (s, z)).wait_recv()

    gat[...] = dot(to_patches(), a2r[...].reshape(FRAMES * SLOT, D)).astype(bf16)
    trade(GAT).start()
    gto[...] = dot_nt(gat[...], loads.get(4)).astype(bf16)
    loads.start(7)
    trade(GTO).start()
    gtm[...] = dot_nt(gto[...], loads.get(5)).astype(bf16)
    loads.start(8)
    red.step2(SPACE_OUT)
    red.step3(EXPAND)
    red.step4(REDUCE, False)
    d_reduce[:, 0:384] = total[REDUCE][0]
    d_reduce[:, 384:768] = total[REDUCE][1]
    trade(5).wait_recv()
    trade(GAT).wait_recv()
    mine = half_of(gat, 384, core)
    put(MIX, ALL, dot_tn(o_t[...], mine[...]) + dot_tn(o_t2[...], gat2[...]))
    red.step1(MIX)
    trade(6).wait_recv()
    trade(GTO).wait_recv()
    mine = half_of(gto, 384, core)
    put(TIME_OUT, ALL, dot_tn(m_t[...], mine[...]) + dot_tn(m_t2[...], gto2[...]))
    red.step1(TIME_OUT)
    attend_back(j_t, tbias, gtm, gjt, 5, TIME_BLOCK)
    trade(GJT).start()
    red.step2(SPACE_JOIN)
    red.step3(SPACE_OUT)
    red.step4(EXPAND)
    trade(7).wait_recv()
    trade(GJT).wait_recv()
    mine = half_of(gjt, 1152, core)
    put(TIME_JOIN, ALL, dot_tn(n_t[...], mine[...]) + dot_tn(n_t2[...], gjt2[...]))
    red.step1(TIME_JOIN)
    rows = pl.ds(0, TIME_ROWS)
    wide[rows] = dot_nt(gjt[:, 0:D], loads.get(6))
    wide[rows] += dot_nt(gjt[:, D : 2 * D], loads.get(7))
    wide[rows] += dot_nt(gjt[:, 2 * D : 3 * D], loads.get(8))
    red.step2(MIX)
    red.step2(TIME_OUT)
    red.step3(SPACE_JOIN)
    red.step4(SPACE_OUT)
    gain = vec[0:1]

    def time_back(rows):
        back = norm_back(x_t, gain, 32, 80, rows)
        d_video[rows] = gat[rows].astype(f32) + back

    over_blocks(5, 80, time_back)
    vt[3:4] = dot(ones_t, gat[...])[0:1]
    vt[2:3] = dot(ones_t, gto[...])[0:1]
    for row, at in ((4, 16), (5, 24), (0, 32), (1, 40)):
        vt[row : row + 1] = jnp.sum(vt[at : at + 8], axis=0, keepdims=True)
    place_at = picks(iota((16, 128), 0) == iota((16, 128), 1))
    put(NARROW, ALL, dot_tn(vt[0:16].astype(bf16), place_at))
    lane = iota((24, 128), 1)
    for y in range(2):
        for x in range(2):
            pieces = []
            for z in range(4):
                piece = jnp.zeros((24, 128), f32)
                for k in range(4):
                    column = bias_col[y, pl.ds(x * 384 + z * 96 + k, 24, stride=4), :]
                    piece = jnp.where(lane == 10 + k, column, piece)
                pieces.append(piece)
            at = parts[NARROW].at[y, x, core]
            at[...] = (at[...].astype(f32) + jnp.concatenate(pieces, axis=0)).astype(bf16)
    red.step1(NARROW)

    def place_halves(w, out, half):
        red.step5(w)
        mine = half_of(out, half, core)
        mine[...] = total[w][core]
        other = half_of(out, half, 1 - core)
        other[...] = rc[w][...]

    for k in (1, 3, 2):
        z = lax.rem(f + k, 4)
        remote(cls.at[f], cls.at[z], csend.at[0], crecv.at[z], (s, z)).wait_recv()
    d_class[...] = gmid[CLASS : CLASS + 1] + ((cls[0] + cls[1]) + (cls[2] + cls[3]))[0:1]
    red.step5(EXPAND)
    for y in range(2):
        for x in range(2):
            lanes = slice((y * 2 + x) * 384, (y * 2 + x + 1) * 384)
            for c, piece in ((core, total[EXPAND][core]), (1 - core, rc[EXPAND][...])):
                start = pl.multiple_of(((y * 2 + x) * 2 + c) * 384, 128)
                d_expand[:, pl.ds(start, 384)] = piece[:, lanes]
    red.step2(TIME_JOIN)
    red.step3(MIX)
    red.step3(TIME_OUT)
    red.step4(SPACE_JOIN)
    place_halves(SPACE_OUT, d_so, 384)
    red.step2(NARROW)
    red.step3(TIME_JOIN)
    red.step4(MIX)
    red.step4(TIME_OUT)
    place_halves(SPACE_JOIN, d_sp, 1152)
    red.step3(NARROW)
    place_halves(MIX, d_tm, 384)
    place_halves(TIME_OUT, d_to, 384)
    red.step4(TIME_JOIN)
    red.step4(NARROW)
    place_halves(TIME_JOIN, d_tp, 1152)
    red.step5(NARROW)
    d_narrow[...] = total[NARROW][core] + rc[NARROW][...]
    for w in range(8):
        red.drain(w, w != REDUCE)
    for k in range(12):
        trade(k).wait_send()
    for k in (1, 2, 3):
        a_copy(k).wait_send()
        c_copy(k).wait_send()


def backward(frame_clip, patch_clip, padding, vec, saved, fulls):
    (x_t, n_t, j_t, m_t, o_t, x_s, n_s, j_s, m_s, n_f, cot, act, gh, act_sib, gh_sib, gmid, gb, sums) = saved
    vm = pl.BlockSpec(memory_space=pltpu.VMEM)
    sm = pl.BlockSpec(memory_space=pltpu.SMEM)
    hbm = pl.BlockSpec(memory_space=pl.ANY)
    sds = jax.ShapeDtypeStruct
    sem = pltpu.SemaphoreType.DMA
    v = pltpu.VMEM
    t, p = TIME_ROWS, SPACE_ROWS
    return pl.pallas_call(
        backward_kernel,
        out_shape=[
            sds((t, D), f32), sds((1, D), f32), sds((96, D), f32), sds((24, 4 * D), f32), sds((24, D), f32),
            sds((24, 3 * D), f32), sds((24, D), f32), sds((24, D), f32), sds((24, 3 * D), f32), sds((24, 128), f32),
        ],
        in_specs=[sm] + [vm] * 17 + [hbm] * 9,
        out_specs=[vm] * 10,
        scratch_shapes=[
            [v((2, 2, 2, r, c), bf16) for r, c in PARTS],
            [v((2, r, c), bf16) for r, c in PARTS],
            [v((2, r, c), bf16) for r, c in PARTS],
            [v((r, c), bf16) for r, c in PARTS],
            [v((r, c), bf16) for r, c in PARTS],
            [v((3, r // 2, c), bf16) for r, c in PARTS],
            [v((2, r // 4, c), f32) for r, c in PARTS],
            [v((r // 4, c), f32) for r, c in PARTS],
            sem((8, 16)),
            v((3, D, D), bf16),
            sem((3, 2)),
            v((p, 4 * D), bf16),
            v((p, 4 * D), bf16),
            sem((8,)),
            v((TIME_BLOCK, TIME_BLOCK), f32),
            v((FRAME, FRAME), f32),
            v((16, 256), jnp.int32),
            v((p, D), bf16),
            v((p, D), f32),
            v((t, D), bf16),
            v((t, D), bf16),
            v((t, D), bf16),
            v((4, OWN, SLOT, D), bf16),
            v((4, OWN, SLOT, D), bf16),
            sem((3,)),
            sem((4,)),
            v((4, 8, D), f32),
            sem((3,)),
            sem((4,)),
            v((2, D, 128), f32),
            v((48, D), f32),
            v((p, D), bf16),
            v((p, D), bf16),
            v((p, D), bf16),
            v((p, 384), bf16),
            v((p, D), bf16),
            v((p, 1152), bf16),
            v((t, D), bf16),
            v((t, 384), bf16),
            v((t, D), bf16),
            v((t, 384), bf16),
            v((t, D), bf16),
            v((t, 1152), bf16),
            sem((12,)),
            sem((12,)),
        ],
        compiler_params=pltpu.CompilerParams(
            collective_id=2, has_side_effects=True, vmem_limit_bytes=63 << 20
        ),
        name="backward",
    )(
        frame_clip, patch_clip, padding, vec, sums, x_t, n_t, j_t, m_t, o_t, x_s, n_s, j_s, m_s, n_f, cot, gmid, gb,
        act, gh, act_sib, gh_sib, *fulls[:5]
    )


def settle(share):
    count = lax.axis_size("seq")
    if count == 8:
        return share
    more = count // 8
    groups = [[low + 8 * high for high in range(more)] for low in range(8)]
    share = lax.psum_scatter(share, "seq", scatter_dimension=0, tiled=True, axis_index_groups=groups)
    moves = [
        ((high * 8 + low) * 4 + f, (low * 4 + f) * more + high)
        for high in range(more)
        for low in range(8)
        for f in range(4)
    ]
    return lax.ppermute(share, ("seq", "ft"), moves)


def shards(
    video,
    class_token,
    frame_clip,
    patch_clip,
    padding,
    time_gain,
    time_shift,
    time_project,
    time_output,
    time_output_bias,
    time_mixer,
    time_mixer_bias,
    space_gain,
    space_shift,
    space_project,
    space_output,
    space_output_bias,
    feed_gain,
    feed_shift,
    feed_expand,
    feed_expand_bias,
    feed_reduce,
    feed_reduce_bias,
    grad_output,
    grad_class_out,
):
    vectors = jnp.stack(
        [
            time_gain,
            time_shift,
            time_output_bias,
            time_mixer_bias,
            space_gain,
            space_shift,
            space_output_bias,
            feed_gain,
            feed_shift,
            feed_reduce_bias,
        ]
    )
    vectors = jnp.concatenate(
        [jnp.pad(vectors, ((0, 0), (0, 192))), feed_expand_bias.reshape(2, 384), jnp.zeros((4, 384), bf16)]
    )
    weights = (time_project, time_output, time_mixer, space_project, space_output, feed_expand, feed_reduce)
    done = forward(
        video[0], class_token, frame_clip, patch_clip, padding, vectors, grad_output[0], grad_class_out, weights
    )
    output, class_output = done[0][None], done[1]
    grads = backward(frame_clip, patch_clip, padding, done[27], done[9:27], done[2:9])
    rows, grad_class = grads[:2]
    grad_video = jnp.swapaxes(rows[: HERE * FRAMES].reshape(HERE, FRAMES, D), 0, 1)[None]
    d_reduce, d_expand, d_so, d_sp, d_tm, d_to, d_tp, d_narrow = [settle(g) for g in grads[2:]]
    narrow = [d_narrow[:, i] for i in range(10)]
    return (
        output,
        class_output,
        grad_video,
        grad_class,
        narrow[0],
        narrow[1],
        d_tp,
        d_to,
        narrow[2],
        d_tm,
        narrow[3],
        narrow[4],
        narrow[5],
        d_sp,
        d_so,
        narrow[6],
        narrow[7],
        narrow[8],
        d_expand,
        d_narrow[:, 10:14].reshape(-1),
        d_reduce,
        narrow[9],
    )


def solution(mesh):
    in_specs = (
        P("seq", None, "ft", None),
        P("seq", None),
        P("seq", None),
        P("seq", None),
        P("seq", None),
        P("ft"),
        P("ft"),
        P("ft", None),
        P("ft", None),
        P("ft"),
        P("ft", None),
        P("ft"),
        P("ft"),
        P("ft"),
        P("ft", None),
        P("ft", None),
        P("ft"),
        P("ft"),
        P("ft"),
        P("ft", None),
        P("ft"),
        P("ft", None),
        P("ft"),
        P("seq", "ft", None, None),
        P("seq", None),
    )
    out_specs = (
        P("seq", "ft", None, None),
        P("seq", None),
        P("seq", None, "ft", None),
        P("seq", None),
        P(("seq", "ft")),
        P(("seq", "ft")),
        P(("seq", "ft"), None),
        P(("seq", "ft"), None),
        P(("seq", "ft")),
        P(("seq", "ft"), None),
        P(("seq", "ft")),
        P(("seq", "ft")),
        P(("seq", "ft")),
        P(("seq", "ft"), None),
        P(("seq", "ft"), None),
        P(("seq", "ft")),
        P(("seq", "ft")),
        P(("seq", "ft")),
        P(("seq", "ft"), None),
        P(("seq", "ft")),
        P(("seq", "ft"), None),
        P(("seq", "ft")),
    )
    return jax.shard_map(shards, mesh=mesh, in_specs=in_specs, out_specs=out_specs, check_vma=False)
```

```python
import jax
import jax.numpy as jnp
from jax import lax
from jax.experimental import pallas as pl
from jax.experimental.pallas import tpu as pltpu
from jax.sharding import PartitionSpec as P

MESH = pl.DeviceIdType.MESH
bf16 = jnp.bfloat16
f32 = jnp.float32
D = 768
FRAMES = 8
HERE = 49
OWN = 2
PATCHES = 196
TIME_ROWS = 400
TIME_BLOCK = 80
FRAME = 208
CLASS = 196
SPACE_ROWS = OWN * FRAME
SLOT = 64
EPSILON = 1e-06
UNITS = 7


def iota(shape, axis):
    return lax.broadcasted_iota(jnp.int32, shape, axis)


def dot(left, right):
    return jnp.dot(left, right, preferred_element_type=f32)


def dot_nt(left, right):
    return lax.dot_general(left, right, (((1,), (1,)), ((), ())), preferred_element_type=f32)


def dot_tn(left, right):
    return lax.dot_general(left, right, (((0,), (0,)), ((), ())), preferred_element_type=f32)


def picks(condition):
    return jnp.where(condition, 1.0, 0.0).astype(bf16)


def to_patches():
    r, c = iota((TIME_ROWS, FRAMES * SLOT), 0), iota((TIME_ROWS, FRAMES * SLOT), 1)
    return picks((c == (r & 7) * SLOT + (r >> 3)) & (r < FRAMES * HERE))


def to_frames():
    c, r = iota((FRAMES * SLOT, TIME_ROWS), 0), iota((FRAMES * SLOT, TIME_ROWS), 1)
    return picks((c == (r & 7) * SLOT + (r >> 3)) & (r < FRAMES * HERE))


def source_of(token, frame):
    late = (token >= HERE).astype(jnp.int32) + (token >= 2 * HERE) + (token >= 3 * HERE)
    return token + late * (OWN * SLOT - HERE) + frame * SLOT


def to_tokens():
    r, c = iota((SPACE_ROWS, FRAMES * SLOT), 0), iota((SPACE_ROWS, FRAMES * SLOT), 1)
    frame = (r >= FRAME).astype(jnp.int32)
    token = r - frame * FRAME
    return picks((c == source_of(token, frame)) & (token < PATCHES))


def from_tokens():
    c, r = iota((FRAMES * SLOT, SPACE_ROWS), 0), iota((FRAMES * SLOT, SPACE_ROWS), 1)
    frame = (r >= FRAME).astype(jnp.int32)
    token = r - frame * FRAME
    return picks((c == source_of(token, frame)) & (token < PATCHES))


def from_twos():
    r, c = iota((SPACE_ROWS, OWN * PATCHES), 0), iota((SPACE_ROWS, OWN * PATCHES), 1)
    frame = (r >= FRAME).astype(jnp.int32)
    token = r - frame * FRAME
    return picks((c == 2 * token + frame) & (token < PATCHES))


def to_twos():
    r, c = iota((OWN * PATCHES, SPACE_ROWS), 0), iota((OWN * PATCHES, SPACE_ROWS), 1)
    return picks(c == (r >> 1) + (r & 1) * FRAME)


def normed(rows):
    centred = rows - jnp.mean(rows, axis=-1, keepdims=True)
    scale = lax.rsqrt(jnp.mean(centred * centred, axis=-1, keepdims=True) + EPSILON)
    return centred * scale, scale


def over_blocks(count, size, step):
    def body(i, carry):
        step(pl.ds(pl.multiple_of(i * size, 16), size))
        return carry

    lax.fori_loop(0, count, body, 0)


def halves(scale):
    lane = iota((1, 128), 1)
    first = jnp.where(lane < 64, scale, 0.0).astype(bf16)
    second = jnp.where(lane < 64, 0.0, scale).astype(bf16)
    return first, second


def chances(scores):
    power = jnp.exp(scores - jnp.max(scores, axis=0, keepdims=True))
    return power * (1.0 / jnp.sum(power, axis=0, keepdims=True))


def diagonal(heads):
    shape = (TIME_BLOCK // 8, 8, heads * TIME_BLOCK)
    lane = iota(shape, 2)
    lane = jnp.where(lane < TIME_BLOCK, lane, lane - TIME_BLOCK)
    return iota(shape, 0) == (lane >> 3)


def gathered(scores, where):
    return jnp.sum(jnp.where(where, scores.reshape(where.shape), 0.0), axis=0)


def scattered(scores, where):
    wide = jnp.where(where, jnp.broadcast_to(scores[None], where.shape), 0.0)
    return wide.reshape(TIME_BLOCK, where.shape[2]).astype(bf16)


def pair(i, j, size):
    rows = pl.ds(pl.multiple_of(i * size, 16), size)
    return rows, [pl.ds(pl.multiple_of(k * D + j * 128, 128), 128) for k in range(3)]


def both(values, first, second):
    return jnp.concatenate([values * first, values * second], axis=0)


def unite(values, size):
    return jnp.where(iota((size, 128), 1) < 64, values[:size], values[size:])


def attend_time(joined, bias, mixed, blocks, size, unroll):
    first8, second8 = halves(0.125)
    where = diagonal(1)

    def body(n, carry):
        rows, (ql, kl, vl) = pair(n // 6, lax.rem(n, 6), size)
        query, keys, values = joined[rows, ql], joined[rows, kl], joined[rows, vl]
        out = []
        for part in (query * first8, query * second8):
            scores = gathered(dot_nt(keys, part), where) + bias[:, 0:size]
            out.append(dot_tn(scattered(chances(scores), where), values))
        mixed[rows, ql] = jnp.where(iota((size, 128), 1) < 64, out[0], out[1]).astype(bf16)
        return carry

    lax.fori_loop(0, blocks * 6, body, 0, unroll=unroll)


def attend_space(joined, bias, mixed, blocks, size, unroll):
    first8, second8 = halves(0.125)

    def body(n, carry):
        rows, (ql, kl, vl) = pair(n // 6, lax.rem(n, 6), size)
        query, keys, values = joined[rows, ql], joined[rows, kl], joined[rows, vl]
        chance = chances(dot_nt(keys, both(query, first8, second8)) + bias[...]).astype(bf16)
        mixed[rows, ql] = unite(dot_tn(chance, values), size).astype(bf16)
        return carry

    lax.fori_loop(0, blocks * 6, body, 0, unroll=unroll)


def attend_back(joined, bias, grad_mixed, grad_joined, blocks, size, unroll):
    first8, second8 = halves(0.125)
    first, second = halves(1.0)
    where = diagonal(2) if size == TIME_BLOCK else None

    def body(n, carry):
        rows, (ql, kl, vl) = pair(n // 6, lax.rem(n, 6), size)
        query, keys, values = joined[rows, ql], joined[rows, kl], joined[rows, vl]
        queries, grads = both(query, first8, second8), both(grad_mixed[rows, ql], first, second)
        scores, pull = dot_nt(keys, queries), dot_nt(values, grads)
        if where is not None:
            scores, pull = gathered(scores, where), gathered(pull, where)
        chance = chances(scores + bias[...])
        back = chance * (pull - jnp.sum(chance * pull, axis=0, keepdims=True))
        if where is None:
            chance, back = chance.astype(bf16), back.astype(bf16)
        else:
            chance, back = scattered(chance, where), scattered(back, where)
        grad_joined[rows, ql] = (unite(dot_tn(back, keys), size) * 0.125).astype(bf16)
        grad_joined[rows, kl] = dot(back, queries).astype(bf16)
        grad_joined[rows, vl] = dot(chance, grads).astype(bf16)
        return carry

    lax.fori_loop(0, blocks * 6, body, 0, unroll=unroll)


def time_bias(frame_clip, bias):
    shape = (8, 2 * TIME_BLOCK)
    r, c = iota(shape, 0), iota(shape, 1)
    clip_r, clip_c = jnp.zeros(shape, jnp.int32), jnp.zeros(shape, jnp.int32)
    for f in range(FRAMES):
        clip_r = jnp.where(r == f, frame_clip[0, f], clip_r)
        clip_c = jnp.where((c & 7) == f, frame_clip[0, f], clip_c)
    bias[...] = jnp.where(clip_r == clip_c, 0.0, -1e30)


def space_bias(patch_clip, padding, spare, bias):
    shape = (FRAME, FRAME)
    r, c = iota(shape, 0), iota(shape, 1)
    spare[...] = jnp.full(spare.shape, -1, jnp.int32)
    for half in range(2):
        spare[0:1, half * FRAME : half * FRAME + PATCHES] = patch_clip[...]
    spare[8:9, 0:PATCHES] = padding[...]
    clip = jnp.broadcast_to(spare[0:1, 0:FRAME], shape).astype(f32)
    shut = jnp.broadcast_to(spare[8:9, 0:FRAME], shape).astype(f32)
    own = jnp.sum(jnp.where(r == c, clip, 0.0), axis=1, keepdims=True)
    closed = jnp.sum(jnp.where(r == c, shut, 0.0), axis=1, keepdims=True)
    shape = (FRAME, 2 * FRAME)
    r, c = iota(shape, 0), iota(shape, 1)
    clip = jnp.broadcast_to(spare[0:1, 0 : 2 * FRAME], shape).astype(f32)
    of_class = (c == CLASS) | (c == FRAME + CLASS)
    opened = (r == CLASS) | ((closed == 0.0) & ((clip == own) | of_class))
    bias[...] = jnp.where(opened, 0.0, -1e30)


def place():
    s = lax.axis_index("seq")
    f = lax.axis_index("ft")
    core = lax.rem(s, 2)
    col = lax.rem(s // 2, 2)
    row = lax.rem(s // 4, 2)
    return s, f, core, col, row


def remote(src, dst, send, recv, target):
    return pltpu.make_async_remote_copy(
        src_ref=src, dst_ref=dst, send_sem=send, recv_sem=recv, device_id=target, device_id_type=MESH
    )


class Spread:
    def __init__(self, shards, fulls, send, recv):
        self.shards, self.fulls, self.send, self.recv = shards, fulls, send, recv
        self.s, self.f, self.core, self.col, self.row = place()
        s = self.s
        self.sib = s + 1 - 2 * self.core
        dx, dy = 2 - 4 * self.col, 4 - 8 * self.row
        self.plane = ((s + dx, 1, 0), (s + dy, 0, 1), (s + dx + dy, 1, 1))
        upper = self.f // 2
        near = self.f + upper * (3 - 2 * self.f)
        self.order = [upper * 3 + (1 - 2 * upper) * v for v in (1 - near, 2, 3)]

    def greet(self):
        bar = pltpu.get_barrier_semaphore()
        targets = [(t, self.f) for t in (self.sib,) + tuple(p[0] for p in self.plane)]
        targets += [(self.s, lax.rem(self.f + j, 4)) for j in (1, 2, 3)]
        for t in targets:
            pl.semaphore_signal(bar, inc=1, device_id=t, device_id_type=MESH)
        pl.semaphore_wait(bar, len(targets))

    def cut(self, w, base, row, col):
        rows, wide = self.shards[w].shape
        start = base + self.core * (rows // 2) + row * (rows // 4)
        return (
            pl.ds(pl.multiple_of(start, 16), rows // 4),
            pl.ds(pl.multiple_of(col * (wide // 2), 128), wide // 2),
        )

    def along(self, w, k):
        z = lax.rem(self.f + k, 4)
        rows = self.shards[w].shape[0]
        src = self.shards[w].at[self.cut(w, 0, self.row, self.col)]
        dst = self.fulls[w].at[self.cut(w, self.f * rows, self.row, self.col)]
        return remote(src, dst, self.send.at[w, k - 1], self.recv.at[w, 0, self.f], (self.s, z))

    def start(self, w):
        for k in (1, 3, 2):
            self.along(w, k).start()

    def over(self, w, z, i, mine=True):
        target, dx, dy = self.plane[i]
        rows = self.shards[w].shape[0]
        row, col = (self.row, self.col) if mine else (self.row + dy - 2 * dy * self.row, self.col + dx - 2 * dx * self.col)
        ref = self.fulls[w].at[self.cut(w, z * rows, row, col)]
        return remote(ref, ref, self.send.at[w, 3 + 4 * i + z], self.recv.at[w, 1 + i, z], (target, self.f))

    def across(self, w, z, mine=True):
        rows = self.shards[w].shape[0]
        core = self.core if mine else 1 - self.core
        ref = self.fulls[w].at[pl.ds(pl.multiple_of(z * rows + core * (rows // 2), 16), rows // 2), :]
        return remote(ref, ref, self.send.at[w, 15 + z], self.recv.at[w, 4, z], (self.sib, self.f))

    def fan(self, w):
        rows = self.shards[w].shape[0]
        for z in self.order:
            ref = self.fulls[w].at[self.cut(w, z * rows, self.row, self.col)]
            remote(ref, ref, self.send.at[w, 0], self.recv.at[w, 0, z], (self.s, z)).wait_recv()
            for i in (2, 0, 1):
                self.over(w, z, i).start()

    def lend(self, w):
        for z in self.order:
            for i in range(3):
                self.over(w, z, i, False).wait_recv()
            self.across(w, z).start()

    def finish(self, w):
        for z in self.order:
            self.across(w, z, False).wait_recv()


    def quarter(self, w, base, own=True):
        rows = self.shards[w].shape[0]
        half = lax.rem(self.col + self.row, 2)
        which = 2 * half + self.core if own else 2 * (1 - half) + self.core
        return pl.ds(pl.multiple_of(base + which * (rows // 4), 16), rows // 4)

    def hop(self, w, z, step, src=None):
        dst = self.fulls[w].at[self.quarter(w, z * self.shards[w].shape[0])]
        side = 0 if step == 1 else 1
        src = dst if src is None else src
        return remote(src, dst, self.send.at[w, 4 * side + z], self.recv.at[w, 0, z], (self.s, self.f + step))

    def beside(self, w, z, i, own=True):
        wide = self.shards[w].shape[1]
        rows = self.quarter(w, z * self.shards[w].shape[0], own)
        ref = self.fulls[w].at[rows, i * (wide // 2) : (i + 1) * (wide // 2)]
        return remote(ref, ref, self.send.at[w, 8 + 4 * i + z], self.recv.at[w, 1 + i, z], (self.plane[i][0], self.f))

    def cross(self, w, z, own=True):
        ref = self.fulls[w].at[self.quarter(w, z * self.shards[w].shape[0], own)]
        i = 0 if own else 1
        return remote(ref, ref, self.send.at[w, 16 + 4 * i + z], self.recv.at[w, 3 + i, z], (self.sib, self.f))

    def off(self, w):
        src = self.shards[w].at[self.quarter(w, 0)]

        @pl.when(self.f < 3)
        def _():
            self.hop(w, self.f, 1, src).start()

        @pl.when(self.f > 0)
        def _():
            self.hop(w, self.f, -1, src).start()

    def onward(self, w, t, act):
        z = self.order[t]

        @pl.when((z < self.f) & (self.f < 3))
        def _():
            act(self.hop(w, z, 1))

        @pl.when((z > self.f) & (self.f > 0))
        def _():
            act(self.hop(w, z, -1))

    def relay(self, w, t):
        z = self.order[t]
        self.hop(w, z, 1).wait_recv()
        self.onward(w, t, lambda copy: copy.start())
        self.beside(w, z, 0).start()
        self.beside(w, z, 1).start()
        self.cross(w, z).start()

    def pass_on(self, w, t):
        z = self.order[t]
        for i in range(2):
            self.beside(w, z, i, False).wait_recv()
        self.cross(w, z, False).start()

    def complete(self, w):
        for z in self.order:
            self.cross(w, z).wait_recv()
            self.cross(w, z, False).wait_recv()

    def empty(self, w):
        src = self.shards[w].at[self.quarter(w, 0)]

        @pl.when(self.f < 3)
        def _():
            self.hop(w, self.f, 1, src).wait_send()

        @pl.when(self.f > 0)
        def _():
            self.hop(w, self.f, -1, src).wait_send()

        for t in range(3):
            z = self.order[t]
            self.onward(w, t, lambda copy: copy.wait_send())
            self.beside(w, z, 0).wait_send()
            self.beside(w, z, 1).wait_send()
            self.cross(w, z).wait_send()
            self.cross(w, z, False).wait_send()

    def drain(self, w):
        for k in (1, 2, 3):
            self.along(w, k).wait_send()
        for z in self.order:
            for i in range(3):
                self.over(w, z, i).wait_send()
            self.across(w, z).wait_send()


class Loads:
    def __init__(self, slots, sems, pieces, f):
        self.slots, self.sems, self.pieces, self.f = slots, sems, pieces, f

    def copies(self, i):
        n = i % self.slots.shape[0]
        full, shard, what, spot = self.pieces[i]
        slot = self.slots.at[n]
        if what == "columns":
            lanes = slice(spot * D, (spot + 1) * D)
            out = [(shard.at[:, lanes], slot.at[pl.ds(pl.multiple_of(self.f * 192, 16), 192)], None)]
            for k in (1, 2, 3):
                rows = pl.ds(pl.multiple_of(lax.rem(self.f + k, 4) * 192, 16), 192)
                out.append((full.at[rows, lanes], slot.at[rows], None))
        elif what == "wide":
            core, high = spot
            out = []
            for x in range(2):
                start = pl.multiple_of(((high * 2 + x) * 2 + core) * 384, 128)
                lanes, at = pl.ds(start, 384), slice(x * 384, (x + 1) * 384)
                out.append((shard.at[:, lanes], slot.at[pl.ds(pl.multiple_of(self.f * 192, 16), 192), at], None))
                for k in (1, 2, 3):
                    rows = pl.ds(pl.multiple_of(lax.rem(self.f + k, 4) * 192, 16), 192)
                    out.append((full.at[rows, lanes], slot.at[rows, at], None))
        else:
            core, high = spot
            out = []
            for x in range(2):
                z = high * 2 + x
                at = slot.at[x * 384 : (x + 1) * 384]
                here = shard.at[pl.ds(pl.multiple_of(core * 384, 16), 384)]
                there = full.at[pl.ds(pl.multiple_of(z * 768 + core * 384, 16), 384)]
                out += [(here, at, self.f == z), (there, at, self.f != z)]
        return [
            (pltpu.make_async_copy(src, dst, self.sems.at[n, k]), when) for k, (src, dst, when) in enumerate(out)
        ]

    def each(self, i, act):
        for copy, when in self.copies(i):
            if when is None:
                act(copy)
            else:
                pl.when(when)(lambda copy=copy: act(copy))

    def start(self, i):
        self.each(i, lambda copy: copy.start())

    def get(self, i):
        self.each(i, lambda copy: copy.wait())
        return self.slots[i % self.slots.shape[0]]


ALL = slice(None)


def squares(fulls, shards, w, count):
    return [(fulls[w], shards[w], "columns", i) for i in range(count)]


def forward_kernel(*refs):
    (video, class_token, frame_clip, patch_clip, padding, vectors, expand_bias, grad_output, grad_class_out) = refs[:9]
    shards = refs[9:16]
    outs = refs[16:44]
    (output, class_output) = outs[:2]
    fulls = outs[2:9]
    (x_t, n_t, j_t, m_t, o_t, x_s, n_s, j_s, m_s, n_f, cot, act, gh, act_sib, gh_sib, gmid, gb, sums, small_out) = outs[9:28]
    (send, recv, vec, vec32, vsend, vrecv, slots, slot_sems, a2s, a2r, asend, arecv, tbias, sbias, spare,
     rows_f, acc, acc2, hid, gact, cls, csend, crecv, psend, precv, act_go, gh_go, vec_go) = refs[44:]

    net = Spread(shards, fulls, send, recv)
    s, f, core = net.s, net.f, net.core
    net.greet()

    def vec_copy(k):
        return remote(vec_go, vec.at[f], vsend.at[k - 1], vrecv.at[f], (s, lax.rem(f + k, 4)))

    vec_go[0:16, 0:192] = vectors[...]
    vec_go[0:16, 192:D] = jnp.zeros((16, D - 192), bf16)
    vec_go[16:32] = expand_bias[...]
    for k in (1, 3, 2):
        vec_copy(k).start()
    net.start(0)
    vec[f] = vec_go[...]

    x_t[384:TIME_ROWS] = jnp.zeros((TIME_ROWS - 384, D), bf16)
    x_t[0 : HERE * FRAMES] = video[...]
    time_bias(frame_clip, tbias)
    space_bias(patch_clip, padding, spare, sbias)

    cot[...] = dot(from_twos(), grad_output[...].reshape(OWN * PATCHES, D)).astype(bf16)
    at_class = iota((16, D), 0) == CLASS - 192
    tail = jnp.where(at_class, grad_class_out[...].astype(f32), cot[192:FRAME].astype(f32))
    cot[192:FRAME] = tail.astype(bf16)

    for k in (1, 3, 2):
        z = lax.rem(f + k, 4)
        remote(vec_go, vec.at[z], vsend.at[0], vrecv.at[z], (s, z)).wait_recv()
    small = jnp.zeros((16, D), f32)
    for z in range(4):
        r, c = iota((192, D), 0), iota((192, D), 1) - z * 192
        small += dot(vec[z, 0:16, 0:192], picks(c == r))
        vec32[1 + z] = vec[z, 16:32].astype(f32)
    vec32[0] = small
    small_out[...] = small

    def vector(i):
        return vec32[0, i : i + 1, :]

    gain, shift = vector(0), vector(1)

    def norm_time(rows):
        scaled, unused = normed(x_t[rows].astype(f32))
        n_t[rows] = (scaled * gain + shift).astype(bf16)

    over_blocks(5, 80, norm_time)

    pieces = []
    for w, count in ((0, 3), (1, 1), (2, 1), (3, 3), (4, 1)):
        pieces += squares(fulls, shards, w, count)
    for c, high in ((1 - core, 0), (1 - core, 1), (core, 0), (core, 1)):
        pieces += [(fulls[5], shards[5], "wide", (c, high)), (fulls[6], shards[6], "tall", (c, high))]
    loads = Loads(slots, slot_sems, pieces, f)

    net.fan(0)
    net.start(1)
    net.start(2)
    net.lend(0)
    net.fan(1)
    net.fan(2)
    net.start(3)
    net.finish(0)
    for i in range(3):
        loads.start(i)
    for i in range(3):
        j_t[:, i * D : (i + 1) * D] = dot(n_t[...], loads.get(i)).astype(bf16)
    net.lend(1)
    net.lend(2)
    net.off(5)
    net.fan(3)
    net.start(4)
    net.finish(1)
    loads.start(3)
    net.finish(2)
    loads.start(4)
    attend_time(j_t, tbias, m_t, 5, TIME_BLOCK, 6)
    net.relay(5, 0)
    net.off(6)
    net.lend(3)
    o_t[...] = (dot(m_t[...], loads.get(3)) + vector(2)).astype(bf16)
    after = (x_t[...].astype(f32) + (dot(o_t[...], loads.get(4)) + vector(3))).astype(bf16)
    a2s[...] = dot(to_frames(), after).astype(bf16).reshape(4, OWN, SLOT, D)

    def a_copy(k):
        z = lax.rem(f + k, 4)
        return remote(a2s.at[z], a2r.at[f], asend.at[k - 1], arecv.at[f], (s, z))

    for k in (1, 3, 2):
        a_copy(k).start()
    a2r[f] = a2s[f]
    net.fan(4)
    net.finish(3)
    for i in range(5, 8):
        loads.start(i)
    net.relay(5, 1)
    net.relay(6, 0)
    net.lend(4)
    net.relay(5, 2)
    for k in (1, 3, 2):
        z = lax.rem(f + k, 4)
        remote(a2s.at[z], a2r.at[z], asend.at[0], arecv.at[z], (s, z)).wait_recv()

    spread_rows = dot(to_tokens(), a2r[...].reshape(FRAMES * SLOT, D))
    r = iota((SPACE_ROWS, D), 0)
    is_class = (r == CLASS) | (r == FRAME + CLASS)
    x_s[...] = jnp.where(is_class, class_token[...].astype(f32), spread_rows).astype(bf16)
    gain, shift = vector(4), vector(5)

    def norm_space(rows):
        scaled, unused = normed(x_s[rows].astype(f32))
        n_s[rows] = (scaled * gain + shift).astype(bf16)

    over_blocks(13, 32, norm_space)
    for i in range(3):
        j_s[:, i * D : (i + 1) * D] = dot(n_s[...], loads.get(5 + i)).astype(bf16)
    net.finish(4)
    loads.start(8)
    net.relay(6, 1)
    for i in range(3):
        net.pass_on(5, i)
    net.relay(6, 2)
    attend_space(j_s, sbias, m_s, OWN, FRAME, 6)
    for i in range(3):
        net.pass_on(6, i)
    rows_f[...] = dot(m_s[...], loads.get(8)) + vector(6)
    token = class_token[...].astype(f32)
    cls[f] = jnp.broadcast_to(
        rows_f[CLASS : CLASS + 1] + rows_f[FRAME + CLASS : FRAME + CLASS + 1], (8, D)
    )

    def c_copy(k):
        return remote(cls.at[f], cls.at[f], csend.at[k - 1], crecv.at[f], (s, lax.rem(f + k, 4)))

    for k in (1, 3, 2):
        c_copy(k).start()
    net.complete(5)
    net.complete(6)
    for i in range(9, 12):
        loads.start(i)
    for k in (1, 3, 2):
        z = lax.rem(f + k, 4)
        remote(cls.at[f], cls.at[z], csend.at[0], crecv.at[z], (s, z)).wait_recv()
    mid = token + ((cls[0] + cls[1]) + (cls[2] + cls[3]))[0:1] * (1.0 / FRAMES)
    gain, shift = vector(7), vector(8)
    first = jnp.where(f == 0, 1.0, 0.0)

    def norm_feed(rows):
        r = iota((32, D), 0) + rows.start
        at_class = r == CLASS
        other = r == FRAME + CLASS
        values = x_s[rows].astype(f32) + rows_f[rows]
        values = jnp.where(at_class, mid, jnp.where(other, 0.0, values))
        rows_f[rows] = values
        scaled, unused = normed(values)
        n_f[rows] = (scaled * gain + shift).astype(bf16)
        acc[rows] = values + vector(9)
        acc2[rows] = jnp.zeros((32, D), f32)

    over_blocks(13, 32, norm_feed)

    def sib_copy(k, half, src, dst):
        return remote(src.at[half], dst.at[half], psend.at[k, half], precv.at[k, half], (net.sib, f))

    for j in range(4):
        c = 1 - core if j < 2 else core
        high = j & 1
        bias = jnp.concatenate(
            [vec32[1 + 2 * high + x, 0:1, pl.ds(pl.multiple_of(c * 384, 128), 384)] for x in range(2)], axis=1
        )
        w1 = loads.get(9 + 2 * j)
        hid[...] = dot(n_f[...], w1) + bias
        w2 = loads.get(10 + 2 * j)
        gact[...] = dot_nt(cot[...], w2)
        act_to, gh_to = (act_go, gh_go) if j < 2 else (act, gh)

        def feed(rows):
            hidden = hid[rows]
            tail = 0.5 + 0.5 * lax.erf(hidden * 0.7071067811865476)
            slope = tail + hidden * (jnp.exp(hidden * hidden * -0.5) * 0.3989422804014327)
            act_to[high, rows] = (hidden * tail).astype(bf16)
            gh_to[high, rows] = (gact[rows] * slope).astype(bf16)

        over_blocks(13, 32, feed)
        acc[...] += dot(act_to[high], w2)
        acc2[...] += dot_nt(gh_to[high], w1)
        if j < 3:
            for i in (12 + 2 * j, 13 + 2 * j):
                if i < 17:
                    loads.start(i)

        at_class = iota((16, D), 0) == CLASS - 192
        for ref in (act_to, gh_to):
            piece = ref[high, 192:FRAME].astype(f32)
            ref[high, 192:FRAME] = jnp.where(at_class, piece * first, piece).astype(bf16)
        if j < 2:
            sib_copy(0, high, act_go, act_sib).start()
            sib_copy(1, high, gh_go, gh_sib).start()

    twos = dot(to_twos(), acc[...].astype(bf16)).astype(bf16)
    output[...] = twos.reshape(PATCHES, OWN, D)
    class_output[...] = acc[CLASS : CLASS + 1].astype(bf16)
    gain = vector(7)
    sums[...] = jnp.zeros_like(sums)

    def feed_back(rows):
        r = iota((32, D), 0) + rows.start
        scaled, scale = normed(rows_f[rows])
        pulled = acc2[rows]
        counted = jnp.where(r == CLASS, pulled * first, pulled)
        sums[0:8] += jnp.sum((counted * scaled).reshape(4, 8, D), axis=0)
        sums[8:16] += jnp.sum(counted.reshape(4, 8, D), axis=0)
        up = pulled * gain
        back = scale * (
            up - jnp.mean(up, axis=-1, keepdims=True) - scaled * jnp.mean(up * scaled, axis=-1, keepdims=True)
        )
        grad = cot[rows].astype(f32) + back
        gmid[rows] = grad
        gb[rows] = grad.astype(bf16)

    over_blocks(13, 32, feed_back)
    row = (gmid[CLASS : CLASS + 1] * (1.0 / FRAMES)).astype(bf16).astype(f32)
    for start in (192, FRAME + 192):
        piece = gb[start : start + 16].astype(f32)
        gb[start : start + 16] = jnp.where(at_class, row, piece).astype(bf16)

    for half in range(2):
        for k, src, dst in ((0, act_go, act_sib), (1, gh_go, gh_sib)):
            sib_copy(k, half, src, dst).wait()
    for k in (1, 2, 3):
        vec_copy(k).wait_send()
        a_copy(k).wait_send()
        c_copy(k).wait_send()
    for w in range(5):
        net.drain(w)
    net.empty(5)
    net.empty(6)


def forward(video, class_token, frame_clip, patch_clip, padding, vectors, expand_bias, grad_output, grad_class_out, shards):
    vm = pl.BlockSpec(memory_space=pltpu.VMEM)
    sm = pl.BlockSpec(memory_space=pltpu.SMEM)
    hbm = pl.BlockSpec(memory_space=pl.ANY)
    sds = jax.ShapeDtypeStruct
    sem = pltpu.SemaphoreType.DMA
    v = pltpu.VMEM
    t, p = TIME_ROWS, SPACE_ROWS
    outs = [sds((PATCHES, OWN, D), bf16), sds((1, D), bf16)]
    outs += [sds((4 * a.shape[0], a.shape[1]), bf16) for a in shards]
    outs += [sds((t, D), bf16), sds((t, D), bf16), sds((t, 3 * D), bf16), sds((t, D), bf16), sds((t, D), bf16)]
    outs += [sds((p, D), bf16), sds((p, D), bf16), sds((p, 3 * D), bf16), sds((p, D), bf16), sds((p, D), bf16)]
    outs += [sds((p, D), bf16)] + [sds((2, p, D), bf16)] * 4 + [sds((p, D), f32), sds((p, D), bf16), sds((16, D), f32), sds((16, D), f32)]
    return pl.pallas_call(
        forward_kernel,
        out_shape=outs,
        in_specs=[vm, vm, sm, vm, vm, vm, vm, vm, vm] + [hbm] * 7,
        out_specs=[vm, vm] + [hbm] * 7 + [vm] * 19,
        scratch_shapes=[
            sem((UNITS, 24)),
            sem((UNITS, 5, 4)),
            v((4, 32, D), bf16),
            v((5, 16, D), f32),
            sem((3,)),
            sem((4,)),
            v((4, D, D), bf16),
            sem((4, 8)),
            v((4, OWN, SLOT, D), bf16),
            v((4, OWN, SLOT, D), bf16),
            sem((3,)),
            sem((4,)),
            v((8, 2 * TIME_BLOCK), f32),
            v((FRAME, 2 * FRAME), f32),
            v((16, 512), jnp.int32),
            v((p, D), f32),
            v((p, D), f32),
            v((p, D), f32),
            v((p, D), f32),
            v((p, D), f32),
            v((4, 8, D), f32),
            sem((3,)),
            sem((4,)),
            sem((2, 2)),
            sem((2, 2)),
            v((2, p, D), bf16),
            v((2, p, D), bf16),
            v((32, D), bf16),
        ],
        compiler_params=pltpu.CompilerParams(
            collective_id=1, has_side_effects=True, vmem_limit_bytes=63 << 20
        ),
        name="forward",
    )(video, class_token, frame_clip, patch_clip, padding, vectors, expand_bias, grad_output, grad_class_out, *shards)


class Reduce:
    def __init__(self, parts, ra, rb, ra2, rb2, rz, total, rc, sems):
        self.parts, self.ra, self.rb, self.ra2, self.rb2 = parts, ra, rb, ra2, rb2
        self.rz, self.total, self.rc, self.sems = rz, total, rc, sems
        self.s, self.f, self.core, self.col, self.row = place()
        s = self.s
        self.sib = s + 1 - 2 * self.core
        self.across, self.down = s + 2 - 4 * self.col, s + 4 - 8 * self.row

    def greet(self):
        bar = pltpu.get_barrier_semaphore()
        targets = [(t, self.f) for t in (self.sib, self.across, self.down)]
        targets += [(self.s, lax.rem(self.f + j, 4)) for j in (1, 2, 3)]
        for t in targets:
            pl.semaphore_signal(bar, inc=1, device_id=t, device_id_type=MESH)
        pl.semaphore_wait(bar, len(targets))

    def sem(self, w, i):
        return self.sems.at[w, i]

    def copies1(self, w):
        g = self.parts[w]
        return (
            remote(g.at[:, 1 - self.col, 0], self.ra[w], self.sem(w, 0), self.sem(w, 1), (self.across, self.f)),
            remote(g.at[1 - self.row, :, 1], self.rb[w], self.sem(w, 2), self.sem(w, 3), (self.down, self.f)),
        )

    def copies2(self, w):
        return (
            remote(self.ra[w].at[1 - self.row], self.ra2[w], self.sem(w, 4), self.sem(w, 5), (self.down, self.f)),
            remote(self.rb[w].at[1 - self.col], self.rb2[w], self.sem(w, 6), self.sem(w, 7), (self.across, self.f)),
        )

    def block(self, w, z):
        g = self.parts[w]
        rows = g.shape[3] // 2
        return g.at[z // 2, 1 - self.col, 0, pl.ds(pl.multiple_of(lax.rem(z, 2) * rows, 16), rows), :]

    def copies3(self, w):
        out = []
        for j in (1, 3, 2):
            z = lax.rem(self.f + j, 4)
            out.append(
                remote(self.block(w, z), self.rz[w].at[3 - j], self.sem(w, 7 + j), self.sem(w, 14 - j), (self.s, z))
            )
        return out

    def copy4(self, w):
        return remote(
            self.total[w].at[1 - self.core], self.rc[w], self.sem(w, 14), self.sem(w, 15), (self.sib, self.f)
        )

    def step1(self, w):
        for c in self.copies1(w):
            c.start()

    def step2(self, w):
        a, b = self.copies1(w)
        g, ra, rb = self.parts[w], self.ra[w], self.rb[w]
        row, col = self.row, self.col
        a2, b2 = self.copies2(w)
        a.wait_recv()
        ra[1 - row] = (ra[1 - row].astype(f32) + g[1 - row, col, 0].astype(f32)).astype(bf16)
        a2.start()
        b.wait_recv()
        rb[1 - col] = (rb[1 - col].astype(f32) + g[row, 1 - col, 1].astype(f32)).astype(bf16)
        b2.start()

    def step3(self, w):
        a, b = self.copies1(w)
        a2, b2 = self.copies2(w)
        g = self.parts[w]
        row, col = self.row, self.col
        part = g.shape[3] // 4
        a.wait_send()
        b2.wait_recv()
        a2.wait_recv()
        for z in range(4):
            rows = pl.ds(z * part, part)
            sums = []
            for k, near, far in ((0, self.ra[w].at[row], self.ra2[w]), (1, self.rb[w].at[col], self.rb2[w])):
                own = g.at[row, col, k]
                if part % 16:
                    tops = z * part // 16 * 16
                    high = -(-(z + 1) * part // 16) * 16
                    wide = [ref[tops:high].astype(f32) for ref in (own, near, far)]
                    low = z * part - tops
                    sums.append((wide[0] + wide[1] + wide[2])[low : low + part])
                else:
                    sums.append(own[rows].astype(f32) + near[rows].astype(f32) + far[rows].astype(f32))
            at = self.block(w, z)
            at[...] = jnp.concatenate(sums, axis=0).astype(bf16)
        for c in self.copies3(w):
            c.start()

    def step4(self, w, swap=True):
        for c in self.copies3(w):
            c.wait_recv()
        rz, part = self.rz[w], self.parts[w].shape[3] // 4
        whole = (self.block(w, self.f)[...].astype(f32) + rz[0].astype(f32)) + (
            rz[1].astype(f32) + rz[2].astype(f32)
        )
        self.total[w][0] = whole[:part]
        self.total[w][1] = whole[part:]
        if swap:
            self.copy4(w).start()

    def step5(self, w):
        self.copy4(w).wait_recv()

    def drain(self, w, swap=True):
        a, b = self.copies1(w)
        b.wait_send()
        for c in list(self.copies2(w)) + self.copies3(w) + ([self.copy4(w)] if swap else []):
            c.wait_send()


REDUCE, EXPAND, SPACE_OUT, SPACE_JOIN, MIX, TIME_OUT, TIME_JOIN, NARROW = range(8)
PARTS = ((384, 384), (96, 1536), (96, 384), (96, 1152), (96, 384), (96, 384), (96, 1152), (96, 128))


def backward_kernel(*refs):
    (frame_clip, patch_clip, padding, vec, sums, x_t, n_t, j_t, m_t, o_t, x_s, n_s, j_s, m_s, n_f, cot, gmid, gb) = refs[:18]
    act, gh, act_sib, gh_sib = refs[18:22]
    fulls, shards = refs[22:27], refs[27:32]
    (d_video, d_class, d_reduce, d_expand, d_so, d_sp, d_tm, d_to, d_tp, d_narrow) = refs[32:42]
    (parts, ra, rb, ra2, rb2, rz, total, rc, rsems, slots, slot_sems, act_v, gh_v, feed_sems, tbias, sbias, spare,
     gsm, wide, gat, gto, gtm, a2s, a2r, asend, arecv, cls, csend, crecv, bias_col, vt,
     n_f2, cot2, m_s2, gb2, n_s2, gjs2, o_t2, gat2, m_t2, gto2, n_t2, gjt2, xsend, xrecv) = refs[42:]
    red = Reduce(parts, ra, rb, ra2, rb2, rz, total, rc, rsems)
    s, f, core, sib = red.s, red.f, red.core, red.sib
    red.greet()

    def half_of(ref, wide_half, which):
        return ref.at[:, pl.ds(pl.multiple_of(which * wide_half, 128), wide_half)]

    exchange = [
        (cot, cot2), (n_f, n_f2), (m_s, m_s2), (half_of(gb, 384, 1 - core), gb2), (n_s, n_s2), (o_t, o_t2),
        (m_t, m_t2), (n_t, n_t2),
    ]
    gjs = act_v.at[:, 0 : 3 * D]
    gjt = gh_v.at[0:TIME_ROWS, 0 : 3 * D]
    exchange += [
        (half_of(gjs, 1152, 1 - core), gjs2), (half_of(gat, 384, 1 - core), gat2),
        (half_of(gto, 384, 1 - core), gto2), (half_of(gjt, 1152, 1 - core), gjt2),
    ]
    GJS, GAT, GTO, GJT = 8, 9, 10, 11

    def trade(k):
        src, dst = exchange[k]
        return remote(src, dst, xsend.at[k], xrecv.at[k], (sib, f))

    loads_feed = []
    for k, (src, dst, at) in enumerate(
        ((act, act_v, 0), (act_sib, act_v, 2), (gh, gh_v, 0), (gh_sib, gh_v, 2))
    ):
        for half in range(2):
            lanes = slice((at + half) * D, (at + half + 1) * D)
            loads_feed.append(pltpu.make_async_copy(src.at[half], dst.at[:, lanes], feed_sems.at[2 * k + half]))
    for c in loads_feed:
        c.start()
    for k in range(8):
        trade(k).start()
    pieces = []
    for w, count in ((4, 1), (3, 3), (2, 1), (1, 1), (0, 3)):
        pieces += squares(fulls, shards, w, count)
    loads = Loads(slots, slot_sems, pieces, f)
    for i in range(3):
        loads.start(i)
    time_bias(frame_clip, tbias)
    space_bias(patch_clip, padding, spare, sbias)

    first = jnp.where(f == 0, 1.0, 0.0)
    vt[...] = jnp.zeros_like(vt)
    counts = jnp.where(iota((16, SPACE_ROWS), 1) == CLASS, first, 1.0).astype(bf16)
    ones_s = jnp.ones((16, SPACE_ROWS), bf16)
    ones_t = jnp.ones((16, TIME_ROWS), bf16)
    vt[7:8] = jnp.sum(sums[0:8], axis=0, keepdims=True)
    vt[8:9] = jnp.sum(sums[8:16], axis=0, keepdims=True)
    vt[9:10] = dot(counts, cot[...])[0:1]
    vt[6:7] = dot(ones_s, gb[...])[0:1]

    for c in loads_feed[:4]:
        c.wait()
    trade(0).wait_recv()
    for y in range(2):
        grad = dot_tn(act_v[:, y * D : (y + 1) * D], cot[...]) + dot_tn(act_v[:, (2 + y) * D : (3 + y) * D], cot2[...])
        for x in range(2):
            for k in range(2):
                parts[REDUCE][y, x, k] = grad[x * 384 : (x + 1) * 384, k * 384 : (k + 1) * 384].astype(bf16)
    red.step1(REDUCE)
    for c in loads_feed[4:]:
        c.wait()
    trade(1).wait_recv()

    def put(w, lanes, grad):
        for y in range(2):
            for x in range(2):
                for k in range(2):
                    start = ((y * 2 + x) * 2 + k) * 96
                    parts[w][y, x, k, :, lanes] = grad[start : start + 96].astype(bf16)

    for y in range(2):
        own, other = gh_v[:, y * D : (y + 1) * D], gh_v[:, (2 + y) * D : (3 + y) * D]
        grad = dot_tn(n_f[...], own) + dot_tn(n_f2[...], other)
        put(EXPAND, slice(y * D, (y + 1) * D), grad)
        ones = jnp.ones((SPACE_ROWS, 128), bf16)
        bias_col[y] = dot_tn(own, ones) + dot_tn(other, ones)
    red.step1(EXPAND)

    trade(2).wait_recv()
    trade(3).wait_recv()
    mine = half_of(gb, 384, core)
    put(SPACE_OUT, ALL, dot_tn(m_s[...], mine[...]) + dot_tn(m_s2[...], gb2[...]))
    red.step1(SPACE_OUT)
    gsm[...] = dot_nt(gb[...], loads.get(0)).astype(bf16)
    loads.start(3)
    attend_back(j_s, sbias, gsm, gjs, OWN, FRAME, 3)
    trade(GJS).start()
    red.step2(REDUCE)
    wide[...] = dot_nt(gjs[:, 0:D], loads.get(1))
    loads.start(4)
    wide[...] += dot_nt(gjs[:, D : 2 * D], loads.get(2))
    loads.start(5)
    wide[...] += dot_nt(gjs[:, 2 * D : 3 * D], loads.get(3))
    loads.start(6)
    gain = vec[4:5]

    def norm_back(source, gain, at, size, rows):
        scaled, scale = normed(source[rows].astype(f32))
        pulled = wide[rows]
        vt[at : at + 8] += jnp.sum((pulled * scaled).reshape(size // 8, 8, D), axis=0)
        vt[at + 8 : at + 16] += jnp.sum(pulled.reshape(size // 8, 8, D), axis=0)
        up = pulled * gain
        return scale * (
            up - jnp.mean(up, axis=-1, keepdims=True) - scaled * jnp.mean(up * scaled, axis=-1, keepdims=True)
        )

    def space_back(rows):
        back = norm_back(x_s, gain, 16, 32, rows)
        wide[rows] = back
        gsm[rows] = (gmid[rows] + back).astype(bf16)

    over_blocks(13, 32, space_back)
    a2s[...] = dot(from_tokens(), gsm[...]).astype(bf16).reshape(4, OWN, SLOT, D)

    def a_copy(k):
        z = lax.rem(f + k, 4)
        return remote(a2s.at[z], a2r.at[f], asend.at[k - 1], arecv.at[f], (s, z))

    for k in (1, 3, 2):
        a_copy(k).start()
    a2r[f] = a2s[f]
    cls[f] = jnp.broadcast_to(wide[CLASS : CLASS + 1] + wide[FRAME + CLASS : FRAME + CLASS + 1], (8, D))

    def c_copy(k):
        return remote(cls.at[f], cls.at[f], csend.at[k - 1], crecv.at[f], (s, lax.rem(f + k, 4)))

    for k in (1, 3, 2):
        c_copy(k).start()
    red.step2(EXPAND)
    red.step3(REDUCE)
    trade(4).wait_recv()
    trade(GJS).wait_recv()
    mine = half_of(gjs, 1152, core)
    put(SPACE_JOIN, ALL, dot_tn(n_s[...], mine[...]) + dot_tn(n_s2[...], gjs2[...]))
    red.step1(SPACE_JOIN)
    for k in (1, 3, 2):
        z = lax.rem(f + k, 4)
        remote(a2s.at[z], a2r.at[z], asend.at[0], arecv.at[z], (s, z)).wait_recv()

    gat[...] = dot(to_patches(), a2r[...].reshape(FRAMES * SLOT, D)).astype(bf16)
    trade(GAT).start()
    gto[...] = dot_nt(gat[...], loads.get(4)).astype(bf16)
    loads.start(7)
    trade(GTO).start()
    gtm[...] = dot_nt(gto[...], loads.get(5)).astype(bf16)
    loads.start(8)
    red.step2(SPACE_OUT)
    red.step3(EXPAND)
    red.step4(REDUCE, False)
    d_reduce[:, 0:384] = total[REDUCE][0]
    d_reduce[:, 384:768] = total[REDUCE][1]
    trade(5).wait_recv()
    trade(GAT).wait_recv()
    mine = half_of(gat, 384, core)
    put(MIX, ALL, dot_tn(o_t[...], mine[...]) + dot_tn(o_t2[...], gat2[...]))
    red.step1(MIX)
    trade(6).wait_recv()
    trade(GTO).wait_recv()
    mine = half_of(gto, 384, core)
    put(TIME_OUT, ALL, dot_tn(m_t[...], mine[...]) + dot_tn(m_t2[...], gto2[...]))
    red.step1(TIME_OUT)
    attend_back(j_t, tbias, gtm, gjt, 5, TIME_BLOCK, 6)
    trade(GJT).start()
    red.step2(SPACE_JOIN)
    red.step3(SPACE_OUT)
    red.step4(EXPAND)
    trade(7).wait_recv()
    trade(GJT).wait_recv()
    mine = half_of(gjt, 1152, core)
    put(TIME_JOIN, ALL, dot_tn(n_t[...], mine[...]) + dot_tn(n_t2[...], gjt2[...]))
    red.step1(TIME_JOIN)
    rows = pl.ds(0, TIME_ROWS)
    wide[rows] = dot_nt(gjt[:, 0:D], loads.get(6))
    wide[rows] += dot_nt(gjt[:, D : 2 * D], loads.get(7))
    wide[rows] += dot_nt(gjt[:, 2 * D : 3 * D], loads.get(8))
    red.step2(MIX)
    red.step2(TIME_OUT)
    red.step3(SPACE_JOIN)
    red.step4(SPACE_OUT)
    gain = vec[0:1]

    def time_back(rows):
        back = norm_back(x_t, gain, 32, 80, rows)
        wide[rows] = gat[rows].astype(f32) + back

    over_blocks(5, 80, time_back)
    d_video[...] = wide[0 : HERE * FRAMES]
    vt[3:4] = dot(ones_t, gat[...])[0:1]
    vt[2:3] = dot(ones_t, gto[...])[0:1]
    for row, at in ((4, 16), (5, 24), (0, 32), (1, 40)):
        vt[row : row + 1] = jnp.sum(vt[at : at + 8], axis=0, keepdims=True)
    place_at = picks(iota((16, 128), 0) == iota((16, 128), 1))
    put(NARROW, ALL, dot_tn(vt[0:16].astype(bf16), place_at))
    lane = iota((24, 128), 1)
    for y in range(2):
        for x in range(2):
            pieces = []
            for z in range(4):
                piece = jnp.zeros((24, 128), f32)
                for k in range(4):
                    column = bias_col[y, pl.ds(x * 384 + z * 96 + k, 24, stride=4), :]
                    piece = jnp.where(lane == 10 + k, column, piece)
                pieces.append(piece)
            at = parts[NARROW].at[y, x, core]
            at[...] = (at[...].astype(f32) + jnp.concatenate(pieces, axis=0)).astype(bf16)
    red.step1(NARROW)

    def place_halves(w, out, half):
        red.step5(w)
        mine = half_of(out, half, core)
        mine[...] = total[w][core]
        other = half_of(out, half, 1 - core)
        other[...] = rc[w][...]

    for k in (1, 3, 2):
        z = lax.rem(f + k, 4)
        remote(cls.at[f], cls.at[z], csend.at[0], crecv.at[z], (s, z)).wait_recv()
    d_class[...] = gmid[CLASS : CLASS + 1] + ((cls[0] + cls[1]) + (cls[2] + cls[3]))[0:1]
    red.step5(EXPAND)
    for y in range(2):
        for x in range(2):
            lanes = slice((y * 2 + x) * 384, (y * 2 + x + 1) * 384)
            for c, piece in ((core, total[EXPAND][core]), (1 - core, rc[EXPAND][...])):
                start = pl.multiple_of(((y * 2 + x) * 2 + c) * 384, 128)
                d_expand[:, pl.ds(start, 384)] = piece[:, lanes]
    red.step2(TIME_JOIN)
    red.step3(MIX)
    red.step3(TIME_OUT)
    red.step4(SPACE_JOIN)
    place_halves(SPACE_OUT, d_so, 384)
    red.step2(NARROW)
    red.step3(TIME_JOIN)
    red.step4(MIX)
    red.step4(TIME_OUT)
    place_halves(SPACE_JOIN, d_sp, 1152)
    red.step3(NARROW)
    place_halves(MIX, d_tm, 384)
    place_halves(TIME_OUT, d_to, 384)
    red.step4(TIME_JOIN)
    red.step4(NARROW)
    place_halves(TIME_JOIN, d_tp, 1152)
    red.step5(NARROW)
    d_narrow[...] = total[NARROW][core] + rc[NARROW][...]
    for w in range(8):
        red.drain(w, w != REDUCE)
    for k in range(12):
        trade(k).wait_send()
    for k in (1, 2, 3):
        a_copy(k).wait_send()
        c_copy(k).wait_send()


def backward(frame_clip, patch_clip, padding, vec, saved, fulls, shards):
    (x_t, n_t, j_t, m_t, o_t, x_s, n_s, j_s, m_s, n_f, cot, act, gh, act_sib, gh_sib, gmid, gb, sums) = saved
    vm = pl.BlockSpec(memory_space=pltpu.VMEM)
    sm = pl.BlockSpec(memory_space=pltpu.SMEM)
    hbm = pl.BlockSpec(memory_space=pl.ANY)
    sds = jax.ShapeDtypeStruct
    sem = pltpu.SemaphoreType.DMA
    v = pltpu.VMEM
    t, p = TIME_ROWS, SPACE_ROWS
    return pl.pallas_call(
        backward_kernel,
        out_shape=[
            sds((HERE * FRAMES, D), f32), sds((1, D), f32), sds((96, D), f32), sds((24, 4 * D), f32), sds((24, D), f32),
            sds((24, 3 * D), f32), sds((24, D), f32), sds((24, D), f32), sds((24, 3 * D), f32), sds((24, 128), f32),
        ],
        in_specs=[sm] + [vm] * 17 + [hbm] * 14,
        out_specs=[vm] * 10,
        scratch_shapes=[
            [v((2, 2, 2, r, c), bf16) for r, c in PARTS],
            [v((2, r, c), bf16) for r, c in PARTS],
            [v((2, r, c), bf16) for r, c in PARTS],
            [v((r, c), bf16) for r, c in PARTS],
            [v((r, c), bf16) for r, c in PARTS],
            [v((3, r // 2, c), bf16) for r, c in PARTS],
            [v((2, r // 4, c), f32) for r, c in PARTS],
            [v((r // 4, c), f32) for r, c in PARTS],
            sem((8, 16)),
            v((3, D, D), bf16),
            sem((3, 8)),
            v((p, 4 * D), bf16),
            v((p, 4 * D), bf16),
            sem((8,)),
            v((8, 2 * TIME_BLOCK), f32),
            v((FRAME, 2 * FRAME), f32),
            v((16, 512), jnp.int32),
            v((p, D), bf16),
            v((p, D), f32),
            v((t, D), bf16),
            v((t, D), bf16),
            v((t, D), bf16),
            v((4, OWN, SLOT, D), bf16),
            v((4, OWN, SLOT, D), bf16),
            sem((3,)),
            sem((4,)),
            v((4, 8, D), f32),
            sem((3,)),
            sem((4,)),
            v((2, D, 128), f32),
            v((48, D), f32),
            v((p, D), bf16),
            v((p, D), bf16),
            v((p, D), bf16),
            v((p, 384), bf16),
            v((p, D), bf16),
            v((p, 1152), bf16),
            v((t, D), bf16),
            v((t, 384), bf16),
            v((t, D), bf16),
            v((t, 384), bf16),
            v((t, D), bf16),
            v((t, 1152), bf16),
            sem((12,)),
            sem((12,)),
        ],
        compiler_params=pltpu.CompilerParams(
            collective_id=2, has_side_effects=True, vmem_limit_bytes=63 << 20
        ),
        name="backward",
    )(
        frame_clip, patch_clip, padding, vec, sums, x_t, n_t, j_t, m_t, o_t, x_s, n_s, j_s, m_s, n_f, cot, gmid, gb,
        act, gh, act_sib, gh_sib, *fulls[:5], *shards[:5]
    )


def settle(share):
    count = lax.axis_size("seq")
    if count == 8:
        return share
    more = count // 8
    groups = [[low + 8 * high for high in range(more)] for low in range(8)]
    share = lax.psum_scatter(share, "seq", scatter_dimension=0, tiled=True, axis_index_groups=groups)
    moves = [
        ((high * 8 + low) * 4 + f, (low * 4 + f) * more + high)
        for high in range(more)
        for low in range(8)
        for f in range(4)
    ]
    return lax.ppermute(share, ("seq", "ft"), moves)


def shards(
    video,
    class_token,
    frame_clip,
    patch_clip,
    padding,
    time_gain,
    time_shift,
    time_project,
    time_output,
    time_output_bias,
    time_mixer,
    time_mixer_bias,
    space_gain,
    space_shift,
    space_project,
    space_output,
    space_output_bias,
    feed_gain,
    feed_shift,
    feed_expand,
    feed_expand_bias,
    feed_reduce,
    feed_reduce_bias,
    grad_output,
    grad_class_out,
):
    vectors = jnp.zeros((16, D // 4), bf16)
    row = lax.broadcasted_iota(jnp.int32, vectors.shape, 0)
    for i, item in enumerate(
        (
            time_gain,
            time_shift,
            time_output_bias,
            time_mixer_bias,
            space_gain,
            space_shift,
            space_output_bias,
            feed_gain,
            feed_shift,
            feed_reduce_bias,
        )
    ):
        vectors = jnp.where(row == i, item[None, :], vectors)
    expand_bias = jnp.broadcast_to(feed_expand_bias[None, :], (16, D))
    weights = (time_project, time_output, time_mixer, space_project, space_output, feed_expand, feed_reduce)
    cotangent = jnp.swapaxes(grad_output[0], 0, 1)
    done = forward(
        jnp.swapaxes(video[0], 0, 1).reshape(HERE * FRAMES, D), class_token, frame_clip, patch_clip, padding, vectors, expand_bias, cotangent, grad_class_out, weights
    )
    output, class_output = jnp.swapaxes(done[0], 0, 1)[None], done[1]
    grads = backward(frame_clip, patch_clip, padding, done[27], done[9:27], done[2:9], weights)
    rows, grad_class = grads[:2]
    grad_video = jnp.swapaxes(rows.reshape(HERE, FRAMES, D), 0, 1)[None]
    d_reduce, d_expand, d_so, d_sp, d_tm, d_to, d_tp, d_narrow = [settle(g) for g in grads[2:]]
    narrow = [d_narrow[:, i] for i in range(10)]
    return (
        output,
        class_output,
        grad_video,
        grad_class,
        narrow[0],
        narrow[1],
        d_tp,
        d_to,
        narrow[2],
        d_tm,
        narrow[3],
        narrow[4],
        narrow[5],
        d_sp,
        d_so,
        narrow[6],
        narrow[7],
        narrow[8],
        d_expand,
        d_narrow[:, 10:14].reshape(-1),
        d_reduce,
        narrow[9],
    )


def solution(mesh):
    in_specs = (
        P("seq", None, "ft", None),
        P("seq", None),
        P("seq", None),
        P("seq", None),
        P("seq", None),
        P("ft"),
        P("ft"),
        P("ft", None),
        P("ft", None),
        P("ft"),
        P("ft", None),
        P("ft"),
        P("ft"),
        P("ft"),
        P("ft", None),
        P("ft", None),
        P("ft"),
        P("ft"),
        P("ft"),
        P("ft", None),
        P("ft"),
        P("ft", None),
        P("ft"),
        P("seq", "ft", None, None),
        P("seq", None),
    )
    out_specs = (
        P("seq", "ft", None, None),
        P("seq", None),
        P("seq", None, "ft", None),
        P("seq", None),
        P(("seq", "ft")),
        P(("seq", "ft")),
        P(("seq", "ft"), None),
        P(("seq", "ft"), None),
        P(("seq", "ft")),
        P(("seq", "ft"), None),
        P(("seq", "ft")),
        P(("seq", "ft")),
        P(("seq", "ft")),
        P(("seq", "ft"), None),
        P(("seq", "ft"), None),
        P(("seq", "ft")),
        P(("seq", "ft")),
        P(("seq", "ft")),
        P(("seq", "ft"), None),
        P(("seq", "ft")),
        P(("seq", "ft"), None),
        P(("seq", "ft")),
    )
    return jax.shard_map(shards, mesh=mesh, in_specs=in_specs, out_specs=out_specs, check_vma=False)
```

```python
import jax
import jax.numpy as jnp
from jax import lax
from jax.experimental import pallas as pl
from jax.experimental.pallas import tpu as pltpu
from jax.sharding import PartitionSpec as P

MESH = pl.DeviceIdType.MESH
bf16 = jnp.bfloat16
f32 = jnp.float32
D = 768
FRAMES = 8
HERE = 49
OWN = 2
PATCHES = 196
TIME_ROWS = 400
TIME_BLOCK = 80
FRAME = 208
CLASS = 196
SPACE_ROWS = OWN * FRAME
SLOT = 112
EPSILON = 1e-06
UNITS = 7


def iota(shape, axis):
    return lax.broadcasted_iota(jnp.int32, shape, axis)


def dot(left, right):
    return jnp.dot(left, right, preferred_element_type=f32)


def dot_nt(left, right):
    return lax.dot_general(left, right, (((1,), (1,)), ((), ())), preferred_element_type=f32)


def dot_tn(left, right):
    return lax.dot_general(left, right, (((0,), (0,)), ((), ())), preferred_element_type=f32)


def picks(condition):
    return jnp.where(condition, 1.0, 0.0).astype(bf16)


def between(r):
    return ((r & 7) >> 1) * SLOT + (r & 1) * HERE + (r >> 3)


def to_patches():
    r, c = iota((TIME_ROWS, 4 * SLOT), 0), iota((TIME_ROWS, 4 * SLOT), 1)
    return picks((c == between(r)) & (r < FRAMES * HERE))


def to_frames():
    c, r = iota((4 * SLOT, TIME_ROWS), 0), iota((4 * SLOT, TIME_ROWS), 1)
    return picks((c == between(r)) & (r < FRAMES * HERE))


def source_of(token, frame):
    late = (token >= HERE).astype(jnp.int32) + (token >= 2 * HERE) + (token >= 3 * HERE)
    return token + late * (SLOT - HERE) + frame * HERE


def to_tokens():
    r, c = iota((SPACE_ROWS, 4 * SLOT), 0), iota((SPACE_ROWS, 4 * SLOT), 1)
    frame = (r >= FRAME).astype(jnp.int32)
    token = r - frame * FRAME
    return picks((c == source_of(token, frame)) & (token < PATCHES))


def from_tokens():
    c, r = iota((4 * SLOT, SPACE_ROWS), 0), iota((4 * SLOT, SPACE_ROWS), 1)
    frame = (r >= FRAME).astype(jnp.int32)
    token = r - frame * FRAME
    return picks((c == source_of(token, frame)) & (token < PATCHES))


def from_twos():
    r, c = iota((SPACE_ROWS, OWN * PATCHES), 0), iota((SPACE_ROWS, OWN * PATCHES), 1)
    frame = (r >= FRAME).astype(jnp.int32)
    token = r - frame * FRAME
    return picks((c == 2 * token + frame) & (token < PATCHES))


def to_twos():
    r, c = iota((OWN * PATCHES, SPACE_ROWS), 0), iota((OWN * PATCHES, SPACE_ROWS), 1)
    return picks(c == (r >> 1) + (r & 1) * FRAME)


def normed(rows):
    centred = rows - jnp.mean(rows, axis=-1, keepdims=True)
    scale = lax.rsqrt(jnp.mean(centred * centred, axis=-1, keepdims=True) + EPSILON)
    return centred * scale, scale


def over_blocks(count, size, step):
    def body(i, carry):
        step(pl.ds(pl.multiple_of(i * size, 16), size))
        return carry

    lax.fori_loop(0, count, body, 0, unroll=True)


def halves(scale):
    lane = iota((1, 128), 1)
    first = jnp.where(lane < 64, scale, 0.0).astype(bf16)
    second = jnp.where(lane < 64, 0.0, scale).astype(bf16)
    return first, second


def chances(scores):
    power = jnp.exp(scores - jnp.max(scores, axis=0, keepdims=True))
    return power * (1.0 / jnp.sum(power, axis=0, keepdims=True))


def diagonal(heads):
    shape = (TIME_BLOCK // 8, 8, heads * TIME_BLOCK)
    lane = iota(shape, 2)
    lane = jnp.where(lane < TIME_BLOCK, lane, lane - TIME_BLOCK)
    return iota(shape, 0) == (lane >> 3)


def gathered(scores, where):
    return jnp.sum(jnp.where(where, scores.reshape(where.shape), 0.0), axis=0)


def scattered(scores, where):
    wide = jnp.where(where, jnp.broadcast_to(scores[None], where.shape), 0.0)
    return wide.reshape(TIME_BLOCK, where.shape[2]).astype(bf16)


def pair(i, j, size):
    rows = pl.ds(pl.multiple_of(i * size, 16), size)
    return rows, [pl.ds(pl.multiple_of(k * D + j * 128, 128), 128) for k in range(3)]


def both(values, first, second):
    return jnp.concatenate([values * first, values * second], axis=0)


def unite(values, size):
    return jnp.where(iota((size, 128), 1) < 64, values[:size], values[size:])


def attend_time(joined, bias, mixed, blocks, size, unroll):
    first8, second8 = halves(0.125)
    where = diagonal(1)

    def body(n, carry):
        rows, (ql, kl, vl) = pair(n // 6, lax.rem(n, 6), size)
        query, keys, values = joined[rows, ql], joined[rows, kl], joined[rows, vl]
        out = []
        for part in (query * first8, query * second8):
            scores = gathered(dot_nt(keys, part), where) + bias[:, 0:size]
            out.append(dot_tn(scattered(chances(scores), where), values))
        mixed[rows, ql] = jnp.where(iota((size, 128), 1) < 64, out[0], out[1]).astype(bf16)
        return carry

    lax.fori_loop(0, blocks * 6, body, 0, unroll=unroll)


def attend_space(joined, bias, mixed, blocks, size, unroll):
    first8, second8 = halves(0.125)

    def body(n, carry):
        rows, (ql, kl, vl) = pair(n // 6, lax.rem(n, 6), size)
        query, keys, values = joined[rows, ql], joined[rows, kl], joined[rows, vl]
        chance = chances(dot_nt(keys, both(query, first8, second8)) + bias[...]).astype(bf16)
        mixed[rows, ql] = unite(dot_tn(chance, values), size).astype(bf16)
        return carry

    lax.fori_loop(0, blocks * 6, body, 0, unroll=unroll)


def attend_back(joined, bias, grad_mixed, grad_joined, blocks, size, unroll):
    first8, second8 = halves(0.125)
    first, second = halves(1.0)
    where = diagonal(2) if size == TIME_BLOCK else None

    def body(n, carry):
        rows, (ql, kl, vl) = pair(n // 6, lax.rem(n, 6), size)
        query, keys, values = joined[rows, ql], joined[rows, kl], joined[rows, vl]
        queries, grads = both(query, first8, second8), both(grad_mixed[rows, ql], first, second)
        scores, pull = dot_nt(keys, queries), dot_nt(values, grads)
        if where is not None:
            scores, pull = gathered(scores, where), gathered(pull, where)
        chance = chances(scores + bias[...])
        back = chance * (pull - jnp.sum(chance * pull, axis=0, keepdims=True))
        if where is None:
            chance, back = chance.astype(bf16), back.astype(bf16)
        else:
            chance, back = scattered(chance, where), scattered(back, where)
        grad_joined[rows, ql] = (unite(dot_tn(back, keys), size) * 0.125).astype(bf16)
        grad_joined[rows, kl] = dot(back, queries).astype(bf16)
        grad_joined[rows, vl] = dot(chance, grads).astype(bf16)
        return carry

    lax.fori_loop(0, blocks * 6, body, 0, unroll=unroll)


def time_bias(frame_clip, bias):
    shape = (8, 2 * TIME_BLOCK)
    r, c = iota(shape, 0), iota(shape, 1)
    clip_r, clip_c = jnp.zeros(shape, jnp.int32), jnp.zeros(shape, jnp.int32)
    for f in range(FRAMES):
        clip_r = jnp.where(r == f, frame_clip[0, f], clip_r)
        clip_c = jnp.where((c & 7) == f, frame_clip[0, f], clip_c)
    bias[...] = jnp.where(clip_r == clip_c, 0.0, -1e30)


def space_bias(patch_clip, padding, spare, bias):
    shape = (FRAME, FRAME)
    r, c = iota(shape, 0), iota(shape, 1)
    spare[...] = jnp.full(spare.shape, -1, jnp.int32)
    for half in range(2):
        spare[0:1, half * FRAME : half * FRAME + PATCHES] = patch_clip[...]
    spare[8:9, 0:PATCHES] = padding[...]
    clip = jnp.broadcast_to(spare[0:1, 0:FRAME], shape).astype(f32)
    shut = jnp.broadcast_to(spare[8:9, 0:FRAME], shape).astype(f32)
    own = jnp.sum(jnp.where(r == c, clip, 0.0), axis=1, keepdims=True)
    closed = jnp.sum(jnp.where(r == c, shut, 0.0), axis=1, keepdims=True)
    shape = (FRAME, 2 * FRAME)
    r, c = iota(shape, 0), iota(shape, 1)
    clip = jnp.broadcast_to(spare[0:1, 0 : 2 * FRAME], shape).astype(f32)
    of_class = (c == CLASS) | (c == FRAME + CLASS)
    opened = (r == CLASS) | ((closed == 0.0) & ((clip == own) | of_class))
    bias[...] = jnp.where(opened, 0.0, -1e30)


def place():
    s = lax.axis_index("seq")
    f = lax.axis_index("ft")
    core = lax.rem(s, 2)
    col = lax.rem(s // 2, 2)
    row = lax.rem(s // 4, 2)
    return s, f, core, col, row


def remote(src, dst, send, recv, target):
    return pltpu.make_async_remote_copy(
        src_ref=src, dst_ref=dst, send_sem=send, recv_sem=recv, device_id=target, device_id_type=MESH
    )


class Spread:
    def __init__(self, shards, fulls, send, recv):
        self.shards, self.fulls, self.send, self.recv = shards, fulls, send, recv
        self.s, self.f, self.core, self.col, self.row = place()
        s = self.s
        self.sib = s + 1 - 2 * self.core
        dx, dy = 2 - 4 * self.col, 4 - 8 * self.row
        self.plane = ((s + dx, 1, 0), (s + dy, 0, 1), (s + dx + dy, 1, 1))
        upper = self.f // 2
        near = self.f + upper * (3 - 2 * self.f)
        self.order = [upper * 3 + (1 - 2 * upper) * v for v in (1 - near, 2, 3)]

    def greet(self):
        bar = pltpu.get_barrier_semaphore()
        targets = [(t, self.f) for t in (self.sib,) + tuple(p[0] for p in self.plane)]
        targets += [(self.s, lax.rem(self.f + j, 4)) for j in (1, 2, 3)]
        for t in targets:
            pl.semaphore_signal(bar, inc=1, device_id=t, device_id_type=MESH)
        pl.semaphore_wait(bar, len(targets))

    def cut(self, w, base, row, col):
        rows, wide = self.shards[w].shape
        start = base + self.core * (rows // 2) + row * (rows // 4)
        return (
            pl.ds(pl.multiple_of(start, 16), rows // 4),
            pl.ds(pl.multiple_of(col * (wide // 2), 128), wide // 2),
        )

    def along(self, w, k):
        z = lax.rem(self.f + k, 4)
        rows = self.shards[w].shape[0]
        src = self.shards[w].at[self.cut(w, 0, self.row, self.col)]
        dst = self.fulls[w].at[self.cut(w, self.f * rows, self.row, self.col)]
        return remote(src, dst, self.send.at[w, k - 1], self.recv.at[w, 0, self.f], (self.s, z))

    def start(self, w):
        for k in (1, 3, 2):
            self.along(w, k).start()

    def over(self, w, z, i, mine=True):
        target, dx, dy = self.plane[i]
        rows = self.shards[w].shape[0]
        row, col = (self.row, self.col) if mine else (self.row + dy - 2 * dy * self.row, self.col + dx - 2 * dx * self.col)
        ref = self.fulls[w].at[self.cut(w, z * rows, row, col)]
        return remote(ref, ref, self.send.at[w, 3 + 4 * i + z], self.recv.at[w, 1 + i, z], (target, self.f))

    def across(self, w, z, mine=True):
        rows = self.shards[w].shape[0]
        core = self.core if mine else 1 - self.core
        ref = self.fulls[w].at[pl.ds(pl.multiple_of(z * rows + core * (rows // 2), 16), rows // 2), :]
        return remote(ref, ref, self.send.at[w, 15 + z], self.recv.at[w, 4, z], (self.sib, self.f))

    def fan(self, w, nearest=(0, 1, 2)):
        rows = self.shards[w].shape[0]
        for t in nearest:
            z = self.order[t]
            ref = self.fulls[w].at[self.cut(w, z * rows, self.row, self.col)]
            remote(ref, ref, self.send.at[w, 0], self.recv.at[w, 0, z], (self.s, z)).wait_recv()
            for i in (2, 0, 1):
                self.over(w, z, i).start()

    def lend(self, w):
        for z in self.order:
            for i in range(3):
                self.over(w, z, i, False).wait_recv()
            self.across(w, z).start()

    def finish(self, w):
        for z in self.order:
            self.across(w, z, False).wait_recv()


    def quarter(self, w, base, own=True):
        rows = self.shards[w].shape[0]
        half = lax.rem(self.col + self.row, 2)
        which = 2 * half + self.core if own else 2 * (1 - half) + self.core
        return pl.ds(pl.multiple_of(base + which * (rows // 4), 16), rows // 4)

    def hop(self, w, z, step, src=None):
        dst = self.fulls[w].at[self.quarter(w, z * self.shards[w].shape[0])]
        side = 0 if step == 1 else 1
        src = dst if src is None else src
        return remote(src, dst, self.send.at[w, 4 * side + z], self.recv.at[w, 0, z], (self.s, self.f + step))

    def beside(self, w, z, i, own=True):
        wide = self.shards[w].shape[1]
        rows = self.quarter(w, z * self.shards[w].shape[0], own)
        ref = self.fulls[w].at[rows, i * (wide // 2) : (i + 1) * (wide // 2)]
        return remote(ref, ref, self.send.at[w, 8 + 4 * i + z], self.recv.at[w, 1 + i, z], (self.plane[i][0], self.f))

    def cross(self, w, z, own=True):
        ref = self.fulls[w].at[self.quarter(w, z * self.shards[w].shape[0], own)]
        i = 0 if own else 1
        return remote(ref, ref, self.send.at[w, 16 + 4 * i + z], self.recv.at[w, 3 + i, z], (self.sib, self.f))

    def off(self, w):
        src = self.shards[w].at[self.quarter(w, 0)]

        @pl.when(self.f < 3)
        def _():
            self.hop(w, self.f, 1, src).start()

        @pl.when(self.f > 0)
        def _():
            self.hop(w, self.f, -1, src).start()

    def onward(self, w, t, act):
        z = self.order[t]

        @pl.when((z < self.f) & (self.f < 3))
        def _():
            act(self.hop(w, z, 1))

        @pl.when((z > self.f) & (self.f > 0))
        def _():
            act(self.hop(w, z, -1))

    def relay(self, w, t):
        z = self.order[t]
        self.hop(w, z, 1).wait_recv()
        self.onward(w, t, lambda copy: copy.start())
        self.beside(w, z, 0).start()
        self.beside(w, z, 1).start()
        self.cross(w, z).start()

    def pass_on(self, w, t):
        z = self.order[t]
        for i in range(2):
            self.beside(w, z, i, False).wait_recv()
        self.cross(w, z, False).start()

    def complete(self, w):
        for z in self.order:
            self.cross(w, z).wait_recv()
            self.cross(w, z, False).wait_recv()

    def empty(self, w):
        src = self.shards[w].at[self.quarter(w, 0)]

        @pl.when(self.f < 3)
        def _():
            self.hop(w, self.f, 1, src).wait_send()

        @pl.when(self.f > 0)
        def _():
            self.hop(w, self.f, -1, src).wait_send()

        for t in range(3):
            z = self.order[t]
            self.onward(w, t, lambda copy: copy.wait_send())
            self.beside(w, z, 0).wait_send()
            self.beside(w, z, 1).wait_send()
            self.cross(w, z).wait_send()
            self.cross(w, z, False).wait_send()

    def drain(self, w):
        for k in (1, 2, 3):
            self.along(w, k).wait_send()
        for z in self.order:
            for i in range(3):
                self.over(w, z, i).wait_send()
            self.across(w, z).wait_send()


class Loads:
    def __init__(self, slots, sems, pieces, f):
        self.slots, self.sems, self.pieces, self.f = slots, sems, pieces, f

    def copies(self, i):
        n = i % self.slots.shape[0]
        full, shard, what, spot = self.pieces[i]
        slot = self.slots.at[n]
        if what == "columns":
            lanes = slice(spot * D, (spot + 1) * D)
            out = [(shard.at[:, lanes], slot.at[pl.ds(pl.multiple_of(self.f * 192, 16), 192)], None)]
            for k in (1, 2, 3):
                rows = pl.ds(pl.multiple_of(lax.rem(self.f + k, 4) * 192, 16), 192)
                out.append((full.at[rows, lanes], slot.at[rows], None))
        elif what == "wide":
            core, high = spot
            out = []
            for x in range(2):
                start = pl.multiple_of(((high * 2 + x) * 2 + core) * 384, 128)
                lanes, at = pl.ds(start, 384), slice(x * 384, (x + 1) * 384)
                out.append((shard.at[:, lanes], slot.at[pl.ds(pl.multiple_of(self.f * 192, 16), 192), at], None))
                for k in (1, 2, 3):
                    rows = pl.ds(pl.multiple_of(lax.rem(self.f + k, 4) * 192, 16), 192)
                    out.append((full.at[rows, lanes], slot.at[rows, at], None))
        else:
            core, high = spot
            out = []
            for x in range(2):
                z = high * 2 + x
                at = slot.at[x * 384 : (x + 1) * 384]
                here = shard.at[pl.ds(pl.multiple_of(core * 384, 16), 384)]
                there = full.at[pl.ds(pl.multiple_of(z * 768 + core * 384, 16), 384)]
                out += [(here, at, self.f == z), (there, at, self.f != z)]
        return [
            (pltpu.make_async_copy(src, dst, self.sems.at[n, k]), when) for k, (src, dst, when) in enumerate(out)
        ]

    def each(self, i, act):
        for copy, when in self.copies(i):
            if when is None:
                act(copy)
            else:
                pl.when(when)(lambda copy=copy: act(copy))

    def start(self, i):
        self.each(i, lambda copy: copy.start())

    def get(self, i):
        self.each(i, lambda copy: copy.wait())
        return self.slots[i % self.slots.shape[0]]


ALL = slice(None)


def squares(fulls, shards, w, count):
    return [(fulls[w], shards[w], "columns", i) for i in range(count)]


def forward_kernel(*refs):
    (video, class_token, frame_clip, patch_clip, padding, vectors, expand_bias, grad_output, grad_class_out) = refs[:9]
    shards = refs[9:16]
    outs = refs[16:44]
    (output, class_output) = outs[:2]
    fulls = outs[2:9]
    saved_out = outs[9:20] + outs[20:22] + outs[24:26]
    act_sib, gh_sib, sums, small_out = outs[22], outs[23], outs[26], outs[27]
    (send, recv, vec, vec32, vsend, vrecv, slots, slot_sems, a2s, a2r, asend, arecv, tbias, sbias, spare,
     rows_f, acc, acc2, hid, gact, cls, csend, crecv, psend, precv, act_go, gh_go, vec_go,
     x_t, n_t, j_t, m_t, o_t, x_s, n_s, j_s, m_s, n_f, cot, act, gh, gmid, gb, save_sems) = refs[44:]
    made = (x_t, n_t, j_t, m_t, o_t, x_s, n_s, j_s, m_s, n_f, cot, act, gh, gmid, gb)
    X_T, N_T, J_T, M_T, O_T, X_S, N_S, J_S, M_S, N_F, COT, ACT, GH, GMID, GB = range(15)

    def save(k):
        return pltpu.make_async_copy(made[k], saved_out[k], save_sems.at[k])


    net = Spread(shards, fulls, send, recv)
    s, f, core = net.s, net.f, net.core
    net.greet()

    def vec_copy(k):
        return remote(vec_go, vec.at[f], vsend.at[k - 1], vrecv.at[f], (s, lax.rem(f + k, 4)))

    vec_go[0:16, 0:192] = vectors[...]
    vec_go[0:16, 192:D] = jnp.zeros((16, D - 192), bf16)
    vec_go[16:32] = expand_bias[...]
    for k in (1, 3, 2):
        vec_copy(k).start()
    net.start(0)
    vec[f] = vec_go[...]

    x_t[384:TIME_ROWS] = jnp.zeros((TIME_ROWS - 384, D), bf16)
    x_t[0 : HERE * FRAMES] = video[...]
    save(X_T).start()
    time_bias(frame_clip, tbias)
    for k in (1, 3, 2):
        z = lax.rem(f + k, 4)
        remote(vec_go, vec.at[z], vsend.at[0], vrecv.at[z], (s, z)).wait_recv()
    net.fan(0, (0,))
    small = jnp.zeros((16, D), f32)
    for z in range(4):
        r, c = iota((192, D), 0), iota((192, D), 1) - z * 192
        small += dot(vec[z, 0:16, 0:192], picks(c == r))
        vec32[1 + z] = vec[z, 16:32].astype(f32)
    vec32[0] = small
    small_out[...] = small
    net.fan(0, (1,))

    def vector(i):
        return vec32[0, i : i + 1, :]

    gain, shift = vector(0), vector(1)

    def norm_time(rows):
        scaled, unused = normed(x_t[rows].astype(f32))
        n_t[rows] = (scaled * gain + shift).astype(bf16)

    over_blocks(5, 80, norm_time)
    save(N_T).start()
    net.start(1)
    net.start(2)
    net.fan(0, (2,))
    net.off(3)
    net.start(4)
    net.off(5)

    cot[...] = dot(from_twos(), grad_output[...].reshape(OWN * PATCHES, D)).astype(bf16)
    at_class = iota((16, D), 0) == CLASS - 192
    tail = jnp.where(at_class, grad_class_out[...].astype(f32), cot[192:FRAME].astype(f32))
    cot[192:FRAME] = tail.astype(bf16)
    save(COT).start()
    space_bias(patch_clip, padding, spare, sbias)

    pieces = []
    for w, count in ((0, 3), (1, 1), (2, 1), (3, 3), (4, 1)):
        pieces += squares(fulls, shards, w, count)
    for c, high in ((1 - core, 0), (1 - core, 1), (core, 0), (core, 1)):
        pieces += [(fulls[5], shards[5], "wide", (c, high)), (fulls[6], shards[6], "tall", (c, high))]
    loads = Loads(slots, slot_sems, pieces, f)

    net.lend(0)
    net.fan(1)
    net.fan(2)
    net.relay(3, 0)
    net.finish(0)
    for i in range(3):
        loads.start(i)
    for i in range(3):
        j_t[:, i * D : (i + 1) * D] = dot(n_t[...], loads.get(i)).astype(bf16)
    save(J_T).start()
    net.relay(3, 1)
    attend_time(j_t, tbias, m_t, 5, TIME_BLOCK, 6)
    net.lend(1)
    net.lend(2)
    net.relay(3, 2)
    net.finish(1)
    loads.start(3)
    net.finish(2)
    loads.start(4)
    net.relay(5, 0)
    o_t[...] = (dot(m_t[...], loads.get(3)) + vector(2)).astype(bf16)
    save(M_T).start()
    save(O_T).start()
    after = (x_t[...].astype(f32) + (dot(o_t[...], loads.get(4)) + vector(3))).astype(bf16)
    a2s[...] = dot(to_frames(), after).astype(bf16).reshape(4, SLOT, D)

    def a_copy(k):
        z = lax.rem(f + k, 4)
        return remote(a2s.at[z], a2r.at[f], asend.at[k - 1], arecv.at[f], (s, z))

    for k in (1, 3, 2):
        a_copy(k).start()
    net.off(6)
    a2r[f] = a2s[f]
    net.fan(4)
    for i in range(3):
        net.pass_on(3, i)
    net.complete(3)
    for i in range(5, 8):
        loads.start(i)
    net.relay(5, 1)
    net.lend(4)
    net.finish(4)
    for k in (1, 3, 2):
        z = lax.rem(f + k, 4)
        with jax.named_scope("a_wait"):
            remote(a2s.at[z], a2r.at[z], asend.at[0], arecv.at[z], (s, z)).wait_recv()
    net.relay(6, 0)

    spread_rows = dot(to_tokens(), a2r[...].reshape(4 * SLOT, D))
    r = iota((SPACE_ROWS, D), 0)
    is_class = (r == CLASS) | (r == FRAME + CLASS)
    x_s[...] = jnp.where(is_class, class_token[...].astype(f32), spread_rows).astype(bf16)
    gain, shift = vector(4), vector(5)

    def norm_space(rows):
        scaled, unused = normed(x_s[rows].astype(f32))
        n_s[rows] = (scaled * gain + shift).astype(bf16)

    over_blocks(13, 32, norm_space)
    save(X_S).start()
    save(N_S).start()
    for i in range(3):
        j_s[:, i * D : (i + 1) * D] = dot(n_s[...], loads.get(5 + i)).astype(bf16)
    save(J_S).start()
    loads.start(8)
    net.relay(5, 2)
    attend_space(j_s, sbias, m_s, OWN, FRAME, 6)
    net.relay(6, 1)
    rows_f[...] = dot(m_s[...], loads.get(8)) + vector(6)
    save(M_S).start()
    token = class_token[...].astype(f32)
    cls[f] = jnp.broadcast_to(
        rows_f[CLASS : CLASS + 1] + rows_f[FRAME + CLASS : FRAME + CLASS + 1], (8, D)
    )

    def c_copy(k):
        return remote(cls.at[f], cls.at[f], csend.at[k - 1], crecv.at[f], (s, lax.rem(f + k, 4)))

    for k in (1, 3, 2):
        c_copy(k).start()
    for i in range(3):
        net.pass_on(5, i)
    net.relay(6, 2)
    for k in (1, 3, 2):
        z = lax.rem(f + k, 4)
        remote(cls.at[f], cls.at[z], csend.at[0], crecv.at[z], (s, z)).wait_recv()
    mid = token + ((cls[0] + cls[1]) + (cls[2] + cls[3]))[0:1] * (1.0 / FRAMES)
    gain, shift = vector(7), vector(8)
    first = jnp.where(f == 0, 1.0, 0.0)

    def norm_feed(rows):
        r = iota((32, D), 0) + rows.start
        at_class = r == CLASS
        other = r == FRAME + CLASS
        values = x_s[rows].astype(f32) + rows_f[rows]
        values = jnp.where(at_class, mid, jnp.where(other, 0.0, values))
        rows_f[rows] = values
        scaled, unused = normed(values)
        n_f[rows] = (scaled * gain + shift).astype(bf16)
        acc[rows] = values + vector(9)
        acc2[rows] = jnp.zeros((32, D), f32)

    over_blocks(13, 32, norm_feed)
    save(N_F).start()
    net.complete(5)
    loads.start(9)
    for i in range(3):
        net.pass_on(6, i)

    def sib_copy(k, half, src, dst):
        return remote(src.at[half], dst.at[half], psend.at[k, half], precv.at[k, half], (net.sib, f))

    for j in range(4):
        c = 1 - core if j < 2 else core
        high = j & 1
        bias = jnp.concatenate(
            [vec32[1 + 2 * high + x, 0:1, pl.ds(pl.multiple_of(c * 384, 128), 384)] for x in range(2)], axis=1
        )
        w1 = loads.get(9 + 2 * j)
        hid[...] = dot(n_f[...], w1) + bias
        if j == 0:
            net.complete(6)
            for i in (10, 11, 12):
                loads.start(i)
        w2 = loads.get(10 + 2 * j)
        gact[...] = dot_nt(cot[...], w2)
        act_to, gh_to = (act_go, gh_go) if j < 2 else (act, gh)

        def feed(rows):
            hidden = hid[rows]
            tail = 0.5 + 0.5 * lax.erf(hidden * 0.7071067811865476)
            slope = tail + hidden * (jnp.exp(hidden * hidden * -0.5) * 0.3989422804014327)
            act_to[high, rows] = (hidden * tail).astype(bf16)
            gh_to[high, rows] = (gact[rows] * slope).astype(bf16)

        over_blocks(13, 32, feed)
        acc[...] += dot(act_to[high], w2)
        acc2[...] += dot_nt(gh_to[high], w1)
        for i in (13 + 2 * j, 14 + 2 * j):
            if i < 17:
                loads.start(i)

        at_class = iota((16, D), 0) == CLASS - 192
        for ref in (act_to, gh_to):
            piece = ref[high, 192:FRAME].astype(f32)
            ref[high, 192:FRAME] = jnp.where(at_class, piece * first, piece).astype(bf16)
        if j < 2:
            sib_copy(0, high, act_go, act_sib).start()
            sib_copy(1, high, gh_go, gh_sib).start()

    save(ACT).start()
    save(GH).start()

    twos = dot(to_twos(), acc[...].astype(bf16)).astype(bf16)
    output[...] = twos.reshape(PATCHES, OWN, D)
    class_output[...] = acc[CLASS : CLASS + 1].astype(bf16)
    gain = vector(7)
    sums[...] = jnp.zeros_like(sums)

    def feed_back(rows):
        r = iota((32, D), 0) + rows.start
        scaled, scale = normed(rows_f[rows])
        pulled = acc2[rows]
        counted = jnp.where(r == CLASS, pulled * first, pulled)
        sums[0:8] += jnp.sum((counted * scaled).reshape(4, 8, D), axis=0)
        sums[8:16] += jnp.sum(counted.reshape(4, 8, D), axis=0)
        up = pulled * gain
        back = scale * (
            up - jnp.mean(up, axis=-1, keepdims=True) - scaled * jnp.mean(up * scaled, axis=-1, keepdims=True)
        )
        grad = cot[rows].astype(f32) + back
        gmid[rows] = grad
        gb[rows] = grad.astype(bf16)

    over_blocks(13, 32, feed_back)
    row = (gmid[CLASS : CLASS + 1] * (1.0 / FRAMES)).astype(bf16).astype(f32)
    for start in (192, FRAME + 192):
        piece = gb[start : start + 16].astype(f32)
        gb[start : start + 16] = jnp.where(at_class, row, piece).astype(bf16)

    save(GMID).start()
    save(GB).start()
    for half in range(2):
        for k, src, dst in ((0, act_go, act_sib), (1, gh_go, gh_sib)):
            sib_copy(k, half, src, dst).wait()
    for k in (1, 2, 3):
        vec_copy(k).wait_send()
        a_copy(k).wait_send()
        c_copy(k).wait_send()
    for k in range(15):
        save(k).wait()
    for w in (0, 1, 2, 4):
        net.drain(w)
    for w in (3, 5, 6):
        net.empty(w)


def forward(video, class_token, frame_clip, patch_clip, padding, vectors, expand_bias, grad_output, grad_class_out, shards):
    vm = pl.BlockSpec(memory_space=pltpu.VMEM)
    sm = pl.BlockSpec(memory_space=pltpu.SMEM)
    hbm = pl.BlockSpec(memory_space=pl.ANY)
    sds = jax.ShapeDtypeStruct
    sem = pltpu.SemaphoreType.DMA
    v = pltpu.VMEM
    t, p = TIME_ROWS, SPACE_ROWS
    outs = [sds((PATCHES, OWN, D), bf16), sds((1, D), bf16)]
    outs += [sds((4 * a.shape[0], a.shape[1]), bf16) for a in shards]
    outs += [sds((t, D), bf16), sds((t, D), bf16), sds((t, 3 * D), bf16), sds((t, D), bf16), sds((t, D), bf16)]
    outs += [sds((p, D), bf16), sds((p, D), bf16), sds((p, 3 * D), bf16), sds((p, D), bf16), sds((p, D), bf16)]
    outs += [sds((p, D), bf16)] + [sds((2, p, D), bf16)] * 4 + [sds((p, D), f32), sds((p, D), bf16), sds((16, D), f32), sds((16, D), f32)]
    return pl.pallas_call(
        forward_kernel,
        out_shape=outs,
        in_specs=[vm, vm, sm, vm, vm, vm, vm, vm, vm] + [hbm] * 7,
        out_specs=[vm, vm] + [hbm] * 7 + [hbm] * 17 + [vm] * 2,
        scratch_shapes=[
            sem((UNITS, 24)),
            sem((UNITS, 5, 4)),
            v((4, 32, D), bf16),
            v((5, 16, D), f32),
            sem((3,)),
            sem((4,)),
            v((4, D, D), bf16),
            sem((4, 8)),
            v((4, SLOT, D), bf16),
            v((4, SLOT, D), bf16),
            sem((3,)),
            sem((4,)),
            v((8, 2 * TIME_BLOCK), f32),
            v((FRAME, 2 * FRAME), f32),
            v((16, 512), jnp.int32),
            v((p, D), f32),
            v((p, D), f32),
            v((p, D), f32),
            v((p, D), f32),
            v((p, D), f32),
            v((4, 8, D), f32),
            sem((3,)),
            sem((4,)),
            sem((2, 2)),
            sem((2, 2)),
            v((2, p, D), bf16),
            v((2, p, D), bf16),
            v((32, D), bf16),
            v((t, D), bf16),
            v((t, D), bf16),
            v((t, 3 * D), bf16),
            v((t, D), bf16),
            v((t, D), bf16),
            v((p, D), bf16),
            v((p, D), bf16),
            v((p, 3 * D), bf16),
            v((p, D), bf16),
            v((p, D), bf16),
            v((p, D), bf16),
            v((2, p, D), bf16),
            v((2, p, D), bf16),
            v((p, D), f32),
            v((p, D), bf16),
            sem((15,)),
        ],
        compiler_params=pltpu.CompilerParams(
            collective_id=1, has_side_effects=True, vmem_limit_bytes=63 << 20
        ),
        name="forward",
    )(video, class_token, frame_clip, patch_clip, padding, vectors, expand_bias, grad_output, grad_class_out, *shards)


class Reduce:
    def __init__(self, parts, ra, rb, ra2, rb2, rz, total, rc, sems):
        self.parts, self.ra, self.rb, self.ra2, self.rb2 = parts, ra, rb, ra2, rb2
        self.rz, self.total, self.rc, self.sems = rz, total, rc, sems
        self.s, self.f, self.core, self.col, self.row = place()
        s = self.s
        self.sib = s + 1 - 2 * self.core
        self.across, self.down = s + 2 - 4 * self.col, s + 4 - 8 * self.row

    def greet(self):
        bar = pltpu.get_barrier_semaphore()
        targets = [(t, self.f) for t in (self.sib, self.across, self.down)]
        targets += [(self.s, lax.rem(self.f + j, 4)) for j in (1, 2, 3)]
        for t in targets:
            pl.semaphore_signal(bar, inc=1, device_id=t, device_id_type=MESH)
        pl.semaphore_wait(bar, len(targets))

    def sem(self, w, i):
        return self.sems.at[w, i]

    def copies1(self, w):
        g = self.parts[w]
        return (
            remote(g.at[:, 1 - self.col, 0], self.ra[w], self.sem(w, 0), self.sem(w, 1), (self.across, self.f)),
            remote(g.at[1 - self.row, :, 1], self.rb[w], self.sem(w, 2), self.sem(w, 3), (self.down, self.f)),
        )

    def copies2(self, w):
        return (
            remote(self.ra[w].at[1 - self.row], self.ra2[w], self.sem(w, 4), self.sem(w, 5), (self.down, self.f)),
            remote(self.rb[w].at[1 - self.col], self.rb2[w], self.sem(w, 6), self.sem(w, 7), (self.across, self.f)),
        )

    def block(self, w, z):
        g = self.parts[w]
        rows = g.shape[3] // 2
        return g.at[z // 2, 1 - self.col, 0, pl.ds(pl.multiple_of(lax.rem(z, 2) * rows, 16), rows), :]

    def copies3(self, w):
        out = []
        for j in (1, 3, 2):
            z = lax.rem(self.f + j, 4)
            out.append(
                remote(self.block(w, z), self.rz[w].at[3 - j], self.sem(w, 7 + j), self.sem(w, 14 - j), (self.s, z))
            )
        return out

    def copy4(self, w):
        return remote(
            self.total[w].at[1 - self.core], self.rc[w], self.sem(w, 14), self.sem(w, 15), (self.sib, self.f)
        )

    def step1(self, w):
        for c in self.copies1(w):
            c.start()

    def step2(self, w):
        a, b = self.copies1(w)
        g, ra, rb = self.parts[w], self.ra[w], self.rb[w]
        row, col = self.row, self.col
        a2, b2 = self.copies2(w)
        a.wait_recv()
        ra[1 - row] = (ra[1 - row].astype(f32) + g[1 - row, col, 0].astype(f32)).astype(bf16)
        a2.start()
        b.wait_recv()
        rb[1 - col] = (rb[1 - col].astype(f32) + g[row, 1 - col, 1].astype(f32)).astype(bf16)
        b2.start()

    def step3(self, w):
        a, b = self.copies1(w)
        a2, b2 = self.copies2(w)
        g = self.parts[w]
        row, col = self.row, self.col
        part = g.shape[3] // 4
        a.wait_send()
        b2.wait_recv()
        a2.wait_recv()
        for z in range(4):
            rows = pl.ds(z * part, part)
            sums = []
            for k, near, far in ((0, self.ra[w].at[row], self.ra2[w]), (1, self.rb[w].at[col], self.rb2[w])):
                own = g.at[row, col, k]
                if part % 16:
                    tops = z * part // 16 * 16
                    high = -(-(z + 1) * part // 16) * 16
                    wide = [ref[tops:high].astype(f32) for ref in (own, near, far)]
                    low = z * part - tops
                    sums.append((wide[0] + wide[1] + wide[2])[low : low + part])
                else:
                    sums.append(own[rows].astype(f32) + near[rows].astype(f32) + far[rows].astype(f32))
            at = self.block(w, z)
            at[...] = jnp.concatenate(sums, axis=0).astype(bf16)
        for c in self.copies3(w):
            c.start()

    def step4(self, w, swap=True):
        for c in self.copies3(w):
            c.wait_recv()
        rz, part = self.rz[w], self.parts[w].shape[3] // 4
        whole = (self.block(w, self.f)[...].astype(f32) + rz[0].astype(f32)) + (
            rz[1].astype(f32) + rz[2].astype(f32)
        )
        self.total[w][0] = whole[:part]
        self.total[w][1] = whole[part:]
        if swap:
            self.copy4(w).start()

    def step5(self, w):
        self.copy4(w).wait_recv()

    def drain(self, w, swap=True):
        a, b = self.copies1(w)
        b.wait_send()
        for c in list(self.copies2(w)) + self.copies3(w) + ([self.copy4(w)] if swap else []):
            c.wait_send()


REDUCE, EXPAND, SPACE_OUT, SPACE_JOIN, MIX, TIME_OUT, TIME_JOIN, NARROW = range(8)
PARTS = ((384, 384), (96, 1536), (96, 384), (96, 1152), (96, 384), (96, 384), (96, 1152), (96, 128))


def backward_kernel(*refs):
    (frame_clip, patch_clip, padding, vec, sums) = refs[:5]
    stored = refs[5:18]
    act, gh, act_sib, gh_sib = refs[18:22]
    fulls, shards = refs[22:27], refs[27:32]
    (d_video, d_class, d_reduce, d_expand, d_so, d_sp, d_tm, d_to, d_tp, d_narrow) = refs[32:42]
    (parts, ra, rb, ra2, rb2, rz, total, rc, rsems, slots, slot_sems, act_v, gh_v, feed_sems, tbias, sbias, spare,
     gsm, wide, gat, gto, gtm, a2s, a2r, asend, arecv, cls, csend, crecv, bias_col, vt,
     n_f2, cot2, m_s2, gb2, n_s2, gjs2, o_t2, gat2, m_t2, gto2, n_t2, gjt2, xsend, xrecv,
     x_t, n_t, j_t, m_t, o_t, x_s, n_s, j_s, m_s, n_f, cot, gmid, gb, take_sems) = refs[42:]
    taken = (x_t, n_t, j_t, m_t, o_t, x_s, n_s, j_s, m_s, n_f, cot, gmid, gb)
    X_T, N_T, J_T, M_T, O_T, X_S, N_S, J_S, M_S, N_F, COT, GMID, GB = range(13)

    def take(k):
        return pltpu.make_async_copy(stored[k], taken[k], take_sems.at[k])

    for k in (COT, N_F):
        take(k).start()

    red = Reduce(parts, ra, rb, ra2, rb2, rz, total, rc, rsems)
    s, f, core, sib = red.s, red.f, red.core, red.sib
    red.greet()

    def half_of(ref, wide_half, which):
        return ref.at[:, pl.ds(pl.multiple_of(which * wide_half, 128), wide_half)]

    exchange = [
        (stored[COT], cot2), (stored[N_F], n_f2), (stored[M_S], m_s2), (half_of(stored[GB], 384, 1 - core), gb2),
        (stored[N_S], n_s2), (stored[O_T], o_t2), (stored[M_T], m_t2), (stored[N_T], n_t2),
    ]
    gjs = act_v.at[:, 0 : 3 * D]
    gjt = gh_v.at[0:TIME_ROWS, 0 : 3 * D]
    exchange += [
        (half_of(gjs, 1152, 1 - core), gjs2), (half_of(gat, 384, 1 - core), gat2),
        (half_of(gto, 384, 1 - core), gto2), (half_of(gjt, 1152, 1 - core), gjt2),
    ]
    GJS, GAT, GTO, GJT = 8, 9, 10, 11

    def trade(k):
        src, dst = exchange[k]
        return remote(src, dst, xsend.at[k], xrecv.at[k], (sib, f))

    loads_feed = []
    for k, (src, dst, at) in enumerate(
        ((act, act_v, 0), (act_sib, act_v, 2), (gh, gh_v, 0), (gh_sib, gh_v, 2))
    ):
        for half in range(2):
            lanes = slice((at + half) * D, (at + half + 1) * D)
            loads_feed.append(pltpu.make_async_copy(src.at[half], dst.at[:, lanes], feed_sems.at[2 * k + half]))
    for c in loads_feed:
        c.start()
    for k in (M_S, GB, J_S, X_S, GMID, N_S, O_T, M_T, J_T, N_T, X_T):
        take(k).start()
    for k in range(8):
        trade(k).start()
    pieces = []
    for w, count in ((4, 1), (3, 3), (2, 1), (1, 1), (0, 3)):
        pieces += squares(fulls, shards, w, count)
    loads = Loads(slots, slot_sems, pieces, f)
    for i in range(3):
        loads.start(i)
    time_bias(frame_clip, tbias)
    space_bias(patch_clip, padding, spare, sbias)

    first = jnp.where(f == 0, 1.0, 0.0)
    vt[...] = jnp.zeros_like(vt)
    counts = jnp.where(iota((16, SPACE_ROWS), 1) == CLASS, first, 1.0).astype(bf16)
    ones_s = jnp.ones((16, SPACE_ROWS), bf16)
    ones_t = jnp.ones((16, TIME_ROWS), bf16)
    vt[7:8] = jnp.sum(sums[0:8], axis=0, keepdims=True)
    vt[8:9] = jnp.sum(sums[8:16], axis=0, keepdims=True)
    take(COT).wait()
    vt[9:10] = dot(counts, cot[...])[0:1]

    for c in loads_feed[:4]:
        c.wait()
    trade(0).wait_recv()
    for y in range(2):
        grad = dot_tn(act_v[:, y * D : (y + 1) * D], cot[...]) + dot_tn(act_v[:, (2 + y) * D : (3 + y) * D], cot2[...])
        for x in range(2):
            for k in range(2):
                parts[REDUCE][y, x, k] = grad[x * 384 : (x + 1) * 384, k * 384 : (k + 1) * 384].astype(bf16)
    red.step1(REDUCE)
    for c in loads_feed[4:]:
        c.wait()
    take(N_F).wait()
    trade(1).wait_recv()

    def put(w, lanes, grad):
        for y in range(2):
            for x in range(2):
                for k in range(2):
                    start = ((y * 2 + x) * 2 + k) * 96
                    parts[w][y, x, k, :, lanes] = grad[start : start + 96].astype(bf16)

    for y in range(2):
        own, other = gh_v[:, y * D : (y + 1) * D], gh_v[:, (2 + y) * D : (3 + y) * D]
        grad = dot_tn(n_f[...], own) + dot_tn(n_f2[...], other)
        put(EXPAND, slice(y * D, (y + 1) * D), grad)
        ones = jnp.ones((SPACE_ROWS, 128), bf16)
        bias_col[y] = dot_tn(own, ones) + dot_tn(other, ones)
    red.step1(EXPAND)

    for k in (M_S, GB, J_S, X_S, GMID):
        take(k).wait()
    vt[6:7] = dot(ones_s, gb[...])[0:1]
    trade(2).wait_recv()
    trade(3).wait_recv()
    mine = half_of(gb, 384, core)
    put(SPACE_OUT, ALL, dot_tn(m_s[...], mine[...]) + dot_tn(m_s2[...], gb2[...]))
    red.step1(SPACE_OUT)
    gsm[...] = dot_nt(gb[...], loads.get(0)).astype(bf16)
    loads.start(3)
    attend_back(j_s, sbias, gsm, gjs, OWN, FRAME, 3)
    trade(GJS).start()
    red.step2(REDUCE)
    wide[...] = dot_nt(gjs[:, 0:D], loads.get(1))
    loads.start(4)
    wide[...] += dot_nt(gjs[:, D : 2 * D], loads.get(2))
    loads.start(5)
    wide[...] += dot_nt(gjs[:, 2 * D : 3 * D], loads.get(3))
    loads.start(6)
    gain = vec[4:5]

    def norm_back(source, gain, at, size, rows):
        scaled, scale = normed(source[rows].astype(f32))
        pulled = wide[rows]
        vt[at : at + 8] += jnp.sum((pulled * scaled).reshape(size // 8, 8, D), axis=0)
        vt[at + 8 : at + 16] += jnp.sum(pulled.reshape(size // 8, 8, D), axis=0)
        up = pulled * gain
        return scale * (
            up - jnp.mean(up, axis=-1, keepdims=True) - scaled * jnp.mean(up * scaled, axis=-1, keepdims=True)
        )

    def space_back(rows):
        back = norm_back(x_s, gain, 16, 32, rows)
        wide[rows] = back
        gsm[rows] = (gmid[rows] + back).astype(bf16)

    over_blocks(13, 32, space_back)
    a2s[...] = dot(from_tokens(), gsm[...]).astype(bf16).reshape(4, SLOT, D)

    def a_copy(k):
        z = lax.rem(f + k, 4)
        return remote(a2s.at[z], a2r.at[f], asend.at[k - 1], arecv.at[f], (s, z))

    for k in (1, 3, 2):
        a_copy(k).start()
    a2r[f] = a2s[f]
    cls[f] = jnp.broadcast_to(wide[CLASS : CLASS + 1] + wide[FRAME + CLASS : FRAME + CLASS + 1], (8, D))

    def c_copy(k):
        return remote(cls.at[f], cls.at[f], csend.at[k - 1], crecv.at[f], (s, lax.rem(f + k, 4)))

    for k in (1, 3, 2):
        c_copy(k).start()
    take(N_S).wait()
    trade(4).wait_recv()
    trade(GJS).wait_recv()
    mine = half_of(gjs, 1152, core)
    put(SPACE_JOIN, ALL, dot_tn(n_s[...], mine[...]) + dot_tn(n_s2[...], gjs2[...]))
    red.step1(SPACE_JOIN)
    red.step2(EXPAND)
    for k in (1, 3, 2):
        z = lax.rem(f + k, 4)
        with jax.named_scope("a_wait"):
            remote(a2s.at[z], a2r.at[z], asend.at[0], arecv.at[z], (s, z)).wait_recv()

    gat[...] = dot(to_patches(), a2r[...].reshape(4 * SLOT, D)).astype(bf16)
    trade(GAT).start()
    gto[...] = dot_nt(gat[...], loads.get(4)).astype(bf16)
    loads.start(7)
    trade(GTO).start()
    gtm[...] = dot_nt(gto[...], loads.get(5)).astype(bf16)
    loads.start(8)
    red.step2(SPACE_OUT)
    red.step3(REDUCE)
    for k in (O_T, M_T, J_T, N_T, X_T):
        take(k).wait()
    attend_back(j_t, tbias, gtm, gjt, 5, TIME_BLOCK, 6)
    trade(GJT).start()
    red.step2(SPACE_JOIN)
    trade(5).wait_recv()
    trade(GAT).wait_recv()
    mine = half_of(gat, 384, core)
    put(MIX, ALL, dot_tn(o_t[...], mine[...]) + dot_tn(o_t2[...], gat2[...]))
    red.step1(MIX)
    trade(6).wait_recv()
    trade(GTO).wait_recv()
    mine = half_of(gto, 384, core)
    put(TIME_OUT, ALL, dot_tn(m_t[...], mine[...]) + dot_tn(m_t2[...], gto2[...]))
    red.step1(TIME_OUT)
    trade(7).wait_recv()
    trade(GJT).wait_recv()
    mine = half_of(gjt, 1152, core)
    put(TIME_JOIN, ALL, dot_tn(n_t[...], mine[...]) + dot_tn(n_t2[...], gjt2[...]))
    red.step1(TIME_JOIN)
    red.step3(EXPAND)
    red.step3(SPACE_OUT)
    rows = pl.ds(0, TIME_ROWS)
    wide[rows] = dot_nt(gjt[:, 0:D], loads.get(6))
    wide[rows] += dot_nt(gjt[:, D : 2 * D], loads.get(7))
    wide[rows] += dot_nt(gjt[:, 2 * D : 3 * D], loads.get(8))
    gain = vec[0:1]

    def time_back(rows):
        back = norm_back(x_t, gain, 32, 80, rows)
        wide[rows] = gat[rows].astype(f32) + back

    over_blocks(5, 80, time_back)
    d_video[...] = wide[0 : HERE * FRAMES]
    vt[3:4] = dot(ones_t, gat[...])[0:1]
    vt[2:3] = dot(ones_t, gto[...])[0:1]
    for row, at in ((4, 16), (5, 24), (0, 32), (1, 40)):
        vt[row : row + 1] = jnp.sum(vt[at : at + 8], axis=0, keepdims=True)
    place_at = picks(iota((16, 128), 0) == iota((16, 128), 1))
    put(NARROW, ALL, dot_tn(vt[0:16].astype(bf16), place_at))
    lane = iota((24, 128), 1)
    for y in range(2):
        for x in range(2):
            pieces = []
            for z in range(4):
                piece = jnp.zeros((24, 128), f32)
                for k in range(4):
                    column = bias_col[y, pl.ds(x * 384 + z * 96 + k, 24, stride=4), :]
                    piece = jnp.where(lane == 10 + k, column, piece)
                pieces.append(piece)
            at = parts[NARROW].at[y, x, core]
            at[...] = (at[...].astype(f32) + jnp.concatenate(pieces, axis=0)).astype(bf16)
    red.step1(NARROW)

    def place_halves(w, out, half):
        red.step5(w)
        mine = half_of(out, half, core)
        mine[...] = total[w][core]
        other = half_of(out, half, 1 - core)
        other[...] = rc[w][...]

    red.step2(MIX)
    red.step2(TIME_OUT)
    red.step3(SPACE_JOIN)
    red.step2(TIME_JOIN)
    red.step2(NARROW)
    for k in (1, 3, 2):
        z = lax.rem(f + k, 4)
        remote(cls.at[f], cls.at[z], csend.at[0], crecv.at[z], (s, z)).wait_recv()
    d_class[...] = gmid[CLASS : CLASS + 1] + ((cls[0] + cls[1]) + (cls[2] + cls[3]))[0:1]
    red.step4(REDUCE, False)
    d_reduce[:, 0:384] = total[REDUCE][0]
    d_reduce[:, 384:768] = total[REDUCE][1]
    red.step4(EXPAND)
    red.step3(MIX)
    red.step3(TIME_OUT)
    red.step4(SPACE_OUT)
    red.step5(EXPAND)
    for y in range(2):
        for x in range(2):
            lanes = slice((y * 2 + x) * 384, (y * 2 + x + 1) * 384)
            for c, piece in ((core, total[EXPAND][core]), (1 - core, rc[EXPAND][...])):
                start = pl.multiple_of(((y * 2 + x) * 2 + c) * 384, 128)
                d_expand[:, pl.ds(start, 384)] = piece[:, lanes]
    red.step3(TIME_JOIN)
    red.step3(NARROW)
    red.step4(SPACE_JOIN)
    place_halves(SPACE_OUT, d_so, 384)
    red.step4(MIX)
    red.step4(TIME_OUT)
    place_halves(SPACE_JOIN, d_sp, 1152)
    place_halves(MIX, d_tm, 384)
    place_halves(TIME_OUT, d_to, 384)
    red.step4(TIME_JOIN)
    red.step4(NARROW)
    place_halves(TIME_JOIN, d_tp, 1152)
    red.step5(NARROW)
    d_narrow[...] = total[NARROW][core] + rc[NARROW][...]
    for w in range(8):
        red.drain(w, w != REDUCE)
    for k in range(12):
        trade(k).wait_send()
    for k in (1, 2, 3):
        a_copy(k).wait_send()
        c_copy(k).wait_send()


def backward(frame_clip, patch_clip, padding, vec, saved, fulls, shards):
    (x_t, n_t, j_t, m_t, o_t, x_s, n_s, j_s, m_s, n_f, cot, act, gh, act_sib, gh_sib, gmid, gb, sums) = saved
    vm = pl.BlockSpec(memory_space=pltpu.VMEM)
    sm = pl.BlockSpec(memory_space=pltpu.SMEM)
    hbm = pl.BlockSpec(memory_space=pl.ANY)
    sds = jax.ShapeDtypeStruct
    sem = pltpu.SemaphoreType.DMA
    v = pltpu.VMEM
    t, p = TIME_ROWS, SPACE_ROWS
    return pl.pallas_call(
        backward_kernel,
        out_shape=[
            sds((HERE * FRAMES, D), f32), sds((1, D), f32), sds((96, D), f32), sds((24, 4 * D), f32), sds((24, D), f32),
            sds((24, 3 * D), f32), sds((24, D), f32), sds((24, D), f32), sds((24, 3 * D), f32), sds((24, 128), f32),
        ],
        in_specs=[sm] + [vm] * 4 + [hbm] * 27,
        out_specs=[vm] * 10,
        scratch_shapes=[
            [v((2, 2, 2, r, c), bf16) for r, c in PARTS],
            [v((2, r, c), bf16) for r, c in PARTS],
            [v((2, r, c), bf16) for r, c in PARTS],
            [v((r, c), bf16) for r, c in PARTS],
            [v((r, c), bf16) for r, c in PARTS],
            [v((3, r // 2, c), bf16) for r, c in PARTS],
            [v((2, r // 4, c), f32) for r, c in PARTS],
            [v((r // 4, c), f32) for r, c in PARTS],
            sem((8, 16)),
            v((3, D, D), bf16),
            sem((3, 8)),
            v((p, 4 * D), bf16),
            v((p, 4 * D), bf16),
            sem((8,)),
            v((8, 2 * TIME_BLOCK), f32),
            v((FRAME, 2 * FRAME), f32),
            v((16, 512), jnp.int32),
            v((p, D), bf16),
            v((p, D), f32),
            v((t, D), bf16),
            v((t, D), bf16),
            v((t, D), bf16),
            v((4, SLOT, D), bf16),
            v((4, SLOT, D), bf16),
            sem((3,)),
            sem((4,)),
            v((4, 8, D), f32),
            sem((3,)),
            sem((4,)),
            v((2, D, 128), f32),
            v((48, D), f32),
            v((p, D), bf16),
            v((p, D), bf16),
            v((p, D), bf16),
            v((p, 384), bf16),
            v((p, D), bf16),
            v((p, 1152), bf16),
            v((t, D), bf16),
            v((t, 384), bf16),
            v((t, D), bf16),
            v((t, 384), bf16),
            v((t, D), bf16),
            v((t, 1152), bf16),
            sem((12,)),
            sem((12,)),
            v((t, D), bf16),
            v((t, D), bf16),
            v((t, 3 * D), bf16),
            v((t, D), bf16),
            v((t, D), bf16),
            v((p, D), bf16),
            v((p, D), bf16),
            v((p, 3 * D), bf16),
            v((p, D), bf16),
            v((p, D), bf16),
            v((p, D), bf16),
            v((p, D), f32),
            v((p, D), bf16),
            sem((13,)),
        ],
        compiler_params=pltpu.CompilerParams(
            collective_id=2, has_side_effects=True, vmem_limit_bytes=63 << 20
        ),
        name="backward",
    )(
        frame_clip, patch_clip, padding, vec, sums, x_t, n_t, j_t, m_t, o_t, x_s, n_s, j_s, m_s, n_f, cot, gmid, gb,
        act, gh, act_sib, gh_sib, *fulls[:5], *shards[:5]
    )


def settle(share):
    count = lax.axis_size("seq")
    if count == 8:
        return share
    more = count // 8
    groups = [[low + 8 * high for high in range(more)] for low in range(8)]
    share = lax.psum_scatter(share, "seq", scatter_dimension=0, tiled=True, axis_index_groups=groups)
    moves = [
        ((high * 8 + low) * 4 + f, (low * 4 + f) * more + high)
        for high in range(more)
        for low in range(8)
        for f in range(4)
    ]
    return lax.ppermute(share, ("seq", "ft"), moves)


def shards(
    video,
    class_token,
    frame_clip,
    patch_clip,
    padding,
    time_gain,
    time_shift,
    time_project,
    time_output,
    time_output_bias,
    time_mixer,
    time_mixer_bias,
    space_gain,
    space_shift,
    space_project,
    space_output,
    space_output_bias,
    feed_gain,
    feed_shift,
    feed_expand,
    feed_expand_bias,
    feed_reduce,
    feed_reduce_bias,
    grad_output,
    grad_class_out,
):
    vectors = jnp.zeros((16, D // 4), bf16)
    row = lax.broadcasted_iota(jnp.int32, vectors.shape, 0)
    for i, item in enumerate(
        (
            time_gain,
            time_shift,
            time_output_bias,
            time_mixer_bias,
            space_gain,
            space_shift,
            space_output_bias,
            feed_gain,
            feed_shift,
            feed_reduce_bias,
        )
    ):
        vectors = jnp.where(row == i, item[None, :], vectors)
    expand_bias = jnp.broadcast_to(feed_expand_bias[None, :], (16, D))
    weights = (time_project, time_output, time_mixer, space_project, space_output, feed_expand, feed_reduce)
    cotangent = jnp.swapaxes(grad_output[0], 0, 1)
    done = forward(
        jnp.swapaxes(video[0], 0, 1).reshape(HERE * FRAMES, D), class_token, frame_clip, patch_clip, padding, vectors, expand_bias, cotangent, grad_class_out, weights
    )
    output, class_output = jnp.swapaxes(done[0], 0, 1)[None], done[1]
    grads = backward(frame_clip, patch_clip, padding, done[27], done[9:27], done[2:9], weights)
    rows, grad_class = grads[:2]
    grad_video = jnp.swapaxes(rows.reshape(HERE, FRAMES, D), 0, 1)[None]
    d_reduce, d_expand, d_so, d_sp, d_tm, d_to, d_tp, d_narrow = [settle(g) for g in grads[2:]]
    narrow = [d_narrow[:, i] for i in range(10)]
    return (
        output,
        class_output,
        grad_video,
        grad_class,
        narrow[0],
        narrow[1],
        d_tp,
        d_to,
        narrow[2],
        d_tm,
        narrow[3],
        narrow[4],
        narrow[5],
        d_sp,
        d_so,
        narrow[6],
        narrow[7],
        narrow[8],
        d_expand,
        d_narrow[:, 10:14].reshape(-1),
        d_reduce,
        narrow[9],
    )


def solution(mesh):
    in_specs = (
        P("seq", None, "ft", None),
        P("seq", None),
        P("seq", None),
        P("seq", None),
        P("seq", None),
        P("ft"),
        P("ft"),
        P("ft", None),
        P("ft", None),
        P("ft"),
        P("ft", None),
        P("ft"),
        P("ft"),
        P("ft"),
        P("ft", None),
        P("ft", None),
        P("ft"),
        P("ft"),
        P("ft"),
        P("ft", None),
        P("ft"),
        P("ft", None),
        P("ft"),
        P("seq", "ft", None, None),
        P("seq", None),
    )
    out_specs = (
        P("seq", "ft", None, None),
        P("seq", None),
        P("seq", None, "ft", None),
        P("seq", None),
        P(("seq", "ft")),
        P(("seq", "ft")),
        P(("seq", "ft"), None),
        P(("seq", "ft"), None),
        P(("seq", "ft")),
        P(("seq", "ft"), None),
        P(("seq", "ft")),
        P(("seq", "ft")),
        P(("seq", "ft")),
        P(("seq", "ft"), None),
        P(("seq", "ft"), None),
        P(("seq", "ft")),
        P(("seq", "ft")),
        P(("seq", "ft")),
        P(("seq", "ft"), None),
        P(("seq", "ft")),
        P(("seq", "ft"), None),
        P(("seq", "ft")),
    )
    return jax.shard_map(shards, mesh=mesh, in_specs=in_specs, out_specs=out_specs, check_vma=False)
```

```python
import jax
import jax.numpy as jnp
from jax import lax
from jax.experimental import pallas as pl
from jax.experimental.pallas import tpu as pltpu
from jax.sharding import PartitionSpec as P

MESH = pl.DeviceIdType.MESH
bf16 = jnp.bfloat16
f32 = jnp.float32
D = 768
FRAMES = 8
HERE = 49
OWN = 2
PATCHES = 196
TIME_ROWS = 400
TIME_BLOCK = 80
FRAME = 208
CLASS = 196
SPACE_ROWS = OWN * FRAME
SLOT = 112
EPSILON = 1e-06
UNITS = 7


def iota(shape, axis):
    return lax.broadcasted_iota(jnp.int32, shape, axis)


def dot(left, right):
    return jnp.dot(left, right, preferred_element_type=f32)


def dot_nt(left, right):
    return lax.dot_general(left, right, (((1,), (1,)), ((), ())), preferred_element_type=f32)


def dot_tn(left, right):
    return lax.dot_general(left, right, (((0,), (0,)), ((), ())), preferred_element_type=f32)


def picks(condition):
    return jnp.where(condition, 1.0, 0.0).astype(bf16)


def between(r):
    return ((r & 7) >> 1) * SLOT + (r & 1) * HERE + (r >> 3)


def to_patches():
    r, c = iota((TIME_ROWS, 4 * SLOT), 0), iota((TIME_ROWS, 4 * SLOT), 1)
    return picks((c == between(r)) & (r < FRAMES * HERE))


def to_frames():
    c, r = iota((4 * SLOT, TIME_ROWS), 0), iota((4 * SLOT, TIME_ROWS), 1)
    return picks((c == between(r)) & (r < FRAMES * HERE))


def source_of(token, frame):
    late = (token >= HERE).astype(jnp.int32) + (token >= 2 * HERE) + (token >= 3 * HERE)
    return token + late * (SLOT - HERE) + frame * HERE


def to_tokens():
    r, c = iota((SPACE_ROWS, 4 * SLOT), 0), iota((SPACE_ROWS, 4 * SLOT), 1)
    frame = (r >= FRAME).astype(jnp.int32)
    token = r - frame * FRAME
    return picks((c == source_of(token, frame)) & (token < PATCHES))


def from_tokens():
    c, r = iota((4 * SLOT, SPACE_ROWS), 0), iota((4 * SLOT, SPACE_ROWS), 1)
    frame = (r >= FRAME).astype(jnp.int32)
    token = r - frame * FRAME
    return picks((c == source_of(token, frame)) & (token < PATCHES))


def from_twos():
    r, c = iota((SPACE_ROWS, OWN * PATCHES), 0), iota((SPACE_ROWS, OWN * PATCHES), 1)
    frame = (r >= FRAME).astype(jnp.int32)
    token = r - frame * FRAME
    return picks((c == 2 * token + frame) & (token < PATCHES))


def to_twos():
    r, c = iota((OWN * PATCHES, SPACE_ROWS), 0), iota((OWN * PATCHES, SPACE_ROWS), 1)
    return picks(c == (r >> 1) + (r & 1) * FRAME)


def normed(rows):
    centred = rows - jnp.mean(rows, axis=-1, keepdims=True)
    scale = lax.rsqrt(jnp.mean(centred * centred, axis=-1, keepdims=True) + EPSILON)
    return centred * scale, scale


def over_blocks(count, size, step):
    def body(i, carry):
        step(pl.ds(pl.multiple_of(i * size, 16), size))
        return carry

    lax.fori_loop(0, count, body, 0, unroll=True)


def halves(scale):
    lane = iota((1, 128), 1)
    first = jnp.where(lane < 64, scale, 0.0).astype(bf16)
    second = jnp.where(lane < 64, 0.0, scale).astype(bf16)
    return first, second


def chances(scores):
    power = jnp.exp(scores - jnp.max(scores, axis=0, keepdims=True))
    return power * (1.0 / jnp.sum(power, axis=0, keepdims=True))


def diagonal(heads):
    shape = (TIME_BLOCK // 8, 8, heads * TIME_BLOCK)
    lane = iota(shape, 2)
    lane = jnp.where(lane < TIME_BLOCK, lane, lane - TIME_BLOCK)
    return iota(shape, 0) == (lane >> 3)


def gathered(scores, where):
    return jnp.sum(jnp.where(where, scores.reshape(where.shape), 0.0), axis=0)


def scattered(scores, where):
    wide = jnp.where(where, jnp.broadcast_to(scores[None], where.shape), 0.0)
    return wide.reshape(TIME_BLOCK, where.shape[2]).astype(bf16)


def pair(i, j, size):
    rows = pl.ds(pl.multiple_of(i * size, 16), size)
    return rows, [pl.ds(pl.multiple_of(k * D + j * 128, 128), 128) for k in range(3)]


def both(values, first, second):
    return jnp.concatenate([values * first, values * second], axis=0)


def unite(values, size):
    return jnp.where(iota((size, 128), 1) < 64, values[:size], values[size:])


def attend_time(joined, bias, mixed, blocks, size, unroll):
    first8, second8 = halves(0.125)
    where = diagonal(1)

    def body(n, carry):
        rows, (ql, kl, vl) = pair(n // 6, lax.rem(n, 6), size)
        query, keys, values = joined[rows, ql], joined[rows, kl], joined[rows, vl]
        out = []
        for part in (query * first8, query * second8):
            scores = gathered(dot_nt(keys, part), where) + bias[:, 0:size]
            out.append(dot_tn(scattered(chances(scores), where), values))
        mixed[rows, ql] = jnp.where(iota((size, 128), 1) < 64, out[0], out[1]).astype(bf16)
        return carry

    lax.fori_loop(0, blocks * 6, body, 0, unroll=unroll)


def attend_space(joined, bias, mixed, blocks, size, unroll):
    first8, second8 = halves(0.125)

    def body(n, carry):
        rows, (ql, kl, vl) = pair(n // 6, lax.rem(n, 6), size)
        query, keys, values = joined[rows, ql], joined[rows, kl], joined[rows, vl]
        chance = chances(dot_nt(keys, both(query, first8, second8)) + bias[...]).astype(bf16)
        mixed[rows, ql] = unite(dot_tn(chance, values), size).astype(bf16)
        return carry

    lax.fori_loop(0, blocks * 6, body, 0, unroll=unroll)


def attend_back(joined, bias, grad_mixed, grad_joined, blocks, size, unroll):
    first8, second8 = halves(0.125)
    first, second = halves(1.0)
    where = diagonal(2) if size == TIME_BLOCK else None

    def body(n, carry):
        rows, (ql, kl, vl) = pair(n // 6, lax.rem(n, 6), size)
        query, keys, values = joined[rows, ql], joined[rows, kl], joined[rows, vl]
        queries, grads = both(query, first8, second8), both(grad_mixed[rows, ql], first, second)
        scores, pull = dot_nt(keys, queries), dot_nt(values, grads)
        if where is not None:
            scores, pull = gathered(scores, where), gathered(pull, where)
        chance = chances(scores + bias[...])
        back = chance * (pull - jnp.sum(chance * pull, axis=0, keepdims=True))
        if where is None:
            chance, back = chance.astype(bf16), back.astype(bf16)
        else:
            chance, back = scattered(chance, where), scattered(back, where)
        grad_joined[rows, ql] = (unite(dot_tn(back, keys), size) * 0.125).astype(bf16)
        grad_joined[rows, kl] = dot(back, queries).astype(bf16)
        grad_joined[rows, vl] = dot(chance, grads).astype(bf16)
        return carry

    lax.fori_loop(0, blocks * 6, body, 0, unroll=unroll)


def time_bias(frame_clip, bias):
    shape = (8, 2 * TIME_BLOCK)
    r, c = iota(shape, 0), iota(shape, 1)
    clip_r, clip_c = jnp.zeros(shape, jnp.int32), jnp.zeros(shape, jnp.int32)
    for f in range(FRAMES):
        clip_r = jnp.where(r == f, frame_clip[0, f], clip_r)
        clip_c = jnp.where((c & 7) == f, frame_clip[0, f], clip_c)
    bias[...] = jnp.where(clip_r == clip_c, 0.0, -1e30)


def space_bias(patch_clip, padding, spare, bias):
    shape = (FRAME, FRAME)
    r, c = iota(shape, 0), iota(shape, 1)
    spare[...] = jnp.full(spare.shape, -1, jnp.int32)
    for half in range(2):
        spare[0:1, half * FRAME : half * FRAME + PATCHES] = patch_clip[...]
    spare[8:9, 0:PATCHES] = padding[...]
    clip = jnp.broadcast_to(spare[0:1, 0:FRAME], shape).astype(f32)
    shut = jnp.broadcast_to(spare[8:9, 0:FRAME], shape).astype(f32)
    own = jnp.sum(jnp.where(r == c, clip, 0.0), axis=1, keepdims=True)
    closed = jnp.sum(jnp.where(r == c, shut, 0.0), axis=1, keepdims=True)
    shape = (FRAME, 2 * FRAME)
    r, c = iota(shape, 0), iota(shape, 1)
    clip = jnp.broadcast_to(spare[0:1, 0 : 2 * FRAME], shape).astype(f32)
    of_class = (c == CLASS) | (c == FRAME + CLASS)
    opened = (r == CLASS) | ((closed == 0.0) & ((clip == own) | of_class))
    bias[...] = jnp.where(opened, 0.0, -1e30)


def place():
    s = lax.axis_index("seq")
    f = lax.axis_index("ft")
    core = lax.rem(s, 2)
    col = lax.rem(s // 2, 2)
    row = lax.rem(s // 4, 2)
    return s, f, core, col, row


def remote(src, dst, send, recv, target):
    return pltpu.make_async_remote_copy(
        src_ref=src, dst_ref=dst, send_sem=send, recv_sem=recv, device_id=target, device_id_type=MESH
    )


class Spread:
    def __init__(self, shards, fulls, send, recv):
        self.shards, self.fulls, self.send, self.recv = shards, fulls, send, recv
        self.s, self.f, self.core, self.col, self.row = place()
        s = self.s
        self.sib = s + 1 - 2 * self.core
        dx, dy = 2 - 4 * self.col, 4 - 8 * self.row
        self.plane = ((s + dx, 1, 0), (s + dy, 0, 1), (s + dx + dy, 1, 1))
        upper = self.f // 2
        near = self.f + upper * (3 - 2 * self.f)
        self.order = [upper * 3 + (1 - 2 * upper) * v for v in (1 - near, 2, 3)]

    def greet(self):
        bar = pltpu.get_barrier_semaphore()
        targets = [(t, self.f) for t in (self.sib,) + tuple(p[0] for p in self.plane)]
        targets += [(self.s, lax.rem(self.f + j, 4)) for j in (1, 2, 3)]
        for t in targets:
            pl.semaphore_signal(bar, inc=1, device_id=t, device_id_type=MESH)
        pl.semaphore_wait(bar, len(targets))

    def cut(self, w, base, row, col):
        rows, wide = self.shards[w].shape
        start = base + self.core * (rows // 2) + row * (rows // 4)
        return (
            pl.ds(pl.multiple_of(start, 16), rows // 4),
            pl.ds(pl.multiple_of(col * (wide // 2), 128), wide // 2),
        )

    def along(self, w, k):
        z = lax.rem(self.f + k, 4)
        rows = self.shards[w].shape[0]
        src = self.shards[w].at[self.cut(w, 0, self.row, self.col)]
        dst = self.fulls[w].at[self.cut(w, self.f * rows, self.row, self.col)]
        return remote(src, dst, self.send.at[w, k - 1], self.recv.at[w, 0, self.f], (self.s, z))

    def start(self, w):
        for k in (1, 3, 2):
            self.along(w, k).start()

    def over(self, w, z, i, mine=True):
        target, dx, dy = self.plane[i]
        rows = self.shards[w].shape[0]
        row, col = (self.row, self.col) if mine else (self.row + dy - 2 * dy * self.row, self.col + dx - 2 * dx * self.col)
        ref = self.fulls[w].at[self.cut(w, z * rows, row, col)]
        return remote(ref, ref, self.send.at[w, 3 + 4 * i + z], self.recv.at[w, 1 + i, z], (target, self.f))

    def across(self, w, z, mine=True):
        rows = self.shards[w].shape[0]
        core = self.core if mine else 1 - self.core
        ref = self.fulls[w].at[pl.ds(pl.multiple_of(z * rows + core * (rows // 2), 16), rows // 2), :]
        return remote(ref, ref, self.send.at[w, 15 + z], self.recv.at[w, 4, z], (self.sib, self.f))

    def fan(self, w, nearest=(0, 1, 2)):
        rows = self.shards[w].shape[0]
        for t in nearest:
            z = self.order[t]
            ref = self.fulls[w].at[self.cut(w, z * rows, self.row, self.col)]
            remote(ref, ref, self.send.at[w, 0], self.recv.at[w, 0, z], (self.s, z)).wait_recv()
            for i in (2, 0, 1):
                self.over(w, z, i).start()

    def lend(self, w):
        for z in self.order:
            for i in range(3):
                self.over(w, z, i, False).wait_recv()
            self.across(w, z).start()

    def finish(self, w):
        for z in self.order:
            self.across(w, z, False).wait_recv()


    def quarter(self, w, base, own=True):
        rows = self.shards[w].shape[0]
        half = lax.rem(self.col + self.row, 2)
        which = 2 * half + self.core if own else 2 * (1 - half) + self.core
        return pl.ds(pl.multiple_of(base + which * (rows // 4), 16), rows // 4)

    def hop(self, w, z, step, src=None):
        dst = self.fulls[w].at[self.quarter(w, z * self.shards[w].shape[0])]
        side = 0 if step == 1 else 1
        src = dst if src is None else src
        return remote(src, dst, self.send.at[w, 4 * side + z], self.recv.at[w, 0, z], (self.s, self.f + step))

    def beside(self, w, z, i, own=True):
        wide = self.shards[w].shape[1]
        rows = self.quarter(w, z * self.shards[w].shape[0], own)
        ref = self.fulls[w].at[rows, i * (wide // 2) : (i + 1) * (wide // 2)]
        return remote(ref, ref, self.send.at[w, 8 + 4 * i + z], self.recv.at[w, 1 + i, z], (self.plane[i][0], self.f))

    def cross(self, w, z, own=True):
        ref = self.fulls[w].at[self.quarter(w, z * self.shards[w].shape[0], own)]
        i = 0 if own else 1
        return remote(ref, ref, self.send.at[w, 16 + 4 * i + z], self.recv.at[w, 3 + i, z], (self.sib, self.f))

    def off(self, w):
        src = self.shards[w].at[self.quarter(w, 0)]

        @pl.when(self.f < 3)
        def _():
            self.hop(w, self.f, 1, src).start()

        @pl.when(self.f > 0)
        def _():
            self.hop(w, self.f, -1, src).start()

    def onward(self, w, t, act):
        z = self.order[t]

        @pl.when((z < self.f) & (self.f < 3))
        def _():
            act(self.hop(w, z, 1))

        @pl.when((z > self.f) & (self.f > 0))
        def _():
            act(self.hop(w, z, -1))

    def relay(self, w, t):
        z = self.order[t]
        self.hop(w, z, 1).wait_recv()
        self.onward(w, t, lambda copy: copy.start())
        self.beside(w, z, 0).start()
        self.beside(w, z, 1).start()
        self.cross(w, z).start()

    def pass_on(self, w, t):
        z = self.order[t]
        for i in range(2):
            self.beside(w, z, i, False).wait_recv()
        self.cross(w, z, False).start()

    def complete(self, w):
        for z in self.order:
            self.cross(w, z).wait_recv()
            self.cross(w, z, False).wait_recv()

    def empty(self, w):
        src = self.shards[w].at[self.quarter(w, 0)]

        @pl.when(self.f < 3)
        def _():
            self.hop(w, self.f, 1, src).wait_send()

        @pl.when(self.f > 0)
        def _():
            self.hop(w, self.f, -1, src).wait_send()

        for t in range(3):
            z = self.order[t]
            self.onward(w, t, lambda copy: copy.wait_send())
            self.beside(w, z, 0).wait_send()
            self.beside(w, z, 1).wait_send()
            self.cross(w, z).wait_send()
            self.cross(w, z, False).wait_send()

    def drain(self, w):
        for k in (1, 2, 3):
            self.along(w, k).wait_send()
        for z in self.order:
            for i in range(3):
                self.over(w, z, i).wait_send()
            self.across(w, z).wait_send()


class Loads:
    def __init__(self, slots, sems, pieces, f):
        self.slots, self.sems, self.pieces, self.f = slots, sems, pieces, f

    def copies(self, i):
        n = i % self.slots.shape[0]
        full, shard, what, spot = self.pieces[i]
        slot = self.slots.at[n]
        if what == "columns":
            lanes = slice(spot * D, (spot + 1) * D)
            out = [(shard.at[:, lanes], slot.at[pl.ds(pl.multiple_of(self.f * 192, 16), 192)], None)]
            for k in (1, 2, 3):
                rows = pl.ds(pl.multiple_of(lax.rem(self.f + k, 4) * 192, 16), 192)
                out.append((full.at[rows, lanes], slot.at[rows], None))
        elif what == "wide":
            core, high = spot
            out = []
            for x in range(2):
                start = pl.multiple_of(((high * 2 + x) * 2 + core) * 384, 128)
                lanes, at = pl.ds(start, 384), slice(x * 384, (x + 1) * 384)
                out.append((shard.at[:, lanes], slot.at[pl.ds(pl.multiple_of(self.f * 192, 16), 192), at], None))
                for k in (1, 2, 3):
                    rows = pl.ds(pl.multiple_of(lax.rem(self.f + k, 4) * 192, 16), 192)
                    out.append((full.at[rows, lanes], slot.at[rows, at], None))
        else:
            core, high = spot
            out = []
            for x in range(2):
                z = high * 2 + x
                at = slot.at[x * 384 : (x + 1) * 384]
                here = shard.at[pl.ds(pl.multiple_of(core * 384, 16), 384)]
                there = full.at[pl.ds(pl.multiple_of(z * 768 + core * 384, 16), 384)]
                out += [(here, at, self.f == z), (there, at, self.f != z)]
        return [
            (pltpu.make_async_copy(src, dst, self.sems.at[n, k]), when) for k, (src, dst, when) in enumerate(out)
        ]

    def each(self, i, act):
        for copy, when in self.copies(i):
            if when is None:
                act(copy)
            else:
                pl.when(when)(lambda copy=copy: act(copy))

    def start(self, i):
        self.each(i, lambda copy: copy.start())

    def get(self, i):
        self.each(i, lambda copy: copy.wait())
        return self.slots[i % self.slots.shape[0]]


ALL = slice(None)


def squares(fulls, shards, w, count):
    return [(fulls[w], shards[w], "columns", i) for i in range(count)]


def forward_kernel(*refs):
    (video, class_token, frame_clip, patch_clip, padding, vectors, expand_bias, grad_output, grad_class_out) = refs[:9]
    shards = refs[9:16]
    outs = refs[16:44]
    (output, class_output) = outs[:2]
    fulls = outs[2:9]
    saved_out = outs[9:20] + outs[20:22] + outs[24:26]
    act_sib, gh_sib, sums, small_out = outs[22], outs[23], outs[26], outs[27]
    (send, recv, vec, vec32, vsend, vrecv, slots, slot_sems, a2s, a2r, asend, arecv, tbias, sbias, spare,
     rows_f, acc, acc2, hid, gact, cls, csend, crecv, psend, precv, act_go, gh_go, vec_go,
     x_t, n_t, j_t, m_t, o_t, x_s, n_s, j_s, m_s, n_f, cot, act, gh, gmid, gb, save_sems) = refs[44:]
    made = (x_t, n_t, j_t, m_t, o_t, x_s, n_s, j_s, m_s, n_f, cot, act, gh, gmid, gb)
    X_T, N_T, J_T, M_T, O_T, X_S, N_S, J_S, M_S, N_F, COT, ACT, GH, GMID, GB = range(15)

    def save(k):
        return pltpu.make_async_copy(made[k], saved_out[k], save_sems.at[k])


    net = Spread(shards, fulls, send, recv)
    s, f, core = net.s, net.f, net.core
    net.greet()

    def vec_copy(k):
        return remote(vec_go, vec.at[f], vsend.at[k - 1], vrecv.at[f], (s, lax.rem(f + k, 4)))

    vec_go[0:16, 0:192] = vectors[...]
    vec_go[0:16, 192:D] = jnp.zeros((16, D - 192), bf16)
    vec_go[16:32] = expand_bias[...]
    for k in (1, 3, 2):
        vec_copy(k).start()
    net.start(0)
    vec[f] = vec_go[...]

    x_t[384:TIME_ROWS] = jnp.zeros((TIME_ROWS - 384, D), bf16)
    x_t[0 : HERE * FRAMES] = video[...]
    save(X_T).start()
    time_bias(frame_clip, tbias)
    for k in (1, 3, 2):
        z = lax.rem(f + k, 4)
        remote(vec_go, vec.at[z], vsend.at[0], vrecv.at[z], (s, z)).wait_recv()
    net.fan(0, (0,))
    small = jnp.zeros((16, D), f32)
    for z in range(4):
        r, c = iota((192, D), 0), iota((192, D), 1) - z * 192
        small += dot(vec[z, 0:16, 0:192], picks(c == r))
        vec32[1 + z] = vec[z, 16:32].astype(f32)
    vec32[0] = small
    small_out[...] = small
    net.fan(0, (1,))

    def vector(i):
        return vec32[0, i : i + 1, :]

    gain, shift = vector(0), vector(1)

    def norm_time(rows):
        scaled, unused = normed(x_t[rows].astype(f32))
        n_t[rows] = (scaled * gain + shift).astype(bf16)

    over_blocks(5, 80, norm_time)
    save(N_T).start()
    net.start(1)
    net.start(2)
    net.fan(0, (2,))
    net.off(3)
    net.start(4)
    net.off(5)

    cot[...] = dot(from_twos(), grad_output[...].reshape(OWN * PATCHES, D)).astype(bf16)
    at_class = iota((16, D), 0) == CLASS - 192
    tail = jnp.where(at_class, grad_class_out[...].astype(f32), cot[192:FRAME].astype(f32))
    cot[192:FRAME] = tail.astype(bf16)
    save(COT).start()
    space_bias(patch_clip, padding, spare, sbias)

    pieces = []
    for w, count in ((0, 3), (1, 1), (2, 1), (3, 3), (4, 1)):
        pieces += squares(fulls, shards, w, count)
    for c, high in ((1 - core, 0), (1 - core, 1), (core, 0), (core, 1)):
        pieces += [(fulls[5], shards[5], "wide", (c, high)), (fulls[6], shards[6], "tall", (c, high))]
    loads = Loads(slots, slot_sems, pieces, f)

    net.lend(0)
    net.fan(1)
    net.fan(2)
    net.relay(3, 0)
    net.finish(0)
    for i in range(3):
        loads.start(i)
    for i in range(3):
        j_t[:, i * D : (i + 1) * D] = dot(n_t[...], loads.get(i)).astype(bf16)
    save(J_T).start()
    net.relay(3, 1)
    attend_time(j_t, tbias, m_t, 5, TIME_BLOCK, 6)
    net.lend(1)
    net.lend(2)
    net.relay(3, 2)
    net.finish(1)
    loads.start(3)
    net.finish(2)
    loads.start(4)
    net.relay(5, 0)
    o_t[...] = (dot(m_t[...], loads.get(3)) + vector(2)).astype(bf16)
    save(M_T).start()
    save(O_T).start()
    after = (x_t[...].astype(f32) + (dot(o_t[...], loads.get(4)) + vector(3))).astype(bf16)
    a2s[...] = dot(to_frames(), after).astype(bf16).reshape(4, SLOT, D)

    def a_copy(k):
        z = lax.rem(f + k, 4)
        return remote(a2s.at[z], a2r.at[f], asend.at[k - 1], arecv.at[f], (s, z))

    for k in (1, 3, 2):
        a_copy(k).start()
    net.off(6)
    a2r[f] = a2s[f]
    net.fan(4)
    for i in range(3):
        net.pass_on(3, i)
    net.complete(3)
    for i in range(5, 8):
        loads.start(i)
    net.relay(5, 1)
    net.lend(4)
    net.finish(4)
    for k in (1, 3, 2):
        z = lax.rem(f + k, 4)
        with jax.named_scope("a_wait"):
            remote(a2s.at[z], a2r.at[z], asend.at[0], arecv.at[z], (s, z)).wait_recv()
    net.relay(6, 0)

    spread_rows = dot(to_tokens(), a2r[...].reshape(4 * SLOT, D))
    r = iota((SPACE_ROWS, D), 0)
    is_class = (r == CLASS) | (r == FRAME + CLASS)
    x_s[...] = jnp.where(is_class, class_token[...].astype(f32), spread_rows).astype(bf16)
    gain, shift = vector(4), vector(5)

    def norm_space(rows):
        scaled, unused = normed(x_s[rows].astype(f32))
        n_s[rows] = (scaled * gain + shift).astype(bf16)

    over_blocks(13, 32, norm_space)
    save(X_S).start()
    save(N_S).start()
    for i in range(3):
        j_s[:, i * D : (i + 1) * D] = dot(n_s[...], loads.get(5 + i)).astype(bf16)
    save(J_S).start()
    loads.start(8)
    net.relay(5, 2)
    attend_space(j_s, sbias, m_s, OWN, FRAME, 6)
    net.relay(6, 1)
    rows_f[...] = dot(m_s[...], loads.get(8)) + vector(6)
    save(M_S).start()
    token = class_token[...].astype(f32)
    cls[f] = jnp.broadcast_to(
        rows_f[CLASS : CLASS + 1] + rows_f[FRAME + CLASS : FRAME + CLASS + 1], (8, D)
    )

    def c_copy(k):
        return remote(cls.at[f], cls.at[f], csend.at[k - 1], crecv.at[f], (s, lax.rem(f + k, 4)))

    for k in (1, 3, 2):
        c_copy(k).start()
    for i in range(3):
        net.pass_on(5, i)
    net.relay(6, 2)
    for k in (1, 3, 2):
        z = lax.rem(f + k, 4)
        remote(cls.at[f], cls.at[z], csend.at[0], crecv.at[z], (s, z)).wait_recv()
    mid = token + ((cls[0] + cls[1]) + (cls[2] + cls[3]))[0:1] * (1.0 / FRAMES)
    gain, shift = vector(7), vector(8)
    first = jnp.where(f == 0, 1.0, 0.0)

    def norm_feed(rows):
        r = iota((32, D), 0) + rows.start
        at_class = r == CLASS
        other = r == FRAME + CLASS
        values = x_s[rows].astype(f32) + rows_f[rows]
        values = jnp.where(at_class, mid, jnp.where(other, 0.0, values))
        rows_f[rows] = values
        scaled, unused = normed(values)
        n_f[rows] = (scaled * gain + shift).astype(bf16)
        acc[rows] = values + vector(9)
        acc2[rows] = jnp.zeros((32, D), f32)

    over_blocks(13, 32, norm_feed)
    save(N_F).start()
    net.complete(5)
    loads.start(9)
    for i in range(3):
        net.pass_on(6, i)

    def sib_copy(k, half, src, dst):
        return remote(src.at[half], dst.at[half], psend.at[k, half], precv.at[k, half], (net.sib, f))

    for j in range(4):
        c = 1 - core if j < 2 else core
        high = j & 1
        bias = jnp.concatenate(
            [vec32[1 + 2 * high + x, 0:1, pl.ds(pl.multiple_of(c * 384, 128), 384)] for x in range(2)], axis=1
        )
        w1 = loads.get(9 + 2 * j)
        hid[...] = dot(n_f[...], w1) + bias
        if j == 0:
            net.complete(6)
            for i in (10, 11, 12):
                loads.start(i)
        w2 = loads.get(10 + 2 * j)
        gact[...] = dot_nt(cot[...], w2)
        act_to, gh_to = (act_go, gh_go) if j < 2 else (act, gh)

        def feed(rows):
            hidden = hid[rows]
            tail = 0.5 + 0.5 * lax.erf(hidden * 0.7071067811865476)
            slope = tail + hidden * (jnp.exp(hidden * hidden * -0.5) * 0.3989422804014327)
            act_to[high, rows] = (hidden * tail).astype(bf16)
            gh_to[high, rows] = (gact[rows] * slope).astype(bf16)

        over_blocks(13, 32, feed)
        acc[...] += dot(act_to[high], w2)
        acc2[...] += dot_nt(gh_to[high], w1)
        for i in (13 + 2 * j, 14 + 2 * j):
            if i < 17:
                loads.start(i)

        at_class = iota((16, D), 0) == CLASS - 192
        for ref in (act_to, gh_to):
            piece = ref[high, 192:FRAME].astype(f32)
            ref[high, 192:FRAME] = jnp.where(at_class, piece * first, piece).astype(bf16)
        if j < 2:
            sib_copy(0, high, act_go, act_sib).start()
            sib_copy(1, high, gh_go, gh_sib).start()

    save(ACT).start()
    save(GH).start()

    twos = dot(to_twos(), acc[...].astype(bf16)).astype(bf16)
    output[...] = twos.reshape(PATCHES, OWN, D)
    class_output[...] = acc[CLASS : CLASS + 1].astype(bf16)
    gain = vector(7)
    sums[...] = jnp.zeros_like(sums)

    def feed_back(rows):
        r = iota((32, D), 0) + rows.start
        scaled, scale = normed(rows_f[rows])
        pulled = acc2[rows]
        counted = jnp.where(r == CLASS, pulled * first, pulled)
        sums[0:8] += jnp.sum((counted * scaled).reshape(4, 8, D), axis=0)
        sums[8:16] += jnp.sum(counted.reshape(4, 8, D), axis=0)
        up = pulled * gain
        back = scale * (
            up - jnp.mean(up, axis=-1, keepdims=True) - scaled * jnp.mean(up * scaled, axis=-1, keepdims=True)
        )
        grad = cot[rows].astype(f32) + back
        gmid[rows] = grad
        gb[rows] = grad.astype(bf16)

    over_blocks(13, 32, feed_back)
    row = (gmid[CLASS : CLASS + 1] * (1.0 / FRAMES)).astype(bf16).astype(f32)
    for start in (192, FRAME + 192):
        piece = gb[start : start + 16].astype(f32)
        gb[start : start + 16] = jnp.where(at_class, row, piece).astype(bf16)

    save(GMID).start()
    save(GB).start()
    for half in range(2):
        for k, src, dst in ((0, act_go, act_sib), (1, gh_go, gh_sib)):
            sib_copy(k, half, src, dst).wait()
    for k in (1, 2, 3):
        vec_copy(k).wait_send()
        a_copy(k).wait_send()
        c_copy(k).wait_send()
    for k in range(15):
        save(k).wait()
    for w in (0, 1, 2, 4):
        net.drain(w)
    for w in (3, 5, 6):
        net.empty(w)


def forward(video, class_token, frame_clip, patch_clip, padding, vectors, expand_bias, grad_output, grad_class_out, shards):
    vm = pl.BlockSpec(memory_space=pltpu.VMEM)
    sm = pl.BlockSpec(memory_space=pltpu.SMEM)
    hbm = pl.BlockSpec(memory_space=pl.ANY)
    sds = jax.ShapeDtypeStruct
    sem = pltpu.SemaphoreType.DMA
    v = pltpu.VMEM
    t, p = TIME_ROWS, SPACE_ROWS
    outs = [sds((PATCHES, OWN, D), bf16), sds((1, D), bf16)]
    outs += [sds((4 * a.shape[0], a.shape[1]), bf16) for a in shards]
    outs += [sds((t, D), bf16), sds((t, D), bf16), sds((t, 3 * D), bf16), sds((t, D), bf16), sds((t, D), bf16)]
    outs += [sds((p, D), bf16), sds((p, D), bf16), sds((p, 3 * D), bf16), sds((p, D), bf16), sds((p, D), bf16)]
    outs += [sds((p, D), bf16)] + [sds((2, p, D), bf16)] * 4 + [sds((p, D), f32), sds((p, D), bf16), sds((16, D), f32), sds((16, D), f32)]
    return pl.pallas_call(
        forward_kernel,
        out_shape=outs,
        in_specs=[vm, vm, sm, vm, vm, vm, vm, vm, vm] + [hbm] * 7,
        out_specs=[vm, vm] + [hbm] * 7 + [hbm] * 17 + [vm] * 2,
        scratch_shapes=[
            sem((UNITS, 24)),
            sem((UNITS, 5, 4)),
            v((4, 32, D), bf16),
            v((5, 16, D), f32),
            sem((3,)),
            sem((4,)),
            v((4, D, D), bf16),
            sem((4, 8)),
            v((4, SLOT, D), bf16),
            v((4, SLOT, D), bf16),
            sem((3,)),
            sem((4,)),
            v((8, 2 * TIME_BLOCK), f32),
            v((FRAME, 2 * FRAME), f32),
            v((16, 512), jnp.int32),
            v((p, D), f32),
            v((p, D), f32),
            v((p, D), f32),
            v((p, D), f32),
            v((p, D), f32),
            v((4, 8, D), f32),
            sem((3,)),
            sem((4,)),
            sem((2, 2)),
            sem((2, 2)),
            v((2, p, D), bf16),
            v((2, p, D), bf16),
            v((32, D), bf16),
            v((t, D), bf16),
            v((t, D), bf16),
            v((t, 3 * D), bf16),
            v((t, D), bf16),
            v((t, D), bf16),
            v((p, D), bf16),
            v((p, D), bf16),
            v((p, 3 * D), bf16),
            v((p, D), bf16),
            v((p, D), bf16),
            v((p, D), bf16),
            v((2, p, D), bf16),
            v((2, p, D), bf16),
            v((p, D), f32),
            v((p, D), bf16),
            sem((15,)),
        ],
        compiler_params=pltpu.CompilerParams(
            collective_id=1, has_side_effects=True, vmem_limit_bytes=63 << 20
        ),
        name="forward",
    )(video, class_token, frame_clip, patch_clip, padding, vectors, expand_bias, grad_output, grad_class_out, *shards)


class Reduce:
    def __init__(self, parts, ra, rb, ra2, rb2, rz, total, rc, sems):
        self.parts, self.ra, self.rb, self.ra2, self.rb2 = parts, ra, rb, ra2, rb2
        self.rz, self.total, self.rc, self.sems = rz, total, rc, sems
        self.s, self.f, self.core, self.col, self.row = place()
        s = self.s
        self.sib = s + 1 - 2 * self.core
        self.across, self.down = s + 2 - 4 * self.col, s + 4 - 8 * self.row

    def greet(self):
        bar = pltpu.get_barrier_semaphore()
        targets = [(t, self.f) for t in (self.sib, self.across, self.down)]
        targets += [(self.s, lax.rem(self.f + j, 4)) for j in (1, 2, 3)]
        for t in targets:
            pl.semaphore_signal(bar, inc=1, device_id=t, device_id_type=MESH)
        pl.semaphore_wait(bar, len(targets))

    def sem(self, w, i):
        return self.sems.at[w, i]

    def copies1(self, w):
        g = self.parts[w]
        return (
            remote(g.at[:, 1 - self.col, 0], self.ra[w], self.sem(w, 0), self.sem(w, 1), (self.across, self.f)),
            remote(g.at[1 - self.row, :, 1], self.rb[w], self.sem(w, 2), self.sem(w, 3), (self.down, self.f)),
        )

    def copies2(self, w):
        return (
            remote(self.ra[w].at[1 - self.row], self.ra2[w], self.sem(w, 4), self.sem(w, 5), (self.down, self.f)),
            remote(self.rb[w].at[1 - self.col], self.rb2[w], self.sem(w, 6), self.sem(w, 7), (self.across, self.f)),
        )

    def block(self, w, z):
        g = self.parts[w]
        rows = g.shape[3] // 2
        return g.at[z // 2, 1 - self.col, 0, pl.ds(pl.multiple_of(lax.rem(z, 2) * rows, 16), rows), :]

    def copies3(self, w):
        out = []
        for j in (1, 3, 2):
            z = lax.rem(self.f + j, 4)
            out.append(
                remote(self.block(w, z), self.rz[w].at[3 - j], self.sem(w, 7 + j), self.sem(w, 14 - j), (self.s, z))
            )
        return out

    def copy4(self, w):
        return remote(
            self.total[w].at[1 - self.core], self.rc[w], self.sem(w, 14), self.sem(w, 15), (self.sib, self.f)
        )

    def step1(self, w):
        for c in self.copies1(w):
            c.start()

    def step2(self, w):
        a, b = self.copies1(w)
        g, ra, rb = self.parts[w], self.ra[w], self.rb[w]
        row, col = self.row, self.col
        a2, b2 = self.copies2(w)
        a.wait_recv()
        ra[1 - row] = (ra[1 - row].astype(f32) + g[1 - row, col, 0].astype(f32)).astype(bf16)
        a2.start()
        b.wait_recv()
        rb[1 - col] = (rb[1 - col].astype(f32) + g[row, 1 - col, 1].astype(f32)).astype(bf16)
        b2.start()

    def step3(self, w):
        a, b = self.copies1(w)
        a2, b2 = self.copies2(w)
        g = self.parts[w]
        row, col = self.row, self.col
        part = g.shape[3] // 4
        a.wait_send()
        b2.wait_recv()
        a2.wait_recv()
        for z in range(4):
            rows = pl.ds(z * part, part)
            sums = []
            for k, near, far in ((0, self.ra[w].at[row], self.ra2[w]), (1, self.rb[w].at[col], self.rb2[w])):
                own = g.at[row, col, k]
                if part % 16:
                    tops = z * part // 16 * 16
                    high = -(-(z + 1) * part // 16) * 16
                    wide = [ref[tops:high].astype(f32) for ref in (own, near, far)]
                    low = z * part - tops
                    sums.append((wide[0] + wide[1] + wide[2])[low : low + part])
                else:
                    sums.append(own[rows].astype(f32) + near[rows].astype(f32) + far[rows].astype(f32))
            at = self.block(w, z)
            at[...] = jnp.concatenate(sums, axis=0).astype(bf16)
        for c in self.copies3(w):
            c.start()

    def step4(self, w, swap=True):
        for c in self.copies3(w):
            c.wait_recv()
        rz, part = self.rz[w], self.parts[w].shape[3] // 4
        whole = (self.block(w, self.f)[...].astype(f32) + rz[0].astype(f32)) + (
            rz[1].astype(f32) + rz[2].astype(f32)
        )
        self.total[w][0] = whole[:part]
        self.total[w][1] = whole[part:]
        if swap:
            self.copy4(w).start()

    def step5(self, w):
        self.copy4(w).wait_recv()

    def drain(self, w, swap=True):
        a, b = self.copies1(w)
        b.wait_send()
        for c in list(self.copies2(w)) + self.copies3(w) + ([self.copy4(w)] if swap else []):
            c.wait_send()


REDUCE, EXPAND, SPACE_OUT, SPACE_JOIN, MIX, TIME_OUT, TIME_JOIN, NARROW = range(8)
PARTS = ((384, 384), (96, 1536), (96, 384), (96, 1152), (96, 384), (96, 384), (96, 1152), (96, 128))


def backward_kernel(*refs):
    (frame_clip, patch_clip, padding, vec, sums) = refs[:5]
    stored = refs[5:18]
    act, gh, act_sib, gh_sib = refs[18:22]
    fulls, shards = refs[22:27], refs[27:32]
    (d_video, d_class, d_reduce, d_expand, d_so, d_sp, d_tm, d_to, d_tp, d_narrow) = refs[32:42]
    (parts, ra, rb, ra2, rb2, rz, total, rc, rsems, slots, slot_sems, act_v, gh_v, feed_sems, tbias, sbias, spare,
     gsm, wide, gat, gto, gtm, a2s, a2r, asend, arecv, cls, csend, crecv, bias_col, vt,
     n_f2, cot2, m_s2, gb2, n_s2, gjs2, o_t2, gat2, m_t2, gto2, n_t2, gjt2, xsend, xrecv,
     x_t, n_t, j_t, m_t, o_t, x_s, n_s, j_s, m_s, n_f, cot, gmid, gb, take_sems) = refs[42:]
    taken = (x_t, n_t, j_t, m_t, o_t, x_s, n_s, j_s, m_s, n_f, cot, gmid, gb)
    X_T, N_T, J_T, M_T, O_T, X_S, N_S, J_S, M_S, N_F, COT, GMID, GB = range(13)

    def take(k):
        return pltpu.make_async_copy(stored[k], taken[k], take_sems.at[k])

    for k in (COT, N_F):
        take(k).start()

    red = Reduce(parts, ra, rb, ra2, rb2, rz, total, rc, rsems)
    s, f, core, sib = red.s, red.f, red.core, red.sib
    red.greet()

    def half_of(ref, wide_half, which):
        return ref.at[:, pl.ds(pl.multiple_of(which * wide_half, 128), wide_half)]

    exchange = [
        (stored[COT], cot2), (stored[N_F], n_f2), (stored[M_S], m_s2), (half_of(stored[GB], 384, 1 - core), gb2),
        (stored[N_S], n_s2), (stored[O_T], o_t2), (stored[M_T], m_t2), (stored[N_T], n_t2),
    ]
    gjs = act_v.at[:, 0 : 3 * D]
    gjt = gh_v.at[0:TIME_ROWS, 0 : 3 * D]
    exchange += [
        (half_of(gjs, 1152, 1 - core), gjs2), (half_of(gat, 384, 1 - core), gat2),
        (half_of(gto, 384, 1 - core), gto2), (half_of(gjt, 1152, 1 - core), gjt2),
    ]
    GJS, GAT, GTO, GJT = 8, 9, 10, 11

    def trade(k):
        src, dst = exchange[k]
        return remote(src, dst, xsend.at[k], xrecv.at[k], (sib, f))

    loads_feed = []
    for k, (src, dst, at) in enumerate(
        ((act, act_v, 0), (act_sib, act_v, 2), (gh, gh_v, 0), (gh_sib, gh_v, 2))
    ):
        for half in range(2):
            lanes = slice((at + half) * D, (at + half + 1) * D)
            loads_feed.append(pltpu.make_async_copy(src.at[half], dst.at[:, lanes], feed_sems.at[2 * k + half]))
    for c in loads_feed:
        c.start()
    for k in (M_S, GB, J_S, X_S, GMID, N_S, O_T, M_T, J_T, N_T, X_T):
        take(k).start()
    for k in range(8):
        trade(k).start()
    pieces = []
    for w, count in ((4, 1), (3, 3), (2, 1), (1, 1), (0, 3)):
        pieces += squares(fulls, shards, w, count)
    loads = Loads(slots, slot_sems, pieces, f)
    for i in range(3):
        loads.start(i)
    time_bias(frame_clip, tbias)
    space_bias(patch_clip, padding, spare, sbias)

    first = jnp.where(f == 0, 1.0, 0.0)
    vt[...] = jnp.zeros_like(vt)
    counts = jnp.where(iota((16, SPACE_ROWS), 1) == CLASS, first, 1.0).astype(bf16)
    ones_s = jnp.ones((16, SPACE_ROWS), bf16)
    ones_t = jnp.ones((16, TIME_ROWS), bf16)
    vt[7:8] = jnp.sum(sums[0:8], axis=0, keepdims=True)
    vt[8:9] = jnp.sum(sums[8:16], axis=0, keepdims=True)
    take(COT).wait()
    vt[9:10] = dot(counts, cot[...])[0:1]

    for c in loads_feed[:4]:
        c.wait()
    trade(0).wait_recv()
    for y in range(2):
        grad = dot_tn(act_v[:, y * D : (y + 1) * D], cot[...]) + dot_tn(act_v[:, (2 + y) * D : (3 + y) * D], cot2[...])
        for x in range(2):
            for k in range(2):
                parts[REDUCE][y, x, k] = grad[x * 384 : (x + 1) * 384, k * 384 : (k + 1) * 384].astype(bf16)
    red.step1(REDUCE)
    for c in loads_feed[4:]:
        c.wait()
    take(N_F).wait()
    trade(1).wait_recv()

    def put(w, lanes, grad):
        for y in range(2):
            for x in range(2):
                for k in range(2):
                    start = ((y * 2 + x) * 2 + k) * 96
                    parts[w][y, x, k, :, lanes] = grad[start : start + 96].astype(bf16)

    for y in range(2):
        own, other = gh_v[:, y * D : (y + 1) * D], gh_v[:, (2 + y) * D : (3 + y) * D]
        grad = dot_tn(n_f[...], own) + dot_tn(n_f2[...], other)
        put(EXPAND, slice(y * D, (y + 1) * D), grad)
        ones = jnp.ones((SPACE_ROWS, 128), bf16)
        bias_col[y] = dot_tn(own, ones) + dot_tn(other, ones)
    red.step1(EXPAND)

    for k in (M_S, GB, J_S, X_S, GMID):
        take(k).wait()
    vt[6:7] = dot(ones_s, gb[...])[0:1]
    trade(2).wait_recv()
    trade(3).wait_recv()
    mine = half_of(gb, 384, core)
    put(SPACE_OUT, ALL, dot_tn(m_s[...], mine[...]) + dot_tn(m_s2[...], gb2[...]))
    red.step1(SPACE_OUT)
    gsm[...] = dot_nt(gb[...], loads.get(0)).astype(bf16)
    loads.start(3)
    attend_back(j_s, sbias, gsm, gjs, OWN, FRAME, 3)
    trade(GJS).start()
    red.step2(REDUCE)
    wide[...] = dot_nt(gjs[:, 0:D], loads.get(1))
    loads.start(4)
    wide[...] += dot_nt(gjs[:, D : 2 * D], loads.get(2))
    loads.start(5)
    wide[...] += dot_nt(gjs[:, 2 * D : 3 * D], loads.get(3))
    loads.start(6)
    gain = vec[4:5]

    def norm_back(source, gain, at, size, rows):
        scaled, scale = normed(source[rows].astype(f32))
        pulled = wide[rows]
        vt[at : at + 8] += jnp.sum((pulled * scaled).reshape(size // 8, 8, D), axis=0)
        vt[at + 8 : at + 16] += jnp.sum(pulled.reshape(size // 8, 8, D), axis=0)
        up = pulled * gain
        return scale * (
            up - jnp.mean(up, axis=-1, keepdims=True) - scaled * jnp.mean(up * scaled, axis=-1, keepdims=True)
        )

    def space_back(rows):
        back = norm_back(x_s, gain, 16, 32, rows)
        wide[rows] = back
        gsm[rows] = (gmid[rows] + back).astype(bf16)

    over_blocks(13, 32, space_back)
    a2s[...] = dot(from_tokens(), gsm[...]).astype(bf16).reshape(4, SLOT, D)

    def a_copy(k):
        z = lax.rem(f + k, 4)
        return remote(a2s.at[z], a2r.at[f], asend.at[k - 1], arecv.at[f], (s, z))

    for k in (1, 3, 2):
        a_copy(k).start()
    a2r[f] = a2s[f]
    cls[f] = jnp.broadcast_to(wide[CLASS : CLASS + 1] + wide[FRAME + CLASS : FRAME + CLASS + 1], (8, D))

    def c_copy(k):
        return remote(cls.at[f], cls.at[f], csend.at[k - 1], crecv.at[f], (s, lax.rem(f + k, 4)))

    for k in (1, 3, 2):
        c_copy(k).start()
    take(N_S).wait()
    trade(4).wait_recv()
    trade(GJS).wait_recv()
    mine = half_of(gjs, 1152, core)
    put(SPACE_JOIN, ALL, dot_tn(n_s[...], mine[...]) + dot_tn(n_s2[...], gjs2[...]))
    red.step1(SPACE_JOIN)
    red.step2(EXPAND)
    for k in (1, 3, 2):
        z = lax.rem(f + k, 4)
        with jax.named_scope("a_wait"):
            remote(a2s.at[z], a2r.at[z], asend.at[0], arecv.at[z], (s, z)).wait_recv()

    gat[...] = dot(to_patches(), a2r[...].reshape(4 * SLOT, D)).astype(bf16)
    trade(GAT).start()
    gto[...] = dot_nt(gat[...], loads.get(4)).astype(bf16)
    loads.start(7)
    trade(GTO).start()
    gtm[...] = dot_nt(gto[...], loads.get(5)).astype(bf16)
    loads.start(8)
    red.step2(SPACE_OUT)
    red.step3(REDUCE)
    for k in (O_T, M_T, J_T, N_T, X_T):
        take(k).wait()
    attend_back(j_t, tbias, gtm, gjt, 5, TIME_BLOCK, 6)
    trade(GJT).start()
    red.step2(SPACE_JOIN)
    trade(5).wait_recv()
    trade(GAT).wait_recv()
    mine = half_of(gat, 384, core)
    put(MIX, ALL, dot_tn(o_t[...], mine[...]) + dot_tn(o_t2[...], gat2[...]))
    red.step1(MIX)
    trade(6).wait_recv()
    trade(GTO).wait_recv()
    mine = half_of(gto, 384, core)
    put(TIME_OUT, ALL, dot_tn(m_t[...], mine[...]) + dot_tn(m_t2[...], gto2[...]))
    red.step1(TIME_OUT)
    trade(7).wait_recv()
    trade(GJT).wait_recv()
    mine = half_of(gjt, 1152, core)
    put(TIME_JOIN, ALL, dot_tn(n_t[...], mine[...]) + dot_tn(n_t2[...], gjt2[...]))
    red.step1(TIME_JOIN)
    red.step3(EXPAND)
    red.step3(SPACE_OUT)
    rows = pl.ds(0, TIME_ROWS)
    wide[rows] = dot_nt(gjt[:, 0:D], loads.get(6))
    wide[rows] += dot_nt(gjt[:, D : 2 * D], loads.get(7))
    wide[rows] += dot_nt(gjt[:, 2 * D : 3 * D], loads.get(8))
    gain = vec[0:1]

    def time_back(rows):
        back = norm_back(x_t, gain, 32, 80, rows)
        wide[rows] = gat[rows].astype(f32) + back

    over_blocks(5, 80, time_back)
    d_video[...] = wide[0 : HERE * FRAMES]
    vt[3:4] = dot(ones_t, gat[...])[0:1]
    vt[2:3] = dot(ones_t, gto[...])[0:1]
    for row, at in ((4, 16), (5, 24), (0, 32), (1, 40)):
        vt[row : row + 1] = jnp.sum(vt[at : at + 8], axis=0, keepdims=True)
    place_at = picks(iota((16, 128), 0) == iota((16, 128), 1))
    put(NARROW, ALL, dot_tn(vt[0:16].astype(bf16), place_at))
    lane = iota((24, 128), 1)
    for y in range(2):
        for x in range(2):
            pieces = []
            for z in range(4):
                piece = jnp.zeros((24, 128), f32)
                for k in range(4):
                    column = bias_col[y, pl.ds(x * 384 + z * 96 + k, 24, stride=4), :]
                    piece = jnp.where(lane == 10 + k, column, piece)
                pieces.append(piece)
            at = parts[NARROW].at[y, x, core]
            at[...] = (at[...].astype(f32) + jnp.concatenate(pieces, axis=0)).astype(bf16)
    red.step1(NARROW)

    def place_halves(w, out, half):
        red.step5(w)
        mine = half_of(out, half, core)
        mine[...] = total[w][core]
        other = half_of(out, half, 1 - core)
        other[...] = rc[w][...]

    red.step2(MIX)
    red.step2(TIME_OUT)
    red.step3(SPACE_JOIN)
    red.step2(TIME_JOIN)
    red.step2(NARROW)
    for k in (1, 3, 2):
        z = lax.rem(f + k, 4)
        remote(cls.at[f], cls.at[z], csend.at[0], crecv.at[z], (s, z)).wait_recv()
    d_class[...] = gmid[CLASS : CLASS + 1] + ((cls[0] + cls[1]) + (cls[2] + cls[3]))[0:1]
    red.step4(REDUCE, False)
    d_reduce[:, 0:384] = total[REDUCE][0]
    d_reduce[:, 384:768] = total[REDUCE][1]
    red.step4(EXPAND)
    red.step3(MIX)
    red.step3(TIME_OUT)
    red.step4(SPACE_OUT)
    red.step5(EXPAND)
    for y in range(2):
        for x in range(2):
            lanes = slice((y * 2 + x) * 384, (y * 2 + x + 1) * 384)
            for c, piece in ((core, total[EXPAND][core]), (1 - core, rc[EXPAND][...])):
                start = pl.multiple_of(((y * 2 + x) * 2 + c) * 384, 128)
                d_expand[:, pl.ds(start, 384)] = piece[:, lanes]
    red.step3(TIME_JOIN)
    red.step3(NARROW)
    red.step4(SPACE_JOIN)
    place_halves(SPACE_OUT, d_so, 384)
    red.step4(MIX)
    red.step4(TIME_OUT)
    place_halves(SPACE_JOIN, d_sp, 1152)
    place_halves(MIX, d_tm, 384)
    place_halves(TIME_OUT, d_to, 384)
    red.step4(TIME_JOIN)
    red.step4(NARROW)
    place_halves(TIME_JOIN, d_tp, 1152)
    red.step5(NARROW)
    d_narrow[...] = total[NARROW][core] + rc[NARROW][...]
    for w in range(8):
        red.drain(w, w != REDUCE)
    for k in range(12):
        trade(k).wait_send()
    for k in (1, 2, 3):
        a_copy(k).wait_send()
        c_copy(k).wait_send()


def backward(frame_clip, patch_clip, padding, vec, saved, fulls, shards):
    (x_t, n_t, j_t, m_t, o_t, x_s, n_s, j_s, m_s, n_f, cot, act, gh, act_sib, gh_sib, gmid, gb, sums) = saved
    vm = pl.BlockSpec(memory_space=pltpu.VMEM)
    sm = pl.BlockSpec(memory_space=pltpu.SMEM)
    hbm = pl.BlockSpec(memory_space=pl.ANY)
    sds = jax.ShapeDtypeStruct
    sem = pltpu.SemaphoreType.DMA
    v = pltpu.VMEM
    t, p = TIME_ROWS, SPACE_ROWS
    return pl.pallas_call(
        backward_kernel,
        out_shape=[
            sds((HERE * FRAMES, D), f32), sds((1, D), f32), sds((96, D), f32), sds((24, 4 * D), f32), sds((24, D), f32),
            sds((24, 3 * D), f32), sds((24, D), f32), sds((24, D), f32), sds((24, 3 * D), f32), sds((24, 128), f32),
        ],
        in_specs=[sm] + [vm] * 4 + [hbm] * 27,
        out_specs=[vm] * 10,
        scratch_shapes=[
            [v((2, 2, 2, r, c), bf16) for r, c in PARTS],
            [v((2, r, c), bf16) for r, c in PARTS],
            [v((2, r, c), bf16) for r, c in PARTS],
            [v((r, c), bf16) for r, c in PARTS],
            [v((r, c), bf16) for r, c in PARTS],
            [v((3, r // 2, c), bf16) for r, c in PARTS],
            [v((2, r // 4, c), f32) for r, c in PARTS],
            [v((r // 4, c), f32) for r, c in PARTS],
            sem((8, 16)),
            v((3, D, D), bf16),
            sem((3, 8)),
            v((p, 4 * D), bf16),
            v((p, 4 * D), bf16),
            sem((8,)),
            v((8, 2 * TIME_BLOCK), f32),
            v((FRAME, 2 * FRAME), f32),
            v((16, 512), jnp.int32),
            v((p, D), bf16),
            v((p, D), f32),
            v((t, D), bf16),
            v((t, D), bf16),
            v((t, D), bf16),
            v((4, SLOT, D), bf16),
            v((4, SLOT, D), bf16),
            sem((3,)),
            sem((4,)),
            v((4, 8, D), f32),
            sem((3,)),
            sem((4,)),
            v((2, D, 128), f32),
            v((48, D), f32),
            v((p, D), bf16),
            v((p, D), bf16),
            v((p, D), bf16),
            v((p, 384), bf16),
            v((p, D), bf16),
            v((p, 1152), bf16),
            v((t, D), bf16),
            v((t, 384), bf16),
            v((t, D), bf16),
            v((t, 384), bf16),
            v((t, D), bf16),
            v((t, 1152), bf16),
            sem((12,)),
            sem((12,)),
            v((t, D), bf16),
            v((t, D), bf16),
            v((t, 3 * D), bf16),
            v((t, D), bf16),
            v((t, D), bf16),
            v((p, D), bf16),
            v((p, D), bf16),
            v((p, 3 * D), bf16),
            v((p, D), bf16),
            v((p, D), bf16),
            v((p, D), bf16),
            v((p, D), f32),
            v((p, D), bf16),
            sem((13,)),
        ],
        compiler_params=pltpu.CompilerParams(
            collective_id=2, has_side_effects=True, vmem_limit_bytes=63 << 20
        ),
        name="backward",
    )(
        frame_clip, patch_clip, padding, vec, sums, x_t, n_t, j_t, m_t, o_t, x_s, n_s, j_s, m_s, n_f, cot, gmid, gb,
        act, gh, act_sib, gh_sib, *fulls[:5], *shards[:5]
    )


def finish_kernel(*refs):
    count = (len(refs) - 12) // 2
    for src, dst in zip(refs[:count], refs[count + 1 :]):
        dst[...] = src[...]
    narrow, outs = refs[count], refs[2 * count + 1 :]
    turned = jnp.transpose(jnp.concatenate([narrow[...], jnp.zeros((104, 128), f32)], axis=0))
    for i in range(10):
        outs[i][...] = turned[i, 0:24]
    r, c = iota((128, 96), 0), iota((128, 96), 1)
    bias = jnp.zeros((8, 96), f32)
    for k in range(4):
        rows = jnp.broadcast_to(turned[10 + k : 11 + k], (8, 128))
        spread = jnp.where(c == 4 * r + k, 1.0, 0.0)
        bias += jnp.dot(rows, spread, preferred_element_type=f32, precision=lax.Precision.HIGHEST)
    outs[10][...] = bias[0]


def finish(plain, narrow):
    vm = pl.BlockSpec(memory_space=pltpu.VMEM)
    outs = [jax.ShapeDtypeStruct(a.shape, a.dtype) for a in plain]
    outs += [jax.ShapeDtypeStruct((24,), f32)] * 10 + [jax.ShapeDtypeStruct((96,), f32)]
    return pl.pallas_call(
        finish_kernel,
        out_shape=outs,
        in_specs=[vm] * (len(plain) + 1),
        out_specs=[vm] * len(outs),
        compiler_params=pltpu.CompilerParams(vmem_limit_bytes=62 << 20),
        name="finish",
    )(*plain, narrow)


def settle(share):
    count = lax.axis_size("seq")
    if count == 8:
        return share
    more = count // 8
    groups = [[low + 8 * high for high in range(more)] for low in range(8)]
    share = lax.psum_scatter(share, "seq", scatter_dimension=0, tiled=True, axis_index_groups=groups)
    moves = [
        ((high * 8 + low) * 4 + f, (low * 4 + f) * more + high)
        for high in range(more)
        for low in range(8)
        for f in range(4)
    ]
    return lax.ppermute(share, ("seq", "ft"), moves)


def shards(
    video,
    class_token,
    frame_clip,
    patch_clip,
    padding,
    time_gain,
    time_shift,
    time_project,
    time_output,
    time_output_bias,
    time_mixer,
    time_mixer_bias,
    space_gain,
    space_shift,
    space_project,
    space_output,
    space_output_bias,
    feed_gain,
    feed_shift,
    feed_expand,
    feed_expand_bias,
    feed_reduce,
    feed_reduce_bias,
    grad_output,
    grad_class_out,
):
    vectors = jnp.zeros((16, D // 4), bf16)
    row = lax.broadcasted_iota(jnp.int32, vectors.shape, 0)
    for i, item in enumerate(
        (
            time_gain,
            time_shift,
            time_output_bias,
            time_mixer_bias,
            space_gain,
            space_shift,
            space_output_bias,
            feed_gain,
            feed_shift,
            feed_reduce_bias,
        )
    ):
        vectors = jnp.where(row == i, item[None, :], vectors)
    expand_bias = jnp.broadcast_to(feed_expand_bias[None, :], (16, D))
    weights = (time_project, time_output, time_mixer, space_project, space_output, feed_expand, feed_reduce)
    cotangent = jnp.swapaxes(grad_output[0], 0, 1)
    done = forward(
        jnp.swapaxes(video[0], 0, 1).reshape(HERE * FRAMES, D), class_token, frame_clip, patch_clip, padding, vectors, expand_bias, cotangent, grad_class_out, weights
    )
    output, class_output = jnp.swapaxes(done[0], 0, 1)[None], done[1]
    grads = backward(frame_clip, patch_clip, padding, done[27], done[9:27], done[2:9], weights)
    rows, grad_class = grads[:2]
    d_reduce, d_expand, d_so, d_sp, d_tm, d_to, d_tp, d_narrow = [settle(g) for g in grads[2:]]
    if lax.axis_size("seq") == 8:
        last = finish((done[0], class_output, rows, grad_class, d_reduce, d_expand, d_so, d_sp, d_tm, d_to, d_tp), d_narrow)
        twos, class_output, rows, grad_class, d_reduce, d_expand, d_so, d_sp, d_tm, d_to, d_tp = last[:11]
        output = jnp.swapaxes(twos, 0, 1)[None]
        narrow, d_bias = last[11:21], last[21]
    else:
        narrow = [d_narrow[:, i] for i in range(10)]
        d_bias = d_narrow[:, 10:14].reshape(-1)
    grad_video = jnp.swapaxes(rows.reshape(HERE, FRAMES, D), 0, 1)[None]
    return (
        output,
        class_output,
        grad_video,
        grad_class,
        narrow[0],
        narrow[1],
        d_tp,
        d_to,
        narrow[2],
        d_tm,
        narrow[3],
        narrow[4],
        narrow[5],
        d_sp,
        d_so,
        narrow[6],
        narrow[7],
        narrow[8],
        d_expand,
        d_bias,
        d_reduce,
        narrow[9],
    )


def solution(mesh):
    in_specs = (
        P("seq", None, "ft", None),
        P("seq", None),
        P("seq", None),
        P("seq", None),
        P("seq", None),
        P("ft"),
        P("ft"),
        P("ft", None),
        P("ft", None),
        P("ft"),
        P("ft", None),
        P("ft"),
        P("ft"),
        P("ft"),
        P("ft", None),
        P("ft", None),
        P("ft"),
        P("ft"),
        P("ft"),
        P("ft", None),
        P("ft"),
        P("ft", None),
        P("ft"),
        P("seq", "ft", None, None),
        P("seq", None),
    )
    out_specs = (
        P("seq", "ft", None, None),
        P("seq", None),
        P("seq", None, "ft", None),
        P("seq", None),
        P(("seq", "ft")),
        P(("seq", "ft")),
        P(("seq", "ft"), None),
        P(("seq", "ft"), None),
        P(("seq", "ft")),
        P(("seq", "ft"), None),
        P(("seq", "ft")),
        P(("seq", "ft")),
        P(("seq", "ft")),
        P(("seq", "ft"), None),
        P(("seq", "ft"), None),
        P(("seq", "ft")),
        P(("seq", "ft")),
        P(("seq", "ft")),
        P(("seq", "ft"), None),
        P(("seq", "ft")),
        P(("seq", "ft"), None),
        P(("seq", "ft")),
    )
    return jax.shard_map(shards, mesh=mesh, in_specs=in_specs, out_specs=out_specs, check_vma=False)
```

```python
import jax
import jax.numpy as jnp
from jax import lax
from jax.experimental import pallas as pl
from jax.experimental.pallas import tpu as pltpu
from jax.sharding import PartitionSpec as P

MESH = pl.DeviceIdType.MESH
bf16 = jnp.bfloat16
f32 = jnp.float32
D = 768
FRAMES = 8
HERE = 49
OWN = 2
PATCHES = 196
TIME_ROWS = 400
TIME_BLOCK = 80
FRAME = 208
CLASS = 196
SPACE_ROWS = OWN * FRAME
SLOT = 112
EPSILON = 1e-06
UNITS = 7


def iota(shape, axis):
    return lax.broadcasted_iota(jnp.int32, shape, axis)


def dot(left, right):
    return jnp.dot(left, right, preferred_element_type=f32)


def dot_nt(left, right):
    return lax.dot_general(left, right, (((1,), (1,)), ((), ())), preferred_element_type=f32)


def dot_tn(left, right):
    return lax.dot_general(left, right, (((0,), (0,)), ((), ())), preferred_element_type=f32)


def picks(condition):
    return jnp.where(condition, 1.0, 0.0).astype(bf16)


def between(r):
    return ((r & 7) >> 1) * SLOT + (r & 1) * HERE + (r >> 3)


def to_patches():
    r, c = iota((TIME_ROWS, 4 * SLOT), 0), iota((TIME_ROWS, 4 * SLOT), 1)
    return picks((c == between(r)) & (r < FRAMES * HERE))


def to_frames():
    c, r = iota((4 * SLOT, TIME_ROWS), 0), iota((4 * SLOT, TIME_ROWS), 1)
    return picks((c == between(r)) & (r < FRAMES * HERE))


def source_of(token, frame):
    late = (token >= HERE).astype(jnp.int32) + (token >= 2 * HERE) + (token >= 3 * HERE)
    return token + late * (SLOT - HERE) + frame * HERE


def to_tokens():
    r, c = iota((SPACE_ROWS, 4 * SLOT), 0), iota((SPACE_ROWS, 4 * SLOT), 1)
    frame = (r >= FRAME).astype(jnp.int32)
    token = r - frame * FRAME
    return picks((c == source_of(token, frame)) & (token < PATCHES))


def from_tokens():
    c, r = iota((4 * SLOT, SPACE_ROWS), 0), iota((4 * SLOT, SPACE_ROWS), 1)
    frame = (r >= FRAME).astype(jnp.int32)
    token = r - frame * FRAME
    return picks((c == source_of(token, frame)) & (token < PATCHES))


def from_twos():
    r, c = iota((SPACE_ROWS, OWN * PATCHES), 0), iota((SPACE_ROWS, OWN * PATCHES), 1)
    frame = (r >= FRAME).astype(jnp.int32)
    token = r - frame * FRAME
    return picks((c == 2 * token + frame) & (token < PATCHES))


def to_twos():
    r, c = iota((OWN * PATCHES, SPACE_ROWS), 0), iota((OWN * PATCHES, SPACE_ROWS), 1)
    return picks(c == (r >> 1) + (r & 1) * FRAME)


def normed(rows):
    centred = rows - jnp.mean(rows, axis=-1, keepdims=True)
    scale = lax.rsqrt(jnp.mean(centred * centred, axis=-1, keepdims=True) + EPSILON)
    return centred * scale, scale


def over_blocks(count, size, step):
    def body(i, carry):
        step(pl.ds(pl.multiple_of(i * size, 16), size))
        return carry

    lax.fori_loop(0, count, body, 0, unroll=True)


def halves(scale):
    lane = iota((1, 128), 1)
    first = jnp.where(lane < 64, scale, 0.0).astype(bf16)
    second = jnp.where(lane < 64, 0.0, scale).astype(bf16)
    return first, second


def chances(scores):
    power = jnp.exp(scores - jnp.max(scores, axis=0, keepdims=True))
    return power * (1.0 / jnp.sum(power, axis=0, keepdims=True))


def diagonal(heads):
    shape = (TIME_BLOCK // 8, 8, heads * TIME_BLOCK)
    lane = iota(shape, 2)
    lane = jnp.where(lane < TIME_BLOCK, lane, lane - TIME_BLOCK)
    return iota(shape, 0) == (lane >> 3)


def gathered(scores, where):
    return jnp.sum(jnp.where(where, scores.reshape(where.shape), 0.0), axis=0)


def scattered(scores, where):
    wide = jnp.where(where, jnp.broadcast_to(scores[None], where.shape), 0.0)
    return wide.reshape(TIME_BLOCK, where.shape[2]).astype(bf16)


def pair(i, j, size):
    rows = pl.ds(pl.multiple_of(i * size, 16), size)
    return rows, [pl.ds(pl.multiple_of(k * D + j * 128, 128), 128) for k in range(3)]


def both(values, first, second):
    return jnp.concatenate([values * first, values * second], axis=0)


def unite(values, size):
    return jnp.where(iota((size, 128), 1) < 64, values[:size], values[size:])


def attend_time(joined, bias, mixed, blocks, size, unroll):
    first8, second8 = halves(0.125)
    where = diagonal(1)

    def body(n, carry):
        rows, (ql, kl, vl) = pair(n // 6, lax.rem(n, 6), size)
        query, keys, values = joined[rows, ql], joined[rows, kl], joined[rows, vl]
        out = []
        for part in (query * first8, query * second8):
            scores = gathered(dot_nt(keys, part), where) + bias[:, 0:size]
            out.append(dot_tn(scattered(chances(scores), where), values))
        mixed[rows, ql] = jnp.where(iota((size, 128), 1) < 64, out[0], out[1]).astype(bf16)
        return carry

    lax.fori_loop(0, blocks * 6, body, 0, unroll=unroll)


def attend_space(joined, bias, mixed, blocks, size, unroll):
    first8, second8 = halves(0.125)

    def body(n, carry):
        rows, (ql, kl, vl) = pair(n // 6, lax.rem(n, 6), size)
        query, keys, values = joined[rows, ql], joined[rows, kl], joined[rows, vl]
        chance = chances(dot_nt(keys, both(query, first8, second8)) + bias[...]).astype(bf16)
        mixed[rows, ql] = unite(dot_tn(chance, values), size).astype(bf16)
        return carry

    lax.fori_loop(0, blocks * 6, body, 0, unroll=unroll)


def attend_back(joined, bias, grad_mixed, grad_joined, blocks, size, unroll):
    first8, second8 = halves(0.125)
    first, second = halves(1.0)
    where = diagonal(2) if size == TIME_BLOCK else None

    def body(n, carry):
        rows, (ql, kl, vl) = pair(n // 6, lax.rem(n, 6), size)
        query, keys, values = joined[rows, ql], joined[rows, kl], joined[rows, vl]
        queries, grads = both(query, first8, second8), both(grad_mixed[rows, ql], first, second)
        scores, pull = dot_nt(keys, queries), dot_nt(values, grads)
        if where is not None:
            scores, pull = gathered(scores, where), gathered(pull, where)
        chance = chances(scores + bias[...])
        back = chance * (pull - jnp.sum(chance * pull, axis=0, keepdims=True))
        if where is None:
            chance, back = chance.astype(bf16), back.astype(bf16)
        else:
            chance, back = scattered(chance, where), scattered(back, where)
        grad_joined[rows, ql] = (unite(dot_tn(back, keys), size) * 0.125).astype(bf16)
        grad_joined[rows, kl] = dot(back, queries).astype(bf16)
        grad_joined[rows, vl] = dot(chance, grads).astype(bf16)
        return carry

    lax.fori_loop(0, blocks * 6, body, 0, unroll=unroll)


def time_bias(frame_clip, bias):
    shape = (8, 2 * TIME_BLOCK)
    r, c = iota(shape, 0), iota(shape, 1)
    clip_r, clip_c = jnp.zeros(shape, jnp.int32), jnp.zeros(shape, jnp.int32)
    for f in range(FRAMES):
        clip_r = jnp.where(r == f, frame_clip[0, f], clip_r)
        clip_c = jnp.where((c & 7) == f, frame_clip[0, f], clip_c)
    bias[...] = jnp.where(clip_r == clip_c, 0.0, -1e30)


def space_bias(patch_clip, padding, spare, bias):
    shape = (FRAME, FRAME)
    r, c = iota(shape, 0), iota(shape, 1)
    spare[...] = jnp.full(spare.shape, -1, jnp.int32)
    for half in range(2):
        spare[0:1, half * FRAME : half * FRAME + PATCHES] = patch_clip[...]
    spare[8:9, 0:PATCHES] = padding[...]
    clip = jnp.broadcast_to(spare[0:1, 0:FRAME], shape).astype(f32)
    shut = jnp.broadcast_to(spare[8:9, 0:FRAME], shape).astype(f32)
    own = jnp.sum(jnp.where(r == c, clip, 0.0), axis=1, keepdims=True)
    closed = jnp.sum(jnp.where(r == c, shut, 0.0), axis=1, keepdims=True)
    shape = (FRAME, 2 * FRAME)
    r, c = iota(shape, 0), iota(shape, 1)
    clip = jnp.broadcast_to(spare[0:1, 0 : 2 * FRAME], shape).astype(f32)
    of_class = (c == CLASS) | (c == FRAME + CLASS)
    opened = (r == CLASS) | ((closed == 0.0) & ((clip == own) | of_class))
    bias[...] = jnp.where(opened, 0.0, -1e30)


def place():
    s = lax.axis_index("seq")
    f = lax.axis_index("ft")
    core = lax.rem(s, 2)
    col = lax.rem(s // 2, 2)
    row = lax.rem(s // 4, 2)
    return s, f, core, col, row


def remote(src, dst, send, recv, target):
    return pltpu.make_async_remote_copy(
        src_ref=src, dst_ref=dst, send_sem=send, recv_sem=recv, device_id=target, device_id_type=MESH
    )


class Spread:
    def __init__(self, shards, fulls, send, recv):
        self.shards, self.fulls, self.send, self.recv = shards, fulls, send, recv
        self.s, self.f, self.core, self.col, self.row = place()
        s = self.s
        self.sib = s + 1 - 2 * self.core
        dx, dy = 2 - 4 * self.col, 4 - 8 * self.row
        self.plane = ((s + dx, 1, 0), (s + dy, 0, 1), (s + dx + dy, 1, 1))
        upper = self.f // 2
        near = self.f + upper * (3 - 2 * self.f)
        self.order = [upper * 3 + (1 - 2 * upper) * v for v in (1 - near, 2, 3)]

    def greet(self):
        bar = pltpu.get_barrier_semaphore()
        targets = [(t, self.f) for t in (self.sib,) + tuple(p[0] for p in self.plane)]
        targets += [(self.s, lax.rem(self.f + j, 4)) for j in (1, 2, 3)]
        for t in targets:
            pl.semaphore_signal(bar, inc=1, device_id=t, device_id_type=MESH)
        pl.semaphore_wait(bar, len(targets))

    def cut(self, w, base, row, col):
        rows, wide = self.shards[w].shape
        start = base + self.core * (rows // 2) + row * (rows // 4)
        return (
            pl.ds(pl.multiple_of(start, 16), rows // 4),
            pl.ds(pl.multiple_of(col * (wide // 2), 128), wide // 2),
        )

    def along(self, w, k):
        z = lax.rem(self.f + k, 4)
        rows = self.shards[w].shape[0]
        src = self.shards[w].at[self.cut(w, 0, self.row, self.col)]
        dst = self.fulls[w].at[self.cut(w, self.f * rows, self.row, self.col)]
        return remote(src, dst, self.send.at[w, k - 1], self.recv.at[w, 0, self.f], (self.s, z))

    def start(self, w):
        for k in (1, 3, 2):
            self.along(w, k).start()

    def over(self, w, z, i, mine=True):
        target, dx, dy = self.plane[i]
        rows = self.shards[w].shape[0]
        row, col = (self.row, self.col) if mine else (self.row + dy - 2 * dy * self.row, self.col + dx - 2 * dx * self.col)
        ref = self.fulls[w].at[self.cut(w, z * rows, row, col)]
        return remote(ref, ref, self.send.at[w, 3 + 4 * i + z], self.recv.at[w, 1 + i, z], (target, self.f))

    def across(self, w, z, mine=True):
        rows = self.shards[w].shape[0]
        core = self.core if mine else 1 - self.core
        ref = self.fulls[w].at[pl.ds(pl.multiple_of(z * rows + core * (rows // 2), 16), rows // 2), :]
        return remote(ref, ref, self.send.at[w, 15 + z], self.recv.at[w, 4, z], (self.sib, self.f))

    def fan(self, w, nearest=(0, 1, 2)):
        rows = self.shards[w].shape[0]
        for t in nearest:
            z = self.order[t]
            ref = self.fulls[w].at[self.cut(w, z * rows, self.row, self.col)]
            remote(ref, ref, self.send.at[w, 0], self.recv.at[w, 0, z], (self.s, z)).wait_recv()
            for i in (2, 0, 1):
                self.over(w, z, i).start()

    def lend(self, w):
        for z in self.order:
            for i in range(3):
                self.over(w, z, i, False).wait_recv()
            self.across(w, z).start()

    def finish(self, w):
        for z in self.order:
            self.across(w, z, False).wait_recv()


    def quarter(self, w, base, own=True):
        rows = self.shards[w].shape[0]
        half = lax.rem(self.col + self.row, 2)
        which = 2 * half + self.core if own else 2 * (1 - half) + self.core
        return pl.ds(pl.multiple_of(base + which * (rows // 4), 16), rows // 4)

    def hop(self, w, z, step, src=None):
        dst = self.fulls[w].at[self.quarter(w, z * self.shards[w].shape[0])]
        side = 0 if step == 1 else 1
        src = dst if src is None else src
        return remote(src, dst, self.send.at[w, 4 * side + z], self.recv.at[w, 0, z], (self.s, self.f + step))

    def beside(self, w, z, i, own=True):
        wide = self.shards[w].shape[1]
        rows = self.quarter(w, z * self.shards[w].shape[0], own)
        ref = self.fulls[w].at[rows, i * (wide // 2) : (i + 1) * (wide // 2)]
        return remote(ref, ref, self.send.at[w, 8 + 4 * i + z], self.recv.at[w, 1 + i, z], (self.plane[i][0], self.f))

    def cross(self, w, z, own=True):
        ref = self.fulls[w].at[self.quarter(w, z * self.shards[w].shape[0], own)]
        i = 0 if own else 1
        return remote(ref, ref, self.send.at[w, 16 + 4 * i + z], self.recv.at[w, 3 + i, z], (self.sib, self.f))

    def off(self, w):
        src = self.shards[w].at[self.quarter(w, 0)]

        @pl.when(self.f < 3)
        def _():
            self.hop(w, self.f, 1, src).start()

        @pl.when(self.f > 0)
        def _():
            self.hop(w, self.f, -1, src).start()

    def onward(self, w, t, act):
        z = self.order[t]

        @pl.when((z < self.f) & (self.f < 3))
        def _():
            act(self.hop(w, z, 1))

        @pl.when((z > self.f) & (self.f > 0))
        def _():
            act(self.hop(w, z, -1))

    def relay(self, w, hops):
        outer = (self.f == 0) | (self.f == 3)
        inner = (self.f > 0) & (self.f < 3)
        if hops == 0:
            self.one(w, 0)
            pl.when(inner)(lambda: self.one(w, 1))
        elif hops == 1:
            pl.when(outer)(lambda: self.one(w, 1))
            pl.when(inner)(lambda: self.one(w, 2))
        else:
            pl.when(outer)(lambda: self.one(w, 2))

    def one(self, w, t):
        z = self.order[t]
        self.hop(w, z, 1).wait_recv()
        self.onward(w, t, lambda copy: copy.start())
        self.beside(w, z, 0).start()
        self.beside(w, z, 1).start()
        self.cross(w, z).start()

    def pass_on(self, w, t):
        z = self.order[t]
        for i in range(2):
            self.beside(w, z, i, False).wait_recv()
        self.cross(w, z, False).start()

    def complete(self, w):
        for z in self.order:
            self.cross(w, z).wait_recv()
            self.cross(w, z, False).wait_recv()

    def empty(self, w):
        src = self.shards[w].at[self.quarter(w, 0)]

        @pl.when(self.f < 3)
        def _():
            self.hop(w, self.f, 1, src).wait_send()

        @pl.when(self.f > 0)
        def _():
            self.hop(w, self.f, -1, src).wait_send()

        for t in range(3):
            z = self.order[t]
            self.onward(w, t, lambda copy: copy.wait_send())
            self.beside(w, z, 0).wait_send()
            self.beside(w, z, 1).wait_send()
            self.cross(w, z).wait_send()
            self.cross(w, z, False).wait_send()

    def drain(self, w):
        for k in (1, 2, 3):
            self.along(w, k).wait_send()
        for z in self.order:
            for i in range(3):
                self.over(w, z, i).wait_send()
            self.across(w, z).wait_send()


class Loads:
    def __init__(self, slots, sems, pieces, f):
        self.slots, self.sems, self.pieces, self.f = slots, sems, pieces, f

    def copies(self, i):
        n = i % self.slots.shape[0]
        full, shard, what, spot = self.pieces[i]
        slot = self.slots.at[n]
        if what == "columns":
            lanes = slice(spot * D, (spot + 1) * D)
            out = [(shard.at[:, lanes], slot.at[pl.ds(pl.multiple_of(self.f * 192, 16), 192)], None)]
            for k in (1, 2, 3):
                rows = pl.ds(pl.multiple_of(lax.rem(self.f + k, 4) * 192, 16), 192)
                out.append((full.at[rows, lanes], slot.at[rows], None))
        elif what == "wide":
            core, high = spot
            out = []
            for x in range(2):
                start = pl.multiple_of(((high * 2 + x) * 2 + core) * 384, 128)
                lanes, at = pl.ds(start, 384), slice(x * 384, (x + 1) * 384)
                out.append((shard.at[:, lanes], slot.at[pl.ds(pl.multiple_of(self.f * 192, 16), 192), at], None))
                for k in (1, 2, 3):
                    rows = pl.ds(pl.multiple_of(lax.rem(self.f + k, 4) * 192, 16), 192)
                    out.append((full.at[rows, lanes], slot.at[rows, at], None))
        else:
            core, high = spot
            out = []
            for x in range(2):
                z = high * 2 + x
                at = slot.at[x * 384 : (x + 1) * 384]
                here = shard.at[pl.ds(pl.multiple_of(core * 384, 16), 384)]
                there = full.at[pl.ds(pl.multiple_of(z * 768 + core * 384, 16), 384)]
                out += [(here, at, self.f == z), (there, at, self.f != z)]
        return [
            (pltpu.make_async_copy(src, dst, self.sems.at[n, k]), when) for k, (src, dst, when) in enumerate(out)
        ]

    def each(self, i, act):
        for copy, when in self.copies(i):
            if when is None:
                act(copy)
            else:
                pl.when(when)(lambda copy=copy: act(copy))

    def start(self, i):
        self.each(i, lambda copy: copy.start())

    def get(self, i):
        self.each(i, lambda copy: copy.wait())
        return self.slots[i % self.slots.shape[0]]


ALL = slice(None)


def squares(fulls, shards, w, count):
    return [(fulls[w], shards[w], "columns", i) for i in range(count)]


def forward_kernel(*refs):
    (video, class_token, frame_clip, patch_clip, padding, vectors, expand_bias, grad_output, grad_class_out) = refs[:9]
    shards = refs[9:16]
    outs = refs[16:44]
    (output, class_output) = outs[:2]
    fulls = outs[2:9]
    saved_out = outs[9:20] + outs[20:22] + outs[24:26]
    act_sib, gh_sib, sums, small_out = outs[22], outs[23], outs[26], outs[27]
    (send, recv, vec, vec32, vsend, vrecv, slots, slot_sems, a2s, a2r, asend, arecv, tbias, sbias, spare,
     rows_f, acc, acc2, hid, gact, cls, csend, crecv, psend, precv, act_go, gh_go, vec_go,
     x_t, n_t, j_t, m_t, o_t, x_s, n_s, j_s, m_s, n_f, cot, act, gh, gmid, gb, save_sems) = refs[44:]
    made = (x_t, n_t, j_t, m_t, o_t, x_s, n_s, j_s, m_s, n_f, cot, act, gh, gmid, gb)
    X_T, N_T, J_T, M_T, O_T, X_S, N_S, J_S, M_S, N_F, COT, ACT, GH, GMID, GB = range(15)

    def save(k):
        return pltpu.make_async_copy(made[k], saved_out[k], save_sems.at[k])


    net = Spread(shards, fulls, send, recv)
    s, f, core = net.s, net.f, net.core
    net.greet()

    def vec_copy(k):
        return remote(vec_go, vec.at[f], vsend.at[k - 1], vrecv.at[f], (s, lax.rem(f + k, 4)))

    vec_go[0:16, 0:192] = vectors[...]
    vec_go[0:16, 192:D] = jnp.zeros((16, D - 192), bf16)
    wide = expand_bias[...].astype(f32)
    wide = jnp.concatenate([wide[i : i + 1] for i in range(6)], axis=1)
    vec_go[16:32] = jnp.broadcast_to(wide, (16, D)).astype(bf16)
    for k in (1, 3, 2):
        vec_copy(k).start()
    net.start(0)
    vec[f] = vec_go[...]

    x_t[384:TIME_ROWS] = jnp.zeros((TIME_ROWS - 384, D), bf16)
    x_t[0 : HERE * FRAMES] = video[...]
    save(X_T).start()
    time_bias(frame_clip, tbias)
    for k in (1, 3, 2):
        z = lax.rem(f + k, 4)
        remote(vec_go, vec.at[z], vsend.at[0], vrecv.at[z], (s, z)).wait_recv()
    net.fan(0, (0,))
    small = jnp.zeros((16, D), f32)
    for z in range(4):
        r, c = iota((192, D), 0), iota((192, D), 1) - z * 192
        small += dot(vec[z, 0:16, 0:192], picks(c == r))
        vec32[1 + z] = vec[z, 16:32].astype(f32)
    vec32[0] = small
    small_out[...] = small
    net.fan(0, (1,))

    def vector(i):
        return vec32[0, i : i + 1, :]

    gain, shift = vector(0), vector(1)

    def norm_time(rows):
        scaled, unused = normed(x_t[rows].astype(f32))
        n_t[rows] = (scaled * gain + shift).astype(bf16)

    over_blocks(5, 80, norm_time)
    save(N_T).start()
    net.start(1)
    net.start(2)
    net.fan(0, (2,))
    net.start(3)
    net.off(4)
    net.off(5)

    cot[...] = dot(from_twos(), grad_output[...].reshape(OWN * PATCHES, D)).astype(bf16)
    at_class = iota((16, D), 0) == CLASS - 192
    tail = jnp.where(at_class, grad_class_out[...].astype(f32), cot[192:FRAME].astype(f32))
    cot[192:FRAME] = tail.astype(bf16)
    save(COT).start()
    space_bias(patch_clip, padding, spare, sbias)

    pieces = []
    for w, count in ((0, 3), (1, 1), (2, 1), (3, 3), (4, 1)):
        pieces += squares(fulls, shards, w, count)
    for c, high in ((1 - core, 0), (1 - core, 1), (core, 0), (core, 1)):
        pieces += [(fulls[5], shards[5], "wide", (c, high)), (fulls[6], shards[6], "tall", (c, high))]
    loads = Loads(slots, slot_sems, pieces, f)

    net.lend(0)
    net.fan(1)
    net.fan(2)
    net.finish(0)
    for i in range(3):
        loads.start(i)
    for i in range(3):
        j_t[:, i * D : (i + 1) * D] = dot(n_t[...], loads.get(i)).astype(bf16)
    save(J_T).start()
    net.fan(3, (0, 1))
    attend_time(j_t, tbias, m_t, 5, TIME_BLOCK, 6)
    net.fan(3, (2,))
    net.lend(1)
    net.lend(2)
    net.relay(4, 0)
    net.finish(1)
    loads.start(3)
    net.finish(2)
    loads.start(4)
    net.relay(5, 0)
    o_t[...] = (dot(m_t[...], loads.get(3)) + vector(2)).astype(bf16)
    save(M_T).start()
    save(O_T).start()
    after = (x_t[...].astype(f32) + (dot(o_t[...], loads.get(4)) + vector(3))).astype(bf16)
    a2s[...] = dot(to_frames(), after).astype(bf16).reshape(4, SLOT, D)

    def a_copy(k):
        z = lax.rem(f + k, 4)
        return remote(a2s.at[z], a2r.at[f], asend.at[k - 1], arecv.at[f], (s, z))

    for k in (1, 3, 2):
        a_copy(k).start()
    net.off(6)
    a2r[f] = a2s[f]
    net.relay(4, 1)
    net.lend(3)
    net.finish(3)
    for i in range(5, 8):
        loads.start(i)
    net.relay(4, 2)
    net.relay(5, 1)
    for k in (1, 3, 2):
        z = lax.rem(f + k, 4)
        with jax.named_scope("a_wait"):
            remote(a2s.at[z], a2r.at[z], asend.at[0], arecv.at[z], (s, z)).wait_recv()
    net.relay(6, 0)

    spread_rows = dot(to_tokens(), a2r[...].reshape(4 * SLOT, D))
    r = iota((SPACE_ROWS, D), 0)
    is_class = (r == CLASS) | (r == FRAME + CLASS)
    x_s[...] = jnp.where(is_class, class_token[...].astype(f32), spread_rows).astype(bf16)
    gain, shift = vector(4), vector(5)

    def norm_space(rows):
        scaled, unused = normed(x_s[rows].astype(f32))
        n_s[rows] = (scaled * gain + shift).astype(bf16)

    over_blocks(13, 32, norm_space)
    save(X_S).start()
    save(N_S).start()
    for i in range(3):
        j_s[:, i * D : (i + 1) * D] = dot(n_s[...], loads.get(5 + i)).astype(bf16)
    save(J_S).start()
    for i in range(3):
        net.pass_on(4, i)
    net.relay(5, 2)
    attend_space(j_s, sbias, m_s, OWN, FRAME, 6)
    net.relay(6, 1)
    net.complete(4)
    loads.start(8)
    rows_f[...] = dot(m_s[...], loads.get(8)) + vector(6)
    save(M_S).start()
    token = class_token[...].astype(f32)
    cls[f] = jnp.broadcast_to(
        rows_f[CLASS : CLASS + 1] + rows_f[FRAME + CLASS : FRAME + CLASS + 1], (8, D)
    )

    def c_copy(k):
        return remote(cls.at[f], cls.at[f], csend.at[k - 1], crecv.at[f], (s, lax.rem(f + k, 4)))

    for k in (1, 3, 2):
        c_copy(k).start()
    for i in range(3):
        net.pass_on(5, i)
    net.relay(6, 2)
    for k in (1, 3, 2):
        z = lax.rem(f + k, 4)
        remote(cls.at[f], cls.at[z], csend.at[0], crecv.at[z], (s, z)).wait_recv()
    mid = token + ((cls[0] + cls[1]) + (cls[2] + cls[3]))[0:1] * (1.0 / FRAMES)
    gain, shift = vector(7), vector(8)
    first = jnp.where(f == 0, 1.0, 0.0)

    def norm_feed(rows):
        r = iota((32, D), 0) + rows.start
        at_class = r == CLASS
        other = r == FRAME + CLASS
        values = x_s[rows].astype(f32) + rows_f[rows]
        values = jnp.where(at_class, mid, jnp.where(other, 0.0, values))
        rows_f[rows] = values
        scaled, unused = normed(values)
        n_f[rows] = (scaled * gain + shift).astype(bf16)
        acc[rows] = values + vector(9)
        acc2[rows] = jnp.zeros((32, D), f32)

    over_blocks(13, 32, norm_feed)
    save(N_F).start()
    net.complete(5)
    loads.start(9)
    for i in range(3):
        net.pass_on(6, i)

    def sib_copy(k, half, src, dst):
        return remote(src.at[half], dst.at[half], psend.at[k, half], precv.at[k, half], (net.sib, f))

    for j in range(4):
        c = 1 - core if j < 2 else core
        high = j & 1
        bias = jnp.concatenate(
            [vec32[1 + 2 * high + x, 0:1, pl.ds(pl.multiple_of(c * 384, 128), 384)] for x in range(2)], axis=1
        )
        w1 = loads.get(9 + 2 * j)
        hid[...] = dot(n_f[...], w1) + bias
        if j == 0:
            net.complete(6)
            for i in (10, 11, 12):
                loads.start(i)
        w2 = loads.get(10 + 2 * j)
        gact[...] = dot_nt(cot[...], w2)
        act_to, gh_to = (act_go, gh_go) if j < 2 else (act, gh)

        def feed(rows):
            hidden = hid[rows]
            tail = 0.5 + 0.5 * lax.erf(hidden * 0.7071067811865476)
            slope = tail + hidden * (jnp.exp(hidden * hidden * -0.5) * 0.3989422804014327)
            act_to[high, rows] = (hidden * tail).astype(bf16)
            gh_to[high, rows] = (gact[rows] * slope).astype(bf16)

        over_blocks(13, 32, feed)
        acc[...] += dot(act_to[high], w2)
        acc2[...] += dot_nt(gh_to[high], w1)
        for i in (13 + 2 * j, 14 + 2 * j):
            if i < 17:
                loads.start(i)

        at_class = iota((16, D), 0) == CLASS - 192
        for ref in (act_to, gh_to):
            piece = ref[high, 192:FRAME].astype(f32)
            ref[high, 192:FRAME] = jnp.where(at_class, piece * first, piece).astype(bf16)
        if j < 2:
            sib_copy(0, high, act_go, act_sib).start()
            sib_copy(1, high, gh_go, gh_sib).start()

    save(ACT).start()
    save(GH).start()

    twos = dot(to_twos(), acc[...].astype(bf16)).astype(bf16)
    output[...] = twos.reshape(PATCHES, OWN, D)
    class_output[...] = acc[CLASS : CLASS + 1].astype(bf16)
    gain = vector(7)
    sums[...] = jnp.zeros_like(sums)

    def feed_back(rows):
        r = iota((32, D), 0) + rows.start
        scaled, scale = normed(rows_f[rows])
        pulled = acc2[rows]
        counted = jnp.where(r == CLASS, pulled * first, pulled)
        sums[0:8] += jnp.sum((counted * scaled).reshape(4, 8, D), axis=0)
        sums[8:16] += jnp.sum(counted.reshape(4, 8, D), axis=0)
        up = pulled * gain
        back = scale * (
            up - jnp.mean(up, axis=-1, keepdims=True) - scaled * jnp.mean(up * scaled, axis=-1, keepdims=True)
        )
        grad = cot[rows].astype(f32) + back
        gmid[rows] = grad
        gb[rows] = grad.astype(bf16)

    over_blocks(13, 32, feed_back)
    row = (gmid[CLASS : CLASS + 1] * (1.0 / FRAMES)).astype(bf16).astype(f32)
    for start in (192, FRAME + 192):
        piece = gb[start : start + 16].astype(f32)
        gb[start : start + 16] = jnp.where(at_class, row, piece).astype(bf16)

    save(GMID).start()
    save(GB).start()
    for half in range(2):
        for k, src, dst in ((0, act_go, act_sib), (1, gh_go, gh_sib)):
            sib_copy(k, half, src, dst).wait()
    for k in (1, 2, 3):
        vec_copy(k).wait_send()
        a_copy(k).wait_send()
        c_copy(k).wait_send()
    for k in range(15):
        save(k).wait()
    for w in range(4):
        net.drain(w)
    for w in range(4, 7):
        net.empty(w)


def forward(video, class_token, frame_clip, patch_clip, padding, vectors, expand_bias, grad_output, grad_class_out, shards):
    vm = pl.BlockSpec(memory_space=pltpu.VMEM)
    sm = pl.BlockSpec(memory_space=pltpu.SMEM)
    hbm = pl.BlockSpec(memory_space=pl.ANY)
    sds = jax.ShapeDtypeStruct
    sem = pltpu.SemaphoreType.DMA
    v = pltpu.VMEM
    t, p = TIME_ROWS, SPACE_ROWS
    outs = [sds((PATCHES, OWN, D), bf16), sds((1, D), bf16)]
    outs += [sds((4 * a.shape[0], a.shape[1]), bf16) for a in shards]
    outs += [sds((t, D), bf16), sds((t, D), bf16), sds((t, 3 * D), bf16), sds((t, D), bf16), sds((t, D), bf16)]
    outs += [sds((p, D), bf16), sds((p, D), bf16), sds((p, 3 * D), bf16), sds((p, D), bf16), sds((p, D), bf16)]
    outs += [sds((p, D), bf16)] + [sds((2, p, D), bf16)] * 4 + [sds((p, D), f32), sds((p, D), bf16), sds((16, D), f32), sds((16, D), f32)]
    return pl.pallas_call(
        forward_kernel,
        out_shape=outs,
        in_specs=[vm, vm, sm, vm, vm, vm, vm, vm, vm] + [hbm] * 7,
        out_specs=[vm, vm] + [hbm] * 7 + [hbm] * 17 + [vm] * 2,
        scratch_shapes=[
            sem((UNITS, 24)),
            sem((UNITS, 5, 4)),
            v((4, 32, D), bf16),
            v((5, 16, D), f32),
            sem((3,)),
            sem((4,)),
            v((4, D, D), bf16),
            sem((4, 8)),
            v((4, SLOT, D), bf16),
            v((4, SLOT, D), bf16),
            sem((3,)),
            sem((4,)),
            v((8, 2 * TIME_BLOCK), f32),
            v((FRAME, 2 * FRAME), f32),
            v((16, 512), jnp.int32),
            v((p, D), f32),
            v((p, D), f32),
            v((p, D), f32),
            v((p, D), f32),
            v((p, D), f32),
            v((4, 8, D), f32),
            sem((3,)),
            sem((4,)),
            sem((2, 2)),
            sem((2, 2)),
            v((2, p, D), bf16),
            v((2, p, D), bf16),
            v((32, D), bf16),
            v((t, D), bf16),
            v((t, D), bf16),
            v((t, 3 * D), bf16),
            v((t, D), bf16),
            v((t, D), bf16),
            v((p, D), bf16),
            v((p, D), bf16),
            v((p, 3 * D), bf16),
            v((p, D), bf16),
            v((p, D), bf16),
            v((p, D), bf16),
            v((2, p, D), bf16),
            v((2, p, D), bf16),
            v((p, D), f32),
            v((p, D), bf16),
            sem((15,)),
        ],
        compiler_params=pltpu.CompilerParams(
            collective_id=1, has_side_effects=True, vmem_limit_bytes=63 << 20
        ),
        name="forward",
    )(video, class_token, frame_clip, patch_clip, padding, vectors, expand_bias, grad_output, grad_class_out, *shards)


class Reduce:
    def __init__(self, parts, ra, rb, ra2, rb2, rz, total, rc, sems):
        self.parts, self.ra, self.rb, self.ra2, self.rb2 = parts, ra, rb, ra2, rb2
        self.rz, self.total, self.rc, self.sems = rz, total, rc, sems
        self.s, self.f, self.core, self.col, self.row = place()
        s = self.s
        self.sib = s + 1 - 2 * self.core
        self.across, self.down = s + 2 - 4 * self.col, s + 4 - 8 * self.row

    def greet(self):
        bar = pltpu.get_barrier_semaphore()
        targets = [(t, self.f) for t in (self.sib, self.across, self.down)]
        targets += [(self.s, lax.rem(self.f + j, 4)) for j in (1, 2, 3)]
        for t in targets:
            pl.semaphore_signal(bar, inc=1, device_id=t, device_id_type=MESH)
        pl.semaphore_wait(bar, len(targets))

    def sem(self, w, i):
        return self.sems.at[w, i]

    def copies1(self, w):
        g = self.parts[w]
        return (
            remote(g.at[:, 1 - self.col, 0], self.ra[w], self.sem(w, 0), self.sem(w, 1), (self.across, self.f)),
            remote(g.at[1 - self.row, :, 1], self.rb[w], self.sem(w, 2), self.sem(w, 3), (self.down, self.f)),
        )

    def copies2(self, w):
        return (
            remote(self.ra[w].at[1 - self.row], self.ra2[w], self.sem(w, 4), self.sem(w, 5), (self.down, self.f)),
            remote(self.rb[w].at[1 - self.col], self.rb2[w], self.sem(w, 6), self.sem(w, 7), (self.across, self.f)),
        )

    def block(self, w, z):
        g = self.parts[w]
        rows = g.shape[3] // 2
        return g.at[z // 2, 1 - self.col, 0, pl.ds(pl.multiple_of(lax.rem(z, 2) * rows, 16), rows), :]

    def copies3(self, w):
        out = []
        for j in (1, 3, 2):
            z = lax.rem(self.f + j, 4)
            out.append(
                remote(self.block(w, z), self.rz[w].at[3 - j], self.sem(w, 7 + j), self.sem(w, 14 - j), (self.s, z))
            )
        return out

    def copy4(self, w):
        return remote(
            self.total[w].at[1 - self.core], self.rc[w], self.sem(w, 14), self.sem(w, 15), (self.sib, self.f)
        )

    def step1(self, w):
        for c in self.copies1(w):
            c.start()

    def step2(self, w):
        a, b = self.copies1(w)
        g, ra, rb = self.parts[w], self.ra[w], self.rb[w]
        row, col = self.row, self.col
        a2, b2 = self.copies2(w)
        a.wait_recv()
        ra[1 - row] = (ra[1 - row].astype(f32) + g[1 - row, col, 0].astype(f32)).astype(bf16)
        a2.start()
        b.wait_recv()
        rb[1 - col] = (rb[1 - col].astype(f32) + g[row, 1 - col, 1].astype(f32)).astype(bf16)
        b2.start()

    def step3(self, w):
        a, b = self.copies1(w)
        a2, b2 = self.copies2(w)
        g = self.parts[w]
        row, col = self.row, self.col
        part = g.shape[3] // 4
        a.wait_send()
        b2.wait_recv()
        a2.wait_recv()
        for z in range(4):
            rows = pl.ds(z * part, part)
            sums = []
            for k, near, far in ((0, self.ra[w].at[row], self.ra2[w]), (1, self.rb[w].at[col], self.rb2[w])):
                own = g.at[row, col, k]
                if part % 16:
                    tops = z * part // 16 * 16
                    high = -(-(z + 1) * part // 16) * 16
                    wide = [ref[tops:high].astype(f32) for ref in (own, near, far)]
                    low = z * part - tops
                    sums.append((wide[0] + wide[1] + wide[2])[low : low + part])
                else:
                    sums.append(own[rows].astype(f32) + near[rows].astype(f32) + far[rows].astype(f32))
            at = self.block(w, z)
            at[...] = jnp.concatenate(sums, axis=0).astype(bf16)
        for c in self.copies3(w):
            c.start()

    def step4(self, w, swap=True):
        for c in self.copies3(w):
            c.wait_recv()
        rz, part = self.rz[w], self.parts[w].shape[3] // 4
        whole = (self.block(w, self.f)[...].astype(f32) + rz[0].astype(f32)) + (
            rz[1].astype(f32) + rz[2].astype(f32)
        )
        self.total[w][0] = whole[:part]
        self.total[w][1] = whole[part:]
        if swap:
            self.copy4(w).start()

    def step5(self, w):
        self.copy4(w).wait_recv()

    def drain(self, w, swap=True):
        a, b = self.copies1(w)
        b.wait_send()
        for c in list(self.copies2(w)) + self.copies3(w) + ([self.copy4(w)] if swap else []):
            c.wait_send()


REDUCE, EXPAND, SPACE_OUT, SPACE_JOIN, MIX, TIME_OUT, TIME_JOIN, NARROW = range(8)
PARTS = ((384, 384), (96, 1536), (96, 384), (96, 1152), (96, 384), (96, 384), (96, 1152), (96, 128))


def backward_kernel(*refs):
    (frame_clip, patch_clip, padding, vec, sums) = refs[:5]
    stored = refs[5:18]
    act, gh, act_sib, gh_sib = refs[18:22]
    fulls, shards = refs[22:27], refs[27:32]
    (d_video, d_class, d_reduce, d_expand, d_so, d_sp, d_tm, d_to, d_tp, d_narrow) = refs[32:42]
    (parts, ra, rb, ra2, rb2, rz, total, rc, rsems, slots, slot_sems, act_v, gh_v, feed_sems, tbias, sbias, spare,
     gsm, wide, gat, gto, gtm, a2s, a2r, asend, arecv, cls, csend, crecv, bias_col, vt,
     n_f2, cot2, m_s2, gb2, n_s2, gjs2, o_t2, gat2, m_t2, gto2, n_t2, gjt2, xsend, xrecv,
     x_t, n_t, j_t, m_t, o_t, x_s, n_s, j_s, m_s, n_f, cot, gmid, gb, take_sems) = refs[42:]
    taken = (x_t, n_t, j_t, m_t, o_t, x_s, n_s, j_s, m_s, n_f, cot, gmid, gb)
    X_T, N_T, J_T, M_T, O_T, X_S, N_S, J_S, M_S, N_F, COT, GMID, GB = range(13)

    def take(k):
        return pltpu.make_async_copy(stored[k], taken[k], take_sems.at[k])

    for k in (COT, N_F):
        take(k).start()

    red = Reduce(parts, ra, rb, ra2, rb2, rz, total, rc, rsems)
    s, f, core, sib = red.s, red.f, red.core, red.sib
    red.greet()

    def half_of(ref, wide_half, which):
        return ref.at[:, pl.ds(pl.multiple_of(which * wide_half, 128), wide_half)]

    exchange = [
        (stored[COT], cot2), (stored[N_F], n_f2), (stored[M_S], m_s2), (half_of(stored[GB], 384, 1 - core), gb2),
        (stored[N_S], n_s2), (stored[O_T], o_t2), (stored[M_T], m_t2), (stored[N_T], n_t2),
    ]
    gjs = act_v.at[:, 0 : 3 * D]
    gjt = gh_v.at[0:TIME_ROWS, 0 : 3 * D]
    exchange += [
        (half_of(gjs, 1152, 1 - core), gjs2), (half_of(gat, 384, 1 - core), gat2),
        (half_of(gto, 384, 1 - core), gto2), (half_of(gjt, 1152, 1 - core), gjt2),
    ]
    GJS, GAT, GTO, GJT = 8, 9, 10, 11

    def trade(k):
        src, dst = exchange[k]
        return remote(src, dst, xsend.at[k], xrecv.at[k], (sib, f))

    loads_feed = []
    for k, (src, dst, at) in enumerate(
        ((act, act_v, 0), (act_sib, act_v, 2), (gh, gh_v, 0), (gh_sib, gh_v, 2))
    ):
        for half in range(2):
            lanes = slice((at + half) * D, (at + half + 1) * D)
            loads_feed.append(pltpu.make_async_copy(src.at[half], dst.at[:, lanes], feed_sems.at[2 * k + half]))
    for c in loads_feed:
        c.start()
    for k in (M_S, GB, J_S, X_S, GMID, N_S, O_T, M_T, J_T, N_T, X_T):
        take(k).start()
    for k in range(8):
        trade(k).start()
    pieces = []
    for w, count in ((4, 1), (3, 3), (2, 1), (1, 1), (0, 3)):
        pieces += squares(fulls, shards, w, count)
    loads = Loads(slots, slot_sems, pieces, f)
    for i in range(3):
        loads.start(i)
    time_bias(frame_clip, tbias)
    space_bias(patch_clip, padding, spare, sbias)

    first = jnp.where(f == 0, 1.0, 0.0)
    vt[...] = jnp.zeros_like(vt)
    counts = jnp.where(iota((16, SPACE_ROWS), 1) == CLASS, first, 1.0).astype(bf16)
    ones_s = jnp.ones((16, SPACE_ROWS), bf16)
    ones_t = jnp.ones((16, TIME_ROWS), bf16)
    vt[7:8] = jnp.sum(sums[0:8], axis=0, keepdims=True)
    vt[8:9] = jnp.sum(sums[8:16], axis=0, keepdims=True)
    take(COT).wait()
    vt[9:10] = dot(counts, cot[...])[0:1]

    for c in loads_feed[:4]:
        c.wait()
    trade(0).wait_recv()
    for y in range(2):
        grad = dot_tn(act_v[:, y * D : (y + 1) * D], cot[...]) + dot_tn(act_v[:, (2 + y) * D : (3 + y) * D], cot2[...])
        for x in range(2):
            for k in range(2):
                parts[REDUCE][y, x, k] = grad[x * 384 : (x + 1) * 384, k * 384 : (k + 1) * 384].astype(bf16)
    red.step1(REDUCE)
    for c in loads_feed[4:]:
        c.wait()
    take(N_F).wait()
    trade(1).wait_recv()

    def put(w, lanes, grad):
        for y in range(2):
            for x in range(2):
                for k in range(2):
                    start = ((y * 2 + x) * 2 + k) * 96
                    parts[w][y, x, k, :, lanes] = grad[start : start + 96].astype(bf16)

    for y in range(2):
        own, other = gh_v[:, y * D : (y + 1) * D], gh_v[:, (2 + y) * D : (3 + y) * D]
        grad = dot_tn(n_f[...], own) + dot_tn(n_f2[...], other)
        put(EXPAND, slice(y * D, (y + 1) * D), grad)
        ones = jnp.ones((SPACE_ROWS, 128), bf16)
        bias_col[y] = dot_tn(own, ones) + dot_tn(other, ones)
    red.step1(EXPAND)

    for k in (M_S, GB, J_S, X_S, GMID):
        take(k).wait()
    vt[6:7] = dot(ones_s, gb[...])[0:1]
    trade(2).wait_recv()
    trade(3).wait_recv()
    mine = half_of(gb, 384, core)
    put(SPACE_OUT, ALL, dot_tn(m_s[...], mine[...]) + dot_tn(m_s2[...], gb2[...]))
    red.step1(SPACE_OUT)
    gsm[...] = dot_nt(gb[...], loads.get(0)).astype(bf16)
    loads.start(3)
    attend_back(j_s, sbias, gsm, gjs, OWN, FRAME, 3)
    trade(GJS).start()
    red.step2(REDUCE)
    wide[...] = dot_nt(gjs[:, 0:D], loads.get(1))
    loads.start(4)
    wide[...] += dot_nt(gjs[:, D : 2 * D], loads.get(2))
    loads.start(5)
    wide[...] += dot_nt(gjs[:, 2 * D : 3 * D], loads.get(3))
    loads.start(6)
    gain = vec[4:5]

    def norm_back(source, gain, at, size, rows):
        scaled, scale = normed(source[rows].astype(f32))
        pulled = wide[rows]
        vt[at : at + 8] += jnp.sum((pulled * scaled).reshape(size // 8, 8, D), axis=0)
        vt[at + 8 : at + 16] += jnp.sum(pulled.reshape(size // 8, 8, D), axis=0)
        up = pulled * gain
        return scale * (
            up - jnp.mean(up, axis=-1, keepdims=True) - scaled * jnp.mean(up * scaled, axis=-1, keepdims=True)
        )

    def space_back(rows):
        back = norm_back(x_s, gain, 16, 32, rows)
        wide[rows] = back
        gsm[rows] = (gmid[rows] + back).astype(bf16)

    over_blocks(13, 32, space_back)
    a2s[...] = dot(from_tokens(), gsm[...]).astype(bf16).reshape(4, SLOT, D)

    def a_copy(k):
        z = lax.rem(f + k, 4)
        return remote(a2s.at[z], a2r.at[f], asend.at[k - 1], arecv.at[f], (s, z))

    for k in (1, 3, 2):
        a_copy(k).start()
    a2r[f] = a2s[f]
    cls[f] = jnp.broadcast_to(wide[CLASS : CLASS + 1] + wide[FRAME + CLASS : FRAME + CLASS + 1], (8, D))

    def c_copy(k):
        return remote(cls.at[f], cls.at[f], csend.at[k - 1], crecv.at[f], (s, lax.rem(f + k, 4)))

    for k in (1, 3, 2):
        c_copy(k).start()
    take(N_S).wait()
    trade(4).wait_recv()
    trade(GJS).wait_recv()
    mine = half_of(gjs, 1152, core)
    put(SPACE_JOIN, ALL, dot_tn(n_s[...], mine[...]) + dot_tn(n_s2[...], gjs2[...]))
    red.step1(SPACE_JOIN)
    red.step2(EXPAND)
    for k in (1, 3, 2):
        z = lax.rem(f + k, 4)
        with jax.named_scope("a_wait"):
            remote(a2s.at[z], a2r.at[z], asend.at[0], arecv.at[z], (s, z)).wait_recv()

    gat[...] = dot(to_patches(), a2r[...].reshape(4 * SLOT, D)).astype(bf16)
    trade(GAT).start()
    gto[...] = dot_nt(gat[...], loads.get(4)).astype(bf16)
    loads.start(7)
    trade(GTO).start()
    gtm[...] = dot_nt(gto[...], loads.get(5)).astype(bf16)
    loads.start(8)
    red.step2(SPACE_OUT)
    red.step3(REDUCE)
    for k in (O_T, M_T, J_T, N_T, X_T):
        take(k).wait()
    attend_back(j_t, tbias, gtm, gjt, 5, TIME_BLOCK, 6)
    trade(GJT).start()
    red.step2(SPACE_JOIN)
    trade(5).wait_recv()
    trade(GAT).wait_recv()
    mine = half_of(gat, 384, core)
    put(MIX, ALL, dot_tn(o_t[...], mine[...]) + dot_tn(o_t2[...], gat2[...]))
    red.step1(MIX)
    trade(6).wait_recv()
    trade(GTO).wait_recv()
    mine = half_of(gto, 384, core)
    put(TIME_OUT, ALL, dot_tn(m_t[...], mine[...]) + dot_tn(m_t2[...], gto2[...]))
    red.step1(TIME_OUT)
    trade(7).wait_recv()
    trade(GJT).wait_recv()
    mine = half_of(gjt, 1152, core)
    put(TIME_JOIN, ALL, dot_tn(n_t[...], mine[...]) + dot_tn(n_t2[...], gjt2[...]))
    red.step1(TIME_JOIN)
    red.step3(EXPAND)
    red.step3(SPACE_OUT)
    rows = pl.ds(0, TIME_ROWS)
    wide[rows] = dot_nt(gjt[:, 0:D], loads.get(6))
    wide[rows] += dot_nt(gjt[:, D : 2 * D], loads.get(7))
    wide[rows] += dot_nt(gjt[:, 2 * D : 3 * D], loads.get(8))
    gain = vec[0:1]

    def time_back(rows):
        back = norm_back(x_t, gain, 32, 80, rows)
        wide[rows] = gat[rows].astype(f32) + back

    over_blocks(5, 80, time_back)
    d_video[...] = wide[0 : HERE * FRAMES]
    vt[3:4] = dot(ones_t, gat[...])[0:1]
    vt[2:3] = dot(ones_t, gto[...])[0:1]
    for row, at in ((4, 16), (5, 24), (0, 32), (1, 40)):
        vt[row : row + 1] = jnp.sum(vt[at : at + 8], axis=0, keepdims=True)
    place_at = picks(iota((16, 128), 0) == iota((16, 128), 1))
    put(NARROW, ALL, dot_tn(vt[0:16].astype(bf16), place_at))
    lane = iota((24, 128), 1)
    for y in range(2):
        for x in range(2):
            pieces = []
            for z in range(4):
                piece = jnp.zeros((24, 128), f32)
                for k in range(4):
                    column = bias_col[y, pl.ds(x * 384 + z * 96 + k, 24, stride=4), :]
                    piece = jnp.where(lane == 10 + k, column, piece)
                pieces.append(piece)
            at = parts[NARROW].at[y, x, core]
            at[...] = (at[...].astype(f32) + jnp.concatenate(pieces, axis=0)).astype(bf16)
    red.step1(NARROW)

    def place_halves(w, out, half):
        red.step5(w)
        mine = half_of(out, half, core)
        mine[...] = total[w][core]
        other = half_of(out, half, 1 - core)
        other[...] = rc[w][...]

    red.step2(MIX)
    red.step2(TIME_OUT)
    red.step3(SPACE_JOIN)
    red.step2(TIME_JOIN)
    red.step2(NARROW)
    for k in (1, 3, 2):
        z = lax.rem(f + k, 4)
        remote(cls.at[f], cls.at[z], csend.at[0], crecv.at[z], (s, z)).wait_recv()
    d_class[...] = gmid[CLASS : CLASS + 1] + ((cls[0] + cls[1]) + (cls[2] + cls[3]))[0:1]
    red.step4(REDUCE, False)
    d_reduce[:, 0:384] = total[REDUCE][0]
    d_reduce[:, 384:768] = total[REDUCE][1]
    red.step4(EXPAND)
    red.step3(MIX)
    red.step3(TIME_OUT)
    red.step4(SPACE_OUT)
    red.step5(EXPAND)
    for y in range(2):
        for x in range(2):
            lanes = slice((y * 2 + x) * 384, (y * 2 + x + 1) * 384)
            for c, piece in ((core, total[EXPAND][core]), (1 - core, rc[EXPAND][...])):
                start = pl.multiple_of(((y * 2 + x) * 2 + c) * 384, 128)
                d_expand[:, pl.ds(start, 384)] = piece[:, lanes]
    red.step3(TIME_JOIN)
    red.step3(NARROW)
    red.step4(SPACE_JOIN)
    place_halves(SPACE_OUT, d_so, 384)
    red.step4(MIX)
    red.step4(TIME_OUT)
    place_halves(SPACE_JOIN, d_sp, 1152)
    place_halves(MIX, d_tm, 384)
    place_halves(TIME_OUT, d_to, 384)
    red.step4(TIME_JOIN)
    red.step4(NARROW)
    place_halves(TIME_JOIN, d_tp, 1152)
    red.step5(NARROW)
    d_narrow[...] = total[NARROW][core] + rc[NARROW][...]
    for w in range(8):
        red.drain(w, w != REDUCE)
    for k in range(12):
        trade(k).wait_send()
    for k in (1, 2, 3):
        a_copy(k).wait_send()
        c_copy(k).wait_send()


def backward(frame_clip, patch_clip, padding, vec, saved, fulls, shards):
    (x_t, n_t, j_t, m_t, o_t, x_s, n_s, j_s, m_s, n_f, cot, act, gh, act_sib, gh_sib, gmid, gb, sums) = saved
    vm = pl.BlockSpec(memory_space=pltpu.VMEM)
    sm = pl.BlockSpec(memory_space=pltpu.SMEM)
    hbm = pl.BlockSpec(memory_space=pl.ANY)
    sds = jax.ShapeDtypeStruct
    sem = pltpu.SemaphoreType.DMA
    v = pltpu.VMEM
    t, p = TIME_ROWS, SPACE_ROWS
    return pl.pallas_call(
        backward_kernel,
        out_shape=[
            sds((HERE * FRAMES, D), f32), sds((1, D), f32), sds((96, D), f32), sds((24, 4 * D), f32), sds((24, D), f32),
            sds((24, 3 * D), f32), sds((24, D), f32), sds((24, D), f32), sds((24, 3 * D), f32), sds((24, 128), f32),
        ],
        in_specs=[sm] + [vm] * 4 + [hbm] * 27,
        out_specs=[vm] * 10,
        scratch_shapes=[
            [v((2, 2, 2, r, c), bf16) for r, c in PARTS],
            [v((2, r, c), bf16) for r, c in PARTS],
            [v((2, r, c), bf16) for r, c in PARTS],
            [v((r, c), bf16) for r, c in PARTS],
            [v((r, c), bf16) for r, c in PARTS],
            [v((3, r // 2, c), bf16) for r, c in PARTS],
            [v((2, r // 4, c), f32) for r, c in PARTS],
            [v((r // 4, c), f32) for r, c in PARTS],
            sem((8, 16)),
            v((3, D, D), bf16),
            sem((3, 8)),
            v((p, 4 * D), bf16),
            v((p, 4 * D), bf16),
            sem((8,)),
            v((8, 2 * TIME_BLOCK), f32),
            v((FRAME, 2 * FRAME), f32),
            v((16, 512), jnp.int32),
            v((p, D), bf16),
            v((p, D), f32),
            v((t, D), bf16),
            v((t, D), bf16),
            v((t, D), bf16),
            v((4, SLOT, D), bf16),
            v((4, SLOT, D), bf16),
            sem((3,)),
            sem((4,)),
            v((4, 8, D), f32),
            sem((3,)),
            sem((4,)),
            v((2, D, 128), f32),
            v((48, D), f32),
            v((p, D), bf16),
            v((p, D), bf16),
            v((p, D), bf16),
            v((p, 384), bf16),
            v((p, D), bf16),
            v((p, 1152), bf16),
            v((t, D), bf16),
            v((t, 384), bf16),
            v((t, D), bf16),
            v((t, 384), bf16),
            v((t, D), bf16),
            v((t, 1152), bf16),
            sem((12,)),
            sem((12,)),
            v((t, D), bf16),
            v((t, D), bf16),
            v((t, 3 * D), bf16),
            v((t, D), bf16),
            v((t, D), bf16),
            v((p, D), bf16),
            v((p, D), bf16),
            v((p, 3 * D), bf16),
            v((p, D), bf16),
            v((p, D), bf16),
            v((p, D), bf16),
            v((p, D), f32),
            v((p, D), bf16),
            sem((13,)),
        ],
        compiler_params=pltpu.CompilerParams(
            collective_id=2, has_side_effects=True, vmem_limit_bytes=63 << 20
        ),
        name="backward",
    )(
        frame_clip, patch_clip, padding, vec, sums, x_t, n_t, j_t, m_t, o_t, x_s, n_s, j_s, m_s, n_f, cot, gmid, gb,
        act, gh, act_sib, gh_sib, *fulls[:5], *shards[:5]
    )


def finish_kernel(*refs):
    count = (len(refs) - 12) // 2
    for src, dst in zip(refs[:count], refs[count + 1 :]):
        dst[...] = src[...]
    narrow, outs = refs[count], refs[2 * count + 1 :]
    turned = jnp.transpose(jnp.concatenate([narrow[...], jnp.zeros((104, 128), f32)], axis=0))
    for i in range(10):
        outs[i][...] = turned[i, 0:24]
    r, c = iota((128, 96), 0), iota((128, 96), 1)
    bias = jnp.zeros((8, 96), f32)
    for k in range(4):
        rows = jnp.broadcast_to(turned[10 + k : 11 + k], (8, 128))
        spread = jnp.where(c == 4 * r + k, 1.0, 0.0)
        bias += jnp.dot(rows, spread, preferred_element_type=f32, precision=lax.Precision.HIGHEST)
    outs[10][...] = bias[0]


def finish(plain, narrow):
    vm = pl.BlockSpec(memory_space=pltpu.VMEM)
    outs = [jax.ShapeDtypeStruct(a.shape, a.dtype) for a in plain]
    outs += [jax.ShapeDtypeStruct((24,), f32)] * 10 + [jax.ShapeDtypeStruct((96,), f32)]
    return pl.pallas_call(
        finish_kernel,
        out_shape=outs,
        in_specs=[vm] * (len(plain) + 1),
        out_specs=[vm] * len(outs),
        compiler_params=pltpu.CompilerParams(vmem_limit_bytes=62 << 20),
        name="finish",
    )(*plain, narrow)


def settle(share):
    count = lax.axis_size("seq")
    if count == 8:
        return share
    more = count // 8
    groups = [[low + 8 * high for high in range(more)] for low in range(8)]
    share = lax.psum_scatter(share, "seq", scatter_dimension=0, tiled=True, axis_index_groups=groups)
    moves = [
        ((high * 8 + low) * 4 + f, (low * 4 + f) * more + high)
        for high in range(more)
        for low in range(8)
        for f in range(4)
    ]
    return lax.ppermute(share, ("seq", "ft"), moves)


def shards(
    video,
    class_token,
    frame_clip,
    patch_clip,
    padding,
    time_gain,
    time_shift,
    time_project,
    time_output,
    time_output_bias,
    time_mixer,
    time_mixer_bias,
    space_gain,
    space_shift,
    space_project,
    space_output,
    space_output_bias,
    feed_gain,
    feed_shift,
    feed_expand,
    feed_expand_bias,
    feed_reduce,
    feed_reduce_bias,
    grad_output,
    grad_class_out,
):
    vectors = jnp.zeros((16, D // 4), bf16)
    row = lax.broadcasted_iota(jnp.int32, vectors.shape, 0)
    for i, item in enumerate(
        (
            time_gain,
            time_shift,
            time_output_bias,
            time_mixer_bias,
            space_gain,
            space_shift,
            space_output_bias,
            feed_gain,
            feed_shift,
            feed_reduce_bias,
        )
    ):
        vectors = jnp.where(row == i, item[None, :], vectors)
    expand_bias = feed_expand_bias.reshape(6, 128)
    weights = (time_project, time_output, time_mixer, space_project, space_output, feed_expand, feed_reduce)
    cotangent = jnp.swapaxes(grad_output[0], 0, 1)
    done = forward(
        jnp.swapaxes(video[0], 0, 1).reshape(HERE * FRAMES, D), class_token, frame_clip, patch_clip, padding, vectors, expand_bias, cotangent, grad_class_out, weights
    )
    output, class_output = jnp.swapaxes(done[0], 0, 1)[None], done[1]
    grads = backward(frame_clip, patch_clip, padding, done[27], done[9:27], done[2:9], weights)
    rows, grad_class = grads[:2]
    d_reduce, d_expand, d_so, d_sp, d_tm, d_to, d_tp, d_narrow = [settle(g) for g in grads[2:]]
    if lax.axis_size("seq") == 8:
        last = finish((done[0], class_output, rows, grad_class, d_reduce, d_expand, d_so, d_sp, d_tm, d_to, d_tp), d_narrow)
        twos, class_output, rows, grad_class, d_reduce, d_expand, d_so, d_sp, d_tm, d_to, d_tp = last[:11]
        output = jnp.swapaxes(twos, 0, 1)[None]
        narrow, d_bias = last[11:21], last[21]
    else:
        narrow = [d_narrow[:, i] for i in range(10)]
        d_bias = d_narrow[:, 10:14].reshape(-1)
    grad_video = jnp.swapaxes(rows.reshape(HERE, FRAMES, D), 0, 1)[None]
    return (
        output,
        class_output,
        grad_video,
        grad_class,
        narrow[0],
        narrow[1],
        d_tp,
        d_to,
        narrow[2],
        d_tm,
        narrow[3],
        narrow[4],
        narrow[5],
        d_sp,
        d_so,
        narrow[6],
        narrow[7],
        narrow[8],
        d_expand,
        d_bias,
        d_reduce,
        narrow[9],
    )


def solution(mesh):
    in_specs = (
        P("seq", None, "ft", None),
        P("seq", None),
        P("seq", None),
        P("seq", None),
        P("seq", None),
        P("ft"),
        P("ft"),
        P("ft", None),
        P("ft", None),
        P("ft"),
        P("ft", None),
        P("ft"),
        P("ft"),
        P("ft"),
        P("ft", None),
        P("ft", None),
        P("ft"),
        P("ft"),
        P("ft"),
        P("ft", None),
        P("ft"),
        P("ft", None),
        P("ft"),
        P("seq", "ft", None, None),
        P("seq", None),
    )
    out_specs = (
        P("seq", "ft", None, None),
        P("seq", None),
        P("seq", None, "ft", None),
        P("seq", None),
        P(("seq", "ft")),
        P(("seq", "ft")),
        P(("seq", "ft"), None),
        P(("seq", "ft"), None),
        P(("seq", "ft")),
        P(("seq", "ft"), None),
        P(("seq", "ft")),
        P(("seq", "ft")),
        P(("seq", "ft")),
        P(("seq", "ft"), None),
        P(("seq", "ft"), None),
        P(("seq", "ft")),
        P(("seq", "ft")),
        P(("seq", "ft")),
        P(("seq", "ft"), None),
        P(("seq", "ft")),
        P(("seq", "ft"), None),
        P(("seq", "ft")),
    )
    return jax.shard_map(shards, mesh=mesh, in_specs=in_specs, out_specs=out_specs, check_vma=False)
```

```python
import jax
import jax.numpy as jnp
from jax import lax
from jax.experimental import pallas as pl
from jax.experimental.pallas import tpu as pltpu
from jax.sharding import PartitionSpec as P

MESH = pl.DeviceIdType.MESH
bf16 = jnp.bfloat16
f32 = jnp.float32
D = 768
FRAMES = 8
HERE = 49
OWN = 2
PATCHES = 196
TIME_ROWS = 400
TIME_BLOCK = 80
FRAME = 208
CLASS = 196
SPACE_ROWS = OWN * FRAME
SLOT = 112
EPSILON = 1e-06
UNITS = 7


def iota(shape, axis):
    return lax.broadcasted_iota(jnp.int32, shape, axis)


def dot(left, right):
    return jnp.dot(left, right, preferred_element_type=f32)


def dot_nt(left, right):
    return lax.dot_general(left, right, (((1,), (1,)), ((), ())), preferred_element_type=f32)


def dot_tn(left, right):
    return lax.dot_general(left, right, (((0,), (0,)), ((), ())), preferred_element_type=f32)


def picks(condition):
    return jnp.where(condition, 1.0, 0.0).astype(bf16)


def between(r):
    return ((r & 7) >> 1) * SLOT + (r & 1) * HERE + (r >> 3)


def to_patches():
    r, c = iota((TIME_ROWS, 4 * SLOT), 0), iota((TIME_ROWS, 4 * SLOT), 1)
    return picks((c == between(r)) & (r < FRAMES * HERE))


def to_frames():
    c, r = iota((4 * SLOT, TIME_ROWS), 0), iota((4 * SLOT, TIME_ROWS), 1)
    return picks((c == between(r)) & (r < FRAMES * HERE))


def source_of(token, frame):
    late = (token >= HERE).astype(jnp.int32) + (token >= 2 * HERE) + (token >= 3 * HERE)
    return token + late * (SLOT - HERE) + frame * HERE


def to_tokens():
    r, c = iota((SPACE_ROWS, 4 * SLOT), 0), iota((SPACE_ROWS, 4 * SLOT), 1)
    frame = (r >= FRAME).astype(jnp.int32)
    token = r - frame * FRAME
    return picks((c == source_of(token, frame)) & (token < PATCHES))


def from_tokens():
    c, r = iota((4 * SLOT, SPACE_ROWS), 0), iota((4 * SLOT, SPACE_ROWS), 1)
    frame = (r >= FRAME).astype(jnp.int32)
    token = r - frame * FRAME
    return picks((c == source_of(token, frame)) & (token < PATCHES))


def from_twos():
    r, c = iota((SPACE_ROWS, OWN * PATCHES), 0), iota((SPACE_ROWS, OWN * PATCHES), 1)
    frame = (r >= FRAME).astype(jnp.int32)
    token = r - frame * FRAME
    return picks((c == 2 * token + frame) & (token < PATCHES))


def to_twos():
    r, c = iota((OWN * PATCHES, SPACE_ROWS), 0), iota((OWN * PATCHES, SPACE_ROWS), 1)
    return picks(c == (r >> 1) + (r & 1) * FRAME)


def normed(rows):
    centred = rows - jnp.mean(rows, axis=-1, keepdims=True)
    scale = lax.rsqrt(jnp.mean(centred * centred, axis=-1, keepdims=True) + EPSILON)
    return centred * scale, scale


def over_blocks(count, size, step):
    def body(i, carry):
        step(pl.ds(pl.multiple_of(i * size, 16), size))
        return carry

    lax.fori_loop(0, count, body, 0, unroll=True)


def halves(scale):
    lane = iota((1, 128), 1)
    first = jnp.where(lane < 64, scale, 0.0).astype(bf16)
    second = jnp.where(lane < 64, 0.0, scale).astype(bf16)
    return first, second


def chances(scores):
    power = jnp.exp(scores - jnp.max(scores, axis=0, keepdims=True))
    return power * (1.0 / jnp.sum(power, axis=0, keepdims=True))


def diagonal(heads):
    shape = (TIME_BLOCK // 8, 8, heads * TIME_BLOCK)
    lane = iota(shape, 2)
    lane = jnp.where(lane < TIME_BLOCK, lane, lane - TIME_BLOCK)
    return iota(shape, 0) == (lane >> 3)


def gathered(scores, where):
    return jnp.sum(jnp.where(where, scores.reshape(where.shape), 0.0), axis=0)


def scattered(scores, where):
    wide = jnp.where(where, jnp.broadcast_to(scores[None], where.shape), 0.0)
    return wide.reshape(TIME_BLOCK, where.shape[2]).astype(bf16)


def pair(i, j, size):
    rows = pl.ds(pl.multiple_of(i * size, 16), size)
    return rows, [pl.ds(pl.multiple_of(k * D + j * 128, 128), 128) for k in range(3)]


def both(values, first, second):
    return jnp.concatenate([values * first, values * second], axis=0)


def unite(values, size):
    return jnp.where(iota((size, 128), 1) < 64, values[:size], values[size:])


def attend_time(joined, bias, mixed, blocks, size, unroll):
    first8, second8 = halves(0.125)
    where = diagonal(1)

    def body(n, carry):
        rows, (ql, kl, vl) = pair(n // 6, lax.rem(n, 6), size)
        query, keys, values = joined[rows, ql], joined[rows, kl], joined[rows, vl]
        out = []
        for part in (query * first8, query * second8):
            scores = gathered(dot_nt(keys, part), where) + bias[:, 0:size]
            out.append(dot_tn(scattered(chances(scores), where), values))
        mixed[rows, ql] = jnp.where(iota((size, 128), 1) < 64, out[0], out[1]).astype(bf16)
        return carry

    lax.fori_loop(0, blocks * 6, body, 0, unroll=unroll)


def attend_space(joined, bias, mixed, blocks, size, unroll):
    first8, second8 = halves(0.125)

    def body(n, carry):
        rows, (ql, kl, vl) = pair(n // 6, lax.rem(n, 6), size)
        query, keys, values = joined[rows, ql], joined[rows, kl], joined[rows, vl]
        chance = chances(dot_nt(keys, both(query, first8, second8)) + bias[...]).astype(bf16)
        mixed[rows, ql] = unite(dot_tn(chance, values), size).astype(bf16)
        return carry

    lax.fori_loop(0, blocks * 6, body, 0, unroll=unroll)


def attend_back(joined, bias, grad_mixed, grad_joined, blocks, size, unroll):
    first8, second8 = halves(0.125)
    first, second = halves(1.0)
    where = diagonal(2) if size == TIME_BLOCK else None

    def body(n, carry):
        rows, (ql, kl, vl) = pair(n // 6, lax.rem(n, 6), size)
        query, keys, values = joined[rows, ql], joined[rows, kl], joined[rows, vl]
        queries, grads = both(query, first8, second8), both(grad_mixed[rows, ql], first, second)
        scores, pull = dot_nt(keys, queries), dot_nt(values, grads)
        if where is not None:
            scores, pull = gathered(scores, where), gathered(pull, where)
        chance = chances(scores + bias[...])
        back = chance * (pull - jnp.sum(chance * pull, axis=0, keepdims=True))
        if where is None:
            chance, back = chance.astype(bf16), back.astype(bf16)
        else:
            chance, back = scattered(chance, where), scattered(back, where)
        grad_joined[rows, ql] = (unite(dot_tn(back, keys), size) * 0.125).astype(bf16)
        grad_joined[rows, kl] = dot(back, queries).astype(bf16)
        grad_joined[rows, vl] = dot(chance, grads).astype(bf16)
        return carry

    lax.fori_loop(0, blocks * 6, body, 0, unroll=unroll)


def time_bias(frame_clip, bias):
    shape = (8, 2 * TIME_BLOCK)
    r, c = iota(shape, 0), iota(shape, 1)
    clip_r, clip_c = jnp.zeros(shape, jnp.int32), jnp.zeros(shape, jnp.int32)
    for f in range(FRAMES):
        clip_r = jnp.where(r == f, frame_clip[0, f], clip_r)
        clip_c = jnp.where((c & 7) == f, frame_clip[0, f], clip_c)
    bias[...] = jnp.where(clip_r == clip_c, 0.0, -1e30)


def space_bias(patch_clip, padding, spare, bias):
    shape = (FRAME, FRAME)
    r, c = iota(shape, 0), iota(shape, 1)
    spare[...] = jnp.full(spare.shape, -1, jnp.int32)
    for half in range(2):
        spare[0:1, half * FRAME : half * FRAME + PATCHES] = patch_clip[...]
    spare[8:9, 0:PATCHES] = padding[...]
    clip = jnp.broadcast_to(spare[0:1, 0:FRAME], shape).astype(f32)
    shut = jnp.broadcast_to(spare[8:9, 0:FRAME], shape).astype(f32)
    own = jnp.sum(jnp.where(r == c, clip, 0.0), axis=1, keepdims=True)
    closed = jnp.sum(jnp.where(r == c, shut, 0.0), axis=1, keepdims=True)
    shape = (FRAME, 2 * FRAME)
    r, c = iota(shape, 0), iota(shape, 1)
    clip = jnp.broadcast_to(spare[0:1, 0 : 2 * FRAME], shape).astype(f32)
    of_class = (c == CLASS) | (c == FRAME + CLASS)
    opened = (r == CLASS) | ((closed == 0.0) & ((clip == own) | of_class))
    bias[...] = jnp.where(opened, 0.0, -1e30)


def place():
    s = lax.axis_index("seq")
    f = lax.axis_index("ft")
    core = lax.rem(s, 2)
    col = lax.rem(s // 2, 2)
    row = lax.rem(s // 4, 2)
    return s, f, core, col, row


def remote(src, dst, send, recv, target):
    return pltpu.make_async_remote_copy(
        src_ref=src, dst_ref=dst, send_sem=send, recv_sem=recv, device_id=target, device_id_type=MESH
    )


class Spread:
    def __init__(self, shards, fulls, send, recv):
        self.shards, self.fulls, self.send, self.recv = shards, fulls, send, recv
        self.s, self.f, self.core, self.col, self.row = place()
        s = self.s
        self.sib = s + 1 - 2 * self.core
        dx, dy = 2 - 4 * self.col, 4 - 8 * self.row
        self.plane = ((s + dx, 1, 0), (s + dy, 0, 1), (s + dx + dy, 1, 1))
        upper = self.f // 2
        near = self.f + upper * (3 - 2 * self.f)
        self.order = [upper * 3 + (1 - 2 * upper) * v for v in (1 - near, 2, 3)]

    def greet(self):
        bar = pltpu.get_barrier_semaphore()
        targets = [(t, self.f) for t in (self.sib,) + tuple(p[0] for p in self.plane)]
        targets += [(self.s, lax.rem(self.f + j, 4)) for j in (1, 2, 3)]
        for t in targets:
            pl.semaphore_signal(bar, inc=1, device_id=t, device_id_type=MESH)
        pl.semaphore_wait(bar, len(targets))

    def cut(self, w, base, row, col):
        rows, wide = self.shards[w].shape
        start = base + self.core * (rows // 2) + row * (rows // 4)
        return (
            pl.ds(pl.multiple_of(start, 16), rows // 4),
            pl.ds(pl.multiple_of(col * (wide // 2), 128), wide // 2),
        )

    def along(self, w, k):
        z = lax.rem(self.f + k, 4)
        rows = self.shards[w].shape[0]
        src = self.shards[w].at[self.cut(w, 0, self.row, self.col)]
        dst = self.fulls[w].at[self.cut(w, self.f * rows, self.row, self.col)]
        return remote(src, dst, self.send.at[w, k - 1], self.recv.at[w, 0, self.f], (self.s, z))

    def start(self, w):
        for k in (1, 3, 2):
            self.along(w, k).start()

    def over(self, w, z, i, mine=True):
        target, dx, dy = self.plane[i]
        rows = self.shards[w].shape[0]
        row, col = (self.row, self.col) if mine else (self.row + dy - 2 * dy * self.row, self.col + dx - 2 * dx * self.col)
        ref = self.fulls[w].at[self.cut(w, z * rows, row, col)]
        return remote(ref, ref, self.send.at[w, 3 + 4 * i + z], self.recv.at[w, 1 + i, z], (target, self.f))

    def across(self, w, z, mine=True):
        rows = self.shards[w].shape[0]
        core = self.core if mine else 1 - self.core
        ref = self.fulls[w].at[pl.ds(pl.multiple_of(z * rows + core * (rows // 2), 16), rows // 2), :]
        return remote(ref, ref, self.send.at[w, 15 + z], self.recv.at[w, 4, z], (self.sib, self.f))

    def fan(self, w, nearest=(0, 1, 2)):
        rows = self.shards[w].shape[0]
        for t in nearest:
            z = self.order[t]
            ref = self.fulls[w].at[self.cut(w, z * rows, self.row, self.col)]
            remote(ref, ref, self.send.at[w, 0], self.recv.at[w, 0, z], (self.s, z)).wait_recv()
            for i in (2, 0, 1):
                self.over(w, z, i).start()

    def lend(self, w):
        for z in self.order:
            for i in range(3):
                self.over(w, z, i, False).wait_recv()
            self.across(w, z).start()

    def finish(self, w):
        for z in self.order:
            self.across(w, z, False).wait_recv()


    def quarter(self, w, base, own=True):
        rows = self.shards[w].shape[0]
        half = lax.rem(self.col + self.row, 2)
        which = 2 * half + self.core if own else 2 * (1 - half) + self.core
        return pl.ds(pl.multiple_of(base + which * (rows // 4), 16), rows // 4)

    def hop(self, w, z, step, src=None):
        dst = self.fulls[w].at[self.quarter(w, z * self.shards[w].shape[0])]
        side = 0 if step == 1 else 1
        src = dst if src is None else src
        return remote(src, dst, self.send.at[w, 4 * side + z], self.recv.at[w, 0, z], (self.s, self.f + step))

    def beside(self, w, z, i, own=True):
        wide = self.shards[w].shape[1]
        rows = self.quarter(w, z * self.shards[w].shape[0], own)
        ref = self.fulls[w].at[rows, i * (wide // 2) : (i + 1) * (wide // 2)]
        return remote(ref, ref, self.send.at[w, 8 + 4 * i + z], self.recv.at[w, 1 + i, z], (self.plane[i][0], self.f))

    def cross(self, w, z, own=True):
        ref = self.fulls[w].at[self.quarter(w, z * self.shards[w].shape[0], own)]
        i = 0 if own else 1
        return remote(ref, ref, self.send.at[w, 16 + 4 * i + z], self.recv.at[w, 3 + i, z], (self.sib, self.f))

    def off(self, w):
        src = self.shards[w].at[self.quarter(w, 0)]

        @pl.when(self.f < 3)
        def _():
            self.hop(w, self.f, 1, src).start()

        @pl.when(self.f > 0)
        def _():
            self.hop(w, self.f, -1, src).start()

    def onward(self, w, t, act):
        z = self.order[t]

        @pl.when((z < self.f) & (self.f < 3))
        def _():
            act(self.hop(w, z, 1))

        @pl.when((z > self.f) & (self.f > 0))
        def _():
            act(self.hop(w, z, -1))

    def relay(self, w, hops):
        outer = (self.f == 0) | (self.f == 3)
        inner = (self.f > 0) & (self.f < 3)
        if hops == 0:
            self.one(w, 0)
            pl.when(inner)(lambda: self.one(w, 1))
        elif hops == 1:
            pl.when(outer)(lambda: self.one(w, 1))
            pl.when(inner)(lambda: self.one(w, 2))
        else:
            pl.when(outer)(lambda: self.one(w, 2))

    def one(self, w, t):
        z = self.order[t]
        self.hop(w, z, 1).wait_recv()
        self.onward(w, t, lambda copy: copy.start())
        self.beside(w, z, 0).start()
        self.beside(w, z, 1).start()
        self.cross(w, z).start()

    def pass_on(self, w, t):
        z = self.order[t]
        for i in range(2):
            self.beside(w, z, i, False).wait_recv()
        self.cross(w, z, False).start()

    def complete(self, w):
        for z in self.order:
            self.cross(w, z).wait_recv()
            self.cross(w, z, False).wait_recv()

    def empty(self, w):
        src = self.shards[w].at[self.quarter(w, 0)]

        @pl.when(self.f < 3)
        def _():
            self.hop(w, self.f, 1, src).wait_send()

        @pl.when(self.f > 0)
        def _():
            self.hop(w, self.f, -1, src).wait_send()

        for t in range(3):
            z = self.order[t]
            self.onward(w, t, lambda copy: copy.wait_send())
            self.beside(w, z, 0).wait_send()
            self.beside(w, z, 1).wait_send()
            self.cross(w, z).wait_send()
            self.cross(w, z, False).wait_send()

    def drain(self, w):
        for k in (1, 2, 3):
            self.along(w, k).wait_send()
        for z in self.order:
            for i in range(3):
                self.over(w, z, i).wait_send()
            self.across(w, z).wait_send()


class Loads:
    def __init__(self, slots, sems, pieces, f):
        self.slots, self.sems, self.pieces, self.f = slots, sems, pieces, f

    def copies(self, i):
        n = i % self.slots.shape[0]
        full, shard, what, spot = self.pieces[i]
        slot = self.slots.at[n]
        if what == "columns":
            lanes = slice(spot * D, (spot + 1) * D)
            out = [(shard.at[:, lanes], slot.at[pl.ds(pl.multiple_of(self.f * 192, 16), 192)], None)]
            for k in (1, 2, 3):
                rows = pl.ds(pl.multiple_of(lax.rem(self.f + k, 4) * 192, 16), 192)
                out.append((full.at[rows, lanes], slot.at[rows], None))
        elif what == "wide":
            core, high = spot
            out = []
            for x in range(2):
                start = pl.multiple_of(((high * 2 + x) * 2 + core) * 384, 128)
                lanes, at = pl.ds(start, 384), slice(x * 384, (x + 1) * 384)
                out.append((shard.at[:, lanes], slot.at[pl.ds(pl.multiple_of(self.f * 192, 16), 192), at], None))
                for k in (1, 2, 3):
                    rows = pl.ds(pl.multiple_of(lax.rem(self.f + k, 4) * 192, 16), 192)
                    out.append((full.at[rows, lanes], slot.at[rows, at], None))
        else:
            core, high = spot
            out = []
            for x in range(2):
                z = high * 2 + x
                at = slot.at[x * 384 : (x + 1) * 384]
                here = shard.at[pl.ds(pl.multiple_of(core * 384, 16), 384)]
                there = full.at[pl.ds(pl.multiple_of(z * 768 + core * 384, 16), 384)]
                out += [(here, at, self.f == z), (there, at, self.f != z)]
        return [
            (pltpu.make_async_copy(src, dst, self.sems.at[n, k]), when) for k, (src, dst, when) in enumerate(out)
        ]

    def each(self, i, act):
        for copy, when in self.copies(i):
            if when is None:
                act(copy)
            else:
                pl.when(when)(lambda copy=copy: act(copy))

    def start(self, i):
        self.each(i, lambda copy: copy.start())

    def get(self, i):
        self.each(i, lambda copy: copy.wait())
        return self.slots[i % self.slots.shape[0]]


ALL = slice(None)


def squares(fulls, shards, w, count):
    return [(fulls[w], shards[w], "columns", i) for i in range(count)]


def forward_kernel(*refs):
    (video, class_token, frame_clip, patch_clip, padding, vectors, expand_bias, grad_output, grad_class_out) = refs[:9]
    shards = refs[9:16]
    outs = refs[16:44]
    (output, class_output) = outs[:2]
    fulls = outs[2:9]
    saved_out = outs[9:20] + outs[20:22] + outs[24:26]
    act_sib, gh_sib, sums, small_out = outs[22], outs[23], outs[26], outs[27]
    (send, recv, vec, vec32, vsend, vrecv, slots, slot_sems, a2s, a2r, asend, arecv, tbias, sbias, spare,
     rows_f, acc, acc2, hid, gact, cls, csend, crecv, psend, precv, act_go, gh_go, vec_go,
     x_t, n_t, j_t, m_t, o_t, x_s, n_s, j_s, m_s, n_f, cot, act, gh, gmid, gb, save_sems) = refs[44:]
    made = (x_t, n_t, j_t, m_t, o_t, x_s, n_s, j_s, m_s, n_f, cot, act, gh, gmid, gb)
    X_T, N_T, J_T, M_T, O_T, X_S, N_S, J_S, M_S, N_F, COT, ACT, GH, GMID, GB = range(15)

    def save(k):
        return pltpu.make_async_copy(made[k], saved_out[k], save_sems.at[k])


    net = Spread(shards, fulls, send, recv)
    s, f, core = net.s, net.f, net.core
    net.greet()

    def vec_copy(k):
        return remote(vec_go, vec.at[f], vsend.at[k - 1], vrecv.at[f], (s, lax.rem(f + k, 4)))

    vec_go[0:16, 0:192] = vectors[...]
    vec_go[0:16, 192:D] = jnp.zeros((16, D - 192), bf16)
    wide = expand_bias[...].astype(f32)
    wide = jnp.concatenate([wide[i : i + 1] for i in range(6)], axis=1)
    vec_go[16:32] = jnp.broadcast_to(wide, (16, D)).astype(bf16)
    for k in (1, 3, 2):
        vec_copy(k).start()
    net.start(0)
    vec[f] = vec_go[...]

    x_t[384:TIME_ROWS] = jnp.zeros((TIME_ROWS - 384, D), bf16)
    x_t[0 : HERE * FRAMES] = video[...]
    save(X_T).start()
    time_bias(frame_clip, tbias)
    net.fan(0, (0,))
    for k in (1, 3, 2):
        z = lax.rem(f + k, 4)
        remote(vec_go, vec.at[z], vsend.at[0], vrecv.at[z], (s, z)).wait_recv()
    small = jnp.zeros((16, D), f32)
    for z in range(4):
        r, c = iota((192, D), 0), iota((192, D), 1) - z * 192
        small += dot(vec[z, 0:16, 0:192], picks(c == r))
        vec32[1 + z] = vec[z, 16:32].astype(f32)
    vec32[0] = small
    small_out[...] = small
    net.fan(0, (1,))

    def vector(i):
        return vec32[0, i : i + 1, :]

    gain, shift = vector(0), vector(1)

    def norm_time(rows):
        scaled, unused = normed(x_t[rows].astype(f32))
        n_t[rows] = (scaled * gain + shift).astype(bf16)

    over_blocks(5, 80, norm_time)
    save(N_T).start()
    net.start(1)
    net.start(2)
    net.fan(0, (2,))
    net.start(3)
    net.off(4)
    net.off(5)

    cot[...] = dot(from_twos(), grad_output[...].reshape(OWN * PATCHES, D)).astype(bf16)
    at_class = iota((16, D), 0) == CLASS - 192
    tail = jnp.where(at_class, grad_class_out[...].astype(f32), cot[192:FRAME].astype(f32))
    cot[192:FRAME] = tail.astype(bf16)
    save(COT).start()
    space_bias(patch_clip, padding, spare, sbias)

    pieces = []
    for w, count in ((0, 3), (1, 1), (2, 1), (3, 3), (4, 1)):
        pieces += squares(fulls, shards, w, count)
    for c, high in ((1 - core, 0), (1 - core, 1), (core, 0), (core, 1)):
        pieces += [(fulls[5], shards[5], "wide", (c, high)), (fulls[6], shards[6], "tall", (c, high))]
    loads = Loads(slots, slot_sems, pieces, f)

    net.lend(0)
    net.fan(1)
    net.fan(2)
    net.finish(0)
    for i in range(3):
        loads.start(i)
    for i in range(3):
        j_t[:, i * D : (i + 1) * D] = dot(n_t[...], loads.get(i)).astype(bf16)
    save(J_T).start()
    net.fan(3, (0, 1))
    attend_time(j_t, tbias, m_t, 5, TIME_BLOCK, 6)
    net.fan(3, (2,))
    net.lend(1)
    net.lend(2)
    net.relay(4, 0)
    net.finish(1)
    loads.start(3)
    net.finish(2)
    loads.start(4)
    net.relay(5, 0)
    o_t[...] = (dot(m_t[...], loads.get(3)) + vector(2)).astype(bf16)
    save(M_T).start()
    save(O_T).start()
    after = (x_t[...].astype(f32) + (dot(o_t[...], loads.get(4)) + vector(3))).astype(bf16)
    a2s[...] = dot(to_frames(), after).astype(bf16).reshape(4, SLOT, D)

    def a_copy(k):
        z = lax.rem(f + k, 4)
        return remote(a2s.at[z], a2r.at[f], asend.at[k - 1], arecv.at[f], (s, z))

    for k in (1, 3, 2):
        a_copy(k).start()
    net.off(6)
    a2r[f] = a2s[f]
    net.relay(4, 1)
    net.lend(3)
    net.finish(3)
    for i in range(5, 8):
        loads.start(i)
    net.relay(4, 2)
    net.relay(5, 1)
    for k in (1, 3, 2):
        z = lax.rem(f + k, 4)
        with jax.named_scope("a_wait"):
            remote(a2s.at[z], a2r.at[z], asend.at[0], arecv.at[z], (s, z)).wait_recv()
    net.relay(6, 0)

    spread_rows = dot(to_tokens(), a2r[...].reshape(4 * SLOT, D))
    r = iota((SPACE_ROWS, D), 0)
    is_class = (r == CLASS) | (r == FRAME + CLASS)
    x_s[...] = jnp.where(is_class, class_token[...].astype(f32), spread_rows).astype(bf16)
    gain, shift = vector(4), vector(5)

    def norm_space(rows):
        scaled, unused = normed(x_s[rows].astype(f32))
        n_s[rows] = (scaled * gain + shift).astype(bf16)

    over_blocks(13, 32, norm_space)
    save(X_S).start()
    save(N_S).start()
    for i in range(3):
        j_s[:, i * D : (i + 1) * D] = dot(n_s[...], loads.get(5 + i)).astype(bf16)
    save(J_S).start()
    for i in range(3):
        net.pass_on(4, i)
    net.relay(5, 2)
    attend_space(j_s, sbias, m_s, OWN, FRAME, 6)
    net.relay(6, 1)
    net.complete(4)
    loads.start(8)
    rows_f[...] = dot(m_s[...], loads.get(8)) + vector(6)
    save(M_S).start()
    token = class_token[...].astype(f32)
    cls[f] = jnp.broadcast_to(
        rows_f[CLASS : CLASS + 1] + rows_f[FRAME + CLASS : FRAME + CLASS + 1], (8, D)
    )

    def c_copy(k):
        return remote(cls.at[f], cls.at[f], csend.at[k - 1], crecv.at[f], (s, lax.rem(f + k, 4)))

    for k in (1, 3, 2):
        c_copy(k).start()
    for i in range(3):
        net.pass_on(5, i)
    net.relay(6, 2)
    for k in (1, 3, 2):
        z = lax.rem(f + k, 4)
        remote(cls.at[f], cls.at[z], csend.at[0], crecv.at[z], (s, z)).wait_recv()
    mid = token + ((cls[0] + cls[1]) + (cls[2] + cls[3]))[0:1] * (1.0 / FRAMES)
    gain, shift = vector(7), vector(8)
    first = jnp.where(f == 0, 1.0, 0.0)

    def norm_feed(rows):
        r = iota((32, D), 0) + rows.start
        at_class = r == CLASS
        other = r == FRAME + CLASS
        values = x_s[rows].astype(f32) + rows_f[rows]
        values = jnp.where(at_class, mid, jnp.where(other, 0.0, values))
        rows_f[rows] = values
        scaled, unused = normed(values)
        n_f[rows] = (scaled * gain + shift).astype(bf16)
        acc[rows] = values + vector(9)
        acc2[rows] = jnp.zeros((32, D), f32)

    over_blocks(13, 32, norm_feed)
    save(N_F).start()
    net.complete(5)
    loads.start(9)
    for i in range(3):
        net.pass_on(6, i)

    def sib_copy(k, half, src, dst):
        return remote(src.at[half], dst.at[half], psend.at[k, half], precv.at[k, half], (net.sib, f))

    for j in range(4):
        c = 1 - core if j < 2 else core
        high = j & 1
        bias = jnp.concatenate(
            [vec32[1 + 2 * high + x, 0:1, pl.ds(pl.multiple_of(c * 384, 128), 384)] for x in range(2)], axis=1
        )
        w1 = loads.get(9 + 2 * j)
        hid[...] = dot(n_f[...], w1) + bias
        if j == 0:
            net.complete(6)
            for i in (10, 11, 12):
                loads.start(i)
        w2 = loads.get(10 + 2 * j)
        gact[...] = dot_nt(cot[...], w2)
        act_to, gh_to = (act_go, gh_go) if j < 2 else (act, gh)

        def feed(rows):
            hidden = hid[rows]
            tail = 0.5 + 0.5 * lax.erf(hidden * 0.7071067811865476)
            slope = tail + hidden * (jnp.exp(hidden * hidden * -0.5) * 0.3989422804014327)
            act_to[high, rows] = (hidden * tail).astype(bf16)
            gh_to[high, rows] = (gact[rows] * slope).astype(bf16)

        over_blocks(13, 32, feed)
        acc[...] += dot(act_to[high], w2)
        acc2[...] += dot_nt(gh_to[high], w1)
        for i in (13 + 2 * j, 14 + 2 * j):
            if i < 17:
                loads.start(i)

        at_class = iota((16, D), 0) == CLASS - 192
        for ref in (act_to, gh_to):
            piece = ref[high, 192:FRAME].astype(f32)
            ref[high, 192:FRAME] = jnp.where(at_class, piece * first, piece).astype(bf16)
        if j < 2:
            sib_copy(0, high, act_go, act_sib).start()
            sib_copy(1, high, gh_go, gh_sib).start()

    save(ACT).start()
    save(GH).start()

    twos = dot(to_twos(), acc[...].astype(bf16)).astype(bf16)
    output[...] = twos.reshape(PATCHES, OWN, D)
    class_output[...] = acc[CLASS : CLASS + 1].astype(bf16)
    gain = vector(7)
    sums[...] = jnp.zeros_like(sums)

    def feed_back(rows):
        r = iota((32, D), 0) + rows.start
        scaled, scale = normed(rows_f[rows])
        pulled = acc2[rows]
        counted = jnp.where(r == CLASS, pulled * first, pulled)
        sums[0:8] += jnp.sum((counted * scaled).reshape(4, 8, D), axis=0)
        sums[8:16] += jnp.sum(counted.reshape(4, 8, D), axis=0)
        up = pulled * gain
        back = scale * (
            up - jnp.mean(up, axis=-1, keepdims=True) - scaled * jnp.mean(up * scaled, axis=-1, keepdims=True)
        )
        grad = cot[rows].astype(f32) + back
        gmid[rows] = grad
        gb[rows] = grad.astype(bf16)

    over_blocks(13, 32, feed_back)
    row = (gmid[CLASS : CLASS + 1] * (1.0 / FRAMES)).astype(bf16).astype(f32)
    for start in (192, FRAME + 192):
        piece = gb[start : start + 16].astype(f32)
        gb[start : start + 16] = jnp.where(at_class, row, piece).astype(bf16)

    save(GMID).start()
    save(GB).start()
    for half in range(2):
        for k, src, dst in ((0, act_go, act_sib), (1, gh_go, gh_sib)):
            sib_copy(k, half, src, dst).wait()
    for k in (1, 2, 3):
        vec_copy(k).wait_send()
        a_copy(k).wait_send()
        c_copy(k).wait_send()
    for k in range(15):
        save(k).wait()
    for w in range(4):
        net.drain(w)
    for w in range(4, 7):
        net.empty(w)


def forward(video, class_token, frame_clip, patch_clip, padding, vectors, expand_bias, grad_output, grad_class_out, shards):
    vm = pl.BlockSpec(memory_space=pltpu.VMEM)
    sm = pl.BlockSpec(memory_space=pltpu.SMEM)
    hbm = pl.BlockSpec(memory_space=pl.ANY)
    sds = jax.ShapeDtypeStruct
    sem = pltpu.SemaphoreType.DMA
    v = pltpu.VMEM
    t, p = TIME_ROWS, SPACE_ROWS
    outs = [sds((PATCHES, OWN, D), bf16), sds((1, D), bf16)]
    outs += [sds((4 * a.shape[0], a.shape[1]), bf16) for a in shards]
    outs += [sds((t, D), bf16), sds((t, D), bf16), sds((t, 3 * D), bf16), sds((t, D), bf16), sds((t, D), bf16)]
    outs += [sds((p, D), bf16), sds((p, D), bf16), sds((p, 3 * D), bf16), sds((p, D), bf16), sds((p, D), bf16)]
    outs += [sds((p, D), bf16)] + [sds((2, p, D), bf16)] * 4 + [sds((p, D), f32), sds((p, D), bf16), sds((16, D), f32), sds((16, D), f32)]
    return pl.pallas_call(
        forward_kernel,
        out_shape=outs,
        in_specs=[vm, vm, sm, vm, vm, vm, vm, vm, vm] + [hbm] * 7,
        out_specs=[vm, vm] + [hbm] * 7 + [hbm] * 17 + [vm] * 2,
        scratch_shapes=[
            sem((UNITS, 24)),
            sem((UNITS, 5, 4)),
            v((4, 32, D), bf16),
            v((5, 16, D), f32),
            sem((3,)),
            sem((4,)),
            v((4, D, D), bf16),
            sem((4, 8)),
            v((4, SLOT, D), bf16),
            v((4, SLOT, D), bf16),
            sem((3,)),
            sem((4,)),
            v((8, 2 * TIME_BLOCK), f32),
            v((FRAME, 2 * FRAME), f32),
            v((16, 512), jnp.int32),
            v((p, D), f32),
            v((p, D), f32),
            v((p, D), f32),
            v((p, D), f32),
            v((p, D), f32),
            v((4, 8, D), f32),
            sem((3,)),
            sem((4,)),
            sem((2, 2)),
            sem((2, 2)),
            v((2, p, D), bf16),
            v((2, p, D), bf16),
            v((32, D), bf16),
            v((t, D), bf16),
            v((t, D), bf16),
            v((t, 3 * D), bf16),
            v((t, D), bf16),
            v((t, D), bf16),
            v((p, D), bf16),
            v((p, D), bf16),
            v((p, 3 * D), bf16),
            v((p, D), bf16),
            v((p, D), bf16),
            v((p, D), bf16),
            v((2, p, D), bf16),
            v((2, p, D), bf16),
            v((p, D), f32),
            v((p, D), bf16),
            sem((15,)),
        ],
        compiler_params=pltpu.CompilerParams(
            collective_id=1, has_side_effects=True, vmem_limit_bytes=63 << 20
        ),
        name="forward",
    )(video, class_token, frame_clip, patch_clip, padding, vectors, expand_bias, grad_output, grad_class_out, *shards)


class Reduce:
    def __init__(self, parts, ra, rb, ra2, rb2, rz, total, rc, sems):
        self.parts, self.ra, self.rb, self.ra2, self.rb2 = parts, ra, rb, ra2, rb2
        self.rz, self.total, self.rc, self.sems = rz, total, rc, sems
        self.s, self.f, self.core, self.col, self.row = place()
        s = self.s
        self.sib = s + 1 - 2 * self.core
        self.across, self.down = s + 2 - 4 * self.col, s + 4 - 8 * self.row

    def greet(self):
        bar = pltpu.get_barrier_semaphore()
        targets = [(t, self.f) for t in (self.sib, self.across, self.down)]
        targets += [(self.s, lax.rem(self.f + j, 4)) for j in (1, 2, 3)]
        for t in targets:
            pl.semaphore_signal(bar, inc=1, device_id=t, device_id_type=MESH)
        pl.semaphore_wait(bar, len(targets))

    def sem(self, w, i):
        return self.sems.at[w, i]

    def copies1(self, w):
        g = self.parts[w]
        return (
            remote(g.at[:, 1 - self.col, 0], self.ra[w], self.sem(w, 0), self.sem(w, 1), (self.across, self.f)),
            remote(g.at[1 - self.row, :, 1], self.rb[w], self.sem(w, 2), self.sem(w, 3), (self.down, self.f)),
        )

    def copies2(self, w):
        return (
            remote(self.ra[w].at[1 - self.row], self.ra2[w], self.sem(w, 4), self.sem(w, 5), (self.down, self.f)),
            remote(self.rb[w].at[1 - self.col], self.rb2[w], self.sem(w, 6), self.sem(w, 7), (self.across, self.f)),
        )

    def block(self, w, z):
        g = self.parts[w]
        rows = g.shape[3] // 2
        return g.at[z // 2, 1 - self.col, 0, pl.ds(pl.multiple_of(lax.rem(z, 2) * rows, 16), rows), :]

    def copies3(self, w):
        out = []
        for j in (1, 3, 2):
            z = lax.rem(self.f + j, 4)
            out.append(
                remote(self.block(w, z), self.rz[w].at[3 - j], self.sem(w, 7 + j), self.sem(w, 14 - j), (self.s, z))
            )
        return out

    def copy4(self, w):
        return remote(
            self.total[w].at[1 - self.core], self.rc[w], self.sem(w, 14), self.sem(w, 15), (self.sib, self.f)
        )

    def step1(self, w):
        for c in self.copies1(w):
            c.start()

    def step2(self, w):
        a, b = self.copies1(w)
        g, ra, rb = self.parts[w], self.ra[w], self.rb[w]
        row, col = self.row, self.col
        a2, b2 = self.copies2(w)
        a.wait_recv()
        ra[1 - row] = (ra[1 - row].astype(f32) + g[1 - row, col, 0].astype(f32)).astype(bf16)
        a2.start()
        b.wait_recv()
        rb[1 - col] = (rb[1 - col].astype(f32) + g[row, 1 - col, 1].astype(f32)).astype(bf16)
        b2.start()

    def step3(self, w):
        a, b = self.copies1(w)
        a2, b2 = self.copies2(w)
        g = self.parts[w]
        row, col = self.row, self.col
        part = g.shape[3] // 4
        a.wait_send()
        b2.wait_recv()
        a2.wait_recv()
        for z in range(4):
            rows = pl.ds(z * part, part)
            sums = []
            for k, near, far in ((0, self.ra[w].at[row], self.ra2[w]), (1, self.rb[w].at[col], self.rb2[w])):
                own = g.at[row, col, k]
                if part % 16:
                    tops = z * part // 16 * 16
                    high = -(-(z + 1) * part // 16) * 16
                    wide = [ref[tops:high].astype(f32) for ref in (own, near, far)]
                    low = z * part - tops
                    sums.append((wide[0] + wide[1] + wide[2])[low : low + part])
                else:
                    sums.append(own[rows].astype(f32) + near[rows].astype(f32) + far[rows].astype(f32))
            at = self.block(w, z)
            at[...] = jnp.concatenate(sums, axis=0).astype(bf16)
        for c in self.copies3(w):
            c.start()

    def step4(self, w, swap=True):
        for c in self.copies3(w):
            c.wait_recv()
        rz, part = self.rz[w], self.parts[w].shape[3] // 4
        whole = (self.block(w, self.f)[...].astype(f32) + rz[0].astype(f32)) + (
            rz[1].astype(f32) + rz[2].astype(f32)
        )
        self.total[w][0] = whole[:part]
        self.total[w][1] = whole[part:]
        if swap:
            self.copy4(w).start()

    def step5(self, w):
        self.copy4(w).wait_recv()

    def drain(self, w, swap=True):
        a, b = self.copies1(w)
        b.wait_send()
        for c in list(self.copies2(w)) + self.copies3(w) + ([self.copy4(w)] if swap else []):
            c.wait_send()


REDUCE, EXPAND, SPACE_OUT, SPACE_JOIN, MIX, TIME_OUT, TIME_JOIN, NARROW = range(8)
PARTS = ((384, 384), (96, 1536), (96, 384), (96, 1152), (96, 384), (96, 384), (96, 1152), (96, 128))


def backward_kernel(*refs):
    (frame_clip, patch_clip, padding, vec, sums) = refs[:5]
    stored = refs[5:18]
    act, gh, act_sib, gh_sib = refs[18:22]
    fulls, shards = refs[22:27], refs[27:32]
    (d_video, d_class, d_reduce, d_expand, d_so, d_sp, d_tm, d_to, d_tp, d_narrow) = refs[32:42]
    (parts, ra, rb, ra2, rb2, rz, total, rc, rsems, slots, slot_sems, act_v, gh_v, feed_sems, tbias, sbias, spare,
     gsm, wide, gat, gto, gtm, a2s, a2r, asend, arecv, cls, csend, crecv, bias_col, vt,
     n_f2, cot2, m_s2, gb2, n_s2, gjs2, o_t2, gat2, m_t2, gto2, n_t2, gjt2, xsend, xrecv,
     x_t, n_t, j_t, m_t, o_t, x_s, n_s, j_s, m_s, n_f, cot, gmid, gb, take_sems) = refs[42:]
    taken = (x_t, n_t, j_t, m_t, o_t, x_s, n_s, j_s, m_s, n_f, cot, gmid, gb)
    X_T, N_T, J_T, M_T, O_T, X_S, N_S, J_S, M_S, N_F, COT, GMID, GB = range(13)

    def take(k):
        return pltpu.make_async_copy(stored[k], taken[k], take_sems.at[k])

    for k in (COT, N_F):
        take(k).start()

    red = Reduce(parts, ra, rb, ra2, rb2, rz, total, rc, rsems)
    s, f, core, sib = red.s, red.f, red.core, red.sib
    red.greet()

    def half_of(ref, wide_half, which):
        return ref.at[:, pl.ds(pl.multiple_of(which * wide_half, 128), wide_half)]

    exchange = [
        (stored[COT], cot2), (stored[N_F], n_f2), (stored[M_S], m_s2), (half_of(stored[GB], 384, 1 - core), gb2),
        (stored[N_S], n_s2), (stored[O_T], o_t2), (stored[M_T], m_t2), (stored[N_T], n_t2),
    ]
    gjs = act_v.at[:, 0 : 3 * D]
    gjt = gh_v.at[0:TIME_ROWS, 0 : 3 * D]
    exchange += [
        (half_of(gjs, 1152, 1 - core), gjs2), (half_of(gat, 384, 1 - core), gat2),
        (half_of(gto, 384, 1 - core), gto2), (half_of(gjt, 1152, 1 - core), gjt2),
    ]
    GJS, GAT, GTO, GJT = 8, 9, 10, 11

    def trade(k):
        src, dst = exchange[k]
        return remote(src, dst, xsend.at[k], xrecv.at[k], (sib, f))

    loads_feed = []
    for k, (src, dst, at) in enumerate(
        ((act, act_v, 0), (act_sib, act_v, 2), (gh, gh_v, 0), (gh_sib, gh_v, 2))
    ):
        for half in range(2):
            lanes = slice((at + half) * D, (at + half + 1) * D)
            loads_feed.append(pltpu.make_async_copy(src.at[half], dst.at[:, lanes], feed_sems.at[2 * k + half]))
    for c in loads_feed:
        c.start()
    for k in (M_S, GB, J_S, X_S, GMID, N_S, O_T, M_T, J_T, N_T, X_T):
        take(k).start()
    for k in range(8):
        trade(k).start()
    pieces = []
    for w, count in ((4, 1), (3, 3), (2, 1), (1, 1), (0, 3)):
        pieces += squares(fulls, shards, w, count)
    loads = Loads(slots, slot_sems, pieces, f)
    for i in range(3):
        loads.start(i)
    time_bias(frame_clip, tbias)
    space_bias(patch_clip, padding, spare, sbias)

    first = jnp.where(f == 0, 1.0, 0.0)
    vt[...] = jnp.zeros_like(vt)
    counts = jnp.where(iota((16, SPACE_ROWS), 1) == CLASS, first, 1.0).astype(bf16)
    ones_s = jnp.ones((16, SPACE_ROWS), bf16)
    ones_t = jnp.ones((16, TIME_ROWS), bf16)
    vt[7:8] = jnp.sum(sums[0:8], axis=0, keepdims=True)
    vt[8:9] = jnp.sum(sums[8:16], axis=0, keepdims=True)
    take(COT).wait()
    vt[9:10] = dot(counts, cot[...])[0:1]

    for c in loads_feed[:4]:
        c.wait()
    trade(0).wait_recv()
    for y in range(2):
        grad = dot_tn(act_v[:, y * D : (y + 1) * D], cot[...]) + dot_tn(act_v[:, (2 + y) * D : (3 + y) * D], cot2[...])
        for x in range(2):
            for k in range(2):
                parts[REDUCE][y, x, k] = grad[x * 384 : (x + 1) * 384, k * 384 : (k + 1) * 384].astype(bf16)
    red.step1(REDUCE)
    for c in loads_feed[4:]:
        c.wait()
    take(N_F).wait()
    trade(1).wait_recv()

    def put(w, lanes, grad):
        for y in range(2):
            for x in range(2):
                for k in range(2):
                    start = ((y * 2 + x) * 2 + k) * 96
                    parts[w][y, x, k, :, lanes] = grad[start : start + 96].astype(bf16)

    for y in range(2):
        own, other = gh_v[:, y * D : (y + 1) * D], gh_v[:, (2 + y) * D : (3 + y) * D]
        grad = dot_tn(n_f[...], own) + dot_tn(n_f2[...], other)
        put(EXPAND, slice(y * D, (y + 1) * D), grad)
        ones = jnp.ones((SPACE_ROWS, 128), bf16)
        bias_col[y] = dot_tn(own, ones) + dot_tn(other, ones)
    red.step1(EXPAND)

    for k in (M_S, GB, J_S, X_S, GMID):
        take(k).wait()
    vt[6:7] = dot(ones_s, gb[...])[0:1]
    trade(2).wait_recv()
    trade(3).wait_recv()
    mine = half_of(gb, 384, core)
    put(SPACE_OUT, ALL, dot_tn(m_s[...], mine[...]) + dot_tn(m_s2[...], gb2[...]))
    red.step1(SPACE_OUT)
    gsm[...] = dot_nt(gb[...], loads.get(0)).astype(bf16)
    loads.start(3)
    attend_back(j_s, sbias, gsm, gjs, OWN, FRAME, 3)
    trade(GJS).start()
    red.step2(REDUCE)
    wide[...] = dot_nt(gjs[:, 0:D], loads.get(1))
    loads.start(4)
    wide[...] += dot_nt(gjs[:, D : 2 * D], loads.get(2))
    loads.start(5)
    wide[...] += dot_nt(gjs[:, 2 * D : 3 * D], loads.get(3))
    loads.start(6)
    gain = vec[4:5]

    def norm_back(source, gain, at, size, rows):
        scaled, scale = normed(source[rows].astype(f32))
        pulled = wide[rows]
        vt[at : at + 8] += jnp.sum((pulled * scaled).reshape(size // 8, 8, D), axis=0)
        vt[at + 8 : at + 16] += jnp.sum(pulled.reshape(size // 8, 8, D), axis=0)
        up = pulled * gain
        return scale * (
            up - jnp.mean(up, axis=-1, keepdims=True) - scaled * jnp.mean(up * scaled, axis=-1, keepdims=True)
        )

    def space_back(rows):
        back = norm_back(x_s, gain, 16, 32, rows)
        wide[rows] = back
        gsm[rows] = (gmid[rows] + back).astype(bf16)

    over_blocks(13, 32, space_back)
    a2s[...] = dot(from_tokens(), gsm[...]).astype(bf16).reshape(4, SLOT, D)

    def a_copy(k):
        z = lax.rem(f + k, 4)
        return remote(a2s.at[z], a2r.at[f], asend.at[k - 1], arecv.at[f], (s, z))

    for k in (1, 3, 2):
        a_copy(k).start()
    a2r[f] = a2s[f]
    cls[f] = jnp.broadcast_to(wide[CLASS : CLASS + 1] + wide[FRAME + CLASS : FRAME + CLASS + 1], (8, D))

    def c_copy(k):
        return remote(cls.at[f], cls.at[f], csend.at[k - 1], crecv.at[f], (s, lax.rem(f + k, 4)))

    for k in (1, 3, 2):
        c_copy(k).start()
    take(N_S).wait()
    trade(4).wait_recv()
    trade(GJS).wait_recv()
    mine = half_of(gjs, 1152, core)
    put(SPACE_JOIN, ALL, dot_tn(n_s[...], mine[...]) + dot_tn(n_s2[...], gjs2[...]))
    red.step1(SPACE_JOIN)
    red.step2(EXPAND)
    for k in (1, 3, 2):
        z = lax.rem(f + k, 4)
        with jax.named_scope("a_wait"):
            remote(a2s.at[z], a2r.at[z], asend.at[0], arecv.at[z], (s, z)).wait_recv()

    gat[...] = dot(to_patches(), a2r[...].reshape(4 * SLOT, D)).astype(bf16)
    trade(GAT).start()
    gto[...] = dot_nt(gat[...], loads.get(4)).astype(bf16)
    loads.start(7)
    trade(GTO).start()
    gtm[...] = dot_nt(gto[...], loads.get(5)).astype(bf16)
    loads.start(8)
    red.step2(SPACE_OUT)
    red.step3(REDUCE)
    for k in (O_T, M_T, J_T, N_T, X_T):
        take(k).wait()
    attend_back(j_t, tbias, gtm, gjt, 5, TIME_BLOCK, 6)
    trade(GJT).start()
    red.step2(SPACE_JOIN)
    trade(5).wait_recv()
    trade(GAT).wait_recv()
    mine = half_of(gat, 384, core)
    put(MIX, ALL, dot_tn(o_t[...], mine[...]) + dot_tn(o_t2[...], gat2[...]))
    red.step1(MIX)
    trade(6).wait_recv()
    trade(GTO).wait_recv()
    mine = half_of(gto, 384, core)
    put(TIME_OUT, ALL, dot_tn(m_t[...], mine[...]) + dot_tn(m_t2[...], gto2[...]))
    red.step1(TIME_OUT)
    trade(7).wait_recv()
    trade(GJT).wait_recv()
    mine = half_of(gjt, 1152, core)
    put(TIME_JOIN, ALL, dot_tn(n_t[...], mine[...]) + dot_tn(n_t2[...], gjt2[...]))
    red.step1(TIME_JOIN)
    red.step3(EXPAND)
    red.step3(SPACE_OUT)
    rows = pl.ds(0, TIME_ROWS)
    wide[rows] = dot_nt(gjt[:, 0:D], loads.get(6))
    wide[rows] += dot_nt(gjt[:, D : 2 * D], loads.get(7))
    wide[rows] += dot_nt(gjt[:, 2 * D : 3 * D], loads.get(8))
    gain = vec[0:1]

    def time_back(rows):
        back = norm_back(x_t, gain, 32, 80, rows)
        wide[rows] = gat[rows].astype(f32) + back

    over_blocks(5, 80, time_back)
    d_video[...] = wide[0 : HERE * FRAMES]
    vt[3:4] = dot(ones_t, gat[...])[0:1]
    vt[2:3] = dot(ones_t, gto[...])[0:1]
    for row, at in ((4, 16), (5, 24), (0, 32), (1, 40)):
        vt[row : row + 1] = jnp.sum(vt[at : at + 8], axis=0, keepdims=True)
    place_at = picks(iota((16, 128), 0) == iota((16, 128), 1))
    put(NARROW, ALL, dot_tn(vt[0:16].astype(bf16), place_at))
    lane = iota((24, 128), 1)
    for y in range(2):
        for x in range(2):
            pieces = []
            for z in range(4):
                piece = jnp.zeros((24, 128), f32)
                for k in range(4):
                    column = bias_col[y, pl.ds(x * 384 + z * 96 + k, 24, stride=4), :]
                    piece = jnp.where(lane == 10 + k, column, piece)
                pieces.append(piece)
            at = parts[NARROW].at[y, x, core]
            at[...] = (at[...].astype(f32) + jnp.concatenate(pieces, axis=0)).astype(bf16)
    red.step1(NARROW)

    def place_halves(w, out, half):
        red.step5(w)
        mine = half_of(out, half, core)
        mine[...] = total[w][core]
        other = half_of(out, half, 1 - core)
        other[...] = rc[w][...]

    red.step2(MIX)
    red.step2(TIME_OUT)
    red.step3(SPACE_JOIN)
    red.step2(TIME_JOIN)
    red.step2(NARROW)
    for k in (1, 3, 2):
        z = lax.rem(f + k, 4)
        remote(cls.at[f], cls.at[z], csend.at[0], crecv.at[z], (s, z)).wait_recv()
    d_class[...] = gmid[CLASS : CLASS + 1] + ((cls[0] + cls[1]) + (cls[2] + cls[3]))[0:1]
    red.step4(REDUCE, False)
    d_reduce[:, 0:384] = total[REDUCE][0]
    d_reduce[:, 384:768] = total[REDUCE][1]
    red.step4(EXPAND)
    red.step3(MIX)
    red.step3(TIME_OUT)
    red.step4(SPACE_OUT)
    red.step5(EXPAND)
    for y in range(2):
        for x in range(2):
            lanes = slice((y * 2 + x) * 384, (y * 2 + x + 1) * 384)
            for c, piece in ((core, total[EXPAND][core]), (1 - core, rc[EXPAND][...])):
                start = pl.multiple_of(((y * 2 + x) * 2 + c) * 384, 128)
                d_expand[:, pl.ds(start, 384)] = piece[:, lanes]
    red.step3(TIME_JOIN)
    red.step3(NARROW)
    red.step4(SPACE_JOIN)
    place_halves(SPACE_OUT, d_so, 384)
    red.step4(MIX)
    red.step4(TIME_OUT)
    place_halves(SPACE_JOIN, d_sp, 1152)
    place_halves(MIX, d_tm, 384)
    place_halves(TIME_OUT, d_to, 384)
    red.step4(TIME_JOIN)
    red.step4(NARROW)
    place_halves(TIME_JOIN, d_tp, 1152)
    red.step5(NARROW)
    d_narrow[...] = total[NARROW][core] + rc[NARROW][...]
    for w in range(8):
        red.drain(w, w != REDUCE)
    for k in range(12):
        trade(k).wait_send()
    for k in (1, 2, 3):
        a_copy(k).wait_send()
        c_copy(k).wait_send()


def backward(frame_clip, patch_clip, padding, vec, saved, fulls, shards):
    (x_t, n_t, j_t, m_t, o_t, x_s, n_s, j_s, m_s, n_f, cot, act, gh, act_sib, gh_sib, gmid, gb, sums) = saved
    vm = pl.BlockSpec(memory_space=pltpu.VMEM)
    sm = pl.BlockSpec(memory_space=pltpu.SMEM)
    hbm = pl.BlockSpec(memory_space=pl.ANY)
    sds = jax.ShapeDtypeStruct
    sem = pltpu.SemaphoreType.DMA
    v = pltpu.VMEM
    t, p = TIME_ROWS, SPACE_ROWS
    return pl.pallas_call(
        backward_kernel,
        out_shape=[
            sds((HERE * FRAMES, D), f32), sds((1, D), f32), sds((96, D), f32), sds((24, 4 * D), f32), sds((24, D), f32),
            sds((24, 3 * D), f32), sds((24, D), f32), sds((24, D), f32), sds((24, 3 * D), f32), sds((24, 128), f32),
        ],
        in_specs=[sm] + [vm] * 4 + [hbm] * 27,
        out_specs=[vm] * 10,
        scratch_shapes=[
            [v((2, 2, 2, r, c), bf16) for r, c in PARTS],
            [v((2, r, c), bf16) for r, c in PARTS],
            [v((2, r, c), bf16) for r, c in PARTS],
            [v((r, c), bf16) for r, c in PARTS],
            [v((r, c), bf16) for r, c in PARTS],
            [v((3, r // 2, c), bf16) for r, c in PARTS],
            [v((2, r // 4, c), f32) for r, c in PARTS],
            [v((r // 4, c), f32) for r, c in PARTS],
            sem((8, 16)),
            v((3, D, D), bf16),
            sem((3, 8)),
            v((p, 4 * D), bf16),
            v((p, 4 * D), bf16),
            sem((8,)),
            v((8, 2 * TIME_BLOCK), f32),
            v((FRAME, 2 * FRAME), f32),
            v((16, 512), jnp.int32),
            v((p, D), bf16),
            v((p, D), f32),
            v((t, D), bf16),
            v((t, D), bf16),
            v((t, D), bf16),
            v((4, SLOT, D), bf16),
            v((4, SLOT, D), bf16),
            sem((3,)),
            sem((4,)),
            v((4, 8, D), f32),
            sem((3,)),
            sem((4,)),
            v((2, D, 128), f32),
            v((48, D), f32),
            v((p, D), bf16),
            v((p, D), bf16),
            v((p, D), bf16),
            v((p, 384), bf16),
            v((p, D), bf16),
            v((p, 1152), bf16),
            v((t, D), bf16),
            v((t, 384), bf16),
            v((t, D), bf16),
            v((t, 384), bf16),
            v((t, D), bf16),
            v((t, 1152), bf16),
            sem((12,)),
            sem((12,)),
            v((t, D), bf16),
            v((t, D), bf16),
            v((t, 3 * D), bf16),
            v((t, D), bf16),
            v((t, D), bf16),
            v((p, D), bf16),
            v((p, D), bf16),
            v((p, 3 * D), bf16),
            v((p, D), bf16),
            v((p, D), bf16),
            v((p, D), bf16),
            v((p, D), f32),
            v((p, D), bf16),
            sem((13,)),
        ],
        compiler_params=pltpu.CompilerParams(
            collective_id=2, has_side_effects=True, vmem_limit_bytes=63 << 20
        ),
        name="backward",
    )(
        frame_clip, patch_clip, padding, vec, sums, x_t, n_t, j_t, m_t, o_t, x_s, n_s, j_s, m_s, n_f, cot, gmid, gb,
        act, gh, act_sib, gh_sib, *fulls[:5], *shards[:5]
    )


def finish_kernel(*refs):
    count = (len(refs) - 12) // 2
    for src, dst in zip(refs[:count], refs[count + 1 :]):
        dst[...] = src[...]
    narrow, outs = refs[count], refs[2 * count + 1 :]
    turned = jnp.transpose(jnp.concatenate([narrow[...], jnp.zeros((104, 128), f32)], axis=0))
    for i in range(10):
        outs[i][...] = turned[i, 0:24]
    r, c = iota((128, 96), 0), iota((128, 96), 1)
    bias = jnp.zeros((8, 96), f32)
    for k in range(4):
        rows = jnp.broadcast_to(turned[10 + k : 11 + k], (8, 128))
        spread = jnp.where(c == 4 * r + k, 1.0, 0.0)
        bias += jnp.dot(rows, spread, preferred_element_type=f32, precision=lax.Precision.HIGHEST)
    outs[10][...] = bias[0]


def finish(plain, narrow):
    vm = pl.BlockSpec(memory_space=pltpu.VMEM)
    outs = [jax.ShapeDtypeStruct(a.shape, a.dtype) for a in plain]
    outs += [jax.ShapeDtypeStruct((24,), f32)] * 10 + [jax.ShapeDtypeStruct((96,), f32)]
    return pl.pallas_call(
        finish_kernel,
        out_shape=outs,
        in_specs=[vm] * (len(plain) + 1),
        out_specs=[vm] * len(outs),
        compiler_params=pltpu.CompilerParams(vmem_limit_bytes=62 << 20),
        name="finish",
    )(*plain, narrow)


def settle(share):
    count = lax.axis_size("seq")
    if count == 8:
        return share
    more = count // 8
    groups = [[low + 8 * high for high in range(more)] for low in range(8)]
    share = lax.psum_scatter(share, "seq", scatter_dimension=0, tiled=True, axis_index_groups=groups)
    moves = [
        ((high * 8 + low) * 4 + f, (low * 4 + f) * more + high)
        for high in range(more)
        for low in range(8)
        for f in range(4)
    ]
    return lax.ppermute(share, ("seq", "ft"), moves)


def shards(
    video,
    class_token,
    frame_clip,
    patch_clip,
    padding,
    time_gain,
    time_shift,
    time_project,
    time_output,
    time_output_bias,
    time_mixer,
    time_mixer_bias,
    space_gain,
    space_shift,
    space_project,
    space_output,
    space_output_bias,
    feed_gain,
    feed_shift,
    feed_expand,
    feed_expand_bias,
    feed_reduce,
    feed_reduce_bias,
    grad_output,
    grad_class_out,
):
    vectors = jnp.zeros((16, D // 4), bf16)
    row = lax.broadcasted_iota(jnp.int32, vectors.shape, 0)
    for i, item in enumerate(
        (
            time_gain,
            time_shift,
            time_output_bias,
            time_mixer_bias,
            space_gain,
            space_shift,
            space_output_bias,
            feed_gain,
            feed_shift,
            feed_reduce_bias,
        )
    ):
        vectors = jnp.where(row == i, item[None, :], vectors)
    expand_bias = feed_expand_bias.reshape(6, 128)
    weights = (time_project, time_output, time_mixer, space_project, space_output, feed_expand, feed_reduce)
    cotangent = jnp.swapaxes(grad_output[0], 0, 1)
    done = forward(
        jnp.swapaxes(video[0], 0, 1).reshape(HERE * FRAMES, D), class_token, frame_clip, patch_clip, padding, vectors, expand_bias, cotangent, grad_class_out, weights
    )
    output, class_output = jnp.swapaxes(done[0], 0, 1)[None], done[1]
    grads = backward(frame_clip, patch_clip, padding, done[27], done[9:27], done[2:9], weights)
    rows, grad_class = grads[:2]
    d_reduce, d_expand, d_so, d_sp, d_tm, d_to, d_tp, d_narrow = [settle(g) for g in grads[2:]]
    if lax.axis_size("seq") == 8:
        last = finish((done[0], class_output, rows, grad_class, d_reduce, d_expand, d_so, d_sp, d_tm, d_to, d_tp), d_narrow)
        twos, class_output, rows, grad_class, d_reduce, d_expand, d_so, d_sp, d_tm, d_to, d_tp = last[:11]
        output = jnp.swapaxes(twos, 0, 1)[None]
        narrow, d_bias = last[11:21], last[21]
    else:
        narrow = [d_narrow[:, i] for i in range(10)]
        d_bias = d_narrow[:, 10:14].reshape(-1)
    grad_video = jnp.swapaxes(rows.reshape(HERE, FRAMES, D), 0, 1)[None]
    return (
        output,
        class_output,
        grad_video,
        grad_class,
        narrow[0],
        narrow[1],
        d_tp,
        d_to,
        narrow[2],
        d_tm,
        narrow[3],
        narrow[4],
        narrow[5],
        d_sp,
        d_so,
        narrow[6],
        narrow[7],
        narrow[8],
        d_expand,
        d_bias,
        d_reduce,
        narrow[9],
    )


def solution(mesh):
    in_specs = (
        P("seq", None, "ft", None),
        P("seq", None),
        P("seq", None),
        P("seq", None),
        P("seq", None),
        P("ft"),
        P("ft"),
        P("ft", None),
        P("ft", None),
        P("ft"),
        P("ft", None),
        P("ft"),
        P("ft"),
        P("ft"),
        P("ft", None),
        P("ft", None),
        P("ft"),
        P("ft"),
        P("ft"),
        P("ft", None),
        P("ft"),
        P("ft", None),
        P("ft"),
        P("seq", "ft", None, None),
        P("seq", None),
    )
    out_specs = (
        P("seq", "ft", None, None),
        P("seq", None),
        P("seq", None, "ft", None),
        P("seq", None),
        P(("seq", "ft")),
        P(("seq", "ft")),
        P(("seq", "ft"), None),
        P(("seq", "ft"), None),
        P(("seq", "ft")),
        P(("seq", "ft"), None),
        P(("seq", "ft")),
        P(("seq", "ft")),
        P(("seq", "ft")),
        P(("seq", "ft"), None),
        P(("seq", "ft"), None),
        P(("seq", "ft")),
        P(("seq", "ft")),
        P(("seq", "ft")),
        P(("seq", "ft"), None),
        P(("seq", "ft")),
        P(("seq", "ft"), None),
        P(("seq", "ft")),
    )
    return jax.shard_map(shards, mesh=mesh, in_specs=in_specs, out_specs=out_specs, check_vma=False)
```
